32 devices in a mesh: gx: 4 (over z), gy: 2 (over core), gz: 4 (over y, x).
Axes of the slice: x: 2, y: 2, z: 4, core: 2. Of those that a mesh axis runs over, the one named last changes fastest.
Arguments:
- tokens: bfloat16 [16384, 768], P(('gx', 'gy', 'gz')), may hold values from -6 to 6
- segment_ids: int32 [8, 2048], P(('gx', 'gy')), may hold values from 0 to 15, never falling along the last dimension, each value on 1 to 1024 neighbouring positions
- valid_mask: int32 [8, 2048], P(('gx', 'gy')), may hold values from 0 to 1, as said below
- cotangent: bfloat16 [16384, 768], P(('gx', 'gy', 'gz')), may hold values from -6 to 6
- teacher: bfloat16 [16384, 768], P(('gx', 'gy', 'gz')), may hold values from -6 to 6
- w_query: bfloat16 [768, 768], P('gy', 'gz'), may hold values from -0.21875 to 0.21875
- b_query: bfloat16 [768], P('gz'), may hold values from -3 to 3
- w_key: bfloat16 [768, 768], P('gy', 'gz'), may hold values from -0.21875 to 0.21875
- w_value: bfloat16 [768, 768], P('gy', 'gz'), may hold values from -0.21875 to 0.21875
- b_value: bfloat16 [768], P('gz'), may hold values from -0.5 to 0.5
- w_out: bfloat16 [768, 768], P('gz', 'gy'), may hold values from -1.75 to 1.75
- b_out: bfloat16 [768], replicated, may hold values from -1.1953125 to 1.1953125
- norm1_gain: bfloat16 [768], replicated, may hold values from 0.5 to 1.5
- norm1_bias: bfloat16 [768], replicated, may hold values from -1.1953125 to 1.1953125
- w_up: bfloat16 [768, 3072], P('gy', 'gz'), may hold values from -0.21875 to 0.21875
- b_up: bfloat16 [3072], P('gz'), may hold values from -3 to 3
- w_down: bfloat16 [3072, 768], P('gz', 'gy'), may hold values from -0.109375 to 0.109375
- b_down: bfloat16 [768], replicated, may hold values from -1.1953125 to 1.1953125
- norm2_gain: bfloat16 [768], replicated, may hold values from 0.5 to 1.5
- norm2_bias: bfloat16 [768], replicated, may hold values from -1.1953125 to 1.1953125
Outputs:
- output: bfloat16 [16384, 768], P(('gx', 'gy', 'gz'))
- mean_loss: float32 [], replicated
- d_tokens: bfloat16 [16384, 768], P(('gx', 'gy', 'gz'))
- d_w_query: float32 [768, 768], P('gy', 'gz')
- d_b_query: float32 [768], P('gz')
- d_w_key: float32 [768, 768], P('gy', 'gz')
- d_w_value: float32 [768, 768], P('gy', 'gz')
- d_b_value: float32 [768], P('gz')
- d_w_out: float32 [768, 768], P('gz', 'gy')
- d_b_out: float32 [768], replicated
- d_norm1_gain: float32 [768], replicated
- d_norm1_bias: float32 [768], replicated
- d_w_up: float32 [768, 3072], P('gy', 'gz')
- d_b_up: float32 [3072], P('gz')
- d_w_down: float32 [3072, 768], P('gz', 'gy')
- d_b_down: float32 [768], replicated
- d_norm2_gain: float32 [768], replicated
- d_norm2_bias: float32 [768], replicated
The draws below stay inside these ranges and needn't reach their ends.
Inputs may be any that keep to these rules, and one draw needn't show every extreme that they name: `segment_ids`: within a sequence the ids never fall, and each id that occurs forms one run of 1 to 1024 positions. `valid_mask`: in each sequence the valid tokens are a leading run of 512 positions or more, padding after it.
All inputs are finite; a program needn't handle non-finite values.
Results may differ from the reference program's by a relative error of at most 0.02.
Values may be sent and summed in bfloat16 or wider, within the bound.
No kernel may reach another device: no remote copies, remote signals or barrier semaphores. Data moves between devices by JAX's collectives and lax.ppermute only.
A program may use at most 128 MiB of HBM per device.

```python
import math
import jax
import jax.numpy as jnp
import numpy as np
from jax import lax

D = 768
HEADS = 12
HEAD = 64
FF = 3072
SEGS = 16
LEN = 2048
SEQS = 8
TOKENS = 16384


def draw_valid_mask(key, part):
    seq_index = jnp.arange(SEQS, dtype=jnp.int32)
    lowest = LEN // 4 + LEN * 5 // 8 * seq_index // max(SEQS - 1, 1)
    extra = jax.random.randint(key, (SEQS,), 0, LEN // 8 + 1, dtype=jnp.int32)
    lengths = jnp.minimum(lowest + extra, LEN)
    positions = jnp.arange(LEN, dtype=jnp.int32)
    return (positions[None, :] < lengths[:, None]).astype(jnp.int32)


def level_of(rng, shape, cuts, least, high):
    level = 1.0
    for axis_at, blocks in cuts:
        draws = jax.random.uniform(jax.random.fold_in(jax.random.fold_in(rng, 6), axis_at), (blocks,), jnp.float32, least / len(cuts), high / len(cuts))
        level = level * jnp.repeat(jnp.exp(draws), shape[axis_at] // blocks).reshape((-1,) + (1,) * (len(shape) - 1 - axis_at))
    return level


def length_profile(amount, total, limit, skew):
    loads = [(1 << 20) // math.isqrt(grade ** skew) + 1 for grade in range(2, amount + 1)]
    spare, given = total - limit - (amount - 1), [1] * (amount - 1)
    while spare > 0:
        movable = [i for i in range(amount - 1) if given[i] < limit]
        whole, budget = sum([loads[i] for i in movable]), spare
        for i in movable:
            more = min(limit - given[i], max(1, budget * loads[i] // whole), spare)
            given[i] = given[i] + more
            spare = spare - more
    return np.array([limit] + given)


def ragged_sizes(rng, amount, total, bound, slope):
    if amount == 2:
        one = jax.random.randint(rng, (), max(1, total - bound), min(bound, total - 1) + 1)
        return jnp.stack([one, total - one])
    sizes = jnp.asarray(length_profile(amount, total, bound, slope), jnp.int32)
    pairs = (amount - 1) // 2
    giver, taker = sizes[1:1 + 2 * pairs:2], sizes[2:2 + 2 * pairs:2]
    slack = jnp.minimum(giver - 1, bound - taker)
    shifted = jax.random.randint(jax.random.fold_in(rng, 1), (pairs,), 0, 1 << 20) % (slack + 1)
    sizes = sizes.at[1:1 + 2 * pairs:2].set(giver - shifted).at[2:2 + 2 * pairs:2].set(taker + shifted)
    return sizes[jax.random.permutation(jax.random.fold_in(rng, 2), amount)]


def centred(stream_key, shape, scale, reach, split=(), kind=jnp.bfloat16):
    entries = scale * jax.random.normal(stream_key, shape, jnp.float32)
    if split:
        entries = entries * level_of(stream_key, shape, split, -0.22, 0.18)
    return jnp.clip(entries, -reach, reach).astype(kind)


def setup_inputs(seed: int = 0) -> dict:
    streams_of = jax.random.split(jax.random.key(seed), 21)
    return {
        "tokens": centred(streams_of[0], (TOKENS, D), 1.0, 6.0, ((0, 32),)),
        "segment_ids": jax.vmap(lambda own: jnp.searchsorted(jnp.cumsum(ragged_sizes(own, SEGS, LEN, LEN // 2, 2)), jnp.arange(LEN), side="right"))(jax.random.split(streams_of[1], SEQS)).reshape((SEQS, LEN)).astype(jnp.int32),
        "valid_mask": draw_valid_mask(jax.random.fold_in(streams_of[20], 71), 0),
        "cotangent": centred(streams_of[3], (TOKENS, D), 1.0, 6.0, ((0, 32),)),
        "teacher": centred(streams_of[4], (TOKENS, D), 1.0, 6.0, ((0, 32),)),
        "w_query": centred(streams_of[5], (D, D), D ** -0.5, 0.21875, ((0, 2), (1, 4))),
        "b_query": centred(streams_of[6], (D,), 0.5, 3.0, ((0, 4),)),
        "w_key": centred(streams_of[7], (D, D), D ** -0.5, 0.21875, ((0, 2), (1, 4))),
        "w_value": centred(streams_of[8], (D, D), D ** -0.5, 0.21875, ((0, 2), (1, 4))),
        "b_value": centred(streams_of[9], (D,), 0.08, 0.5, ((0, 4),)),
        "w_out": centred(streams_of[10], (D, D), (max(D // 64, 1)) ** -0.5, 1.75, ((0, 4), (1, 2))),
        "b_out": centred(streams_of[11], (D,), 0.2, 1.1953125),
        "norm1_gain": jnp.clip(1.0 + 0.1 * jax.random.normal(streams_of[12], (D,), jnp.float32), 0.5, 1.5).astype(jnp.bfloat16),
        "norm1_bias": centred(streams_of[13], (D,), 0.2, 1.1953125),
        "w_up": centred(streams_of[14], (D, FF), D ** -0.5, 0.21875, ((0, 2), (1, 4))),
        "b_up": centred(streams_of[15], (FF,), 0.5, 3.0, ((0, 4),)),
        "w_down": centred(streams_of[16], (FF, D), FF ** -0.5, 0.109375, ((0, 4), (1, 2))),
        "b_down": centred(streams_of[17], (D,), 0.2, 1.1953125),
        "norm2_gain": jnp.clip(1.0 + 0.1 * jax.random.normal(streams_of[18], (D,), jnp.float32), 0.5, 1.5).astype(jnp.bfloat16),
        "norm2_bias": centred(streams_of[19], (D,), 0.2, 1.1953125),
    }


@jax.custom_vjp
def low(v):
    return lax.optimization_barrier(v.astype(jnp.bfloat16)).astype(jnp.float32)

@jax.custom_vjp
def low_back(v):
    return v

def low_keep(v):
    return (low(v), None)

def low_pass(kept, grad):
    return (grad,)

def back_keep(v):
    return (v, None)

def back_low(kept, grad):
    return (low(grad),)
low.defvjp(low_keep, low_pass)
low_back.defvjp(back_keep, back_low)
HIGHEST = lax.Precision.HIGHEST
MASKED = -1e+30
EPSILON = 1e-05

def matmul(left, right):
    return jnp.dot(left, right, precision=HIGHEST)

def layer_norm(resid, gain, shift):
    average = lax.optimization_barrier(jnp.mean(resid, -1, keepdims=True))
    centered = resid - average
    spread = lax.optimization_barrier(jnp.mean(centered * centered, -1, keepdims=True))
    return centered * lax.rsqrt(spread + EPSILON) * gain + shift

def attend_block(query_block, first_row, key_rows, value_rows, seg_row, valid_row):
    block_rows = query_block.shape[0]
    query_pos = first_row + jnp.arange(block_rows, dtype=jnp.int32)
    key_pos = jnp.arange(key_rows.shape[0], dtype=jnp.int32)
    query_seg = lax.dynamic_slice_in_dim(seg_row, first_row, block_rows)
    allowed = (query_seg[:, None] == seg_row[None, :]) & ((valid_row[None, :] == 1) | (query_pos[:, None] == key_pos[None, :]))
    query_heads = query_block.reshape(block_rows, HEADS, HEAD)
    key_heads = key_rows.reshape(-1, HEADS, HEAD)
    value_heads = value_rows.reshape(-1, HEADS, HEAD)
    scores = jnp.einsum('qhd,khd->hqk', query_heads, key_heads, precision=HIGHEST) * HEAD ** (-0.5)
    scores = jnp.where(allowed[None], low_back(scores), MASKED)
    probs = jax.nn.softmax(scores, axis=-1)
    attended = jnp.einsum('hqk,khd->qhd', low(probs), value_heads, precision=HIGHEST)
    return attended.reshape(block_rows, HEADS * HEAD)

def attend_sequence(queries, key_rows, value_rows, seg_row, valid_row):
    block_rows = min(512, LEN)
    starts = jnp.arange(LEN // block_rows, dtype=jnp.int32) * block_rows
    blocks = queries.reshape(LEN // block_rows, block_rows, HEADS * HEAD)
    step_fn = jax.checkpoint(lambda block_pair: attend_block(block_pair[0], block_pair[1], key_rows, value_rows, seg_row, valid_row))
    return lax.map(step_fn, (blocks, starts)).reshape(LEN, HEADS * HEAD)

def forward(inputs_f, parameters, seg_row, valid_row):
    w_query, b_query, w_key, w_value, b_value, w_out, b_out, norm1_gain, norm1_bias, w_up, b_up, w_down, b_down, norm2_gain, norm2_bias = parameters
    queries = low(low_back(matmul(inputs_f, w_query) + b_query))
    key_rows = low(low_back(matmul(inputs_f, w_key)))
    value_rows = low(low_back(matmul(inputs_f, w_value) + b_value))
    attended = low(low_back(attend_sequence(queries, key_rows, value_rows, seg_row, valid_row)))
    mixed_rows = low_back(matmul(attended, w_out) + b_out)
    hidden = layer_norm(inputs_f + mixed_rows, norm1_gain, norm1_bias)
    preact = low_back(matmul(low(hidden), w_up) + b_up)
    activated = low(jax.nn.gelu(preact, approximate=False))
    branch = low_back(matmul(activated, w_down) + b_down)
    return layer_norm(hidden + branch, norm2_gain, norm2_bias)

def reference(tokens, segment_ids, valid_mask, cotangent, teacher, w_query, b_query, w_key, w_value, b_value, w_out, b_out, norm1_gain, norm1_bias, w_up, b_up, w_down, b_down, norm2_gain, norm2_bias):
    parameters = tuple((weight.astype(jnp.float32) for weight in (w_query, b_query, w_key, w_value, b_value, w_out, b_out, norm1_gain, norm1_bias, w_up, b_up, w_down, b_down, norm2_gain, norm2_bias)))

    def one_sequence(carried, sequence):
        grad_sums, error_sum = carried
        seq_tokens, seg_row, valid_row, seq_cot, seq_teacher = sequence
        output_full, pullback = jax.vjp(lambda inputs_f, *weights: forward(inputs_f, weights, seg_row, valid_row), seq_tokens.astype(jnp.float32), *parameters)
        live_mask = valid_row.astype(jnp.float32)[:, None]
        mismatch = output_full - seq_teacher.astype(jnp.float32)
        gradients = pullback(seq_cot.astype(jnp.float32) + live_mask * mismatch)
        grad_sums = tuple((before + after for before, after in zip(grad_sums, gradients[1:])))
        error_sum = error_sum + jnp.sum(live_mask * mismatch * mismatch)
        return ((grad_sums, error_sum), (output_full.astype(jnp.bfloat16), gradients[0].astype(jnp.bfloat16)))
    zero_grads = tuple((jnp.zeros_like(weight) for weight in parameters))
    sequences = (tokens.reshape(SEQS, LEN, D), segment_ids, valid_mask, cotangent.reshape(SEQS, LEN, D), teacher.reshape(SEQS, LEN, D))
    (grad_sums, error_sum), (outputs, input_grads) = lax.scan(one_sequence, (zero_grads, jnp.zeros((), jnp.float32)), sequences)
    mean_loss = error_sum / (jnp.sum(valid_mask.astype(jnp.float32)) * D)
    d_w_query, d_b_query, d_w_key, d_w_value, d_b_value, d_w_out, d_b_out, d_norm1_gain, d_norm1_bias, d_w_up, d_b_up, d_w_down, d_b_down, d_norm2_gain, d_norm2_bias = grad_sums
    return (outputs.reshape(TOKENS, D), mean_loss, input_grads.reshape(TOKENS, D), d_w_query, d_b_query, d_w_key, d_w_value, d_b_value, d_w_out, d_b_out, d_norm1_gain, d_norm1_bias, d_w_up, d_b_up, d_w_down, d_b_down, d_norm2_gain, d_norm2_bias)
```

```python
import math

import jax
import jax.numpy as jnp
from jax import lax
from jax.experimental import pallas as pl
from jax.experimental.pallas import tpu as pltpu
from jax.sharding import PartitionSpec as P

EPSILON = 1e-05
MASKED = -1e30
PAD_ROWS = 16
BLK = 256
F32 = jnp.float32
BF16 = jnp.bfloat16
NT = (((1,), (1,)), ((), ()))
NN = (((1,), (0,)), ((), ()))

def norm_forward(resid, gain, shift):
    average = jnp.mean(resid, -1, keepdims=True)
    centered = resid - average
    inv_std = lax.rsqrt(jnp.mean(centered * centered, -1, keepdims=True) + EPSILON)
    normed = centered * inv_std
    return (normed * gain + shift, normed, inv_std)


def norm_backward(upstream, normed, inv_std, gain):
    d_gain = jnp.sum(upstream * normed, 0)
    d_shift = jnp.sum(upstream, 0)
    scaled = upstream * gain
    d_resid = inv_std * (
        scaled
        - jnp.mean(scaled, -1, keepdims=True)
        - normed * jnp.mean(scaled * normed, -1, keepdims=True)
    )
    return (d_resid, d_gain, d_shift)


def gelu_parts(preact):
    normal_cdf = 0.5 * (1.0 + lax.erf(preact * (1.0 / math.sqrt(2.0))))
    slope = normal_cdf + preact * jnp.exp(-0.5 * preact * preact) * (1.0 / math.sqrt(2.0 * math.pi))
    return (preact * normal_cdf, slope)


def dot(a,b,dims=NN):
    return lax.dot_general(a,b,dims,preferred_element_type=F32)

def split3(v):
    hi=v.astype(BF16); r=v-hi.astype(F32); mid=r.astype(BF16); lo=(r-mid.astype(F32)).astype(BF16)
    return hi,mid,lo

def fwd_kernel(bounds, t0,t1,t2,t3, wa, wb, encq, enck, vrow, a0,a1,a2,a3, qp,kp,vp,op, wp, bias, s_scr, m_scr, acc_scr):
    heads=3
    half=wa.shape[0]-16
    b0=bounds[2,0]
    lane=lax.broadcasted_iota(jnp.int32,(BLK,128),1)
    wp[...]=jnp.zeros_like(wp)
    for i in range(9):
        wp[:half,i*128:i*128+64]=wa[:half,i*64:(i+1)*64]
        wp[half:,i*128:i*128+64]=wb[:half,i*64:(i+1)*64]
    bias[...]=jnp.zeros_like(bias)
    for i in range(9):
        bias[:,i*128:i*128+64]=wa[half:half+1,i*64:(i+1)*64].astype(F32)
    encv=jnp.where((lane>=64)&(lane<67),1.0,0.0).astype(BF16)
    for kk,t in enumerate((t0,t1,t2,t3)):
        nb=t.shape[0]//BLK
        for r in range(nb):
            rows=slice(kk*t.shape[0]+r*BLK, kk*t.shape[0]+(r+1)*BLK)
            x=t[r*BLK:(r+1)*BLK,:]
            y=dot(x,wp[...])+bias[...]
            for h in range(heads):
                qp[h,rows,:]=y[:,h*128:(h+1)*128].astype(BF16)*jnp.asarray(0.125,BF16)+encq[rows,:]
                kp[h,rows,:]=y[:,(3+h)*128:(4+h)*128].astype(BF16)+enck[rows,:]
                vp[h,rows,:]=y[:,(6+h)*128:(7+h)*128].astype(BF16)+encv
    nblk=qp.shape[1]//BLK
    eye=lax.broadcasted_iota(jnp.int32,(BLK,BLK),0)==lax.broadcasted_iota(jnp.int32,(BLK,BLK),1)
    nolane80=jnp.where(lane==80,0.0,1.0).astype(BF16)
    def relrow(j):
        return pl.multiple_of((j ^ (2*b0))*BLK, BLK)
    def qblock(i,_):
        rows=pl.ds(relrow(i),BLK)
        lo=bounds[0,i]; hi=bounds[1,i]
        below=jnp.maximum(jnp.minimum(hi,i)-lo,0); above=jnp.maximum(hi-(i+1),0)
        cnt=below+above
        ok=(vrow[pl.ds(i ^ (2*b0),1),:]>0)|eye
        for h in range(heads):
            s=dot(qp[h,rows,:]*nolane80,kp[h,rows,:],NT)
            s=jnp.where(ok,s,MASKED)
            s_scr[h,0]=s
            m_scr[h]=jnp.maximum(s[:,:128],s[:,128:])
        def jof(t):
            return jnp.where(t<below, lo+t, i+1+t-below)
        def l1(t,_):
            kr=pl.ds(relrow(jof(t)),BLK)
            for h in range(heads):
                s=dot(qp[h,rows,:],kp[h,kr,:],NT)
                s_scr[h,t+1]=s
                m_scr[h]=jnp.maximum(m_scr[h],jnp.maximum(s[:,:128],s[:,128:]))
            return 0
        lax.fori_loop(0,cnt,l1,0)
        for h in range(heads):
            m=jnp.max(m_scr[h],axis=1,keepdims=True)
            m_scr[h]=jnp.broadcast_to(m,(BLK,128))
        for h in range(heads):
            m=m_scr[h]
            p=jnp.exp(s_scr[h,0]-jnp.concatenate([m,m],1)).astype(BF16)
            acc_scr[h]=dot(p,vp[h,rows,:])
        def l2(t,_):
            kr=pl.ds(relrow(jof(t)),BLK)
            for h in range(heads):
                m=m_scr[h]
                p=jnp.exp(s_scr[h,t+1]-jnp.concatenate([m,m],1)).astype(BF16)
                acc_scr[h]+=dot(p,vp[h,kr,:])
            return 0
        lax.fori_loop(0,cnt,l2,0)
        os=[]
        for h in range(heads):
            acc=acc_scr[h]
            l=acc[:,64:65]
            o=acc*(1.0/l)
            op[h,rows,:]=o
            os.append(o.astype(BF16).astype(F32))
            L=m_scr[h][:,0:1]+jnp.log(l)
            hi_,mid_,lo_=split3(L)
            zero=jnp.zeros((BLK,128),F32)
            add=jnp.where(lane==81,hi_.astype(F32),jnp.where(lane==82,mid_.astype(F32),jnp.where(lane==83,lo_.astype(F32),zero)))
            qp[h,rows,:]=qp[h,rows,:]+add.astype(BF16)
        o01=jnp.where(lane<64,os[0],pltpu.roll(os[1],64,1)).astype(BF16)
        o2=os[2][:,:64].astype(BF16)
        ri=i ^ (2*b0)
        for kk,a in enumerate((a0,a1,a2,a3)):
            @pl.when(ri//2==kk)
            def _():
                rr=pl.ds(pl.multiple_of((ri%2)*BLK,BLK),BLK)
                a[rr,0:128]=o01
                a[rr,128:192]=o2
        return 0
    lax.fori_loop(0,nblk,qblock,0)

def bwd_kernel(bounds, d0,d1,d2,d3, qp,kp,vp,op, vrow, dq_o,dk_o,dv_o, dop, dq_s, dk_s, dv_s):
    heads=3
    b0=bounds[2,0]
    lane=lax.broadcasted_iota(jnp.int32,(BLK,128),1)
    zero64=jnp.zeros((BLK,64),BF16)
    for kk,d in enumerate((d0,d1,d2,d3)):
        for r in range(d.shape[0]//BLK):
            rows=slice(kk*d.shape[0]+r*BLK, kk*d.shape[0]+(r+1)*BLK)
            x01=d[r*BLK:(r+1)*BLK,0:128].astype(F32)
            x2=jnp.concatenate([d[r*BLK:(r+1)*BLK,128:192],zero64],1).astype(F32)
            xs=[jnp.where(lane<64,x01,0.0),jnp.where(lane<64,pltpu.roll(x01,64,1),0.0),x2]
            for h in range(heads):
                delta=jnp.sum(xs[h]*op[h,rows,:],axis=1,keepdims=True)
                hi_,mid_,lo_=split3(-delta)
                v=jnp.where(lane==64,hi_.astype(F32),jnp.where(lane==65,mid_.astype(F32),jnp.where(lane==66,lo_.astype(F32),xs[h])))
                dop[h,rows,:]=v.astype(BF16)
    dk_s[...]=jnp.zeros_like(dk_s)
    dv_s[...]=jnp.zeros_like(dv_s)
    nblk=qp.shape[1]//BLK
    eye=lax.broadcasted_iota(jnp.int32,(BLK,BLK),0)==lax.broadcasted_iota(jnp.int32,(BLK,BLK),1)
    nolane80=jnp.where(lane==80,0.0,1.0).astype(BF16)
    def relrow(j):
        return pl.multiple_of((j ^ (2*b0))*BLK, BLK)
    TN=(((0,),(0,)),((),()))
    def pair(h,rows,kr,diag_ok=None):
        q=qp[h,rows,:]; d=dop[h,rows,:]; k=kp[h,kr,:]; v=vp[h,kr,:]
        if diag_ok is None:
            s=dot(q,k,NT)
        else:
            s=dot(q*nolane80,k,NT)
            s=jnp.where(diag_ok,s,MASKED)
        p=jnp.exp(s)
        dp=dot(d,v,NT)
        ds=(p*dp).astype(BF16); pb=p.astype(BF16)
        dv_s[h,kr,:]+=dot(pb,d,TN)
        dk_s[h,kr,:]+=dot(ds,q,TN)
        return dot(ds,k)
    def qblock(i,_):
        rows=pl.ds(relrow(i),BLK)
        lo=bounds[0,i]; hi=bounds[1,i]
        below=jnp.maximum(jnp.minimum(hi,i)-lo,0); above=jnp.maximum(hi-(i+1),0)
        cnt=below+above
        ok=(vrow[pl.ds(i ^ (2*b0),1),:]>0)|eye
        for h in range(heads):
            dq_s[h]=pair(h,rows,rows,ok)
        def l1(t,_):
            j=jnp.where(t<below, lo+t, i+1+t-below)
            kr=pl.ds(relrow(j),BLK)
            for h in range(heads):
                dq_s[h]+=pair(h,rows,kr)
            return 0
        lax.fori_loop(0,cnt,l1,0)
        q=[dq_s[h]*0.125 for h in range(3)]
        dq_o[rows,0:128]=jnp.where(lane<64,q[0],pltpu.roll(q[1],64,1)).astype(BF16)
        dq_o[rows,128:192]=q[2][:,:64].astype(BF16)
        return 0
    lax.fori_loop(0,nblk,qblock,0)
    for src,dst in ((dk_s,dk_o),(dv_s,dv_o)):
        for r in range(nblk):
            rows=slice(r*BLK,(r+1)*BLK)
            dst[rows,0:128]=jnp.where(lane<64,src[0,rows,:],pltpu.roll(src[1,rows,:],64,1)).astype(BF16)
            dst[rows,128:192]=src[2,rows,:][:,:64].astype(BF16)

VM=pl.BlockSpec(memory_space=pltpu.VMEM)
SM=pl.BlockSpec(memory_space=pltpu.SMEM)
def attention_forward(bounds,ts,wa,wb,encq,enck,vrow):
    n=ts[0].shape[0]*4; d=ts[0].shape[1]
    S=jax.ShapeDtypeStruct
    return pl.pallas_call(fwd_kernel,
        out_shape=[S((n//4,192),BF16)]*4+[S((3,n,128),BF16)]*3+[S((3,n,128),F32)],
        in_specs=[SM]+[VM]*9, out_specs=[VM]*8,
        scratch_shapes=[pltpu.VMEM((d,1152),BF16),pltpu.VMEM((1,1152),F32),pltpu.VMEM((3,n//BLK,BLK,BLK),F32),pltpu.VMEM((3,BLK,128),F32),pltpu.VMEM((3,BLK,128),F32)],
        compiler_params=pltpu.CompilerParams(vmem_limit_bytes=52<<20),
        name="attn_fwd")(bounds,*ts,wa,wb,encq,enck,vrow)
def attention_backward(bounds,ds,qp,kp,vp,op,vrow):
    n=qp.shape[1]
    S=jax.ShapeDtypeStruct
    return pl.pallas_call(bwd_kernel,
        out_shape=[S((n,192),BF16)]*3,
        in_specs=[SM]+[VM]*9, out_specs=[VM]*3,
        scratch_shapes=[pltpu.VMEM((3,n,128),BF16),pltpu.VMEM((3,BLK,128),F32),pltpu.VMEM((3,n,128),F32),pltpu.VMEM((3,n,128),F32)],
        compiler_params=pltpu.CompilerParams(vmem_limit_bytes=52<<20),
        name="attn_bwd")(bounds,*ds,qp,kp,vp,op,vrow)

def mask_tables(code, b0):
    n=code.shape[0]; nb=n//BLK
    seg=code//2; val=code%2
    first=seg[::BLK]; last=seg[BLK-1::BLK]
    lo=jnp.sum(last[None,:]<first[:,None],1)
    nvalid=jnp.sum(val)
    hi=jnp.minimum(jnp.sum(first[None,:]<=last[:,None],1),(nvalid+BLK-1)//BLK)
    b0v=jnp.zeros((nb,),jnp.int32)+b0
    bounds=jnp.stack([lo.astype(jnp.int32),hi.astype(jnp.int32),b0v])
    idx=jnp.arange(4,dtype=jnp.int32)^b0
    crel=jnp.take(code.reshape(4,n//4),idx,axis=0).reshape(n)
    segr=(crel//2)[:,None]; valr=(crel%2)[:,None]
    lane=jnp.arange(128,dtype=jnp.int32)[None,:]
    inoh=(lane>=64)&(lane<80)
    same=(lane-64)==segr
    encq=jnp.where((inoh&same)|(lane==80),1.0,0.0).astype(BF16)
    enck=jnp.where((inoh&~same)|((lane==80)&(valr==0)),MASKED,jnp.where((lane>=81)&(lane<84),-1.0,0.0)).astype(BF16)
    vrow=(crel%2).reshape(nb,BLK)
    return bounds,encq,enck,vrow


def gate_halves(flip, value):
    half = value.shape[-1] // 2
    swapped = jnp.concatenate([value[..., half:], value[..., :half]], -1)
    return jnp.where(flip, swapped, value)


def plane_perm(to):
    return [
        (
            core * 4 + row * 2 + col,
            (lambda t: t[0] * 4 + t[1] * 2 + t[2])(to(core, row, col)),
        )
        for core in range(2)
        for row in range(2)
        for col in range(2)
    ]


CORE_CHIP = ("gy", "gz")
TO_OWNER = [
    plane_perm(lambda core, row, col, a=k // 2, b=k % 2: (row, core ^ a, col ^ b))
    for k in range(4)
]
TO_HEADS = [
    plane_perm(lambda core, row, col, a=k // 2, b=k % 2: (row ^ a, core, col ^ b))
    for k in range(4)
]
CHIP = [[(c, c ^ k) for c in range(4)] for k in range(4)]
CORE = [(0, 1), (1, 0)]


def to_owner(value, k):
    return lax.ppermute(value, CORE_CHIP, TO_OWNER[k])


def to_heads(value, k):
    return lax.ppermute(value, CORE_CHIP, TO_HEADS[k])


def to_chip(value, k):
    return lax.ppermute(value, "gz", CHIP[k])


def to_core(value):
    return lax.ppermute(value, "gy", CORE)


def gather_chips(own):
    half = own.shape[0] // 2
    along_x = to_chip(own, 1)
    along_y = to_chip(own, 2)
    first = to_chip(along_x[:half], 2)
    second = to_chip(along_y[half:], 1)
    return own, along_x, along_y, jnp.concatenate([first, second], 0)


def add_low(left, right):
    return (left.astype(F32) + right.astype(F32)).astype(BF16)


def scatter_chips(pieces):
    half = pieces[0].shape[0] // 2
    upper = [piece[:half] for piece in pieces]
    lower = [piece[half:] for piece in pieces]
    came_x = to_chip(jnp.stack([upper[1], upper[3]]), 1)
    came_y = to_chip(jnp.stack([lower[2], lower[3]]), 2)
    upper_y = to_chip(add_low(upper[2], came_x[1]), 2)
    lower_x = to_chip(add_low(lower[1], came_y[1]), 1)
    upper_sum = upper[0].astype(F32) + came_x[0].astype(F32) + upper_y.astype(F32)
    lower_sum = lower[0].astype(F32) + came_y[0].astype(F32) + lower_x.astype(F32)
    return jnp.concatenate([upper_sum, lower_sum], 0)


def sum_all(vectors):
    vectors = vectors + to_core(vectors)
    swap = jnp.array
    fixed, spread = vectors[:-4], vectors[-4:]
    for k in (1, 2):
        came = to_chip(jnp.concatenate([fixed, spread], 0), k)
        fixed = fixed + came[:-4]
        other = came[-4:]
        if k == 1:
            other = jnp.concatenate([other[1:2], other[0:1], other[3:4], other[2:3]], 0)
        else:
            other = jnp.concatenate([other[2:4], other[0:2]], 0)
        spread = spread + other
    total = jnp.concatenate([fixed, spread[:1]], 0)
    planes = lax.axis_size("gx")
    if planes & (planes - 1):
        return lax.psum(total, "gx")
    step = 1
    while step < planes:
        total = total + lax.ppermute(total, "gx", [(p, p ^ step) for p in range(planes)])
        step *= 2
    return total


def shards(
    tokens,
    segment_ids,
    valid_mask,
    cotangent,
    teacher,
    w_query,
    b_query,
    w_key,
    w_value,
    b_value,
    w_out,
    b_out,
    norm1_gain,
    norm1_bias,
    w_up,
    b_up,
    w_down,
    b_down,
    norm2_gain,
    norm2_bias,
):
    row_count, width = tokens.shape
    half = width // 2
    core = lax.axis_index("gy")
    chip = lax.axis_index("gz")
    flip = core == 1
    block_col = w_query.shape[1]

    valid_row = valid_mask[0]
    own_valid = lax.dynamic_slice_in_dim(valid_row, chip * row_count, row_count).astype(F32)[:, None]

    own_tokens = gate_halves(flip, tokens)
    shard0 = to_owner(own_tokens, 0)
    shard1 = to_owner(own_tokens, 1)
    code = to_owner(segment_ids * 2 + valid_mask, 0)
    qkv_own = jnp.concatenate([w_query, w_key, w_value], 1)
    qkv_bias = jnp.concatenate([b_query, jnp.zeros_like(b_query), b_value])[None, :]
    qkv_own = jnp.concatenate([qkv_own, jnp.broadcast_to(qkv_bias, (PAD_ROWS, 3 * block_col))], 0)
    qkv_other = to_core(qkv_own)
    qkv_a = to_owner(qkv_own, 0)
    qkv_b = to_owner(qkv_other, 0)
    shard2 = to_core(shard0)
    shard3 = to_core(shard1)
    token_shards = (shard0, shard1, shard2, shard3)

    out_own = jnp.concatenate([w_out] + [to_chip(w_out, k) for k in (1, 2, 3)], 0)
    out_full = jnp.concatenate([out_own, to_core(out_own)], 1)
    up_ext = jnp.concatenate([w_up, jnp.broadcast_to(b_up[None, :], (PAD_ROWS, w_up.shape[1]))], 0)
    up_own = jnp.concatenate(gather_chips(up_ext), 1)
    up_other = to_core(up_own[:half])
    up_full = jnp.concatenate([up_own[:half], up_other], 0)
    up_bias = up_own[half].astype(F32)
    down_own = jnp.concatenate(gather_chips(w_down), 0)
    down_full = jnp.concatenate([down_own, to_core(down_own)], 1)

    head_block = core * 2 + chip % 2
    bounds, enc_query, enc_key, valid_rows = mask_tables(code[0], head_block)
    results = attention_forward(
        bounds, token_shards, qkv_a, qkv_b, enc_query, enc_key, valid_rows
    )
    query_pad, key_pad, value_pad, normed_out = results[4:]
    attended = jnp.concatenate([to_owner(results[k], k) for k in range(4)], 1)

    gain1, shift1, gain2, shift2, bias_out, bias_down = (
        gate_halves(flip, v.astype(F32))
        for v in (norm1_gain, norm1_bias, norm2_gain, norm2_bias, b_out, b_down)
    )
    own_cotangent = gate_halves(flip, cotangent)
    own_teacher = gate_halves(flip, teacher)
    mixed = jnp.dot(attended, out_full, preferred_element_type=F32) + bias_out
    resid1 = own_tokens.astype(F32) + mixed
    hidden, normed1, inv_std1 = norm_forward(resid1, gain1, shift1)
    hidden_low = hidden.astype(BF16)
    preact = jnp.dot(hidden_low, up_full, preferred_element_type=F32) + up_bias
    activated, slope = gelu_parts(preact)
    activated = activated.astype(BF16)
    slope = slope.astype(BF16)
    branch = jnp.dot(activated, down_full, preferred_element_type=F32)
    resid2 = hidden + (branch + bias_down)
    output_full, normed2, inv_std2 = norm_forward(resid2, gain2, shift2)
    mismatch = output_full - own_teacher.astype(F32)
    error_part = jnp.sum(own_valid * mismatch * mismatch)
    count_part = jnp.sum(own_valid)
    d_output = own_cotangent.astype(F32) + own_valid * mismatch
    d_resid2, d_gain2, d_shift2 = norm_backward(d_output, normed2, inv_std2, gain2)
    d_branch = d_resid2.astype(BF16)
    d_b_down = jnp.sum(d_branch, 0, dtype=F32)
    d_act = jnp.einsum("lm,fm->lf", d_branch, down_full, preferred_element_type=F32)
    d_pre = (d_act * slope.astype(F32)).astype(BF16)
    d_b_up = jnp.sum(d_pre, 0, dtype=F32)
    d_hidden = d_resid2 + jnp.einsum("lf,mf->lm", d_pre, up_full, preferred_element_type=F32)
    d_resid1, d_gain1, d_shift1 = norm_backward(d_hidden, normed1, inv_std1, gain1)
    d_mixed = d_resid1.astype(BF16)
    d_b_out = jnp.sum(d_mixed, 0, dtype=F32)
    d_attended = jnp.einsum(
        "lm,cm->lc", d_mixed, out_full, preferred_element_type=F32
    ).astype(BF16)
    d_pieces = [
        to_heads(d_attended[:, k * block_col : (k + 1) * block_col], k) for k in range(4)
    ]

    d_down = jnp.einsum("lf,lm->fm", activated, d_branch, preferred_element_type=F32).astype(BF16)
    d_up = jnp.einsum("lm,lf->mf", hidden_low, d_pre, preferred_element_type=F32).astype(BF16)
    d_out = jnp.einsum("lc,lm->cm", attended, d_mixed, preferred_element_type=F32).astype(BF16)
    d_down = add_low(d_down[:, :half], to_core(d_down[:, half:]))
    d_up = add_low(d_up[:half], to_core(d_up[half:]))
    d_out = add_low(d_out[:, :half], to_core(d_out[:, half:]))
    hidden_col = w_up.shape[1]
    grad_down = scatter_chips([d_down[k * hidden_col : (k + 1) * hidden_col] for k in range(4)])
    grad_up = scatter_chips([d_up[:, k * hidden_col : (k + 1) * hidden_col] for k in range(4)])
    grad_out = d_out[:block_col].astype(F32)
    for k in (1, 2, 3):
        grad_out = grad_out + to_chip(d_out[k * block_col : (k + 1) * block_col], k).astype(F32)
    grad_down, grad_up, grad_out = (
        lax.psum(v.astype(BF16), "gx").astype(F32) for v in (grad_down, grad_up, grad_out)
    )

    vectors = [gate_halves(flip, v) for v in (d_gain1, d_shift1, d_gain2, d_shift2, d_b_out, d_b_down)]
    scalars = jnp.concatenate([error_part[None], count_part[None], jnp.zeros((width - 2,), F32)])
    table = jnp.concatenate(
        [jnp.stack(vectors + [scalars]), d_b_up.reshape(4, hidden_col)], 0
    )
    sums = sum_all(table)

    d_query, d_key, d_value = attention_backward(
        bounds, d_pieces, query_pad, key_pad, value_pad, normed_out, valid_rows
    )
    d_qkv = jnp.concatenate([d_query, d_key, d_value], 1)
    qkv_full = jnp.concatenate([qkv_a[:half], qkv_b[:half]], 0)
    term = jnp.einsum("lc,mc->lm", d_qkv, qkv_full, preferred_element_type=F32).astype(BF16)
    group = 2 * row_count
    term = add_low(term[:group], to_core(term[group:]))
    d_tokens = (
        d_resid1
        + to_owner(term[:row_count], 0).astype(F32)
        + to_owner(term[row_count:], 1).astype(F32)
    )
    d_w = jnp.einsum(
        "lm,lc->mc", jnp.concatenate(token_shards, 0), d_qkv, preferred_element_type=F32
    ).astype(BF16)
    d_bias = jnp.sum(d_qkv, 0, dtype=F32)[None, :]
    d_bias_high = d_bias.astype(BF16)
    d_bias_low = (d_bias - d_bias_high.astype(F32)).astype(BF16)
    bias_rows = jnp.concatenate(
        [d_bias_high, d_bias_low, jnp.zeros((PAD_ROWS - 2, 3 * block_col), BF16)], 0
    )
    d_w = to_owner(jnp.concatenate([d_w[:half], bias_rows, d_w[half:], bias_rows], 0), 0)
    split = half + PAD_ROWS
    d_w = add_low(d_w[:split], to_core(d_w[split:]))
    d_w = lax.psum(d_w, "gx").astype(F32)
    grad_qkv = d_w[:half]
    grad_bias = d_w[half] + d_w[half + 1]

    mean_loss = sums[6, 0] / (sums[6, 1] * width)
    return (
        gate_halves(flip, output_full.astype(BF16)),
        mean_loss,
        gate_halves(flip, d_tokens.astype(BF16)),
        grad_qkv[:, :block_col],
        grad_bias[:block_col],
        grad_qkv[:, block_col : 2 * block_col],
        grad_qkv[:, 2 * block_col :],
        grad_bias[2 * block_col :],
        grad_out,
        sums[4],
        sums[0],
        sums[1],
        grad_up,
        sums[7],
        grad_down,
        sums[5],
        sums[2],
        sums[3],
    )


def solution(mesh):
    placed = (
        P(("gx", "gy", "gz"), None),
        P(("gx", "gy"), None),
        P(("gx", "gy"), None),
        P(("gx", "gy", "gz"), None),
        P(("gx", "gy", "gz"), None),
        P("gy", "gz"),
        P("gz"),
        P("gy", "gz"),
        P("gy", "gz"),
        P("gz"),
        P("gz", "gy"),
        P(),
        P(),
        P(),
        P("gy", "gz"),
        P("gz"),
        P("gz", "gy"),
        P(),
        P(),
        P(),
    )
    return jax.shard_map(
        shards,
        mesh=mesh,
        in_specs=placed,
        out_specs=(
            P(("gx", "gy", "gz"), None),
            P(),
            P(("gx", "gy", "gz"), None),
            P("gy", "gz"),
            P("gz"),
            P("gy", "gz"),
            P("gy", "gz"),
            P("gz"),
            P("gz", "gy"),
            P(),
            P(),
            P(),
            P("gy", "gz"),
            P("gz"),
            P("gz", "gy"),
            P(),
            P(),
            P(),
        ),
        check_vma=False,
    )
```

```python
import math

import jax
import jax.numpy as jnp
from jax import lax
from jax.experimental import pallas as pl
from jax.experimental.pallas import tpu as pltpu
from jax.sharding import PartitionSpec as P

EPSILON = 1e-05
MASKED = -1e30
PAD_ROWS = 16
BLK = 256
F32 = jnp.float32
BF16 = jnp.bfloat16
NT = (((1,), (1,)), ((), ()))
NN = (((1,), (0,)), ((), ()))


VMEM_SPEC = pl.BlockSpec(memory_space=pltpu.VMEM)
SMEM_SPEC = pl.BlockSpec(memory_space=pltpu.SMEM)
ROWS = 256
VMEM_LIMIT = 24 << 20


def row_spec(array, rows):
    return pl.BlockSpec((rows,) + array.shape[1:], lambda i: (i,) + (0,) * (len(array.shape) - 1))


def part_spec(rows, cols, block):
    return pl.BlockSpec((rows, cols), lambda i: (block, 0), pipeline_mode=pl.Buffered(1))


def row_call(kernel, name, rows, scalars, row_args, parts, row_outs, whole_outs, scratch, flops):
    S = jax.ShapeDtypeStruct
    steps = row_args[0].shape[0] // rows
    outs = [S(*o) for o in row_outs] + [S(*o) for o in whole_outs]
    return pl.pallas_call(
        kernel,
        grid=(steps,),
        out_shape=outs,
        in_specs=[SMEM_SPEC]
        + [row_spec(a, rows) for a in row_args]
        + [part_spec(r, a.shape[1], b) for a, r, b in parts],
        out_specs=[row_spec(o, rows) for o in outs[: len(row_outs)]]
        + [pl.BlockSpec(o.shape, lambda i: (0, 0)) for o in outs[len(row_outs) :]],
        scratch_shapes=scratch,
        compiler_params=pltpu.CompilerParams(vmem_limit_bytes=VMEM_LIMIT),
        cost_estimate=pl.CostEstimate(flops=flops, bytes_accessed=16 << 20, transcendentals=0),
        name=name,
    )(scalars, *row_args, *(a for a, _, _ in parts))


def half_start(scalars, second, half):
    flip = scalars[0]
    return pl.multiple_of(jnp.where(second, 1 - flip, flip) * half, 128)


def read_swapped(ref, scalars):
    half = ref.shape[-1] // 2
    return jnp.concatenate(
        [
            ref[:, pl.ds(half_start(scalars, False, half), half)].astype(F32),
            ref[:, pl.ds(half_start(scalars, True, half), half)].astype(F32),
        ],
        1,
    )


def write_swapped(ref, rows, value, scalars):
    half = ref.shape[-1] // 2
    ref[rows, pl.ds(half_start(scalars, False, half), half)] = value[:, :half].astype(ref.dtype)
    ref[rows, pl.ds(half_start(scalars, True, half), half)] = value[:, half:].astype(ref.dtype)


def add_swapped(ref, rows, value, scalars):
    half = ref.shape[-1] // 2
    ref[rows, pl.ds(half_start(scalars, False, half), half)] += value[:, :half]
    ref[rows, pl.ds(half_start(scalars, True, half), half)] += value[:, half:]


def column_sum(value):
    return jnp.sum(value, 0, keepdims=True)


def layer_norm(resid):
    average = jnp.mean(resid, -1, keepdims=True)
    centered = resid - average
    inv_std = lax.rsqrt(jnp.mean(centered * centered, -1, keepdims=True) + EPSILON)
    return centered * inv_std, inv_std


def layer_norm_back(upstream, gain, normed, inv_std):
    scaled = upstream * gain
    return inv_std * (
        scaled
        - jnp.mean(scaled, -1, keepdims=True)
        - normed * jnp.mean(scaled * normed, -1, keepdims=True)
    )


def spread_out(blocks, target, half):
    deep = blocks[0].shape[0]
    pairs = [(b, slice(0, half), slice(half, 2 * half)) for b in blocks[:3]]
    at = 0
    for block, left, right in pairs:
        target[at : at + deep, :] = block[:, left]
        target[at + deep : at + 2 * deep, :] = block[:, right]
        at += 2 * deep
    target[at : at + deep, :] = blocks[3][...]
    target[at + deep : at + 2 * deep, :] = blocks[4][...]


def ffn_in_kernel(scalars, *refs):
    att = refs[:4]
    own_tokens = refs[4]
    up_own, up_other, out_own, out_other, up_bias = (refs[5 + 5 * i : 10 + 5 * i] for i in range(5))
    vectors = refs[30]
    hidden_out, normed_out, std_out, low_out, act_out, slope_out = refs[31:37]
    spread = refs[37:]
    block_col = att[0].shape[1]
    half = up_own[4].shape[1]

    @pl.when(pl.program_id(0) == 0)
    def _():
        spread_out(out_own, spread[0], half)
        spread_out(out_other, spread[1], half)

    mixed = []
    for out_ref in spread:
        total = jnp.zeros((att[0].shape[0], half), F32)
        for k in range(4):
            total += dot(att[k][...], out_ref[k * block_col : (k + 1) * block_col, :])
        mixed.append(total)
    resid = own_tokens[...].astype(F32) + (jnp.concatenate(mixed, 1) + vectors[0:1, :])
    normed, inv_std = layer_norm(resid)
    hidden = normed * vectors[1:2, :] + vectors[2:3, :]
    low = hidden.astype(BF16)
    hidden_out[...] = hidden
    normed_out[...] = normed
    std_out[...] = inv_std
    low_out[...] = low
    first = 0
    for own, other, bias in zip(up_own, up_other, up_bias):
        for start in range(0, own.shape[1], half):
            cols = slice(start, start + half)
            preact = (
                dot(low[:, :half], own[:, cols])
                + dot(low[:, half:], other[:, cols])
                + bias[0:1, cols].astype(F32)
            )
            normal_cdf = 0.5 * (1.0 + lax.erf(preact * (1.0 / math.sqrt(2.0))))
            slope = normal_cdf + preact * jnp.exp(-0.5 * preact * preact) * (
                1.0 / math.sqrt(2.0 * math.pi)
            )
            act_out[:, first : first + half] = (preact * normal_cdf).astype(BF16)
            slope_out[:, first : first + half] = slope.astype(BF16)
            first += half


def ffn_mid_kernel(scalars, *refs):
    act, hidden, cotangent, teacher, valid = refs[:5]
    down_own, down_other = refs[5:10], refs[10:15]
    vectors = refs[15]
    output, resid_out, branch_out, sums = refs[16:]
    half = down_own[4].shape[1]
    branch = []
    for parts in (down_own, down_other):
        total = jnp.zeros((act.shape[0], half), F32)
        first = 0
        for part in parts:
            for start in range(0, part.shape[1], half):
                total += dot(act[:, first : first + half], part[:, start : start + half])
                first += half
        branch.append(total)
    gain = vectors[4:5, :]
    resid = hidden[...] + (jnp.concatenate(branch, 1) + vectors[3:4, :])
    normed, inv_std = layer_norm(resid)
    full = normed * gain + vectors[5:6, :]
    write_swapped(output, slice(None), full, scalars)
    mismatch = full - read_swapped(teacher, scalars)
    live = valid[...]
    masked = live * mismatch
    d_output = read_swapped(cotangent, scalars) + masked
    d_resid = layer_norm_back(d_output, gain, normed, inv_std)
    resid_out[...] = d_resid
    low = d_resid.astype(BF16)
    branch_out[...] = low

    @pl.when(pl.program_id(0) == 0)
    def _():
        sums[...] = jnp.zeros_like(sums)

    rows = (
        column_sum(d_output * normed),
        column_sum(d_output),
        column_sum(low.astype(F32)),
        column_sum(masked * mismatch),
        column_sum(jnp.broadcast_to(live, d_output.shape)),
    )
    for at, row in enumerate(rows):
        add_swapped(sums, slice(at, at + 1), row, scalars)


def ffn_back_kernel(scalars, *refs):
    d_branch, slope, d_resid2, normed_ref, std_ref = refs[:5]
    down_own, down_other, up_own, up_other, out_own, out_other = (
        refs[5 + 5 * i : 10 + 5 * i] for i in range(6)
    )
    vectors = refs[35]
    pre_out, mixed_out, resid_out = refs[36:39]
    pieces = refs[39:43]
    sums = refs[43]
    spread = refs[44:]
    half = down_own[4].shape[1]
    block_col = pieces[0].shape[1]

    @pl.when(pl.program_id(0) == 0)
    def _():
        sums[...] = jnp.zeros_like(sums)
        spread_out(out_own, spread[0], half)
        spread_out(out_other, spread[1], half)

    low = d_branch[...]
    parts = [jnp.zeros((low.shape[0], half), F32) for _ in range(2)]
    first = 0
    width = 2 * half
    for k in range(5):
        for start in range(0, down_own[k].shape[1], half):
            cols = slice(start, start + half)
            d_act = dot(low[:, :half], down_own[k][:, cols], NT) + dot(
                low[:, half:], down_other[k][:, cols], NT
            )
            d_pre = (d_act * slope[:, first : first + half].astype(F32)).astype(BF16)
            pre_out[:, first : first + half] = d_pre
            at = 4 + first // width
            sums[at : at + 1, first % width : first % width + half] += column_sum(
                d_pre.astype(F32)
            )
            parts[0] += dot(d_pre, up_own[k][:, cols], NT)
            parts[1] += dot(d_pre, up_other[k][:, cols], NT)
            first += half
    d_hidden = d_resid2[...] + jnp.concatenate(parts, 1)
    normed = normed_ref[...]
    d_resid = layer_norm_back(d_hidden, vectors[1:2, :], normed, std_ref[...])
    resid_out[...] = d_resid
    mixed = d_resid.astype(BF16)
    mixed_out[...] = mixed
    for k in range(4):
        rows = slice(k * block_col, (k + 1) * block_col)
        pieces[k][...] = (
            dot(mixed[:, :half], spread[0][rows, :], NT)
            + dot(mixed[:, half:], spread[1][rows, :], NT)
        ).astype(BF16)
    for at, row in enumerate(
        (column_sum(d_hidden * normed), column_sum(d_hidden), column_sum(mixed.astype(F32)))
    ):
        add_swapped(sums, slice(at, at + 1), row, scalars)


def whole_call(kernel, name, args, outs, scalars=None):
    return pl.pallas_call(
        kernel,
        out_shape=[jax.ShapeDtypeStruct(*o) for o in outs],
        in_specs=([] if scalars is None else [SMEM_SPEC]) + [VMEM_SPEC] * len(args),
        out_specs=[VMEM_SPEC] * len(outs),
        compiler_params=pltpu.CompilerParams(vmem_limit_bytes=24 << 20),
        cost_estimate=pl.CostEstimate(flops=1 << 22, bytes_accessed=6 << 20, transcendentals=0),
        name=name,
    )(*(() if scalars is None else (scalars,)), *args)


def fold_cores(own, came, by_rows):
    def kernel(own_ref, came_ref, *pieces):
        for k, piece in enumerate(pieces):
            rows, cols = piece.shape
            at = (slice(k * rows, (k + 1) * rows), slice(None))
            if not by_rows:
                at = (slice(None), slice(k * cols, (k + 1) * cols))
            piece[...] = (own_ref[at].astype(F32) + came_ref[at].astype(F32)).astype(BF16)

    rows, cols = own.shape
    shape = (rows // 4, cols) if by_rows else (rows, cols // 4)
    return whole_call(kernel, "fold_cores", (own, came), [(shape, BF16)] * 4)


def split_cores(own, came):
    rows, cols = own.shape
    half, cols = rows // 2, cols // 4

    def kernel(own_ref, came_ref, send_x, send_y, keep_upper, keep_lower):
        def total(upper, k):
            at = (slice(0, half) if upper else slice(half, rows), slice(k * cols, (k + 1) * cols))
            return (own_ref[at].astype(F32) + came_ref[at].astype(F32)).astype(BF16)

        for i, k in enumerate((1, 3)):
            send_x[i] = total(True, k)
        for i, k in enumerate((2, 3)):
            send_y[i] = total(False, k)
        for i, k in enumerate((0, 2)):
            keep_upper[i] = total(True, k)
        for i, k in enumerate((0, 1)):
            keep_lower[i] = total(False, k)

    return whole_call(kernel, "split_cores", (own, came), [((2, half, cols), BF16)] * 4)


def second_step(keep_upper, came_x, keep_lower, came_y):
    def kernel(upper, upper_came, lower, lower_came, send_y, send_x):
        send_y[...] = (upper[1].astype(F32) + upper_came[1].astype(F32)).astype(BF16)
        send_x[...] = (lower[1].astype(F32) + lower_came[1].astype(F32)).astype(BF16)

    return whole_call(
        kernel,
        "second_step",
        (keep_upper, came_x, keep_lower, came_y),
        [(keep_upper.shape[1:], BF16)] * 2,
    )


def fold_chips(terms, scalars):
    rows = terms[0].shape[0]
    cols = terms[1].shape[1]
    part = rows // 4
    count = len(terms)

    def kernel(scalars, *refs):
        for k in range(4):
            at = pl.ds(pl.multiple_of((scalars[2] ^ k) * part, 8), part)
            total = refs[0][at, :cols].astype(F32)
            for term in refs[1:count]:
                total += term[at, :].astype(F32)
            refs[count + k][...] = total.astype(BF16)

    return whole_call(kernel, "fold_chips", terms, [((part, cols), BF16)] * 4, scalars)


def fold_halves(upper, lower, scalars):
    half, cols = upper[2].shape
    part = half // 2

    def kernel(scalars, *refs):
        for k in range(4):
            quarter = scalars[2] ^ k
            at = pl.ds(pl.multiple_of(quarter % 2 * part, 8), part)
            for first in (0, 1):

                @pl.when(quarter // 2 == first)
                def _():
                    keep, came, last = refs[3 * first : 3 * first + 3]
                    total = keep[0, at, :].astype(F32) + came[0, at, :].astype(F32)
                    refs[6 + k][...] = (total + last[at, :].astype(F32)).astype(BF16)

    return whole_call(
        kernel, "fold_halves", (*upper, *lower), [((part, cols), BF16)] * 4, scalars
    )


def join_planes(groups, splits, scalars):
    counts = len(groups)
    outs = []
    for group, split in zip(groups, splits):
        rows, cols = 4 * group[0].shape[0], group[0].shape[1]
        outs += [((rows // split, cols), F32)] * split

    def kernel(scalars, *refs):
        ins, targets, scratch = refs[: 4 * counts], refs[4 * counts : -1], refs[-1]
        first = 0
        for g, split in enumerate(splits):
            part, cols = ins[4 * g].shape
            for k in range(4):
                at = pl.ds(pl.multiple_of((scalars[2] ^ k) * part, 8), part)
                value = ins[4 * g + k][...].astype(F32)
                if split == 1:
                    targets[first][at, :] = value
                else:
                    scratch[at, :] = value
            if split > 1:
                rows = 4 * part // split
                for i in range(split):
                    targets[first + i][...] = scratch[i * rows : (i + 1) * rows, :]
            first += split

    args = [v for g in groups for v in g]
    last = groups[splits.index(max(splits))]
    return pl.pallas_call(
        kernel,
        out_shape=[jax.ShapeDtypeStruct(*o) for o in outs],
        in_specs=[SMEM_SPEC] + [VMEM_SPEC] * len(args),
        out_specs=[VMEM_SPEC] * len(outs),
        scratch_shapes=[pltpu.VMEM((4 * last[0].shape[0], last[0].shape[1]), F32)],
        compiler_params=pltpu.CompilerParams(vmem_limit_bytes=24 << 20),
        cost_estimate=pl.CostEstimate(flops=1 << 22, bytes_accessed=12 << 20, transcendentals=0),
        name="join_planes",
    )(scalars, *args)


def dot(left, right, dims=NN):
    return lax.dot_general(left, right, dims, preferred_element_type=F32)


def split3(value):
    high = value.astype(BF16)
    rest = value - high.astype(F32)
    middle = rest.astype(BF16)
    low = (rest - middle.astype(F32)).astype(BF16)
    return high.astype(F32), middle.astype(F32), low.astype(F32)


def key_range(code, span, span_rows, blocks):
    per = span_rows // BLK
    first_seg = code[0, span * span_rows] // 2
    last_seg = code[0, span * span_rows + span_rows - 1] // 2
    low = jnp.int32(0)
    high = jnp.int32(0)
    for other in range(blocks):
        start = code[0, other * BLK]
        low += (code[0, other * BLK + BLK - 1] // 2 < first_seg).astype(jnp.int32)
        high += ((start // 2 <= last_seg) & (start % 2 == 1)).astype(jnp.int32)
    below = jnp.maximum(jnp.minimum(high, span * per) - low, 0)
    above = jnp.maximum(high - (span + 1) * per, 0)
    return low, below, below + above


def key_block(step, low, below, after):
    return jnp.where(step < below, low + step, after + step - below)


def lane_index(rows):
    return lax.broadcasted_iota(jnp.int32, (rows, 128), 1)


def allowed_block(code_rows, block, offset, span_rows):
    row = lax.broadcasted_iota(jnp.int32, (span_rows, BLK), 0)
    col = lax.broadcasted_iota(jnp.int32, (span_rows, BLK), 1)
    return (code_rows[pl.ds(block, 1), :] % 2 == 1) | (row == col + offset)


def attention_forward_kernel(heads, scalars, code, *refs):
    code_rows = refs[0]
    shards_in = refs[1:5]
    weights = refs[5]
    pieces = refs[6:10]
    query_pad, key_pad, value_pad, out_pad = refs[10:14]
    padded, max_scr, acc_scr = refs[14:]
    span_rows, width = shards_in[0].shape
    cols = 64 * heads
    flip = scalars[1]
    per = span_rows // BLK
    blocks = query_pad.shape[1] // BLK
    lane = lane_index(span_rows)
    for i in range(3):
        src = slice(i * cols, (i + 1) * cols)
        padded[i * 256 : i * 256 + cols, :] = weights[src, :]
        padded[i * 256 + cols : (i + 1) * 256, :] = jnp.zeros((256 - cols, width), BF16)
    marks_bias = weights[3 * cols : 3 * cols + 1, :].astype(F32)
    no_bias = jnp.zeros((1, 256 - cols), F32)
    biases = (
        jnp.concatenate([marks_bias[:, :cols], no_bias], 1),
        None,
        jnp.concatenate([marks_bias[:, cols : 2 * cols], no_bias], 1),
    )
    value_ones = jnp.where((lane >= 64) & (lane < 67), 1.0, 0.0)
    for shard, tokens in enumerate(shards_in):
        rows = slice(shard * span_rows, (shard + 1) * span_rows)
        marks = [
            jnp.broadcast_to(
                code_rows[pl.ds((shard ^ flip) * per + part, 1), :].astype(F32), (128, BLK)
            ).T
            for part in range(per)
        ]
        marks = jnp.concatenate(marks, 0).astype(jnp.int32)
        same = lane - 64 == marks // 2
        ids = (lane >= 64) & (lane < 80)
        query_marks = jnp.where((ids & same) | (lane == 80), 1.0, 0.0)
        key_marks = jnp.where(
            (ids & ~same) | ((lane == 80) & (marks % 2 == 0)),
            MASKED,
            jnp.where((lane >= 81) & (lane < 84), -1.0, 0.0),
        )
        for i, (out, extra) in enumerate(
            ((query_pad, query_marks), (key_pad, key_marks), (value_pad, value_ones))
        ):
            projected = dot(tokens[...], padded[i * 256 : (i + 1) * 256, :], NT)
            if biases[i] is not None:
                projected += biases[i]
            if i == 0:
                projected = projected.astype(BF16).astype(F32) * 0.125
            out[0, rows, :] = jnp.where(lane < 64, projected[:, :128], extra).astype(BF16)
            out[1, rows, :] = jnp.where(
                lane < 64, pltpu.roll(projected[:, :128], 64, 1), extra
            ).astype(BF16)
            out[2, rows, :] = jnp.where(lane < 64, projected[:, 128:], extra).astype(BF16)
    no_valid_lane = jnp.where(lane == 80, 0.0, 1.0).astype(BF16)

    def query_step(span, _):
        at = span ^ flip
        rows = pl.ds(pl.multiple_of(at * span_rows, span_rows), span_rows)
        low, below, count = key_range(code, span, span_rows, blocks)

        def keys_of(block):
            place = (block // per ^ flip) * per + block % per
            return pl.ds(pl.multiple_of(place * BLK, BLK), BLK)

        def scores_of(h, keys, allowed=None):
            if allowed is None:
                return dot(query_pad[h, rows, :], key_pad[h, keys, :], NT)
            scores = dot(query_pad[h, rows, :] * no_valid_lane, key_pad[h, keys, :], NT)
            return jnp.where(allowed, scores, MASKED)

        def each_block(visit):
            for part in range(per):
                block = span * per + part
                visit(keys_of(block), allowed_block(code_rows, block, part * BLK, span_rows))

            def step_fn(step, _):
                visit(keys_of(key_block(step, low, below, (span + 1) * per)), None)
                return 0

            lax.fori_loop(0, count, step_fn, 0)

        acc_scr[...] = jnp.zeros_like(acc_scr)
        max_scr[...] = jnp.zeros_like(max_scr)

        def plain(keys, allowed):
            for h in range(heads):
                probs = jnp.exp(scores_of(h, keys, allowed)).astype(BF16)
                acc_scr[h] += dot(probs, value_pad[h, keys, :])

        each_block(plain)
        least, most = jnp.float32(1.0), jnp.float32(1.0)
        for h in range(heads):
            total = jnp.where(lane == 64, acc_scr[h], 1.0)
            good = (total > 1e-25) & (total < 1e30)
            least = jnp.minimum(least, jnp.min(jnp.where(good, 1.0, 0.0)))

        @pl.when(least < 0.5)
        def _():
            max_scr[...] = jnp.full_like(max_scr, MASKED)

            def find_max(keys, allowed):
                for h in range(heads):
                    scores = scores_of(h, keys, allowed)
                    max_scr[h] = jnp.maximum(
                        max_scr[h], jnp.maximum(scores[:, :128], scores[:, 128:])
                    )

            each_block(find_max)
            for h in range(heads):
                max_scr[h] = jnp.broadcast_to(
                    jnp.max(max_scr[h], axis=1, keepdims=True), (span_rows, 128)
                )
            acc_scr[...] = jnp.zeros_like(acc_scr)

            def shifted(keys, allowed):
                for h in range(heads):
                    row_max = max_scr[h]
                    scores = scores_of(h, keys, allowed)
                    probs = jnp.exp(scores - jnp.concatenate([row_max, row_max], 1))
                    acc_scr[h] += dot(probs.astype(BF16), value_pad[h, keys, :])

            each_block(shifted)

        outs = []
        for h in range(heads):
            acc = acc_scr[h]
            total = jnp.broadcast_to(acc[:, 64:65], acc.shape)
            out = acc / total
            out_pad[h, rows, :] = out
            outs.append(out)
            high, middle, rest = split3(max_scr[h] + jnp.log(total))
            extra = jnp.where(
                lane == 81,
                high,
                jnp.where(lane == 82, middle, jnp.where(lane == 83, rest, 0.0)),
            )
            query_pad[h, rows, :] = query_pad[h, rows, :] + extra.astype(BF16)
        pair = jnp.where(lane < 64, outs[0], pltpu.roll(outs[1], 64, 1)).astype(BF16)
        last = outs[2][:, :64].astype(BF16)
        for k, piece in enumerate(pieces):

            @pl.when(at == k)
            def _():
                piece[:, 0:128] = pair
                piece[:, 128:cols] = last

        return 0

    lax.fori_loop(0, len(shards_in), query_step, 0)


def attention_forward(scalars, code, token_shards, weights):
    rows, width = token_shards[0].shape
    length = code.shape[1]
    cols = (weights.shape[0] - PAD_ROWS) // 3
    heads = cols // 64
    S = jax.ShapeDtypeStruct
    flops = 2 * length * width * 3 * 256 + 3 * length * length * 128
    return pl.pallas_call(
        lambda *refs: attention_forward_kernel(heads, *refs),
        out_shape=[S((rows, cols), BF16)] * 4
        + [S((heads, length, 128), BF16)] * 3
        + [S((heads, length, 128), F32)],
        in_specs=[SMEM_SPEC] * 2 + [VMEM_SPEC] * 6,
        out_specs=[VMEM_SPEC] * 8,
        scratch_shapes=[
            pltpu.VMEM((3 * 256, width), BF16),
            pltpu.VMEM((heads, rows, 128), F32),
            pltpu.VMEM((heads, rows, 128), F32),
        ],
        compiler_params=pltpu.CompilerParams(vmem_limit_bytes=VMEM_LIMIT),
        cost_estimate=pl.CostEstimate(
            flops=3 * flops, bytes_accessed=16 << 20, transcendentals=heads * length * 1024
        ),
        name="attention_forward",
    )(scalars, code, code.reshape(length // BLK, BLK), *token_shards, weights)


def attention_backward_kernel(heads, scalars, code, *refs):
    code_rows = refs[0]
    grads = refs[1:5]
    query_pad, key_pad, value_pad, out_pad = refs[5:9]
    shards_in = refs[9:13]
    weights = refs[13]
    own_term, other_term, weight_grad, bias_sum = refs[14:18]
    grad_pad, query_sum, key_sum, value_sum, low_scr, grad_scr = refs[18:]
    span_rows = grads[0].shape[0]
    flip = scalars[1]
    per = span_rows // BLK
    blocks = query_pad.shape[1] // BLK
    lane = lane_index(span_rows)
    gap = jnp.zeros((span_rows, 64), BF16)
    for shard, grad in enumerate(grads):
        rows = slice(shard * span_rows, (shard + 1) * span_rows)
        pair = grad[:, 0:128].astype(F32)
        last = jnp.concatenate([grad[:, 128:192], gap], 1).astype(F32)
        for h, block in enumerate((pair, pltpu.roll(pair, 64, 1), last)):
            block = jnp.where(lane < 64, block, 0.0)
            delta = jnp.sum(block * out_pad[h, rows, :], axis=1, keepdims=True)
            high, middle, rest = split3(-delta)
            block = jnp.where(
                lane == 64,
                high,
                jnp.where(lane == 65, middle, jnp.where(lane == 66, rest, block)),
            )
            grad_pad[h, rows, :] = block.astype(BF16)
    key_sum[...] = jnp.zeros_like(key_sum)
    value_sum[...] = jnp.zeros_like(value_sum)
    query_sum[...] = jnp.zeros_like(query_sum)
    no_valid_lane = jnp.where(lane == 80, 0.0, 1.0).astype(BF16)

    def query_step(span, _):
        at = span ^ flip
        rows = pl.ds(pl.multiple_of(at * span_rows, span_rows), span_rows)
        low, below, count = key_range(code, span, span_rows, blocks)

        def visit(block, allowed):
            place = (block // per ^ flip) * per + block % per
            keys = pl.ds(pl.multiple_of(place * BLK, BLK), BLK)
            for h in range(heads):
                query, grad = query_pad[h, rows, :], grad_pad[h, rows, :]
                key, value = key_pad[h, keys, :], value_pad[h, keys, :]
                if allowed is None:
                    scores = dot(key, query, NT)
                else:
                    scores = jnp.where(allowed, dot(key, query * no_valid_lane, NT), MASKED)
                probs = jnp.exp(scores)
                d_scores = (probs * dot(value, grad, NT)).astype(BF16)
                value_sum[h, keys, :] += dot(probs.astype(BF16), grad)
                key_sum[h, keys, :] += dot(d_scores, query)
                query_sum[h, rows, :] += dot(d_scores, key, (((0,), (0,)), ((), ())))

        for part in range(per):
            block = span * per + part
            key_at = lax.broadcasted_iota(jnp.int32, (BLK, span_rows), 0)
            query_at = lax.broadcasted_iota(jnp.int32, (BLK, span_rows), 1)
            marks = jnp.broadcast_to(
                code_rows[pl.ds(block, 1), :].astype(F32), (128, BLK)
            ).T.astype(jnp.int32)
            valid = jnp.concatenate([marks] * (span_rows // 128), 1) % 2 == 1
            visit(block, valid | (query_at == key_at + part * BLK))

        def step_fn(step, _):
            visit(key_block(step, low, below, (span + 1) * per), None)
            return 0

        lax.fori_loop(0, count, step_fn, 0)
        return 0

    lax.fori_loop(0, len(grads), query_step, 0)
    bias_sum[...] = jnp.zeros_like(bias_sum)
    for shard in range(len(grads)):
        rows = slice(shard * span_rows, (shard + 1) * span_rows)
        parts = [query_sum[h, rows, :] * 0.125 for h in range(heads)]
        parts += [sums[h, rows, :] for sums in (key_sum, value_sum) for h in range(heads)]
        for at in range(0, len(parts), 2):
            if at + 1 < len(parts):
                value = jnp.where(lane < 64, parts[at], pltpu.roll(parts[at + 1], 64, 1))
            else:
                value = parts[at][:, :64]
            low = value.astype(BF16)
            cols = slice(at * 64, at * 64 + low.shape[1])
            low_scr[:, cols] = low
            bias_sum[0:1, cols] += column_sum(low.astype(F32))
        low = low_scr[...]
        depth = low.shape[1]
        term = dot(low, weights[:depth, :]).astype(BF16)
        if shard < 2:
            own_term[shard] = term
        else:
            other_term[shard - 2] = term
        part = dot(low, shards_in[shard][...], (((0,), (0,)), ((), ())))
        if shard == 0:
            grad_scr[...] = part
        elif shard < 3:
            grad_scr[...] += part
        else:
            weight_grad[...] = (grad_scr[...] + part).astype(BF16)


def attention_backward(scalars, code, grads, saved, token_shards, weights):
    length = code.shape[1]
    heads = saved[0].shape[0]
    rows, width = token_shards[0].shape
    cols = 3 * heads * 64
    S = jax.ShapeDtypeStruct
    return pl.pallas_call(
        lambda *refs: attention_backward_kernel(heads, *refs),
        out_shape=[
            S((2, rows, width), BF16),
            S((2, rows, width), BF16),
            S((cols, width), BF16),
            S((8, cols), F32),
        ],
        in_specs=[SMEM_SPEC] * 2 + [VMEM_SPEC] * 14,
        out_specs=[VMEM_SPEC] * 4,
        scratch_shapes=[
            pltpu.VMEM((heads, length, 128), BF16),
            pltpu.VMEM((heads, length, 128), F32),
            pltpu.VMEM((heads, length, 128), F32),
            pltpu.VMEM((heads, length, 128), F32),
            pltpu.VMEM((rows, cols), BF16),
            pltpu.VMEM((cols, width), F32),
        ],
        compiler_params=pltpu.CompilerParams(vmem_limit_bytes=32 << 20),
        cost_estimate=pl.CostEstimate(
            flops=heads * length * length * 1500, bytes_accessed=8 << 20, transcendentals=0
        ),
        name="attention_backward",
    )(
        scalars,
        code,
        code.reshape(length // BLK, BLK),
        *grads,
        *saved,
        *token_shards,
        weights,
    )


CORE_CHIP = ("gy", "gz")
CHIP = [[(c, c ^ k) for c in range(4)] for k in range(4)]
PLANE = [[(p, p ^ k) for p in range(4)] for k in range(4)]
CORE = [(0, 1), (1, 0)]
SIDE_EARLY = [(d, d ^ 1) for d in range(8) if d // 4 == d // 2 % 2]
SIDE_LATE = [(d, d ^ 1) for d in range(8) if d // 4 != d // 2 % 2]


def plane_perm(to):
    pairs = []
    for device in range(8):
        core, row, col = device // 4, device // 2 % 2, device % 2
        core_to, row_to, col_to = to(core, row, col)
        pairs.append((device, core_to * 4 + row_to * 2 + col_to))
    return pairs


TO_OWNER = [
    plane_perm(lambda core, row, col, a=k // 2, b=k % 2: (row, core ^ a, col ^ b))
    for k in range(4)
]
TO_HEADS = [
    plane_perm(lambda core, row, col, a=k // 2, b=k % 2: (row ^ a, core, col ^ b))
    for k in range(4)
]


def to_owner(value, k):
    return lax.ppermute(value, CORE_CHIP, TO_OWNER[k])


def to_heads(value, k):
    return lax.ppermute(value, CORE_CHIP, TO_HEADS[k])


def to_chip(value, k):
    return lax.ppermute(value, "gz", CHIP[k])


def to_core(value):
    return lax.ppermute(value, "gy", CORE)


def to_plane(value, k):
    return lax.ppermute(value, "gx", PLANE[k])


def after(value, *others):
    return lax.optimization_barrier((value,) + others)[0]


def swap_halves(flip, value):
    half = value.shape[-1] // 2
    swapped = jnp.concatenate([value[..., half:], value[..., :half]], -1)
    return jnp.where(flip, swapped, value)


def add_low(left, right):
    return (left.astype(F32) + right.astype(F32)).astype(BF16)


def reduce_planes(parts):
    if lax.axis_size("gx") != 4:
        return lax.psum(jnp.concatenate(parts, 0), "gx")
    total = parts[0].astype(F32)
    for k in (1, 2, 3):
        total += to_plane(parts[k], k).astype(F32)
    return total.astype(BF16)


def spread_planes(total):
    if lax.axis_size("gx") != 4:
        return jnp.split(total, 4, 0)
    return [total] + [to_plane(total, k) for k in (1, 2, 3)]


def sum_planes(parts):
    return spread_planes(reduce_planes(parts))


def sum_all(table):
    table = table + to_core(table)
    fixed, spread = table[:-4], table[-4:]
    for k in (1, 2):
        came = to_chip(jnp.concatenate([fixed, spread], 0), k)
        fixed = fixed + came[:-4]
        other = came[-4:]
        order = (1, 0, 3, 2) if k == 1 else (2, 3, 0, 1)
        spread = spread + jnp.concatenate([other[i : i + 1] for i in order], 0)
    return sum_over_planes(jnp.concatenate([fixed, spread[:1]], 0))


def sum_over_planes(total):
    planes = lax.axis_size("gx")
    if planes & (planes - 1):
        return lax.psum(total, "gx")
    step = 1
    while step < planes:
        total = total + lax.ppermute(total, "gx", [(p, p ^ step) for p in range(planes)])
        step *= 2
    return total


def shards(
    tokens,
    segment_ids,
    valid_mask,
    cotangent,
    teacher,
    w_query,
    b_query,
    w_key,
    w_value,
    b_value,
    w_out,
    b_out,
    norm1_gain,
    norm1_bias,
    w_up,
    b_up,
    w_down,
    b_down,
    norm2_gain,
    norm2_bias,
):
    row_count, width = tokens.shape
    half = width // 2
    core = lax.axis_index("gy")
    chip = lax.axis_index("gz")
    flip = core == 1
    block_col = w_query.shape[1]
    hidden_col = w_up.shape[1]
    plane = lax.axis_index("gx") if lax.axis_size("gx") == 4 else jnp.int32(0)
    scalars = jnp.stack([core, core * 2 + chip % 2, plane]).astype(jnp.int32)

    code = to_owner(segment_ids * 2 + valid_mask, 0)
    own_tokens = after(swap_halves(flip, tokens), code)
    shard0 = to_owner(own_tokens, 0)
    early = lax.ppermute(own_tokens, CORE_CHIP, SIDE_EARLY)
    bias_row = jnp.concatenate([b_query, b_value])[None, :]
    qkv_own = jnp.concatenate(
        [w_query.T, w_key.T, w_value.T, jnp.broadcast_to(bias_row, (PAD_ROWS, half))], 0
    )
    qkv = to_owner(jnp.concatenate([qkv_own, to_core(qkv_own)], 1), 0)
    late = lax.ppermute(shard0, CORE_CHIP, SIDE_LATE)
    shard1 = early + late
    token_shards = (shard0, shard1, to_core(shard0), to_core(shard1))

    vectors = jnp.stack([b_out, norm1_gain, norm1_bias, b_down, norm2_gain, norm2_bias] + [b_out] * 2)
    vectors = swap_halves(flip, vectors.astype(F32))
    own_valid = lax.dynamic_slice_in_dim(valid_mask[0], chip * row_count, row_count)
    own_valid = own_valid.astype(F32)[:, None]
    packed = jnp.concatenate(
        [
            jnp.concatenate([w_down[: hidden_col // 2], w_down[hidden_col // 2 :]], 1),
            w_up,
            jnp.concatenate([w_out[: block_col // 2], w_out[block_col // 2 :]], 1),
            jnp.broadcast_to(b_up[None, :], (PAD_ROWS, hidden_col)),
        ],
        0,
    )

    packed, vectors, own_valid, *_ = lax.optimization_barrier(
        (packed, vectors, own_valid, shard0, shard1, qkv, code)
    )
    pack_x, pack_y = to_chip(packed, 1), to_chip(packed, 2)
    packs = (packed, pack_x, pack_y)
    packed_other = to_core(packed)

    scalars = after(scalars, packed, vectors, own_valid)
    results = attention_forward(scalars, code, token_shards, qkv)
    saved = results[4:]
    attended = [to_owner(results[k], k) for k in range(4)]

    deep = hidden_col // 2
    pack_x, pack_y = lax.optimization_barrier((pack_x, pack_y, results[0]))[:2]
    in_own = (to_chip(pack_x[deep:, :half], 2), to_chip(pack_y[deep:, half:], 1))
    down_x, down_y = after(pack_x[:deep, :half], attended[0]), after(pack_y[:deep, half:], attended[0])
    down_own = (to_chip(down_x, 2), to_chip(down_y, 1))
    packs = (packed, pack_x, pack_y)
    packs_other = (packed_other, to_core(pack_x), to_core(pack_y))
    in_other = tuple(to_core(v) for v in in_own)
    down_other = tuple(to_core(v) for v in down_own)

    out_deep = block_col // 2
    out_at = 2 * deep // out_deep

    def ups(big, small):
        return [(v, half, 1) for v in big] + [(v, half, 0) for v in small]

    def outs(big, small):
        return [(v, out_deep, (deep + half) // out_deep) for v in big] + [
            (v, out_deep, half // out_deep) for v in small
        ]

    def biases(big, small):
        at = (half + out_deep) // PAD_ROWS
        return [(v, PAD_ROWS, deep // PAD_ROWS + at) for v in big] + [
            (v, PAD_ROWS, at) for v in small
        ]

    def downs(big, small):
        return [(v, deep, 0) for v in big] + [(v, deep, 0) for v in small]

    whole_vectors = [(vectors, 8, 0)]
    out_scratch = [pltpu.VMEM((4 * block_col, half), BF16)] * 2

    inner = 4 * hidden_col
    square = 2 * row_count * width * inner
    full = (row_count, width)
    rows = min(ROWS, row_count)
    hidden, normed, inv_std, hidden_low, act, slope = row_call(
        ffn_in_kernel,
        "ffn_in",
        rows,
        scalars,
        (*attended, own_tokens),
        ups(packs, in_own)
        + ups(packs_other, in_other)
        + outs(packs, in_own)
        + outs(packs_other, in_other)
        + biases(packs, in_own)
        + whole_vectors,
        (
            (full, F32),
            (full, F32),
            ((row_count, 1), F32),
            (full, BF16),
            ((row_count, inner), BF16),
            ((row_count, inner), BF16),
        ),
        (),
        out_scratch,
        3 * square,
    )
    output, d_resid2, d_branch, sums_mid = row_call(
        ffn_mid_kernel,
        "ffn_mid",
        rows,
        scalars,
        (act, hidden, cotangent, teacher, own_valid),
        downs(packs, down_own) + downs(packs_other, down_other) + whole_vectors,
        ((full, BF16), (full, F32), (full, BF16)),
        (((8, width), F32),),
        [],
        2 * square,
    )
    d_down_other = jnp.einsum("lf,lm->fm", act, d_branch[:, half:], preferred_element_type=F32)
    d_down_came = to_core(d_down_other.astype(BF16))
    d_down = jnp.einsum("lf,lm->fm", act, d_branch[:, :half], preferred_element_type=F32)
    down_parts = fold_cores(d_down.astype(BF16), d_down_came, True)
    d_branch = after(d_branch, *down_parts)
    down_terms = [down_parts[0]] + [to_chip(down_parts[k], k) for k in (1, 2, 3)]
    d_pre, d_mixed, d_resid1, *back = row_call(
        ffn_back_kernel,
        "ffn_back",
        rows,
        scalars,
        (d_branch, slope, d_resid2, normed, inv_std),
        downs(packs, down_own)
        + downs(packs_other, down_other)
        + ups(packs, in_own)
        + ups(packs_other, in_other)
        + outs(packs, in_own)
        + outs(packs_other, in_other)
        + whole_vectors,
        (((row_count, inner), BF16), (full, BF16), (full, F32))
        + tuple(((row_count, block_col), BF16) for _ in range(4)),
        (((8, width), F32),),
        out_scratch,
        3 * square,
    )
    sums_back = back[4]
    d_pieces = [to_heads(back[k], k) for k in range(4)]

    d_up_other = jnp.einsum("lm,lf->mf", hidden_low[:, half:], d_pre, preferred_element_type=F32)
    d_up_came = to_core(d_up_other.astype(BF16))
    d_out = [
        jnp.einsum("lc,lm->cm", attended[k], d_mixed, preferred_element_type=F32) for k in range(4)
    ]
    d_out = jnp.concatenate(d_out, 0).astype(BF16)
    d_out_came = to_core(d_out[:, half:])
    d_up = jnp.einsum("lm,lf->mf", hidden_low[:, :half], d_pre, preferred_element_type=F32)
    up_x, up_y, keep_upper, keep_lower = split_cores(d_up.astype(BF16), d_up_came)
    out_parts = fold_cores(d_out[:, :half], d_out_came, True)
    out_terms = [out_parts[0]] + [to_chip(out_parts[k], k) for k in (1, 2, 3)]
    came_x, came_y = to_chip(up_x, 1), to_chip(up_y, 2)
    down_quarters = fold_chips(down_terms, scalars)
    d_pieces[0] = after(d_pieces[0], up_x, *out_parts, *down_quarters)

    own_term, other_term, d_w, d_bias = attention_backward(
        scalars, code, d_pieces, saved, token_shards, qkv
    )
    down_sum = reduce_planes(down_quarters)
    step_y, step_x = second_step(keep_upper, came_x, keep_lower, came_y)
    out_quarters = fold_chips(out_terms, scalars)
    d_w, other_term, *_ = lax.optimization_barrier((d_w, other_term, step_y, down_sum))
    d_w = to_owner(d_w, 0)
    other_term = to_core(other_term)
    down_grad = spread_planes(down_sum)
    last_y, last_x = to_chip(step_y, 2), to_chip(step_x, 1)
    term0 = add_low(own_term[0], other_term[0])
    term1 = add_low(own_term[1], other_term[1])
    term0, term1, *_ = lax.optimization_barrier((term0, term1, d_w))
    came0, came1 = to_owner(term0, 0), to_owner(term1, 1)
    qkv_quarters = fold_chips((d_w, to_core(d_w[:, half:])), scalars)
    up_quarters = fold_halves(
        (keep_upper, came_x, last_y), (keep_lower, came_y, last_x), scalars
    )
    qkv_grad = sum_planes(qkv_quarters)
    up_grad = sum_planes(up_quarters)
    out_grad = sum_planes(out_quarters)
    grad_down, grad_up, grad_out, *grad_qkv = join_planes(
        (down_grad, up_grad, out_grad, qkv_grad), (1, 1, 1, 3), scalars
    )
    sums = sum_all(jnp.concatenate([sums_mid, sums_back], 0))
    d_tokens = d_resid1 + came0.astype(F32) + came1.astype(F32)
    d_bias = to_owner(d_bias, 0)
    d_bias = sum_over_planes(d_bias + to_core(d_bias))[0]

    mean_loss = jnp.sum(sums[3]) / jnp.sum(sums[4])
    return (
        output,
        mean_loss,
        swap_halves(flip, d_tokens.astype(BF16)),
        grad_qkv[0].T,
        d_bias[:block_col],
        grad_qkv[1].T,
        grad_qkv[2].T,
        d_bias[2 * block_col :],
        grad_out,
        sums[10],
        sums[8],
        sums[9],
        grad_up,
        sums[12],
        grad_down,
        sums[2],
        sums[0],
        sums[1],
    )


def solution(mesh):
    placed = (
        P(("gx", "gy", "gz"), None),
        P(("gx", "gy"), None),
        P(("gx", "gy"), None),
        P(("gx", "gy", "gz"), None),
        P(("gx", "gy", "gz"), None),
        P("gy", "gz"),
        P("gz"),
        P("gy", "gz"),
        P("gy", "gz"),
        P("gz"),
        P("gz", "gy"),
        P(),
        P(),
        P(),
        P("gy", "gz"),
        P("gz"),
        P("gz", "gy"),
        P(),
        P(),
        P(),
    )
    return jax.shard_map(
        shards,
        mesh=mesh,
        in_specs=placed,
        out_specs=(
            P(("gx", "gy", "gz"), None),
            P(),
            P(("gx", "gy", "gz"), None),
            P("gy", "gz"),
            P("gz"),
            P("gy", "gz"),
            P("gy", "gz"),
            P("gz"),
            P("gz", "gy"),
            P(),
            P(),
            P(),
            P("gy", "gz"),
            P("gz"),
            P("gz", "gy"),
            P(),
            P(),
            P(),
        ),
        check_vma=False,
    )
```

```python
import math

import jax
import jax.numpy as jnp
from jax import lax
from jax.experimental import pallas as pl
from jax.experimental.pallas import tpu as pltpu
from jax.sharding import PartitionSpec as P

EPSILON = 1e-05
MASKED = -1e30
PAD_ROWS = 16
GRAD_PAD = 64
BLK = 256
F32 = jnp.float32
BF16 = jnp.bfloat16
NT = (((1,), (1,)), ((), ()))
NN = (((1,), (0,)), ((), ()))
TN = (((0,), (0,)), ((), ()))


VMEM_SPEC = pl.BlockSpec(memory_space=pltpu.VMEM)
SMEM_SPEC = pl.BlockSpec(memory_space=pltpu.SMEM)
HBM_SPEC = pl.BlockSpec(memory_space=pltpu.HBM)
ROWS = 256
VMEM_LIMIT = 24 << 20
SMALL_LIMIT = 20 << 20
SMALL_COST = pl.CostEstimate(flops=1 << 22, bytes_accessed=6 << 20, transcendentals=0)


def in_hbm(array):
    return pltpu.with_memory_space_constraint(array, pltpu.HBM)


def row_spec(array, rows):
    return pl.BlockSpec((rows,) + array.shape[1:], lambda i: (i,) + (0,) * (len(array.shape) - 1))


def part_spec(rows, cols, block):
    return pl.BlockSpec((rows, cols), lambda i: (block, 0), pipeline_mode=pl.Buffered(1))


def row_call(kernel, name, rows, scalars, row_args, parts, row_outs, whole_outs, scratch, flops):
    S = jax.ShapeDtypeStruct
    steps = row_args[0].shape[0] // rows
    outs = [S(*o) for o in row_outs] + [S(*o) for o in whole_outs]
    return pl.pallas_call(
        kernel,
        grid=(steps,),
        out_shape=outs,
        in_specs=[SMEM_SPEC]
        + [row_spec(a, rows) for a in row_args]
        + [part_spec(r, a.shape[1], b) for a, r, b in parts],
        out_specs=[row_spec(o, rows) for o in outs[: len(row_outs)]]
        + [pl.BlockSpec(o.shape, lambda i: (0, 0)) for o in outs[len(row_outs) :]],
        scratch_shapes=scratch,
        compiler_params=pltpu.CompilerParams(vmem_limit_bytes=VMEM_LIMIT),
        cost_estimate=pl.CostEstimate(flops=flops, bytes_accessed=16 << 20, transcendentals=0),
        name=name,
    )(scalars, *(in_hbm(a) for a in row_args), *(in_hbm(a) for a, _, _ in parts))


def half_start(scalars, second, half):
    flip = scalars[0]
    return pl.multiple_of(jnp.where(second, 1 - flip, flip) * half, 128)


def read_swapped(ref, scalars):
    half = ref.shape[-1] // 2
    return jnp.concatenate(
        [
            ref[:, pl.ds(half_start(scalars, False, half), half)].astype(F32),
            ref[:, pl.ds(half_start(scalars, True, half), half)].astype(F32),
        ],
        1,
    )


def write_swapped(ref, rows, value, scalars):
    half = ref.shape[-1] // 2
    ref[rows, pl.ds(half_start(scalars, False, half), half)] = value[:, :half].astype(ref.dtype)
    ref[rows, pl.ds(half_start(scalars, True, half), half)] = value[:, half:].astype(ref.dtype)


def add_swapped(ref, rows, value, scalars):
    half = ref.shape[-1] // 2
    ref[rows, pl.ds(half_start(scalars, False, half), half)] += value[:, :half]
    ref[rows, pl.ds(half_start(scalars, True, half), half)] += value[:, half:]


def column_sum(value):
    return jnp.sum(value, 0, keepdims=True)


def layer_norm(resid):
    average = jnp.mean(resid, -1, keepdims=True)
    centered = resid - average
    inv_std = lax.rsqrt(jnp.mean(centered * centered, -1, keepdims=True) + EPSILON)
    return centered * inv_std, inv_std


def layer_norm_back(upstream, gain, normed, inv_std):
    scaled = upstream * gain
    return inv_std * (
        scaled
        - jnp.mean(scaled, -1, keepdims=True)
        - normed * jnp.mean(scaled * normed, -1, keepdims=True)
    )


def spread_out(blocks, target, half):
    deep = blocks[0].shape[0]
    pairs = [(b, slice(0, half), slice(half, 2 * half)) for b in blocks[:3]]
    at = 0
    for block, left, right in pairs:
        target[at : at + deep, :] = block[:, left]
        target[at + deep : at + 2 * deep, :] = block[:, right]
        at += 2 * deep
    target[at : at + deep, :] = blocks[3][...]
    target[at + deep : at + 2 * deep, :] = blocks[4][...]


def ffn_forward_kernel(scalars, *refs):
    att = refs[:4]
    own_tokens, cotangent, teacher, valid = refs[4:8]
    down_own, down_other, up_own, up_other, out_own, out_other, up_bias = (
        refs[8 + 5 * i : 13 + 5 * i] for i in range(7)
    )
    vectors = refs[43]
    normed_out, std_out, low_out, act_out, slope_out, output, resid_out, branch_out, sums = refs[44:53]
    spread = refs[53:]
    block_col = att[0].shape[1]
    half = up_own[4].shape[1]

    @pl.when(pl.program_id(0) == 0)
    def _():
        sums[...] = jnp.zeros_like(sums)
        spread_out(out_own, spread[0], half)
        spread_out(out_other, spread[1], half)

    mixed = []
    for out_ref in spread:
        total = jnp.zeros((att[0].shape[0], half), F32)
        for k in range(4):
            total += dot(att[k][...], out_ref[k * block_col : (k + 1) * block_col, :])
        mixed.append(total)
    resid = own_tokens[...].astype(F32) + (jnp.concatenate(mixed, 1) + vectors[0:1, :])
    normed, inv_std = layer_norm(resid)
    hidden = normed * vectors[1:2, :] + vectors[2:3, :]
    low = hidden.astype(BF16)
    normed_out[...] = normed
    std_out[...] = inv_std
    low_out[...] = low
    first = 0
    branch = [jnp.zeros((low.shape[0], half), F32) for _ in range(2)]
    for k in range(5):
        for start in range(0, up_own[k].shape[1], half):
            cols = slice(start, start + half)
            preact = (
                dot(low[:, :half], up_own[k][:, cols])
                + dot(low[:, half:], up_other[k][:, cols])
                + up_bias[k][0:1, cols].astype(F32)
            )
            normal_cdf = 0.5 * (1.0 + lax.erf(preact * (1.0 / math.sqrt(2.0))))
            slope = normal_cdf + preact * jnp.exp(-0.5 * preact * preact) * (
                1.0 / math.sqrt(2.0 * math.pi)
            )
            act = (preact * normal_cdf).astype(BF16)
            act_out[:, first : first + half] = act
            slope_out[:, first : first + half] = slope.astype(BF16)
            branch[0] += dot(act, down_own[k][:, cols])
            branch[1] += dot(act, down_other[k][:, cols])
            first += half
    gain = vectors[4:5, :]
    resid = hidden + (jnp.concatenate(branch, 1) + vectors[3:4, :])
    normed, inv_std = layer_norm(resid)
    full = normed * gain + vectors[5:6, :]
    write_swapped(output, slice(None), full, scalars)
    mismatch = full - read_swapped(teacher, scalars)
    masked = valid[...] * mismatch
    d_output = read_swapped(cotangent, scalars) + masked
    d_resid = layer_norm_back(d_output, gain, normed, inv_std)
    resid_out[...] = d_resid
    low = d_resid.astype(BF16)
    branch_out[...] = low
    rows = (
        column_sum(d_output * normed),
        column_sum(d_output),
        column_sum(low.astype(F32)),
        column_sum(masked * mismatch),
    )
    for at, row in enumerate(rows):
        add_swapped(sums, slice(at, at + 1), row, scalars)


def ffn_back_kernel(scalars, *refs):
    d_branch, slope, d_resid2, normed_ref, std_ref = refs[:5]
    down_own, down_other, up_own, up_other, out_own, out_other = (
        refs[5 + 5 * i : 10 + 5 * i] for i in range(6)
    )
    vectors = refs[35]
    pre_out, mixed_out, resid_out = refs[36:39]
    pieces = refs[39:43]
    sums = refs[43]
    spread = refs[44:]
    half = down_own[4].shape[1]
    block_col = pieces[0].shape[1]

    @pl.when(pl.program_id(0) == 0)
    def _():
        sums[...] = jnp.zeros_like(sums)
        spread_out(out_own, spread[0], half)
        spread_out(out_other, spread[1], half)

    low = d_branch[...]
    parts = [jnp.zeros((low.shape[0], half), F32) for _ in range(2)]
    first = 0
    width = 2 * half
    for k in range(5):
        for start in range(0, down_own[k].shape[1], half):
            cols = slice(start, start + half)
            d_act = dot(low[:, :half], down_own[k][:, cols], NT) + dot(
                low[:, half:], down_other[k][:, cols], NT
            )
            d_pre = (d_act * slope[:, first : first + half].astype(F32)).astype(BF16)
            pre_out[:, first : first + half] = d_pre
            at = 4 + first // width
            sums[at : at + 1, first % width : first % width + half] += column_sum(
                d_pre.astype(F32)
            )
            parts[0] += dot(d_pre, up_own[k][:, cols], NT)
            parts[1] += dot(d_pre, up_other[k][:, cols], NT)
            first += half
    d_hidden = d_resid2[...] + jnp.concatenate(parts, 1)
    normed = normed_ref[...]
    d_resid = layer_norm_back(d_hidden, vectors[1:2, :], normed, std_ref[...])
    resid_out[...] = d_resid
    mixed = d_resid.astype(BF16)
    mixed_out[...] = mixed
    for k in range(4):
        rows = slice(k * block_col, (k + 1) * block_col)
        pieces[k][...] = (
            dot(mixed[:, :half], spread[0][rows, :], NT)
            + dot(mixed[:, half:], spread[1][rows, :], NT)
        ).astype(BF16)
    for at, row in enumerate(
        (column_sum(d_hidden * normed), column_sum(d_hidden), column_sum(mixed.astype(F32)))
    ):
        add_swapped(sums, slice(at, at + 1), row, scalars)


def whole_call(kernel, name, args, outs, scalars=None, cost=SMALL_COST):
    return pl.pallas_call(
        kernel,
        out_shape=[jax.ShapeDtypeStruct(*o) for o in outs],
        in_specs=([] if scalars is None else [SMEM_SPEC]) + [VMEM_SPEC] * len(args),
        out_specs=[VMEM_SPEC] * len(outs),
        compiler_params=pltpu.CompilerParams(vmem_limit_bytes=SMALL_LIMIT),
        cost_estimate=cost,
        name=name,
    )(*(() if scalars is None else (scalars,)), *args)


def weight_grads_kernel(hidden, d_pre, att0, att1, att2, att3, d_mixed, sums_mid, sums_back, count, own, other):
    half = hidden.shape[1] // 2
    cols = d_pre.shape[1] // 4
    flipped = hidden[...].astype(F32).T.astype(BF16)
    for k, att in enumerate((att0, att1, att2, att3)):
        block_col = att.shape[1]
        deep = block_col // 2
        grad = dot(flipped, d_pre[:, k * cols : (k + 1) * cols])
        mixed = dot(att[...], d_mixed[...], TN)
        for i, target in enumerate((own, other)):
            target[k, 0:half, :] = grad[i * half : (i + 1) * half, :].astype(BF16)
            part = mixed[:, i * half : (i + 1) * half].astype(BF16)
            target[k, half : half + deep, 0:half] = part[:deep, :]
            target[k, half : half + deep, half:] = part[deep:, :]
            at = half + deep
            rows = jnp.concatenate(
                [
                    sums_mid[0:4, :],
                    sums_back[0:3, :],
                    count[0:1, :],
                    sums_back[4 + k : 5 + k, :],
                    jnp.zeros((target.shape[1] - at - 9, target.shape[2]), F32),
                ],
                0,
            )
            target[k, at:, :] = rows.astype(BF16)


def weight_grads(hidden, d_pre, attended, d_mixed, sums_mid, sums_back, count):
    width = hidden.shape[1]
    rows = width // 2 + 128
    shape = ((4, rows, d_pre.shape[1] // 4), BF16)
    return whole_call(
        weight_grads_kernel,
        "weight_grads",
        (hidden, d_pre, *attended, d_mixed, sums_mid, sums_back, count),
        [shape, shape],
        cost=pl.CostEstimate(flops=6 << 30, bytes_accessed=12 << 20, transcendentals=0),
    )


def fold_cores(own, came):
    _, rows, cols = own.shape

    def kernel(own_ref, came_ref, *outs):
        for k, out in enumerate(outs):
            out[...] = (own_ref[k].astype(F32) + came_ref[k].astype(F32)).astype(BF16)

    return whole_call(kernel, "fold_cores", (own, came), [((rows, cols), BF16)] * 4)


def split_cores(own, came):
    _, rows, cols = own.shape
    half = rows // 2

    def kernel(own_ref, came_ref, send_x, send_y, keep_upper, keep_lower):
        def total(upper, k):
            at = slice(0, half) if upper else slice(half, rows)
            return (own_ref[k, at, :].astype(F32) + came_ref[k, at, :].astype(F32)).astype(BF16)

        for i, k in enumerate((1, 3)):
            send_x[i] = total(True, k)
        for i, k in enumerate((2, 3)):
            send_y[i] = total(False, k)
        for i, k in enumerate((0, 2)):
            keep_upper[i] = total(True, k)
        for i, k in enumerate((0, 1)):
            keep_lower[i] = total(False, k)

    return whole_call(kernel, "split_cores", (own, came), [((2, half, cols), BF16)] * 4)


def second_step(keep_upper, came_x, keep_lower, came_y):
    def kernel(upper, upper_came, lower, lower_came, send_y, send_x, kept):
        half = upper.shape[1]
        send_y[...] = (upper[1].astype(F32) + upper_came[1].astype(F32)).astype(BF16)
        send_x[...] = (lower[1].astype(F32) + lower_came[1].astype(F32)).astype(BF16)
        kept[:half, :] = upper[0].astype(F32) + upper_came[0].astype(F32)
        kept[half:, :] = lower[0].astype(F32) + lower_came[0].astype(F32)

    half, cols = keep_upper.shape[1:]
    return whole_call(
        kernel,
        "second_step",
        (keep_upper, came_x, keep_lower, came_y),
        [((half, cols), BF16)] * 2 + [((2 * half, cols), F32)],
    )


def add_halves(kept, upper, lower):
    def kernel(kept, upper, lower, out):
        half = upper.shape[0]
        out[:half, :] = (kept[:half, :] + upper[...].astype(F32)).astype(BF16)
        out[half:, :] = (kept[half:, :] + lower[...].astype(F32)).astype(BF16)

    return whole_call(kernel, "add_halves", (kept, upper, lower), [(kept.shape, BF16)])[0]


def fold_quarters(terms, scalars):
    rows, cols = terms[0].shape
    part = rows // 4
    count = len(terms)

    def kernel(scalars, *refs):
        for k in range(4):
            at = pl.ds(pl.multiple_of((scalars[2] ^ k) * part, 8), part)
            total = sum(term[at, :].astype(F32) for term in refs[:count])
            refs[count + k % 2][k // 2] = total.astype(BF16)

    return whole_call(kernel, "fold_quarters", terms, [((2, part, cols), BF16)] * 2, scalars)


def finish(dense, qkv, half, block_col, scalars):
    _, part, cols = dense[0].shape
    qkv_part = qkv[0].shape[1]
    deep = block_col // 2

    def kernel(scalars, *refs):
        up, out, table, query, key, value, bias, dense_all, qkv_all = refs[4:]
        for parts, target in ((refs[:2], dense_all), (refs[2:4], qkv_all)):
            for k in range(4):
                piece = parts[k % 2].at[k // 2]
                rows = piece.shape[0]
                at = pl.ds(pl.multiple_of((scalars[2] ^ k) * rows, 8), rows)
                target[at, :] = piece[...].astype(F32)
        up[...] = dense_all[:half, :]
        out[:deep, :] = dense_all[half : half + deep, :half]
        out[deep:, :] = dense_all[half : half + deep, half:]
        table[...] = dense_all[half + deep : half + deep + 16, :]
        for i, target in enumerate((query, key, value)):
            target[...] = qkv_all[i * block_col : (i + 1) * block_col, :]
        bias[...] = qkv_all[3 * block_col : 3 * block_col + 8, :]

    S = jax.ShapeDtypeStruct
    return pl.pallas_call(
        kernel,
        out_shape=[S((half, cols), F32), S((block_col, half), F32), S((16, cols), F32)]
        + [S((block_col, half), F32)] * 3
        + [S((8, half), F32)],
        in_specs=[SMEM_SPEC] + [VMEM_SPEC] * 4,
        out_specs=[VMEM_SPEC] * 7,
        scratch_shapes=[
            pltpu.VMEM((4 * part, cols), F32),
            pltpu.VMEM((4 * qkv_part, half), F32),
        ],
        compiler_params=pltpu.CompilerParams(vmem_limit_bytes=SMALL_LIMIT),
        cost_estimate=SMALL_COST,
        name="finish",
    )(scalars, *dense, *qkv)


def dot(left, right, dims=NN):
    return lax.dot_general(left, right, dims, preferred_element_type=F32)


def split3(value):
    high = value.astype(BF16)
    rest = value - high.astype(F32)
    middle = rest.astype(BF16)
    low = (rest - middle.astype(F32)).astype(BF16)
    return high.astype(F32), middle.astype(F32), low.astype(F32)


def key_range(code, span, span_rows, blocks):
    per = span_rows // BLK
    first_seg = code[span * per, 0] // 2
    last_seg = code[span * per + per - 1, BLK - 1] // 2
    low = jnp.int32(0)
    high = jnp.int32(0)
    for other in range(blocks):
        start = code[other, 0]
        low += (code[other, BLK - 1] // 2 < first_seg).astype(jnp.int32)
        high += ((start // 2 <= last_seg) & (start % 2 == 1)).astype(jnp.int32)
    below = jnp.maximum(jnp.minimum(high, span * per) - low, 0)
    above = jnp.maximum(high - (span + 1) * per, 0)
    return low, below, below + above


def key_block(step, low, below, after):
    return jnp.where(step < below, low + step, after + step - below)


def lane_index(rows):
    return lax.broadcasted_iota(jnp.int32, (rows, 128), 1)


def allowed_block(code_rows, block, offset, span_rows):
    row = lax.broadcasted_iota(jnp.int32, (span_rows, BLK), 0)
    col = lax.broadcasted_iota(jnp.int32, (span_rows, BLK), 1)
    return (code_rows[pl.ds(block, 1), :] % 2 == 1) | (row == col + offset)


def attention_forward_kernel(heads, scalars, code, *refs):
    code_rows = refs[0]
    shards_in = refs[1:5]
    weights = refs[5:7]
    pieces = refs[7:11]
    saved = refs[11:15]
    padded, max_scr, acc_scr, query_pad, key_pad, value_pad, out_pad, whole_sem, span_sem = refs[15:]
    span_rows, width = shards_in[0].shape
    cols = 64 * heads
    flip = scalars[1]
    per = span_rows // BLK
    blocks = query_pad.shape[1] // BLK
    lane = lane_index(span_rows)
    for i in range(3):
        src = slice(i * cols, (i + 1) * cols)
        padded[i * 256 : i * 256 + cols, : width // 2] = weights[0][src, :]
        padded[i * 256 : i * 256 + cols, width // 2 :] = weights[1][src, :]
        padded[i * 256 + cols : (i + 1) * 256, :] = jnp.zeros((256 - cols, width), BF16)
    marks_bias = weights[0][3 * cols : 3 * cols + 1, :].astype(F32)
    no_bias = jnp.zeros((1, 256 - cols), F32)
    biases = (
        jnp.concatenate([marks_bias[:, :cols], no_bias], 1),
        None,
        jnp.concatenate([marks_bias[:, cols : 2 * cols], no_bias], 1),
    )
    value_ones = jnp.where((lane >= 64) & (lane < 67), 1.0, 0.0)
    for shard, tokens in enumerate(shards_in):
        rows = slice(shard * span_rows, (shard + 1) * span_rows)
        marks = [
            jnp.broadcast_to(
                code_rows[pl.ds((shard ^ flip) * per + part, 1), :].astype(F32), (128, BLK)
            ).T
            for part in range(per)
        ]
        marks = jnp.concatenate(marks, 0).astype(jnp.int32)
        same = lane - 64 == marks // 2
        ids = (lane >= 64) & (lane < 80)
        query_marks = jnp.where((ids & same) | (lane == 80), 1.0, 0.0)
        key_marks = jnp.where(
            (ids & ~same) | ((lane == 80) & (marks % 2 == 0)),
            MASKED,
            jnp.where((lane >= 81) & (lane < 84), -1.0, 0.0),
        )
        for i, (out, extra) in enumerate(
            ((query_pad, query_marks), (key_pad, key_marks), (value_pad, value_ones))
        ):
            projected = dot(tokens[...], padded[i * 256 : (i + 1) * 256, :], NT)
            if biases[i] is not None:
                projected += biases[i]
            if i == 0:
                projected = projected.astype(BF16).astype(F32) * 0.125
            out[0, rows, :] = jnp.where(lane < 64, projected[:, :128], extra).astype(BF16)
            out[1, rows, :] = jnp.where(
                lane < 64, pltpu.roll(projected[:, :128], 64, 1), extra
            ).astype(BF16)
            out[2, rows, :] = jnp.where(lane < 64, projected[:, 128:], extra).astype(BF16)
    no_valid_lane = jnp.where(lane == 80, 0.0, 1.0).astype(BF16)
    whole_copies = [
        pltpu.make_async_copy(key_pad, saved[1], whole_sem.at[0]),
        pltpu.make_async_copy(value_pad, saved[2], whole_sem.at[1]),
    ]
    for copy in whole_copies:
        copy.start()

    def span_copies(at):
        rows = pl.ds(pl.multiple_of(at * span_rows, span_rows), span_rows)
        return [
            pltpu.make_async_copy(
                source.at[:, rows, :], saved[i].at[:, rows, :], span_sem.at[i // 3, at]
            )
            for source, i in ((query_pad, 0), (out_pad, 3))
        ]

    def query_step(span, _):
        at = span ^ flip
        rows = pl.ds(pl.multiple_of(at * span_rows, span_rows), span_rows)
        low, below, count = key_range(code, span, span_rows, blocks)

        def keys_of(block):
            place = (block // per ^ flip) * per + block % per
            return pl.ds(pl.multiple_of(place * BLK, BLK), BLK)

        def scores_of(h, keys, allowed=None):
            if allowed is None:
                return dot(query_pad[h, rows, :], key_pad[h, keys, :], NT)
            scores = dot(query_pad[h, rows, :] * no_valid_lane, key_pad[h, keys, :], NT)
            return jnp.where(allowed, scores, MASKED)

        def each_block(visit):
            for part in range(per):
                block = span * per + part
                visit(keys_of(block), allowed_block(code_rows, block, part * BLK, span_rows))

            def step_fn(step, _):
                visit(keys_of(key_block(step, low, below, (span + 1) * per)), None)
                return 0

            lax.fori_loop(0, count, step_fn, 0)

        acc_scr[...] = jnp.zeros_like(acc_scr)
        max_scr[...] = jnp.zeros_like(max_scr)

        def plain(keys, allowed):
            for h in range(heads):
                probs = jnp.exp(scores_of(h, keys, allowed)).astype(BF16)
                acc_scr[h] += dot(probs, value_pad[h, keys, :])

        each_block(plain)
        least, most = jnp.float32(1.0), jnp.float32(1.0)
        for h in range(heads):
            total = jnp.where(lane == 64, acc_scr[h], 1.0)
            good = (total > 1e-25) & (total < 1e30)
            least = jnp.minimum(least, jnp.min(jnp.where(good, 1.0, 0.0)))

        @pl.when(least < 0.5)
        def _():
            max_scr[...] = jnp.full_like(max_scr, MASKED)

            def find_max(keys, allowed):
                for h in range(heads):
                    scores = scores_of(h, keys, allowed)
                    max_scr[h] = jnp.maximum(
                        max_scr[h], jnp.maximum(scores[:, :128], scores[:, 128:])
                    )

            each_block(find_max)
            for h in range(heads):
                max_scr[h] = jnp.broadcast_to(
                    jnp.max(max_scr[h], axis=1, keepdims=True), (span_rows, 128)
                )
            acc_scr[...] = jnp.zeros_like(acc_scr)

            def shifted(keys, allowed):
                for h in range(heads):
                    row_max = max_scr[h]
                    scores = scores_of(h, keys, allowed)
                    probs = jnp.exp(scores - jnp.concatenate([row_max, row_max], 1))
                    acc_scr[h] += dot(probs.astype(BF16), value_pad[h, keys, :])

            each_block(shifted)

        outs = []
        for h in range(heads):
            acc = acc_scr[h]
            total = jnp.broadcast_to(acc[:, 64:65], acc.shape)
            out = acc / total
            out_pad[h, rows, :] = out
            outs.append(out)
            high, middle, rest = split3(max_scr[h] + jnp.log(total))
            extra = jnp.where(
                lane == 81,
                high,
                jnp.where(lane == 82, middle, jnp.where(lane == 83, rest, 0.0)),
            )
            query_pad[h, rows, :] = query_pad[h, rows, :] + extra.astype(BF16)
        pair = jnp.where(lane < 64, outs[0], pltpu.roll(outs[1], 64, 1)).astype(BF16)
        last = outs[2][:, :64].astype(BF16)
        for k, piece in enumerate(pieces):

            @pl.when(at == k)
            def _():
                piece[:, 0:128] = pair
                piece[:, 128:cols] = last

        for copy in span_copies(at):
            copy.start()
        return 0

    lax.fori_loop(0, len(shards_in), query_step, 0)
    for copy in whole_copies:
        copy.wait()
    for at in range(len(shards_in)):
        for copy in span_copies(at):
            copy.wait()


def attention_forward(scalars, code, token_shards, weights):
    rows, width = token_shards[0].shape
    length = code.shape[0] * BLK
    cols = (weights[0].shape[0] - PAD_ROWS) // 3
    heads = cols // 64
    S = jax.ShapeDtypeStruct
    flops = 2 * length * width * 3 * 256 + 3 * length * length * 128
    return pl.pallas_call(
        lambda *refs: attention_forward_kernel(heads, *refs),
        out_shape=[S((rows, cols), BF16)] * 4
        + [pltpu.HBM((heads, length, 128), BF16)] * 3
        + [pltpu.HBM((heads, length, 128), F32)],
        in_specs=[SMEM_SPEC] * 2 + [VMEM_SPEC] * 7,
        out_specs=[VMEM_SPEC] * 4 + [HBM_SPEC] * 4,
        scratch_shapes=[
            pltpu.VMEM((3 * 256, width), BF16),
            pltpu.VMEM((heads, rows, 128), F32),
            pltpu.VMEM((heads, rows, 128), F32),
        ]
        + [pltpu.VMEM((heads, length, 128), BF16)] * 3
        + [
            pltpu.VMEM((heads, length, 128), F32),
            pltpu.SemaphoreType.DMA((2,)),
            pltpu.SemaphoreType.DMA((2, 4)),
        ],
        compiler_params=pltpu.CompilerParams(vmem_limit_bytes=32 << 20),
        cost_estimate=pl.CostEstimate(
            flops=3 * flops, bytes_accessed=16 << 20, transcendentals=heads * length * 1024
        ),
        name="attention_forward",
    )(scalars, code, code, *token_shards, *weights)


def attention_backward_kernel(heads, scalars, code, *refs):
    code_rows = refs[0]
    grads = refs[1:5]
    sources = refs[5:15]
    own_term, other_term, own_grad, other_grad = refs[15:19]
    grad_pad, query_sum, key_sum, value_sum, low_scr, grad_scr, bias_sum = refs[19:26]
    copies = [
        pltpu.make_async_copy(source, target, refs[36].at[i])
        for i, (source, target) in enumerate(zip(sources, refs[26:36]))
    ]
    for i in (3, 0, 1, 2, 4, 5, 6, 7, 8, 9):
        copies[i].start()
    query_pad, key_pad, value_pad, out_pad = refs[26:30]
    shards_in = refs[30:34]
    weights = refs[34:36]
    key_sum[...] = jnp.zeros_like(key_sum)
    value_sum[...] = jnp.zeros_like(value_sum)
    query_sum[...] = jnp.zeros_like(query_sum)
    copies[3].wait()
    span_rows = grads[0].shape[0]
    flip = scalars[1]
    per = span_rows // BLK
    blocks = query_pad.shape[1] // BLK
    lane = lane_index(span_rows)
    gap = jnp.zeros((span_rows, 64), BF16)
    for shard, grad in enumerate(grads):
        rows = slice(shard * span_rows, (shard + 1) * span_rows)
        pair = grad[:, 0:128].astype(F32)
        last = jnp.concatenate([grad[:, 128:192], gap], 1).astype(F32)
        for h, block in enumerate((pair, pltpu.roll(pair, 64, 1), last)):
            block = jnp.where(lane < 64, block, 0.0)
            delta = jnp.sum(block * out_pad[h, rows, :], axis=1, keepdims=True)
            high, middle, rest = split3(-delta)
            block = jnp.where(
                lane == 64,
                high,
                jnp.where(lane == 65, middle, jnp.where(lane == 66, rest, block)),
            )
            grad_pad[h, rows, :] = block.astype(BF16)
    for i in range(3):
        copies[i].wait()
    no_valid_lane = jnp.where(lane == 80, 0.0, 1.0).astype(BF16)

    def query_step(span, _):
        at = span ^ flip
        rows = pl.ds(pl.multiple_of(at * span_rows, span_rows), span_rows)
        low, below, count = key_range(code, span, span_rows, blocks)

        def visit(block, allowed):
            place = (block // per ^ flip) * per + block % per
            keys = pl.ds(pl.multiple_of(place * BLK, BLK), BLK)
            for h in range(heads):
                query, grad = query_pad[h, rows, :], grad_pad[h, rows, :]
                key, value = key_pad[h, keys, :], value_pad[h, keys, :]
                if allowed is None:
                    scores = dot(key, query, NT)
                else:
                    scores = jnp.where(allowed, dot(key, query * no_valid_lane, NT), MASKED)
                probs = jnp.exp(scores)
                d_scores = (probs * dot(value, grad, NT)).astype(BF16)
                value_sum[h, keys, :] += dot(probs.astype(BF16), grad)
                key_sum[h, keys, :] += dot(d_scores, query)
                query_sum[h, rows, :] += dot(d_scores, key, TN)

        for part in range(per):
            block = span * per + part
            key_at = lax.broadcasted_iota(jnp.int32, (BLK, span_rows), 0)
            query_at = lax.broadcasted_iota(jnp.int32, (BLK, span_rows), 1)
            marks = jnp.broadcast_to(
                code_rows[pl.ds(block, 1), :].astype(F32), (128, BLK)
            ).T.astype(jnp.int32)
            valid = jnp.concatenate([marks] * (span_rows // 128), 1) % 2 == 1
            visit(block, valid | (query_at == key_at + part * BLK))

        def step_fn(step, _):
            visit(key_block(step, low, below, (span + 1) * per), None)
            return 0

        lax.fori_loop(0, count, step_fn, 0)
        return 0

    lax.fori_loop(0, len(grads), query_step, 0)
    for i in range(4, 10):
        copies[i].wait()
    bias_sum[...] = jnp.zeros_like(bias_sum)
    for shard in range(len(grads)):
        rows = slice(shard * span_rows, (shard + 1) * span_rows)
        parts = [query_sum[h, rows, :] * 0.125 for h in range(heads)]
        parts += [sums[h, rows, :] for sums in (key_sum, value_sum) for h in range(heads)]
        for at in range(0, len(parts), 2):
            if at + 1 < len(parts):
                value = jnp.where(lane < 64, parts[at], pltpu.roll(parts[at + 1], 64, 1))
            else:
                value = parts[at][:, :64]
            low = value.astype(BF16)
            cols = slice(at * 64, at * 64 + low.shape[1])
            low_scr[:, cols] = low
            bias_sum[0:1, cols] += column_sum(low.astype(F32))
        low = low_scr[...]
        depth = low.shape[1]
        term = jnp.concatenate([dot(low, w[:depth, :]).astype(BF16) for w in weights], 1)
        if shard < 2:
            own_term[shard] = term
        else:
            other_term[shard - 2] = term
        part = dot(low, shards_in[shard][...], TN)
        if shard == 0:
            grad_scr[...] = part
        elif shard < 3:
            grad_scr[...] += part
        else:
            total = (grad_scr[...] + part).astype(BF16)
            half = total.shape[1] // 2
            own_grad[:depth, :] = total[:, :half]
            other_grad[:depth, :] = total[:, half:]
    cols = heads * 64
    bias = jnp.concatenate([bias_sum[:, 0:cols], bias_sum[:, 2 * cols :]], 1).astype(BF16)
    bias = jnp.concatenate([bias] * ((own_grad.shape[0] - depth) // bias.shape[0]), 0)
    own_grad[depth:, :] = bias
    other_grad[depth:, :] = bias


def attention_backward(scalars, code, grads, saved, token_shards, weights):
    length = code.shape[0] * BLK
    heads = saved[0].shape[0]
    rows, width = token_shards[0].shape
    cols = 3 * heads * 64
    S = jax.ShapeDtypeStruct
    return pl.pallas_call(
        lambda *refs: attention_backward_kernel(heads, *refs),
        out_shape=[
            S((2, rows, width), BF16),
            S((2, rows, width), BF16),
            S((cols + GRAD_PAD, width // 2), BF16),
            S((cols + GRAD_PAD, width // 2), BF16),
        ],
        in_specs=[SMEM_SPEC] * 2 + [VMEM_SPEC] * 5 + [HBM_SPEC] * 10,
        out_specs=[VMEM_SPEC] * 4,
        scratch_shapes=[
            pltpu.VMEM((heads, length, 128), BF16),
            pltpu.VMEM((heads, length, 128), F32),
            pltpu.VMEM((heads, length, 128), F32),
            pltpu.VMEM((heads, length, 128), F32),
            pltpu.VMEM((rows, cols), BF16),
            pltpu.VMEM((cols, width), F32),
            pltpu.VMEM((16, cols), F32),
        ]
        + [pltpu.VMEM(a.shape, a.dtype) for a in (*saved, *token_shards, *weights)]
        + [pltpu.SemaphoreType.DMA((10,))],
        compiler_params=pltpu.CompilerParams(vmem_limit_bytes=40 << 20),
        cost_estimate=pl.CostEstimate(
            flops=heads * length * length * 1500, bytes_accessed=8 << 20, transcendentals=0
        ),
        name="attention_backward",
    )(
        scalars,
        code,
        code,
        *grads,
        *(in_hbm(a) for a in (*saved, *token_shards, *weights)),
    )


CORE_CHIP = ("gy", "gz")
CHIP = [[(c, c ^ k) for c in range(4)] for k in range(4)]
PLANE = [[(p, p ^ k) for p in range(4)] for k in range(4)]
CORE = [(0, 1), (1, 0)]


def plane_perm(to):
    pairs = []
    for device in range(8):
        core, row, col = device // 4, device // 2 % 2, device % 2
        core_to, row_to, col_to = to(core, row, col)
        pairs.append((device, core_to * 4 + row_to * 2 + col_to))
    return pairs


TO_OWNER = [
    plane_perm(lambda core, row, col, a=k // 2, b=k % 2: (row, core ^ a, col ^ b))
    for k in range(4)
]
TO_HEADS = [
    plane_perm(lambda core, row, col, a=k // 2, b=k % 2: (row ^ a, core, col ^ b))
    for k in range(4)
]


def to_owner(value, k):
    return lax.ppermute(value, CORE_CHIP, TO_OWNER[k])


def to_heads(value, k):
    return lax.ppermute(value, CORE_CHIP, TO_HEADS[k])


def to_chip(value, k):
    return lax.ppermute(value, "gz", CHIP[k])


def to_core(value):
    return lax.ppermute(value, "gy", CORE)


def to_plane(value, k):
    return lax.ppermute(value, "gx", PLANE[k])


def after(value, *others):
    return lax.optimization_barrier((value,) + others)[0]


def swap_halves(flip, value):
    half = value.shape[-1] // 2
    swapped = jnp.concatenate([value[..., half:], value[..., :half]], -1)
    return jnp.where(flip, swapped, value)


def add_low(left, right):
    return (left.astype(F32) + right.astype(F32)).astype(BF16)


def sum_planes(keep, send):
    if lax.axis_size("gx") != 4:
        total = lax.psum(jnp.stack([keep, send]), "gx")
        return total[0], total[1]
    pair = keep.astype(F32) + to_plane(send, 1).astype(F32)
    total = (pair[0] + to_plane(pair[1].astype(BF16), 2).astype(F32)).astype(BF16)
    pair = jnp.stack([total, to_plane(total, 2)])
    return pair, to_plane(pair, 1)


def shards(
    tokens,
    segment_ids,
    valid_mask,
    cotangent,
    teacher,
    w_query,
    b_query,
    w_key,
    w_value,
    b_value,
    w_out,
    b_out,
    norm1_gain,
    norm1_bias,
    w_up,
    b_up,
    w_down,
    b_down,
    norm2_gain,
    norm2_bias,
):
    row_count, width = tokens.shape
    half = width // 2
    core = lax.axis_index("gy")
    chip = lax.axis_index("gz")
    flip = core == 1
    block_col = w_query.shape[1]
    hidden_col = w_up.shape[1]
    plane = lax.axis_index("gx") if lax.axis_size("gx") == 4 else jnp.int32(0)
    scalars = jnp.stack([core, core * 2 + chip % 2, plane, chip]).astype(jnp.int32)

    own_tokens = swap_halves(flip, tokens)
    shard0, shard1 = to_owner(own_tokens, 0), to_owner(own_tokens, 1)
    code = (segment_ids * 2 + valid_mask).reshape(-1, BLK)
    bias_row = jnp.concatenate([b_query, b_value])[None, :]
    qkv_own = jnp.concatenate(
        [w_query.T, w_key.T, w_value.T, jnp.broadcast_to(bias_row, (PAD_ROWS, half))], 0
    )
    vectors = jnp.stack([b_out, norm1_gain, norm1_bias, b_down, norm2_gain, norm2_bias] + [b_out] * 2)
    vectors = swap_halves(flip, vectors.astype(F32))
    own_valid = lax.dynamic_slice_in_dim(valid_mask, chip * row_count, row_count, 1).astype(F32)
    count = jnp.concatenate([own_valid, jnp.zeros((1, width - row_count), F32)], 1)
    count = jnp.broadcast_to(count, (8, width))
    own_valid = own_valid.T
    packed = jnp.concatenate(
        [
            jnp.concatenate([w_down[: hidden_col // 2], w_down[hidden_col // 2 :]], 1),
            w_up,
            jnp.concatenate([w_out[: block_col // 2], w_out[block_col // 2 :]], 1),
            jnp.broadcast_to(b_up[None, :], (PAD_ROWS, hidden_col)),
        ],
        0,
    )

    code, qkv_own, scalars, packed, vectors, own_valid, count, *_ = lax.optimization_barrier(
        (code, qkv_own, scalars, packed, vectors, own_valid, count, own_tokens)
    )
    code = to_owner(code, 0)
    qkv = (to_owner(qkv_own, 0), to_owner(qkv_own, 2))
    shard0, shard1, packed, code, *qkv = lax.optimization_barrier(
        (shard0, shard1, packed, code, *qkv)
    )
    token_shards = (shard0, shard1, to_core(shard0), to_core(shard1))
    pack_x, pack_y = to_chip(packed, 1), to_chip(packed, 2)
    packed_other = to_core(packed)

    scalars = after(scalars, packed)
    results = attention_forward(scalars, code, token_shards, qkv)
    saved = results[4:]
    attended = [to_owner(results[k], k) for k in range(4)]

    deep = hidden_col // 2
    pack_x, pack_y = lax.optimization_barrier((pack_x, pack_y, results[0]))[:2]
    far = (to_chip(pack_x[:, :half], 2), to_chip(pack_y[:, half:], 1))
    packs = (packed, pack_x, pack_y, *far)
    packs_other = (packed_other, *(to_core(v) for v in packs[1:]))
    out_deep = block_col // 2
    downs = [(v, deep, 0) for v in packs + packs_other]
    ups = [(v, half, 1) for v in packs + packs_other]
    outs = [(v, out_deep, (deep + half) // out_deep) for v in packs + packs_other]
    biases = [(v, PAD_ROWS, (deep + half + out_deep) // PAD_ROWS) for v in packs]
    whole_vectors = [(vectors, 8, 0)]
    out_scratch = [pltpu.VMEM((4 * block_col, half), BF16)] * 2

    inner = 4 * hidden_col
    square = 2 * row_count * width * inner
    full = (row_count, width)
    rows = min(ROWS, row_count)
    normed, inv_std, hidden_low, act, slope, output, d_resid2, d_branch, sums_mid = row_call(
        ffn_forward_kernel,
        "ffn_forward",
        rows,
        scalars,
        (*attended, own_tokens, cotangent, teacher, own_valid),
        downs + ups + outs + biases + whole_vectors,
        (
            (full, F32),
            ((row_count, 1), F32),
            (full, BF16),
            ((row_count, inner), BF16),
            ((row_count, inner), BF16),
            (full, BF16),
            (full, F32),
            (full, BF16),
        ),
        (((8, width), F32),),
        out_scratch,
        5 * square,
    )
    pieces = (4, hidden_col, half)
    d_down_other = jnp.einsum("lf,lm->fm", act, d_branch[:, half:], preferred_element_type=F32)
    d_down_came = to_core(d_down_other.astype(BF16).reshape(pieces))
    d_down = jnp.einsum("lf,lm->fm", act, d_branch[:, :half], preferred_element_type=F32)
    down_x, down_y, down_upper, down_lower = split_cores(
        d_down.astype(BF16).reshape(pieces), d_down_came
    )
    d_branch = after(d_branch, down_upper)
    down_x, down_y = to_chip(down_x, 1), to_chip(down_y, 2)
    d_pre, d_mixed, d_resid1, *back = row_call(
        ffn_back_kernel,
        "ffn_back",
        rows,
        scalars,
        (d_branch, slope, d_resid2, normed, inv_std),
        downs + ups + outs + whole_vectors,
        (((row_count, inner), BF16), (full, BF16), (full, F32))
        + tuple(((row_count, block_col), BF16) for _ in range(4)),
        (((8, width), F32),),
        out_scratch,
        3 * square,
    )
    sums_back = back[4]
    d_pieces = [to_heads(back[k], k) for k in range(4)]

    down_y, down_x, down_kept = second_step(down_upper, down_x, down_lower, down_y)
    hidden_low, down_y, down_x, *_ = lax.optimization_barrier(
        (hidden_low, down_y, down_x, d_pieces[1], d_pieces[2])
    )
    own_grads, other_grads = weight_grads(
        hidden_low, d_pre, attended, d_mixed, sums_mid, sums_back, count
    )
    d_dense = fold_cores(own_grads, to_core(other_grads))
    down_total = add_halves(down_kept, to_chip(down_y, 2), to_chip(down_x, 1))
    grad_down = lax.psum(down_total, "gx")
    d_pieces[0] = after(d_pieces[0], d_dense[0], down_total)
    d_dense = [d_dense[0]] + [to_chip(d_dense[k], k) for k in (1, 2, 3)]

    own_term, other_term, d_own, d_other = attention_backward(
        scalars, code, d_pieces, saved, token_shards, qkv
    )
    d_dense[0] = after(d_dense[0], grad_down)
    quarters = fold_quarters(d_dense, scalars)
    d_own, d_other, other_term, *_ = lax.optimization_barrier(
        (d_own, d_other, other_term, *quarters)
    )
    other_term = to_core(other_term)
    d_w = (to_owner(d_own, 0), to_heads(d_other, 2))
    term0 = add_low(own_term[0], other_term[0])
    term1 = add_low(own_term[1], other_term[1])
    came0, came1 = to_owner(term0, 0), to_owner(term1, 1)
    qkv_grad = sum_planes(*fold_quarters(d_w, scalars))
    dense_grad = sum_planes(*quarters)
    d_tokens = d_resid1 + came0.astype(F32) + came1.astype(F32)
    grad_up, grad_out, table, grad_query, grad_key, grad_value, d_bias = finish(
        dense_grad, qkv_grad, half, block_col, scalars
    )

    mean_loss = jnp.sum(table[3]) / (jnp.sum(table[7]) * width)
    return (
        output,
        mean_loss,
        swap_halves(flip, d_tokens.astype(BF16)),
        grad_query.T,
        d_bias[0, :block_col],
        grad_key.T,
        grad_value.T,
        d_bias[0, block_col:],
        grad_out,
        table[6],
        table[4],
        table[5],
        grad_up,
        table[8],
        grad_down.astype(F32),
        table[2],
        table[0],
        table[1],
    )


def solution(mesh):
    placed = (
        P(("gx", "gy", "gz"), None),
        P(("gx", "gy"), None),
        P(("gx", "gy"), None),
        P(("gx", "gy", "gz"), None),
        P(("gx", "gy", "gz"), None),
        P("gy", "gz"),
        P("gz"),
        P("gy", "gz"),
        P("gy", "gz"),
        P("gz"),
        P("gz", "gy"),
        P(),
        P(),
        P(),
        P("gy", "gz"),
        P("gz"),
        P("gz", "gy"),
        P(),
        P(),
        P(),
    )
    return jax.shard_map(
        shards,
        mesh=mesh,
        in_specs=placed,
        out_specs=(
            P(("gx", "gy", "gz"), None),
            P(),
            P(("gx", "gy", "gz"), None),
            P("gy", "gz"),
            P("gz"),
            P("gy", "gz"),
            P("gy", "gz"),
            P("gz"),
            P("gz", "gy"),
            P(),
            P(),
            P(),
            P("gy", "gz"),
            P("gz"),
            P("gz", "gy"),
            P(),
            P(),
            P(),
        ),
        check_vma=False,
    )
```

```python
import math

import jax
import jax.numpy as jnp
from jax import lax
from jax.experimental import pallas as pl
from jax.experimental.pallas import tpu as pltpu
from jax.sharding import PartitionSpec as P

EPSILON = 1e-05
MASKED = -1e30
PAD_ROWS = 16
GRAD_PAD = 64
BLK = 256
F32 = jnp.float32
BF16 = jnp.bfloat16
NT = (((1,), (1,)), ((), ()))
NN = (((1,), (0,)), ((), ()))
TN = (((0,), (0,)), ((), ()))


VMEM_SPEC = pl.BlockSpec(memory_space=pltpu.VMEM)
SMEM_SPEC = pl.BlockSpec(memory_space=pltpu.SMEM)
HBM_SPEC = pl.BlockSpec(memory_space=pltpu.HBM)
VMEM_LIMIT = 24 << 20
SMALL_LIMIT = 20 << 20
SMALL_COST = pl.CostEstimate(flops=1 << 16, bytes_accessed=1 << 12, transcendentals=0)


def in_hbm(array):
    return pltpu.with_memory_space_constraint(array, pltpu.HBM)


def pack_copies(sources, targets, sems, tops):
    copies = []
    for part, (first, last) in enumerate(tops):
        rows = slice(first, last)
        copies.append(
            [
                pltpu.make_async_copy(source.at[rows, :], target.at[rows, :], sems.at[part, i])
                for i, (source, target) in enumerate(zip(sources, targets))
            ]
        )
    return copies


def half_start(scalars, second, half):
    flip = scalars[0]
    return pl.multiple_of(jnp.where(second, 1 - flip, flip) * half, 128)


def read_swapped(ref, scalars):
    half = ref.shape[-1] // 2
    return jnp.concatenate(
        [
            ref[:, pl.ds(half_start(scalars, False, half), half)].astype(F32),
            ref[:, pl.ds(half_start(scalars, True, half), half)].astype(F32),
        ],
        1,
    )


def write_swapped(ref, rows, value, scalars):
    half = ref.shape[-1] // 2
    ref[rows, pl.ds(half_start(scalars, False, half), half)] = value[:, :half].astype(ref.dtype)
    ref[rows, pl.ds(half_start(scalars, True, half), half)] = value[:, half:].astype(ref.dtype)


def column_sum(value):
    return jnp.sum(value, 0, keepdims=True)


def layer_norm(resid):
    average = jnp.mean(resid, -1, keepdims=True)
    centered = resid - average
    inv_std = lax.rsqrt(jnp.mean(centered * centered, -1, keepdims=True) + EPSILON)
    return centered * inv_std, inv_std


def layer_norm_back(upstream, gain, normed, inv_std):
    scaled = upstream * gain
    return inv_std * (
        scaled
        - jnp.mean(scaled, -1, keepdims=True)
        - normed * jnp.mean(scaled * normed, -1, keepdims=True)
    )


def spread_out(packs, target, first, deep, half):
    rows = slice(first, first + deep)
    at = 0
    for pack in packs[:3]:
        target[at : at + deep, :] = pack[rows, 0:half]
        target[at + deep : at + 2 * deep, :] = pack[rows, half : 2 * half]
        at += 2 * deep
    target[at : at + deep, :] = packs[3][rows, :]
    target[at + deep : at + 2 * deep, :] = packs[4][rows, :]


def chunk_list(packs, half):
    return [(k, start) for k in range(5) for start in range(0, packs[k].shape[1], half)]


def ffn_forward_kernel(deep, scalars, *refs):
    att = refs[:4]
    own_tokens, valid, vectors = refs[4:7]
    cot_source, teach_source = refs[7:9]
    sources = refs[9:19]
    std_out, output, resid_out, branch_out, sums, act_out = refs[19:25]
    normed_hbm, low_hbm, slope_hbm = refs[25:28]
    packs = refs[28:38]
    cotangent, teacher, normed_out, low_out, slope_out = refs[38:43]
    spread = refs[43:45]
    sems, row_sems, chunk_sems = refs[45:]
    block_col = att[0].shape[1]
    half = packs[4].shape[1]
    out_deep = block_col // 2
    top = deep + half
    loads = pack_copies(
        sources, packs, sems, ((top, packs[0].shape[0]), (deep, top), (0, deep))
    )
    row_loads = [
        pltpu.make_async_copy(cot_source, cotangent, row_sems.at[0]),
        pltpu.make_async_copy(teach_source, teacher, row_sems.at[1]),
    ]

    def start_piece(k):
        if k < 5:
            for part in (1, 2):
                loads[part][k].start()
                loads[part][5 + k].start()

    for copy in loads[0]:
        copy.start()
    start_piece(0)
    for copy in loads[0]:
        copy.wait()
    start_piece(1)
    spread_out(packs[:5], spread[0], top, out_deep, half)
    spread_out(packs[5:], spread[1], top, out_deep, half)
    mixed = []
    for out_ref in spread:
        total = jnp.zeros((att[0].shape[0], half), F32)
        for k in range(4):
            total += dot(att[k][...], out_ref[k * block_col : (k + 1) * block_col, :])
        mixed.append(total)
    resid = own_tokens[...].astype(F32) + (jnp.concatenate(mixed, 1) + vectors[0:1, :])
    normed, inv_std = layer_norm(resid)
    hidden = normed * vectors[1:2, :] + vectors[2:3, :]
    normed_out[...] = normed
    std_out[...] = inv_std
    low_out[...] = hidden.astype(BF16)
    stores = [
        pltpu.make_async_copy(normed_out, normed_hbm, row_sems.at[2]),
        pltpu.make_async_copy(low_out, low_hbm, row_sems.at[3]),
    ]
    for copy in stores:
        copy.start()
    bias_row = top + out_deep
    branch = [jnp.zeros((att[0].shape[0], half), F32) for _ in range(2)]
    for at, (k, start) in enumerate(chunk_list(packs, half)):
        if start == 0:
            for part in (1, 2):
                loads[part][k].wait()
                loads[part][5 + k].wait()
            start_piece(k + 2)
            if k == 3:
                for copy in row_loads:
                    copy.start()
        cols = slice(start, start + half)
        preact = (
            dot(low_out[:, :half], packs[k][deep:top, cols])
            + dot(low_out[:, half:], packs[5 + k][deep:top, cols])
            + packs[k][bias_row : bias_row + 1, cols].astype(F32)
        )
        normal_cdf = 0.5 * (1.0 + lax.erf(preact * (1.0 / math.sqrt(2.0))))
        slope = normal_cdf + preact * jnp.exp(-0.5 * preact * preact) * (
            1.0 / math.sqrt(2.0 * math.pi)
        )
        act = (preact * normal_cdf).astype(BF16)
        place = slice(at * half, (at + 1) * half)
        act_out[:, place] = act
        slope_out[:, place] = slope.astype(BF16)
        copy = pltpu.make_async_copy(
            slope_out.at[:, place], slope_hbm.at[:, place], chunk_sems.at[at]
        )
        copy.start()
        stores.append(copy)
        branch[0] += dot(act, packs[k][:deep, cols])
        branch[1] += dot(act, packs[5 + k][:deep, cols])
    for copy in row_loads:
        copy.wait()
    gain = vectors[4:5, :]
    hidden = normed_out[...] * vectors[1:2, :] + vectors[2:3, :]
    resid = hidden + (jnp.concatenate(branch, 1) + vectors[3:4, :])
    normed, inv_std = layer_norm(resid)
    full = normed * gain + vectors[5:6, :]
    write_swapped(output, slice(None), full, scalars)
    mismatch = full - read_swapped(teacher, scalars)
    masked = valid[...] * mismatch
    d_output = read_swapped(cotangent, scalars) + masked
    d_resid = layer_norm_back(d_output, gain, normed, inv_std)
    resid_out[...] = d_resid
    low = d_resid.astype(BF16)
    branch_out[...] = low
    sums[...] = jnp.zeros_like(sums)
    rows = (
        column_sum(d_output * normed),
        column_sum(d_output),
        column_sum(low.astype(F32)),
        column_sum(masked * mismatch),
    )
    for at, row in enumerate(rows):
        write_swapped(sums, slice(at, at + 1), row, scalars)
    for copy in stores:
        copy.wait()


def pack_scratch(packs, half, block_col):
    return [pltpu.VMEM(p.shape, p.dtype) for p in packs], [
        pltpu.VMEM((4 * block_col, half), BF16)
    ] * 2


def ffn_forward(scalars, attended, own_tokens, valid, vectors, cotangent, teacher, packs, deep):
    rows, width = own_tokens.shape
    half = width // 2
    inner = 8 * half
    full = (rows, width)
    pack_scr, spread = pack_scratch(packs, half, attended[0].shape[1])
    S = jax.ShapeDtypeStruct
    return pl.pallas_call(
        lambda *refs: ffn_forward_kernel(deep, *refs),
        out_shape=[S((rows, 1), F32), S(full, BF16), S(full, F32), S(full, BF16)]
        + [S((8, width), F32), S((rows, inner), BF16)]
        + [pltpu.HBM(full, F32), pltpu.HBM(full, BF16), pltpu.HBM((rows, inner), BF16)],
        in_specs=[SMEM_SPEC] + [VMEM_SPEC] * 7 + [HBM_SPEC] * 12,
        out_specs=[VMEM_SPEC] * 6 + [HBM_SPEC] * 3,
        scratch_shapes=pack_scr
        + [pltpu.VMEM(full, BF16)] * 2
        + [pltpu.VMEM(full, F32), pltpu.VMEM(full, BF16), pltpu.VMEM((rows, inner), BF16)]
        + spread
        + [
            pltpu.SemaphoreType.DMA((3, 10)),
            pltpu.SemaphoreType.DMA((4,)),
            pltpu.SemaphoreType.DMA((8,)),
        ],
        compiler_params=pltpu.CompilerParams(vmem_limit_bytes=48 << 20),
        cost_estimate=pl.CostEstimate(
            flops=10 * rows * width * inner, bytes_accessed=24 << 20, transcendentals=0
        ),
        name="ffn_forward",
    )(
        scalars,
        *attended,
        own_tokens,
        valid,
        vectors,
        *(in_hbm(a) for a in (cotangent, teacher, *packs)),
    )


def ffn_back_kernel(deep, scalars, *refs):
    d_branch, std_ref, vectors, d_resid2, sums_mid, count = refs[:6]
    att = refs[6:10]
    normed_source, slope_source, hidden_source = refs[10:13]
    sources = refs[13:23]
    resid_out = refs[23]
    pieces = refs[24:28]
    own_hbm, other_hbm = refs[28:30]
    packs = refs[30:40]
    normed_ref, slope, hidden, flipped, own, other, sums = refs[40:47]
    spread = refs[47:49]
    sems, row_sem, chunk_sems, grad_sems = refs[49:]
    half = packs[4].shape[1]
    block_col = pieces[0].shape[1]
    out_deep = block_col // 2
    top = deep + half
    loads = pack_copies(sources, packs, sems, ((0, deep), (deep, top), (top, top + out_deep)))
    normed_load = pltpu.make_async_copy(normed_source, normed_ref, row_sem.at[0])
    hidden_load = pltpu.make_async_copy(hidden_source, hidden, row_sem.at[1])
    chunks = chunk_list(packs, half)
    slopes = [
        pltpu.make_async_copy(
            slope_source.at[:, at * half : (at + 1) * half],
            slope.at[:, at * half : (at + 1) * half],
            chunk_sems.at[at],
        )
        for at in range(len(chunks))
    ]
    stores = []

    def store(i, source, target, k, rows):
        copy = pltpu.make_async_copy(
            source.at[k, rows, :], target.at[k, rows, :], grad_sems.at[i, len(stores) // 2]
        )
        copy.start()
        stores.append(copy)

    def start_piece(piece):
        if piece == 4:
            normed_load.start()
            for copy in loads[2]:
                copy.start()
        if piece < 5:
            loads[0][piece].start()
            loads[0][5 + piece].start()
            for at, (k, _) in enumerate(chunks):
                if k == piece:
                    slopes[at].start()
            loads[1][piece].start()
            loads[1][5 + piece].start()

    hidden_load.start()
    start_piece(0)
    start_piece(1)
    sums[...] = jnp.zeros_like(sums)
    hidden_load.wait()
    flipped[...] = hidden[...].astype(F32).T.astype(BF16)
    parts = [jnp.zeros((d_branch.shape[0], half), F32) for _ in range(2)]
    for at, (k, start) in enumerate(chunks):
        if start == 0:
            loads[0][k].wait()
            loads[0][5 + k].wait()
            start_piece(k + 2)
        cols = slice(start, start + half)
        place = slice(at * half, (at + 1) * half)
        d_act = dot(d_branch[:, :half], packs[k][:deep, cols], NT) + dot(
            d_branch[:, half:], packs[5 + k][:deep, cols], NT
        )
        slopes[at].wait()
        d_pre = (d_act * slope[:, place].astype(F32)).astype(BF16)
        chip, at_col = at // 2, slice(at % 2 * half, at % 2 * half + half)
        sums[4 + chip : 5 + chip, at_col] = column_sum(d_pre.astype(F32))
        if start == 0:
            loads[1][k].wait()
            loads[1][5 + k].wait()
        parts[0] += dot(d_pre, packs[k][deep:top, cols], NT)
        parts[1] += dot(d_pre, packs[5 + k][deep:top, cols], NT)
        grad = dot(flipped[...], d_pre).astype(BF16)
        own[chip, 0:half, at_col] = grad[:half, :]
        other[chip, 0:half, at_col] = grad[half:, :]
        if at % 2 == 1:
            store(0, other, other_hbm, chip, slice(0, half))
            store(1, own, own_hbm, chip, slice(0, half))
    normed_load.wait()
    d_hidden = d_resid2[...] + jnp.concatenate(parts, 1)
    normed = normed_ref[...]
    d_resid = layer_norm_back(d_hidden, vectors[1:2, :], normed, std_ref[...])
    resid_out[...] = d_resid
    mixed = d_resid.astype(BF16)
    for at, row in enumerate(
        (column_sum(d_hidden * normed), column_sum(d_hidden), column_sum(mixed.astype(F32)))
    ):
        write_swapped(sums, slice(at, at + 1), row, scalars)
    for copy in loads[2]:
        copy.wait()
    spread_out(packs[:5], spread[0], top, out_deep, half)
    spread_out(packs[5:], spread[1], top, out_deep, half)
    for k in range(4):
        rows = slice(k * block_col, (k + 1) * block_col)
        pieces[k][...] = (
            dot(mixed[:, :half], spread[0][rows, :], NT)
            + dot(mixed[:, half:], spread[1][rows, :], NT)
        ).astype(BF16)
        out_grad = dot(att[k][...], mixed, TN)
        low = half + out_deep
        table = jnp.concatenate(
            [
                sums_mid[0:4, :],
                sums[0:3, :],
                count[0:1, :],
                sums[4 + k : 5 + k, :],
                jnp.zeros((own.shape[1] - low - 9, own.shape[2]), F32),
            ],
            0,
        ).astype(BF16)
        for i, target in enumerate((own, other)):
            part = out_grad[:, i * half : (i + 1) * half].astype(BF16)
            target[k, half:low, 0:half] = part[:out_deep, :]
            target[k, half:low, half:] = part[out_deep:, :]
            target[k, low:, :] = table
        store(0, other, other_hbm, k, slice(half, own.shape[1]))
        store(1, own, own_hbm, k, slice(half, own.shape[1]))
    for copy in stores:
        copy.wait()


def ffn_back(
    scalars, d_branch, inv_std, vectors, d_resid2, sums_mid, count, attended, normed, slope, hidden, packs, deep
):
    rows, width = d_branch.shape
    half = width // 2
    inner = 8 * half
    full = (rows, width)
    block_col = attended[0].shape[1]
    grads = ((4, half + 128, 2 * half), BF16)
    pack_scr, spread = pack_scratch(packs, half, block_col)
    S = jax.ShapeDtypeStruct
    return pl.pallas_call(
        lambda *refs: ffn_back_kernel(deep, *refs),
        out_shape=[S(full, F32)] + [S((rows, block_col), BF16)] * 4 + [pltpu.HBM(*grads)] * 2,
        in_specs=[SMEM_SPEC] + [VMEM_SPEC] * 10 + [HBM_SPEC] * 13,
        out_specs=[VMEM_SPEC] * 5 + [HBM_SPEC] * 2,
        scratch_shapes=pack_scr
        + [pltpu.VMEM(full, F32), pltpu.VMEM((rows, inner), BF16), pltpu.VMEM(full, BF16)]
        + [pltpu.VMEM((width, rows), BF16)]
        + [pltpu.VMEM(*grads)] * 2
        + [pltpu.VMEM((8, width), F32)]
        + spread
        + [
            pltpu.SemaphoreType.DMA((3, 10)),
            pltpu.SemaphoreType.DMA((2,)),
            pltpu.SemaphoreType.DMA((8,)),
            pltpu.SemaphoreType.DMA((2, 8)),
        ],
        compiler_params=pltpu.CompilerParams(vmem_limit_bytes=48 << 20),
        cost_estimate=pl.CostEstimate(
            flops=10 * rows * width * inner, bytes_accessed=24 << 20, transcendentals=0
        ),
        name="ffn_back",
    )(
        scalars,
        d_branch,
        inv_std,
        vectors,
        d_resid2,
        sums_mid,
        count,
        *attended,
        *(in_hbm(a) for a in (normed, slope, hidden, *packs)),
    )


def whole_call(kernel, name, args, outs, scalars=None, cost=SMALL_COST):
    return pl.pallas_call(
        kernel,
        out_shape=[o if hasattr(o, "memory_space") else jax.ShapeDtypeStruct(*o) for o in outs],
        in_specs=([] if scalars is None else [SMEM_SPEC]) + [VMEM_SPEC] * len(args),
        out_specs=[VMEM_SPEC] * len(outs),
        compiler_params=pltpu.CompilerParams(vmem_limit_bytes=SMALL_LIMIT),
        cost_estimate=cost,
        name=name,
    )(*(() if scalars is None else (scalars,)), *args)


def fold_cores(own, came):
    _, rows, cols = own.shape

    def kernel(own_ref, came_ref, *outs):
        for k, out in enumerate(outs):
            out[...] = (own_ref[k].astype(F32) + came_ref[k].astype(F32)).astype(BF16)

    outs = [pltpu.HBM((rows, cols), BF16)] * 4
    return whole_call(kernel, "fold_cores", (own, came), outs)


def fold_chips(terms):
    def kernel(*refs):
        refs[4][...] = sum(ref[...].astype(F32) for ref in refs[:4]).astype(BF16)

    return whole_call(kernel, "fold_chips", terms, [(terms[0].shape, BF16)])[0]


def fold_quarters(terms, scalars):
    rows, cols = terms[0].shape
    part = rows // 4
    count = len(terms)

    def kernel(scalars, *refs):
        for k in range(4):
            at = pl.ds(pl.multiple_of((scalars[2] ^ k) * part, 8), part)
            total = sum(term[at, :].astype(F32) for term in refs[:count])
            refs[count + k % 2][k // 2] = total.astype(BF16)

    return whole_call(kernel, "fold_quarters", terms, [((2, part, cols), BF16)] * 2, scalars)


def finish(dense, qkv, half, block_col, scalars):
    _, part, cols = dense[0].shape
    qkv_part = qkv[0].shape[1]
    deep = block_col // 2

    def kernel(scalars, *refs):
        up, out, table, query, key, value, bias, dense_all, qkv_all = refs[4:]
        for parts, target in ((refs[:2], dense_all), (refs[2:4], qkv_all)):
            for k in range(4):
                piece = parts[k % 2].at[k // 2]
                rows = piece.shape[0]
                at = pl.ds(pl.multiple_of((scalars[2] ^ k) * rows, 8), rows)
                target[at, :] = piece[...].astype(F32)
        up[...] = dense_all[:half, :]
        out[:deep, :] = dense_all[half : half + deep, :half]
        out[deep:, :] = dense_all[half : half + deep, half:]
        table[...] = dense_all[half + deep : half + deep + 16, :]
        for i, target in enumerate((query, key, value)):
            target[...] = qkv_all[i * block_col : (i + 1) * block_col, :]
        bias[...] = qkv_all[3 * block_col : 3 * block_col + 8, :]

    S = jax.ShapeDtypeStruct
    return pl.pallas_call(
        kernel,
        out_shape=[S((half, cols), F32), S((block_col, half), F32), S((16, cols), F32)]
        + [S((block_col, half), F32)] * 3
        + [S((8, half), F32)],
        in_specs=[SMEM_SPEC] + [VMEM_SPEC] * 4,
        out_specs=[VMEM_SPEC] * 7,
        scratch_shapes=[
            pltpu.VMEM((4 * part, cols), F32),
            pltpu.VMEM((4 * qkv_part, half), F32),
        ],
        compiler_params=pltpu.CompilerParams(vmem_limit_bytes=SMALL_LIMIT),
        cost_estimate=SMALL_COST,
        name="finish",
    )(scalars, *dense, *qkv)


def dot(left, right, dims=NN):
    return lax.dot_general(left, right, dims, preferred_element_type=F32)


def split3(value):
    high = value.astype(BF16)
    rest = value - high.astype(F32)
    middle = rest.astype(BF16)
    low = (rest - middle.astype(F32)).astype(BF16)
    return high.astype(F32), middle.astype(F32), low.astype(F32)


def key_range(code, span, span_rows, blocks):
    per = span_rows // BLK
    first_seg = code[span * per, 0] // 2
    last_seg = code[span * per + per - 1, BLK - 1] // 2
    low = jnp.int32(0)
    high = jnp.int32(0)
    for other in range(blocks):
        start = code[other, 0]
        low += (code[other, BLK - 1] // 2 < first_seg).astype(jnp.int32)
        high += ((start // 2 <= last_seg) & (start % 2 == 1)).astype(jnp.int32)
    below = jnp.maximum(jnp.minimum(high, span * per) - low, 0)
    above = jnp.maximum(high - (span + 1) * per, 0)
    return low, below, below + above


def key_block(step, low, below, after):
    return jnp.where(step < below, low + step, after + step - below)


def lane_index(rows):
    return lax.broadcasted_iota(jnp.int32, (rows, 128), 1)


def allowed_block(code_rows, block, offset, span_rows):
    row = lax.broadcasted_iota(jnp.int32, (span_rows, BLK), 0)
    col = lax.broadcasted_iota(jnp.int32, (span_rows, BLK), 1)
    return (code_rows[pl.ds(block, 1), :] % 2 == 1) | (row == col + offset)


def attention_forward_kernel(heads, scalars, code, *refs):
    code_rows = refs[0]
    shards_in = refs[1:5]
    weights = refs[5:7]
    pieces = refs[7:11]
    saved = refs[11:15]
    padded, max_scr, acc_scr, query_pad, key_pad, value_pad, out_pad, whole_sem, span_sem = refs[15:]
    span_rows, width = shards_in[0].shape
    cols = 64 * heads
    flip = scalars[1]
    per = span_rows // BLK
    blocks = query_pad.shape[1] // BLK
    lane = lane_index(span_rows)
    for i in range(3):
        src = slice(i * cols, (i + 1) * cols)
        padded[i * 256 : i * 256 + cols, : width // 2] = weights[0][src, :]
        padded[i * 256 : i * 256 + cols, width // 2 :] = weights[1][src, :]
        padded[i * 256 + cols : (i + 1) * 256, :] = jnp.zeros((256 - cols, width), BF16)
    marks_bias = weights[0][3 * cols : 3 * cols + 1, :].astype(F32)
    no_bias = jnp.zeros((1, 256 - cols), F32)
    biases = (
        jnp.concatenate([marks_bias[:, :cols], no_bias], 1),
        None,
        jnp.concatenate([marks_bias[:, cols : 2 * cols], no_bias], 1),
    )
    value_ones = jnp.where((lane >= 64) & (lane < 67), 1.0, 0.0)
    for shard, tokens in enumerate(shards_in):
        rows = slice(shard * span_rows, (shard + 1) * span_rows)
        marks = [
            jnp.broadcast_to(
                code_rows[pl.ds((shard ^ flip) * per + part, 1), :].astype(F32), (128, BLK)
            ).T
            for part in range(per)
        ]
        marks = jnp.concatenate(marks, 0).astype(jnp.int32)
        same = lane - 64 == marks // 2
        ids = (lane >= 64) & (lane < 80)
        query_marks = jnp.where((ids & same) | (lane == 80), 1.0, 0.0)
        key_marks = jnp.where(
            (ids & ~same) | ((lane == 80) & (marks % 2 == 0)),
            MASKED,
            jnp.where((lane >= 81) & (lane < 84), -1.0, 0.0),
        )
        for i, (out, extra) in enumerate(
            ((query_pad, query_marks), (key_pad, key_marks), (value_pad, value_ones))
        ):
            projected = dot(tokens[...], padded[i * 256 : (i + 1) * 256, :], NT)
            if biases[i] is not None:
                projected += biases[i]
            if i == 0:
                projected = projected.astype(BF16).astype(F32) * 0.125
            out[0, rows, :] = jnp.where(lane < 64, projected[:, :128], extra).astype(BF16)
            out[1, rows, :] = jnp.where(
                lane < 64, pltpu.roll(projected[:, :128], 64, 1), extra
            ).astype(BF16)
            out[2, rows, :] = jnp.where(lane < 64, projected[:, 128:], extra).astype(BF16)
    no_valid_lane = jnp.where(lane == 80, 0.0, 1.0).astype(BF16)
    whole_copies = [
        pltpu.make_async_copy(key_pad, saved[1], whole_sem.at[0]),
        pltpu.make_async_copy(value_pad, saved[2], whole_sem.at[1]),
    ]
    for copy in whole_copies:
        copy.start()

    def span_copies(at):
        rows = pl.ds(pl.multiple_of(at * span_rows, span_rows), span_rows)
        return [
            pltpu.make_async_copy(
                source.at[:, rows, :], saved[i].at[:, rows, :], span_sem.at[i // 3, at]
            )
            for source, i in ((query_pad, 0), (out_pad, 3))
        ]

    def query_step(span, _):
        at = span ^ flip
        rows = pl.ds(pl.multiple_of(at * span_rows, span_rows), span_rows)
        low, below, count = key_range(code, span, span_rows, blocks)

        def keys_of(block):
            place = (block // per ^ flip) * per + block % per
            return pl.ds(pl.multiple_of(place * BLK, BLK), BLK)

        def scores_of(h, keys, allowed=None):
            if allowed is None:
                return dot(query_pad[h, rows, :], key_pad[h, keys, :], NT)
            scores = dot(query_pad[h, rows, :] * no_valid_lane, key_pad[h, keys, :], NT)
            return jnp.where(allowed, scores, MASKED)

        def each_block(visit):
            for part in range(per):
                block = span * per + part
                visit(keys_of(block), allowed_block(code_rows, block, part * BLK, span_rows))

            def step_fn(step, _):
                visit(keys_of(key_block(step, low, below, (span + 1) * per)), None)
                return 0

            lax.fori_loop(0, count, step_fn, 0)

        acc_scr[...] = jnp.zeros_like(acc_scr)
        max_scr[...] = jnp.zeros_like(max_scr)

        def plain(keys, allowed):
            for h in range(heads):
                probs = jnp.exp(scores_of(h, keys, allowed)).astype(BF16)
                acc_scr[h] += dot(probs, value_pad[h, keys, :])

        each_block(plain)
        least, most = jnp.float32(1.0), jnp.float32(1.0)
        for h in range(heads):
            total = jnp.where(lane == 64, acc_scr[h], 1.0)
            good = (total > 1e-25) & (total < 1e30)
            least = jnp.minimum(least, jnp.min(jnp.where(good, 1.0, 0.0)))

        @pl.when(least < 0.5)
        def _():
            max_scr[...] = jnp.full_like(max_scr, MASKED)

            def find_max(keys, allowed):
                for h in range(heads):
                    scores = scores_of(h, keys, allowed)
                    max_scr[h] = jnp.maximum(
                        max_scr[h], jnp.maximum(scores[:, :128], scores[:, 128:])
                    )

            each_block(find_max)
            for h in range(heads):
                max_scr[h] = jnp.broadcast_to(
                    jnp.max(max_scr[h], axis=1, keepdims=True), (span_rows, 128)
                )
            acc_scr[...] = jnp.zeros_like(acc_scr)

            def shifted(keys, allowed):
                for h in range(heads):
                    row_max = max_scr[h]
                    scores = scores_of(h, keys, allowed)
                    probs = jnp.exp(scores - jnp.concatenate([row_max, row_max], 1))
                    acc_scr[h] += dot(probs.astype(BF16), value_pad[h, keys, :])

            each_block(shifted)

        outs = []
        for h in range(heads):
            acc = acc_scr[h]
            total = jnp.broadcast_to(acc[:, 64:65], acc.shape)
            out = acc / total
            out_pad[h, rows, :] = out
            outs.append(out)
            high, middle, rest = split3(max_scr[h] + jnp.log(total))
            extra = jnp.where(
                lane == 81,
                high,
                jnp.where(lane == 82, middle, jnp.where(lane == 83, rest, 0.0)),
            )
            query_pad[h, rows, :] = query_pad[h, rows, :] + extra.astype(BF16)
        pair = jnp.where(lane < 64, outs[0], pltpu.roll(outs[1], 64, 1)).astype(BF16)
        last = outs[2][:, :64].astype(BF16)
        for k, piece in enumerate(pieces):

            @pl.when(at == k)
            def _():
                piece[:, 0:128] = pair
                piece[:, 128:cols] = last

        for copy in span_copies(at):
            copy.start()
        return 0

    lax.fori_loop(0, len(shards_in), query_step, 0)
    for copy in whole_copies:
        copy.wait()
    for at in range(len(shards_in)):
        for copy in span_copies(at):
            copy.wait()


def attention_forward(scalars, code, token_shards, weights):
    rows, width = token_shards[0].shape
    length = code.shape[0] * BLK
    cols = (weights[0].shape[0] - PAD_ROWS) // 3
    heads = cols // 64
    S = jax.ShapeDtypeStruct
    flops = 2 * length * width * 3 * 256 + 3 * length * length * 128
    return pl.pallas_call(
        lambda *refs: attention_forward_kernel(heads, *refs),
        out_shape=[S((rows, cols), BF16)] * 4
        + [pltpu.HBM((heads, length, 128), BF16)] * 3
        + [pltpu.HBM((heads, length, 128), F32)],
        in_specs=[SMEM_SPEC] * 2 + [VMEM_SPEC] * 7,
        out_specs=[VMEM_SPEC] * 4 + [HBM_SPEC] * 4,
        scratch_shapes=[
            pltpu.VMEM((3 * 256, width), BF16),
            pltpu.VMEM((heads, rows, 128), F32),
            pltpu.VMEM((heads, rows, 128), F32),
        ]
        + [pltpu.VMEM((heads, length, 128), BF16)] * 3
        + [
            pltpu.VMEM((heads, length, 128), F32),
            pltpu.SemaphoreType.DMA((2,)),
            pltpu.SemaphoreType.DMA((2, 4)),
        ],
        compiler_params=pltpu.CompilerParams(vmem_limit_bytes=32 << 20),
        cost_estimate=pl.CostEstimate(
            flops=3 * flops, bytes_accessed=16 << 20, transcendentals=heads * length * 1024
        ),
        name="attention_forward",
    )(scalars, code, code, *token_shards, *weights)


def attention_backward_kernel(heads, scalars, code, *refs):
    code_rows = refs[0]
    sources = refs[5:15] + refs[1:5]
    term_hbm = refs[15:17]
    grad_hbm = refs[17:19]
    grad_pad, query_sum, key_sum, value_sum, low_scr, grad_scr, bias_sum = refs[19:26]
    copies = [
        pltpu.make_async_copy(source, target, refs[36].at[i])
        for i, (source, target) in enumerate(zip(sources, refs[26:36] + refs[37:41]))
    ]
    for i in (3, 10, 11, 12, 13, 0, 1, 2, 4, 5, 6, 7, 8, 9):
        copies[i].start()
    grads = refs[37:41]
    terms, own_grad, other_grad, out_sems = refs[41:45]
    query_pad, key_pad, value_pad, out_pad = refs[26:30]
    shards_in = refs[30:34]
    weights = refs[34:36]
    key_sum[...] = jnp.zeros_like(key_sum)
    value_sum[...] = jnp.zeros_like(value_sum)
    query_sum[...] = jnp.zeros_like(query_sum)
    for i in (3, 10, 11, 12, 13):
        copies[i].wait()
    span_rows = grads[0].shape[0]
    flip = scalars[1]
    per = span_rows // BLK
    blocks = query_pad.shape[1] // BLK
    lane = lane_index(span_rows)
    gap = jnp.zeros((span_rows, 64), BF16)
    for shard, grad in enumerate(grads):
        rows = slice(shard * span_rows, (shard + 1) * span_rows)
        pair = grad[:, 0:128].astype(F32)
        last = jnp.concatenate([grad[:, 128:192], gap], 1).astype(F32)
        for h, block in enumerate((pair, pltpu.roll(pair, 64, 1), last)):
            block = jnp.where(lane < 64, block, 0.0)
            delta = jnp.sum(block * out_pad[h, rows, :], axis=1, keepdims=True)
            high, middle, rest = split3(-delta)
            block = jnp.where(
                lane == 64,
                high,
                jnp.where(lane == 65, middle, jnp.where(lane == 66, rest, block)),
            )
            grad_pad[h, rows, :] = block.astype(BF16)
    for i in range(3):
        copies[i].wait()
    no_valid_lane = jnp.where(lane == 80, 0.0, 1.0).astype(BF16)

    def query_step(span, _):
        at = span ^ flip
        rows = pl.ds(pl.multiple_of(at * span_rows, span_rows), span_rows)
        low, below, count = key_range(code, span, span_rows, blocks)

        def visit(block, allowed):
            place = (block // per ^ flip) * per + block % per
            keys = pl.ds(pl.multiple_of(place * BLK, BLK), BLK)
            for h in range(heads):
                query, grad = query_pad[h, rows, :], grad_pad[h, rows, :]
                key, value = key_pad[h, keys, :], value_pad[h, keys, :]
                if allowed is None:
                    scores = dot(key, query, NT)
                else:
                    scores = jnp.where(allowed, dot(key, query * no_valid_lane, NT), MASKED)
                probs = jnp.exp(scores)
                d_scores = (probs * dot(value, grad, NT)).astype(BF16)
                value_sum[h, keys, :] += dot(probs.astype(BF16), grad)
                key_sum[h, keys, :] += dot(d_scores, query)
                query_sum[h, rows, :] += dot(d_scores, key, TN)

        for part in range(per):
            block = span * per + part
            key_at = lax.broadcasted_iota(jnp.int32, (BLK, span_rows), 0)
            query_at = lax.broadcasted_iota(jnp.int32, (BLK, span_rows), 1)
            marks = jnp.broadcast_to(
                code_rows[pl.ds(block, 1), :].astype(F32), (128, BLK)
            ).T.astype(jnp.int32)
            valid = jnp.concatenate([marks] * (span_rows // 128), 1) % 2 == 1
            visit(block, valid | (query_at == key_at + part * BLK))

        def step_fn(step, _):
            visit(key_block(step, low, below, (span + 1) * per), None)
            return 0

        lax.fori_loop(0, count, step_fn, 0)
        return 0

    lax.fori_loop(0, len(grads), query_step, 0)
    for i in range(4, 10):
        copies[i].wait()
    bias_sum[...] = jnp.zeros_like(bias_sum)
    stores = []
    for shard in range(len(grads)):
        rows = slice(shard * span_rows, (shard + 1) * span_rows)
        parts = [query_sum[h, rows, :] * 0.125 for h in range(heads)]
        parts += [sums[h, rows, :] for sums in (key_sum, value_sum) for h in range(heads)]
        for at in range(0, len(parts), 2):
            if at + 1 < len(parts):
                value = jnp.where(lane < 64, parts[at], pltpu.roll(parts[at + 1], 64, 1))
            else:
                value = parts[at][:, :64]
            low = value.astype(BF16)
            cols = slice(at * 64, at * 64 + low.shape[1])
            low_scr[:, cols] = low
            bias_sum[0:1, cols] += column_sum(low.astype(F32))
        low = low_scr[...]
        depth = low.shape[1]
        term = jnp.concatenate([dot(low, w[:depth, :]).astype(BF16) for w in weights], 1)
        terms[shard] = term
        copy = pltpu.make_async_copy(
            terms.at[shard], term_hbm[shard // 2].at[shard % 2], out_sems.at[shard]
        )
        copy.start()
        stores.append(copy)
        part = dot(low, shards_in[shard][...], TN)
        if shard == 0:
            grad_scr[...] = part
        elif shard < 3:
            grad_scr[...] += part
        else:
            total = (grad_scr[...] + part).astype(BF16)
            half = total.shape[1] // 2
            own_grad[:depth, :] = total[:, :half]
            other_grad[:depth, :] = total[:, half:]
    cols = heads * 64
    bias = jnp.concatenate([bias_sum[:, 0:cols], bias_sum[:, 2 * cols :]], 1).astype(BF16)
    bias = jnp.concatenate([bias] * ((own_grad.shape[0] - depth) // bias.shape[0]), 0)
    own_grad[depth:, :] = bias
    other_grad[depth:, :] = bias
    for i, source in enumerate((own_grad, other_grad)):
        copy = pltpu.make_async_copy(source, grad_hbm[i], out_sems.at[4 + i])
        copy.start()
        stores.append(copy)
    for copy in stores:
        copy.wait()


def attention_backward(scalars, code, grads, saved, token_shards, weights):
    length = code.shape[0] * BLK
    heads = saved[0].shape[0]
    rows, width = token_shards[0].shape
    cols = 3 * heads * 64
    S = jax.ShapeDtypeStruct
    return pl.pallas_call(
        lambda *refs: attention_backward_kernel(heads, *refs),
        out_shape=[
            pltpu.HBM((2, rows, width), BF16),
            pltpu.HBM((2, rows, width), BF16),
            pltpu.HBM((cols + GRAD_PAD, width // 2), BF16),
            pltpu.HBM((cols + GRAD_PAD, width // 2), BF16),
        ],
        in_specs=[SMEM_SPEC] * 2 + [VMEM_SPEC] + [HBM_SPEC] * 14,
        out_specs=[HBM_SPEC] * 4,
        scratch_shapes=[
            pltpu.VMEM((heads, length, 128), BF16),
            pltpu.VMEM((heads, length, 128), F32),
            pltpu.VMEM((heads, length, 128), F32),
            pltpu.VMEM((heads, length, 128), F32),
            pltpu.VMEM((rows, cols), BF16),
            pltpu.VMEM((cols, width), F32),
            pltpu.VMEM((16, cols), F32),
        ]
        + [pltpu.VMEM(a.shape, a.dtype) for a in (*saved, *token_shards, *weights)]
        + [pltpu.SemaphoreType.DMA((14,))]
        + [pltpu.VMEM(a.shape, a.dtype) for a in grads]
        + [
            pltpu.VMEM((4, rows, width), BF16),
            pltpu.VMEM((cols + GRAD_PAD, width // 2), BF16),
            pltpu.VMEM((cols + GRAD_PAD, width // 2), BF16),
            pltpu.SemaphoreType.DMA((6,)),
        ],
        compiler_params=pltpu.CompilerParams(vmem_limit_bytes=46 << 20),
        cost_estimate=pl.CostEstimate(
            flops=heads * length * length * 1500, bytes_accessed=8 << 20, transcendentals=0
        ),
        name="attention_backward",
    )(
        scalars,
        code,
        code,
        *(in_hbm(a) for a in (*grads, *saved, *token_shards, *weights)),
    )


CORE_CHIP = ("gy", "gz")
CHIP = [[(c, c ^ k) for c in range(4)] for k in range(4)]
PLANE = [[(p, p ^ k) for p in range(4)] for k in range(4)]
CORE = [(0, 1), (1, 0)]


def plane_perm(to):
    pairs = []
    for device in range(8):
        core, row, col = device // 4, device // 2 % 2, device % 2
        core_to, row_to, col_to = to(core, row, col)
        pairs.append((device, core_to * 4 + row_to * 2 + col_to))
    return pairs


TO_OWNER = [
    plane_perm(lambda core, row, col, a=k // 2, b=k % 2: (row, core ^ a, col ^ b))
    for k in range(4)
]
TO_HEADS = [
    plane_perm(lambda core, row, col, a=k // 2, b=k % 2: (row ^ a, core, col ^ b))
    for k in range(4)
]


def to_owner(value, k):
    return lax.ppermute(value, CORE_CHIP, TO_OWNER[k])


def to_heads(value, k):
    return lax.ppermute(value, CORE_CHIP, TO_HEADS[k])


def to_chip(value, k):
    return lax.ppermute(value, "gz", CHIP[k])


def to_core(value):
    return lax.ppermute(value, "gy", CORE)


def to_plane(value, k):
    return lax.ppermute(value, "gx", PLANE[k])


def after(value, *others):
    return lax.optimization_barrier((value,) + others)[0]


def swap_halves(flip, value):
    half = value.shape[-1] // 2
    swapped = jnp.concatenate([value[..., half:], value[..., :half]], -1)
    return jnp.where(flip, swapped, value)


def add_low(left, right):
    return (left.astype(F32) + right.astype(F32)).astype(BF16)


def sum_planes(dense, qkv, waits):
    if lax.axis_size("gx") != 4:
        dense, other = jnp.stack(dense), jnp.stack(qkv(dense[0]))
        total = lax.psum((dense, other), "gx")
        return [(t[0], t[1]) for t in total]
    near = dense[0].astype(F32) + to_plane(dense[1], 1).astype(F32)
    step = near[1].astype(BF16)
    keep, send = qkv(step)
    total = (near[0] + to_plane(step, 2).astype(F32)).astype(BF16)
    near = keep.astype(F32) + to_plane(send, 1).astype(F32)
    step = after(near[1].astype(BF16), total)
    pair = jnp.stack([total, to_plane(total, 2)])
    other = (near[0] + to_plane(step, 2).astype(F32)).astype(BF16)
    other = after(other, pair, *waits)
    back = to_plane(pair, 1)
    other_pair = jnp.stack([other, to_plane(other, 2)])
    return [(pair, back), (other_pair, to_plane(other_pair, 1))]


def shards(
    tokens,
    segment_ids,
    valid_mask,
    cotangent,
    teacher,
    w_query,
    b_query,
    w_key,
    w_value,
    b_value,
    w_out,
    b_out,
    norm1_gain,
    norm1_bias,
    w_up,
    b_up,
    w_down,
    b_down,
    norm2_gain,
    norm2_bias,
):
    row_count, width = tokens.shape
    half = width // 2
    core = lax.axis_index("gy")
    chip = lax.axis_index("gz")
    flip = core == 1
    block_col = w_query.shape[1]
    hidden_col = w_up.shape[1]
    plane = lax.axis_index("gx") if lax.axis_size("gx") == 4 else jnp.int32(0)
    scalars = jnp.stack([core, core * 2 + chip % 2, plane, chip]).astype(jnp.int32)

    own_tokens = swap_halves(flip, tokens)
    shard0, shard1 = to_owner(own_tokens, 0), to_owner(own_tokens, 1)
    code = (segment_ids * 2 + valid_mask).reshape(-1, BLK)
    bias_row = jnp.concatenate([b_query, b_value])[None, :]
    qkv_own = jnp.concatenate(
        [w_query.T, w_key.T, w_value.T, jnp.broadcast_to(bias_row, (PAD_ROWS, half))], 0
    )
    vectors = jnp.stack([b_out, norm1_gain, norm1_bias, b_down, norm2_gain, norm2_bias] + [b_out] * 2)
    vectors = swap_halves(flip, vectors.astype(F32))
    own_valid = lax.dynamic_slice_in_dim(valid_mask, chip * row_count, row_count, 1).astype(F32)
    count = jnp.concatenate([own_valid, jnp.zeros((1, width - row_count), F32)], 1)
    count = jnp.broadcast_to(count, (8, width))
    own_valid = own_valid.T
    packed = jnp.concatenate(
        [
            jnp.concatenate([w_down[: hidden_col // 2], w_down[hidden_col // 2 :]], 1),
            w_up,
            jnp.concatenate([w_out[: block_col // 2], w_out[block_col // 2 :]], 1),
            jnp.broadcast_to(b_up[None, :], (PAD_ROWS, hidden_col)),
        ],
        0,
    )

    code, qkv_own, scalars, packed, vectors, own_valid, count, *_ = lax.optimization_barrier(
        (code, qkv_own, scalars, packed, vectors, own_valid, count, own_tokens)
    )
    code = to_owner(code, 0)
    qkv = (to_owner(qkv_own, 0), to_owner(qkv_own, 2))
    shard0, shard1, packed, code, *qkv = lax.optimization_barrier(
        (shard0, shard1, packed, code, *qkv)
    )
    token_shards = (shard0, shard1, to_core(shard0), to_core(shard1))
    pack_x, pack_y = to_chip(packed, 1), to_chip(packed, 2)
    packed_other = to_core(packed)

    scalars = after(scalars, packed)
    results = attention_forward(scalars, code, token_shards, qkv)
    saved = results[4:]
    attended = [to_owner(results[k], k) for k in range(4)]

    deep = hidden_col // 2
    pack_x, pack_y = lax.optimization_barrier((pack_x, pack_y, results[0]))[:2]
    far = (to_chip(pack_x[:, :half], 2), to_chip(pack_y[:, half:], 1))
    packs = (packed, pack_x, pack_y, *far)
    packs += (packed_other, *(to_core(v) for v in packs[1:]))

    inv_std, output, d_resid2, d_branch, sums_mid, act, normed, hidden_low, slope = ffn_forward(
        scalars, attended, own_tokens, own_valid, vectors, cotangent, teacher, packs, deep
    )
    pieces = (4, hidden_col, half)
    d_down_other = jnp.einsum("lf,lm->fm", act, d_branch[:, half:], preferred_element_type=F32)
    d_down_came = to_core(d_down_other.astype(BF16).reshape(pieces))
    d_down = jnp.einsum("lf,lm->fm", act, d_branch[:, :half], preferred_element_type=F32)
    d_down = fold_cores(d_down.astype(BF16).reshape(pieces), d_down_came)
    d_branch = after(d_branch, d_down[0])
    down_total = fold_chips([d_down[0]] + [to_chip(d_down[k], k) for k in (1, 2, 3)])
    d_resid1, *back, own_grads, other_grads = ffn_back(
        scalars,
        d_branch,
        inv_std,
        vectors,
        d_resid2,
        sums_mid,
        count,
        attended,
        normed,
        slope,
        hidden_low,
        packs,
        deep,
    )
    d_pieces = [to_heads(back[k], k) for k in range(4)]

    d_dense = fold_cores(own_grads, to_core(after(other_grads, down_total)))
    grad_down = lax.psum(down_total, "gx")
    d_pieces[0] = after(d_pieces[0], d_dense[0])
    d_dense = [d_dense[0]] + [to_chip(d_dense[k], k) for k in (1, 2, 3)]

    own_term, other_term, d_own, d_other = attention_backward(
        scalars, code, d_pieces, saved, token_shards, qkv
    )
    d_dense[0] = after(d_dense[0], grad_down, own_term)
    quarters = fold_quarters(d_dense, scalars)
    d_own, d_other, other_term, *_ = lax.optimization_barrier(
        (d_own, d_other, other_term, *quarters)
    )
    other_term = to_core(other_term)
    d_w = (to_owner(d_own, 0), to_heads(d_other, 2))
    term0 = add_low(own_term[0], other_term[0])
    term1 = add_low(own_term[1], other_term[1])
    came0, came1 = to_owner(term0, 0), to_owner(term1, 1)
    dense_grad, qkv_grad = sum_planes(
        quarters, lambda first: fold_quarters((after(d_w[0], first), d_w[1]), scalars), (came0, came1)
    )
    d_tokens = d_resid1 + came0.astype(F32) + came1.astype(F32)
    grad_up, grad_out, table, grad_query, grad_key, grad_value, d_bias = finish(
        dense_grad, qkv_grad, half, block_col, scalars
    )

    mean_loss = jnp.sum(table[3]) / (jnp.sum(table[7]) * width)
    return (
        output,
        mean_loss,
        swap_halves(flip, d_tokens.astype(BF16)),
        grad_query.T,
        d_bias[0, :block_col],
        grad_key.T,
        grad_value.T,
        d_bias[0, block_col:],
        grad_out,
        table[6],
        table[4],
        table[5],
        grad_up,
        table[8],
        grad_down.astype(F32),
        table[2],
        table[0],
        table[1],
    )


def solution(mesh):
    placed = (
        P(("gx", "gy", "gz"), None),
        P(("gx", "gy"), None),
        P(("gx", "gy"), None),
        P(("gx", "gy", "gz"), None),
        P(("gx", "gy", "gz"), None),
        P("gy", "gz"),
        P("gz"),
        P("gy", "gz"),
        P("gy", "gz"),
        P("gz"),
        P("gz", "gy"),
        P(),
        P(),
        P(),
        P("gy", "gz"),
        P("gz"),
        P("gz", "gy"),
        P(),
        P(),
        P(),
    )
    return jax.shard_map(
        shards,
        mesh=mesh,
        in_specs=placed,
        out_specs=(
            P(("gx", "gy", "gz"), None),
            P(),
            P(("gx", "gy", "gz"), None),
            P("gy", "gz"),
            P("gz"),
            P("gy", "gz"),
            P("gy", "gz"),
            P("gz"),
            P("gz", "gy"),
            P(),
            P(),
            P(),
            P("gy", "gz"),
            P("gz"),
            P("gz", "gy"),
            P(),
            P(),
            P(),
        ),
        check_vma=False,
    )
```

```python
import math

import jax
import jax.numpy as jnp
from jax import lax
from jax.experimental import pallas as pl
from jax.experimental.pallas import tpu as pltpu
from jax.sharding import PartitionSpec as P

EPSILON = 1e-05
MASKED = -1e30
PAD_ROWS = 16
GRAD_PAD = 64
BLK = 256
F32 = jnp.float32
BF16 = jnp.bfloat16
NT = (((1,), (1,)), ((), ()))
NN = (((1,), (0,)), ((), ()))
TN = (((0,), (0,)), ((), ()))


VMEM_SPEC = pl.BlockSpec(memory_space=pltpu.VMEM)
SMEM_SPEC = pl.BlockSpec(memory_space=pltpu.SMEM)
HBM_SPEC = pl.BlockSpec(memory_space=pltpu.HBM)
VMEM_LIMIT = 24 << 20
SMALL_LIMIT = 20 << 20
FFN_LIMIT = 40 << 20
SMALL_COST = pl.CostEstimate(flops=1 << 16, bytes_accessed=1 << 12, transcendentals=0)


def in_hbm(array):
    return pltpu.with_memory_space_constraint(array, pltpu.HBM)


class Loads:
    def __init__(self, packs, sems):
        self.packs, self.sems, self.used, self.groups = packs, sems, 0, {}

    def add(self, group, source, target):
        copy = pltpu.make_async_copy(source, target, self.sems.at[self.used])
        self.used += 1
        self.groups.setdefault(group, []).append(copy)

    def start(self, *groups):
        for group in groups:
            for copy in self.groups.get(group, ()):
                copy.start()

    def wait(self, *groups):
        for group in groups:
            for copy in self.groups.get(group, ()):
                copy.wait()

    def blocks(self, core):
        packs = self.packs[5 * core : 5 * core + 5]
        half = packs[4].shape[1]
        blocks = [(k, i, packs[k], i * half) for k in range(3) for i in range(2)]
        return half, blocks + [(3, 0, packs[3], 0), (3, 1, packs[4], 0)]

    def lay_out(self, deep, block_col, up_full, down_full, out_full, bias_full):
        for core in range(2):
            half, blocks = self.blocks(core)
            top = deep + half
            out_deep = block_col // 2
            side = slice(core * half, (core + 1) * half)
            for k, i, pack, col in blocks:
                cols = slice(col, col + half)
                hidden = slice((2 * k + i) * half, (2 * k + i + 1) * half)
                self.add(("up", k), pack.at[deep:top, cols], up_full.at[side, hidden])
                self.add(("down", k), pack.at[0:deep, cols], down_full.at[hidden, side])
                first = k * block_col + i * out_deep
                self.add(
                    "out",
                    pack.at[top : top + out_deep, cols],
                    out_full.at[first : first + out_deep, side],
                )
                if core == 0 and bias_full is not None:
                    low = top + out_deep
                    self.add("out", pack.at[low : low + PAD_ROWS, cols], bias_full.at[:, hidden])


def half_start(scalars, second, half):
    flip = scalars[0]
    return pl.multiple_of(jnp.where(second, 1 - flip, flip) * half, 128)


def read_swapped(ref, scalars):
    half = ref.shape[-1] // 2
    return jnp.concatenate(
        [
            ref[:, pl.ds(half_start(scalars, False, half), half)].astype(F32),
            ref[:, pl.ds(half_start(scalars, True, half), half)].astype(F32),
        ],
        1,
    )


def write_swapped(ref, rows, value, scalars):
    half = ref.shape[-1] // 2
    ref[rows, pl.ds(half_start(scalars, False, half), half)] = value[:, :half].astype(ref.dtype)
    ref[rows, pl.ds(half_start(scalars, True, half), half)] = value[:, half:].astype(ref.dtype)


def column_sum(value):
    return jnp.sum(value, 0, keepdims=True)


def layer_norm(resid):
    average = jnp.mean(resid, -1, keepdims=True)
    centered = resid - average
    inv_std = lax.rsqrt(jnp.mean(centered * centered, -1, keepdims=True) + EPSILON)
    return centered * inv_std, inv_std


def layer_norm_back(upstream, gain, normed, inv_std):
    scaled = upstream * gain
    return inv_std * (
        scaled
        - jnp.mean(scaled, -1, keepdims=True)
        - normed * jnp.mean(scaled * normed, -1, keepdims=True)
    )


def ffn_forward_kernel(deep, scalars, *refs):
    att = refs[:4]
    own_tokens, valid, vectors = refs[4:7]
    cot_source, teach_source = refs[7:9]
    packs = refs[9:19]
    std_out, output, resid_out, branch_out, sums, act_out = refs[19:25]
    normed_hbm, low_hbm, slope_hbm = refs[25:28]
    up_full, down_full, out_full, bias_full = refs[28:32]
    cotangent, teacher, normed_out, low_out, slope_out = refs[32:37]
    sems, row_sems, chunk_sems = refs[37:]
    block_col = att[0].shape[1]
    width = own_tokens.shape[1]
    loads = Loads(packs, sems)
    loads.lay_out(deep, block_col, up_full, down_full, out_full, bias_full)
    row_loads = [
        pltpu.make_async_copy(cot_source, cotangent, row_sems.at[0]),
        pltpu.make_async_copy(teach_source, teacher, row_sems.at[1]),
    ]
    loads.start("out", ("up", 0))
    loads.wait("out")
    loads.start(("down", 0), ("up", 1))
    mixed = jnp.zeros(own_tokens.shape, F32)
    for k in range(4):
        mixed += dot(att[k][...], out_full[k * block_col : (k + 1) * block_col, :])
    resid = own_tokens[...].astype(F32) + (mixed + vectors[0:1, :])
    normed, inv_std = layer_norm(resid)
    hidden = normed * vectors[1:2, :] + vectors[2:3, :]
    normed_out[...] = normed
    std_out[...] = inv_std
    low_out[...] = hidden.astype(BF16)
    stores = [
        pltpu.make_async_copy(normed_out, normed_hbm, row_sems.at[2]),
        pltpu.make_async_copy(low_out, low_hbm, row_sems.at[3]),
    ]
    for copy in stores:
        copy.start()
    branch = jnp.zeros(own_tokens.shape, F32)
    for k in range(4):
        loads.wait(("up", k))
        loads.start(("down", k + 1), ("up", k + 2))
        if k == 2:
            for copy in row_loads:
                copy.start()
        place = slice(k * width, (k + 1) * width)
        preact = dot(low_out[...], up_full[:, place]) + bias_full[0:1, place].astype(F32)
        normal_cdf = 0.5 * (1.0 + lax.erf(preact * (1.0 / math.sqrt(2.0))))
        slope = normal_cdf + preact * jnp.exp(-0.5 * preact * preact) * (
            1.0 / math.sqrt(2.0 * math.pi)
        )
        act = (preact * normal_cdf).astype(BF16)
        act_out[:, place] = act
        slope_out[:, place] = slope.astype(BF16)
        copy = pltpu.make_async_copy(
            slope_out.at[:, place], slope_hbm.at[:, place], chunk_sems.at[k]
        )
        copy.start()
        stores.append(copy)
        loads.wait(("down", k))
        branch += dot(act, down_full[place, :])
    for copy in row_loads:
        copy.wait()
    gain = vectors[4:5, :]
    hidden = normed_out[...] * vectors[1:2, :] + vectors[2:3, :]
    resid = hidden + (branch + vectors[3:4, :])
    normed, inv_std = layer_norm(resid)
    full = normed * gain + vectors[5:6, :]
    write_swapped(output, slice(None), full, scalars)
    mismatch = full - read_swapped(teacher, scalars)
    masked = valid[...] * mismatch
    d_output = read_swapped(cotangent, scalars) + masked
    d_resid = layer_norm_back(d_output, gain, normed, inv_std)
    resid_out[...] = d_resid
    low = d_resid.astype(BF16)
    branch_out[...] = low
    sums[...] = jnp.zeros_like(sums)
    rows = (
        column_sum(d_output * normed),
        column_sum(d_output),
        column_sum(low.astype(F32)),
        column_sum(masked * mismatch),
    )
    for at, row in enumerate(rows):
        write_swapped(sums, slice(at, at + 1), row, scalars)
    for copy in stores:
        copy.wait()


def full_scratch(width, inner, block_col):
    return [
        pltpu.VMEM((width, inner), BF16),
        pltpu.VMEM((inner, width), BF16),
        pltpu.VMEM((4 * block_col, width), BF16),
    ]


def ffn_forward(scalars, attended, own_tokens, valid, vectors, cotangent, teacher, packs, deep):
    rows, width = own_tokens.shape
    inner = 4 * width
    full = (rows, width)
    S = jax.ShapeDtypeStruct
    return pl.pallas_call(
        lambda *refs: ffn_forward_kernel(deep, *refs),
        out_shape=[S((rows, 1), F32), S(full, BF16), S(full, F32), S(full, BF16)]
        + [S((8, width), F32), S((rows, inner), BF16)]
        + [pltpu.HBM(full, F32), pltpu.HBM(full, BF16), pltpu.HBM((rows, inner), BF16)],
        in_specs=[SMEM_SPEC] + [VMEM_SPEC] * 7 + [HBM_SPEC] * 12,
        out_specs=[VMEM_SPEC] * 6 + [HBM_SPEC] * 3,
        scratch_shapes=full_scratch(width, inner, attended[0].shape[1])
        + [pltpu.VMEM((PAD_ROWS, inner), BF16)]
        + [pltpu.VMEM(full, BF16)] * 2
        + [pltpu.VMEM(full, F32), pltpu.VMEM(full, BF16), pltpu.VMEM((rows, inner), BF16)]
        + [
            pltpu.SemaphoreType.DMA((56,)),
            pltpu.SemaphoreType.DMA((4,)),
            pltpu.SemaphoreType.DMA((4,)),
        ],
        compiler_params=pltpu.CompilerParams(vmem_limit_bytes=FFN_LIMIT),
        cost_estimate=pl.CostEstimate(
            flops=10 * rows * width * inner, bytes_accessed=24 << 20, transcendentals=0
        ),
        name="ffn_forward",
    )(
        scalars,
        *attended,
        own_tokens,
        valid,
        vectors,
        *(in_hbm(a) for a in (cotangent, teacher, *packs)),
    )


def ffn_back_kernel(deep, scalars, *refs):
    d_branch, std_ref, vectors, d_resid2, sums_mid, count = refs[:6]
    att = refs[6:10]
    normed_source, slope_source, hidden_source = refs[10:13]
    packs = refs[13:23]
    resid_hbm = refs[23]
    piece_hbm = refs[24:28]
    own_hbm, other_hbm = refs[28:30]
    up_full, down_full, out_full = refs[30:33]
    normed_ref, slope, hidden, flipped, own, other, sums, resid_out = refs[33:41]
    pieces = refs[41:45]
    sems, row_sem, chunk_sems, grad_sems, out_sems = refs[45:]
    width = d_branch.shape[1]
    half = width // 2
    block_col = pieces[0].shape[1]
    out_deep = block_col // 2
    loads = Loads(packs, sems)
    loads.lay_out(deep, block_col, up_full, down_full, out_full, None)
    normed_load = pltpu.make_async_copy(normed_source, normed_ref, row_sem.at[0])
    hidden_load = pltpu.make_async_copy(hidden_source, hidden, row_sem.at[1])
    slopes = []
    for k in range(4):
        place = slice(k * width, (k + 1) * width)
        slopes.append(
            pltpu.make_async_copy(slope_source.at[:, place], slope.at[:, place], chunk_sems.at[k])
        )
    stores = []

    def store(i, source, target, k, rows):
        copy = pltpu.make_async_copy(
            source.at[k, rows, :], target.at[k, rows, :], grad_sems.at[i, len(stores) // 2]
        )
        copy.start()
        stores.append(copy)

    loads.start(("down", 0))
    hidden_load.start()
    slopes[0].start()
    loads.start(("up", 0), ("down", 1))
    sums[...] = jnp.zeros_like(sums)
    hidden_load.wait()
    flipped[...] = hidden[...].astype(F32).T.astype(BF16)
    d_hidden = d_resid2[...]
    for k in range(4):
        loads.wait(("down", k))
        loads.start(("up", k + 1), ("down", k + 2))
        if k < 3:
            slopes[k + 1].start()
        else:
            normed_load.start()
            loads.start("out")
        place = slice(k * width, (k + 1) * width)
        d_act = dot(d_branch[...], down_full[place, :], NT)
        slopes[k].wait()
        d_pre = (d_act * slope[:, place].astype(F32)).astype(BF16)
        sums[4 + k : 5 + k, :] = column_sum(d_pre.astype(F32))
        loads.wait(("up", k))
        d_hidden += dot(d_pre, up_full[:, place], NT)
        grad = dot(flipped[...], d_pre).astype(BF16)
        own[k, 0:half, :] = grad[:half, :]
        other[k, 0:half, :] = grad[half:, :]
        store(0, other, other_hbm, k, slice(0, half))
        store(1, own, own_hbm, k, slice(0, half))
    normed_load.wait()
    normed = normed_ref[...]
    d_resid = layer_norm_back(d_hidden, vectors[1:2, :], normed, std_ref[...])
    resid_out[...] = d_resid
    out_copies = [pltpu.make_async_copy(resid_out, resid_hbm, out_sems.at[4])]
    out_copies[0].start()
    mixed = d_resid.astype(BF16)
    loads.wait("out")
    for k in range(4):
        rows = slice(k * block_col, (k + 1) * block_col)
        pieces[k][...] = dot(mixed, out_full[rows, :], NT).astype(BF16)
        copy = pltpu.make_async_copy(pieces[k], piece_hbm[k], out_sems.at[k])
        copy.start()
        out_copies.append(copy)
    for at, row in enumerate(
        (column_sum(d_hidden * normed), column_sum(d_hidden), column_sum(mixed.astype(F32)))
    ):
        write_swapped(sums, slice(at, at + 1), row, scalars)
    for k in range(4):
        out_grad = dot(att[k][...], mixed, TN)
        low = half + out_deep
        table = jnp.concatenate(
            [
                sums_mid[0:4, :],
                sums[0:3, :],
                count[0:1, :],
                sums[4 + k : 5 + k, :],
                jnp.zeros((own.shape[1] - low - 9, own.shape[2]), F32),
            ],
            0,
        ).astype(BF16)
        for i, target in enumerate((own, other)):
            part = out_grad[:, i * half : (i + 1) * half].astype(BF16)
            target[k, half:low, 0:half] = part[:out_deep, :]
            target[k, half:low, half:] = part[out_deep:, :]
            target[k, low:, :] = table
        store(0, other, other_hbm, k, slice(half, own.shape[1]))
        store(1, own, own_hbm, k, slice(half, own.shape[1]))
    for copy in stores + out_copies:
        copy.wait()


def ffn_back(
    scalars, d_branch, inv_std, vectors, d_resid2, sums_mid, count, attended, normed, slope, hidden, packs, deep
):
    rows, width = d_branch.shape
    inner = 4 * width
    full = (rows, width)
    block_col = attended[0].shape[1]
    grads = ((4, width // 2 + 128, width), BF16)
    S = jax.ShapeDtypeStruct
    return pl.pallas_call(
        lambda *refs: ffn_back_kernel(deep, *refs),
        out_shape=[pltpu.HBM(full, F32)]
        + [pltpu.HBM((rows, block_col), BF16)] * 4
        + [pltpu.HBM(*grads)] * 2,
        in_specs=[SMEM_SPEC] + [VMEM_SPEC] * 10 + [HBM_SPEC] * 13,
        out_specs=[HBM_SPEC] * 7,
        scratch_shapes=full_scratch(width, inner, block_col)
        + [pltpu.VMEM(full, F32), pltpu.VMEM((rows, inner), BF16), pltpu.VMEM(full, BF16)]
        + [pltpu.VMEM((width, rows), BF16)]
        + [pltpu.VMEM(*grads)] * 2
        + [pltpu.VMEM((8, width), F32), pltpu.VMEM(full, F32)]
        + [pltpu.VMEM((rows, block_col), BF16)] * 4
        + [
            pltpu.SemaphoreType.DMA((48,)),
            pltpu.SemaphoreType.DMA((2,)),
            pltpu.SemaphoreType.DMA((4,)),
            pltpu.SemaphoreType.DMA((2, 8)),
            pltpu.SemaphoreType.DMA((5,)),
        ],
        compiler_params=pltpu.CompilerParams(vmem_limit_bytes=FFN_LIMIT),
        cost_estimate=pl.CostEstimate(
            flops=10 * rows * width * inner, bytes_accessed=24 << 20, transcendentals=0
        ),
        name="ffn_back",
    )(
        scalars,
        d_branch,
        inv_std,
        vectors,
        d_resid2,
        sums_mid,
        count,
        *attended,
        *(in_hbm(a) for a in (normed, slope, hidden, *packs)),
    )


def whole_call(kernel, name, args, outs, scalars=None, cost=SMALL_COST):
    return pl.pallas_call(
        kernel,
        out_shape=[o if hasattr(o, "memory_space") else jax.ShapeDtypeStruct(*o) for o in outs],
        in_specs=([] if scalars is None else [SMEM_SPEC]) + [VMEM_SPEC] * len(args),
        out_specs=[VMEM_SPEC] * len(outs),
        compiler_params=pltpu.CompilerParams(vmem_limit_bytes=SMALL_LIMIT),
        cost_estimate=cost,
        name=name,
    )(*(() if scalars is None else (scalars,)), *args)


def fold_cores(own, came):
    _, rows, cols = own.shape

    def kernel(own_ref, came_ref, *outs):
        for k, out in enumerate(outs):
            out[...] = (own_ref[k].astype(F32) + came_ref[k].astype(F32)).astype(BF16)

    outs = [pltpu.HBM((rows, cols), BF16)] * 4
    return whole_call(kernel, "fold_cores", (own, came), outs)


def split_cores(own, came):
    _, rows, cols = own.shape
    half = rows // 2

    def kernel(own_ref, came_ref, send_x, send_y, keep_upper, keep_lower):
        def total(upper, k):
            at = slice(0, half) if upper else slice(half, rows)
            return (own_ref[k, at, :].astype(F32) + came_ref[k, at, :].astype(F32)).astype(BF16)

        for i, k in enumerate((1, 3)):
            send_x[i] = total(True, k)
        for i, k in enumerate((2, 3)):
            send_y[i] = total(False, k)
        for i, k in enumerate((0, 2)):
            keep_upper[i] = total(True, k)
        for i, k in enumerate((0, 1)):
            keep_lower[i] = total(False, k)

    return whole_call(kernel, "split_cores", (own, came), [((2, half, cols), BF16)] * 4)


def second_step(keep_upper, came_x, keep_lower, came_y):
    def kernel(upper, upper_came, lower, lower_came, send_y, send_x, kept):
        half = upper.shape[1]
        send_y[...] = (upper[1].astype(F32) + upper_came[1].astype(F32)).astype(BF16)
        send_x[...] = (lower[1].astype(F32) + lower_came[1].astype(F32)).astype(BF16)
        kept[:half, :] = upper[0].astype(F32) + upper_came[0].astype(F32)
        kept[half:, :] = lower[0].astype(F32) + lower_came[0].astype(F32)

    half, cols = keep_upper.shape[1:]
    return whole_call(
        kernel,
        "second_step",
        (keep_upper, came_x, keep_lower, came_y),
        [((half, cols), BF16)] * 2 + [((2 * half, cols), F32)],
    )


def add_halves(kept, upper, lower):
    def kernel(kept, upper, lower, out):
        half = upper.shape[0]
        out[:half, :] = (kept[:half, :] + upper[...].astype(F32)).astype(BF16)
        out[half:, :] = (kept[half:, :] + lower[...].astype(F32)).astype(BF16)

    outs = [pltpu.HBM(kept.shape, BF16)]
    return whole_call(kernel, "add_halves", (kept, upper, lower), outs)[0]


def fold_quarters(terms, scalars):
    rows, cols = terms[0].shape
    part = rows // 4
    count = len(terms)

    def kernel(scalars, *refs):
        for k in range(4):
            at = pl.ds(pl.multiple_of((scalars[2] ^ k) * part, 8), part)
            total = sum(term[at, :].astype(F32) for term in refs[:count])
            refs[count + k % 2][k // 2] = total.astype(BF16)

    return whole_call(kernel, "fold_quarters", terms, [((2, part, cols), BF16)] * 2, scalars)


def finish(dense, qkv, half, block_col, scalars):
    _, part, cols = dense[0].shape
    qkv_part = qkv[0].shape[1]
    deep = block_col // 2

    def kernel(scalars, *refs):
        up, out, table, query, key, value, bias, dense_all, qkv_all = refs[4:]
        for parts, target in ((refs[:2], dense_all), (refs[2:4], qkv_all)):
            for k in range(4):
                piece = parts[k % 2].at[k // 2]
                rows = piece.shape[0]
                at = pl.ds(pl.multiple_of((scalars[2] ^ k) * rows, 8), rows)
                target[at, :] = piece[...].astype(F32)
        up[...] = dense_all[:half, :]
        out[:deep, :] = dense_all[half : half + deep, :half]
        out[deep:, :] = dense_all[half : half + deep, half:]
        table[...] = dense_all[half + deep : half + deep + 16, :]
        for i, target in enumerate((query, key, value)):
            target[...] = qkv_all[i * block_col : (i + 1) * block_col, :]
        bias[...] = qkv_all[3 * block_col : 3 * block_col + 8, :]

    S = jax.ShapeDtypeStruct
    return pl.pallas_call(
        kernel,
        out_shape=[S((half, cols), F32), S((block_col, half), F32), S((16, cols), F32)]
        + [S((block_col, half), F32)] * 3
        + [S((8, half), F32)],
        in_specs=[SMEM_SPEC] + [VMEM_SPEC] * 4,
        out_specs=[VMEM_SPEC] * 7,
        scratch_shapes=[
            pltpu.VMEM((4 * part, cols), F32),
            pltpu.VMEM((4 * qkv_part, half), F32),
        ],
        compiler_params=pltpu.CompilerParams(vmem_limit_bytes=SMALL_LIMIT),
        cost_estimate=SMALL_COST,
        name="finish",
    )(scalars, *dense, *qkv)


def dot(left, right, dims=NN):
    return lax.dot_general(left, right, dims, preferred_element_type=F32)


def split3(value):
    high = value.astype(BF16)
    rest = value - high.astype(F32)
    middle = rest.astype(BF16)
    low = (rest - middle.astype(F32)).astype(BF16)
    return high.astype(F32), middle.astype(F32), low.astype(F32)


def key_range(code, span, span_rows, blocks):
    per = span_rows // BLK
    first_seg = code[span * per, 0] // 2
    last_seg = code[span * per + per - 1, BLK - 1] // 2
    low = jnp.int32(0)
    high = jnp.int32(0)
    for other in range(blocks):
        start = code[other, 0]
        low += (code[other, BLK - 1] // 2 < first_seg).astype(jnp.int32)
        high += ((start // 2 <= last_seg) & (start % 2 == 1)).astype(jnp.int32)
    below = jnp.maximum(jnp.minimum(high, span * per) - low, 0)
    above = jnp.maximum(high - (span + 1) * per, 0)
    return low, below, below + above


def key_block(step, low, below, after):
    return jnp.where(step < below, low + step, after + step - below)


def lane_index(rows):
    return lax.broadcasted_iota(jnp.int32, (rows, 128), 1)


def allowed_block(code_rows, block, offset, span_rows):
    row = lax.broadcasted_iota(jnp.int32, (span_rows, BLK), 0)
    col = lax.broadcasted_iota(jnp.int32, (span_rows, BLK), 1)
    return (code_rows[pl.ds(block, 1), :] % 2 == 1) | (row == col + offset)


def attention_forward_kernel(heads, scalars, code, *refs):
    code_rows = refs[0]
    token_parts = refs[1:6]
    weights = refs[6:8]
    pieces = refs[8:12]
    saved = refs[12:16]
    padded, max_scr, acc_scr, query_pad, key_pad, value_pad, out_pad, whole_sem, span_sem = refs[16:]
    span_rows, width = token_parts[0].shape
    cols = 64 * heads
    flip = scalars[1]
    per = span_rows // BLK
    blocks = query_pad.shape[1] // BLK
    lane = lane_index(span_rows)
    for i in range(3):
        src = slice(i * cols, (i + 1) * cols)
        padded[i * 256 : i * 256 + cols, : width // 2] = weights[0][src, :]
        padded[i * 256 : i * 256 + cols, width // 2 :] = weights[1][src, :]
        padded[i * 256 + cols : (i + 1) * 256, :] = jnp.zeros((256 - cols, width), BF16)
    marks_bias = weights[0][3 * cols : 3 * cols + 1, :].astype(F32)
    no_bias = jnp.zeros((1, 256 - cols), F32)
    biases = (
        jnp.concatenate([marks_bias[:, :cols], no_bias], 1),
        None,
        jnp.concatenate([marks_bias[:, cols : 2 * cols], no_bias], 1),
    )
    first = 0
    for tokens in token_parts:
        rows = slice(first, first + tokens.shape[0])
        marks = []
        for block in range(rows.start // BLK, rows.stop // BLK):
            place = (block // per ^ flip) * per + block % per
            marks.append(
                jnp.broadcast_to(code_rows[pl.ds(place, 1), :].astype(F32), (128, BLK)).T
            )
        first = rows.stop
        lane = lane_index(tokens.shape[0])
        value_ones = jnp.where((lane >= 64) & (lane < 67), 1.0, 0.0)
        marks = jnp.concatenate(marks, 0).astype(jnp.int32)
        same = lane - 64 == marks // 2
        ids = (lane >= 64) & (lane < 80)
        query_marks = jnp.where((ids & same) | (lane == 80), 1.0, 0.0)
        key_marks = jnp.where(
            (ids & ~same) | ((lane == 80) & (marks % 2 == 0)),
            MASKED,
            jnp.where((lane >= 81) & (lane < 84), -1.0, 0.0),
        )
        for i, (out, extra) in enumerate(
            ((query_pad, query_marks), (key_pad, key_marks), (value_pad, value_ones))
        ):
            projected = dot(tokens[...], padded[i * 256 : (i + 1) * 256, :], NT)
            if biases[i] is not None:
                projected += biases[i]
            if i == 0:
                projected = projected.astype(BF16).astype(F32) * 0.125
            out[0, rows, :] = jnp.where(lane < 64, projected[:, :128], extra).astype(BF16)
            out[1, rows, :] = jnp.where(
                lane < 64, pltpu.roll(projected[:, :128], 64, 1), extra
            ).astype(BF16)
            out[2, rows, :] = jnp.where(lane < 64, projected[:, 128:], extra).astype(BF16)
    lane = lane_index(span_rows)
    no_valid_lane = jnp.where(lane == 80, 0.0, 1.0).astype(BF16)
    whole_copies = [
        pltpu.make_async_copy(key_pad, saved[1], whole_sem.at[0]),
        pltpu.make_async_copy(value_pad, saved[2], whole_sem.at[1]),
    ]
    for copy in whole_copies:
        copy.start()

    def span_copies(at):
        rows = pl.ds(pl.multiple_of(at * span_rows, span_rows), span_rows)
        return [
            pltpu.make_async_copy(
                source.at[:, rows, :], saved[i].at[:, rows, :], span_sem.at[i // 3, at]
            )
            for source, i in ((query_pad, 0), (out_pad, 3))
        ]

    def query_step(span, _):
        at = span ^ flip
        rows = pl.ds(pl.multiple_of(at * span_rows, span_rows), span_rows)
        low, below, count = key_range(code, span, span_rows, blocks)

        def keys_of(block):
            place = (block // per ^ flip) * per + block % per
            return pl.ds(pl.multiple_of(place * BLK, BLK), BLK)

        def scores_of(h, keys, allowed=None):
            if allowed is None:
                return dot(query_pad[h, rows, :], key_pad[h, keys, :], NT)
            scores = dot(query_pad[h, rows, :] * no_valid_lane, key_pad[h, keys, :], NT)
            return jnp.where(allowed, scores, MASKED)

        def each_block(visit):
            for part in range(per):
                block = span * per + part
                visit(keys_of(block), allowed_block(code_rows, block, part * BLK, span_rows))

            def step_fn(step, _):
                visit(keys_of(key_block(step, low, below, (span + 1) * per)), None)
                return 0

            lax.fori_loop(0, count, step_fn, 0)

        acc_scr[...] = jnp.zeros_like(acc_scr)
        max_scr[...] = jnp.zeros_like(max_scr)

        def plain(keys, allowed):
            for h in range(heads):
                probs = jnp.exp(scores_of(h, keys, allowed)).astype(BF16)
                acc_scr[h] += dot(probs, value_pad[h, keys, :])

        each_block(plain)
        least, most = jnp.float32(1.0), jnp.float32(1.0)
        for h in range(heads):
            total = jnp.where(lane == 64, acc_scr[h], 1.0)
            good = (total > 1e-25) & (total < 1e30)
            least = jnp.minimum(least, jnp.min(jnp.where(good, 1.0, 0.0)))

        @pl.when(least < 0.5)
        def _():
            max_scr[...] = jnp.full_like(max_scr, MASKED)

            def find_max(keys, allowed):
                for h in range(heads):
                    scores = scores_of(h, keys, allowed)
                    max_scr[h] = jnp.maximum(
                        max_scr[h], jnp.maximum(scores[:, :128], scores[:, 128:])
                    )

            each_block(find_max)
            for h in range(heads):
                max_scr[h] = jnp.broadcast_to(
                    jnp.max(max_scr[h], axis=1, keepdims=True), (span_rows, 128)
                )
            acc_scr[...] = jnp.zeros_like(acc_scr)

            def shifted(keys, allowed):
                for h in range(heads):
                    row_max = max_scr[h]
                    scores = scores_of(h, keys, allowed)
                    probs = jnp.exp(scores - jnp.concatenate([row_max, row_max], 1))
                    acc_scr[h] += dot(probs.astype(BF16), value_pad[h, keys, :])

            each_block(shifted)

        outs = []
        for h in range(heads):
            acc = acc_scr[h]
            total = jnp.broadcast_to(acc[:, 64:65], acc.shape)
            out = acc / total
            out_pad[h, rows, :] = out
            outs.append(out)
            high, middle, rest = split3(max_scr[h] + jnp.log(total))
            extra = jnp.where(
                lane == 81,
                high,
                jnp.where(lane == 82, middle, jnp.where(lane == 83, rest, 0.0)),
            )
            query_pad[h, rows, :] = query_pad[h, rows, :] + extra.astype(BF16)
        pair = jnp.where(lane < 64, outs[0], pltpu.roll(outs[1], 64, 1)).astype(BF16)
        last = outs[2][:, :64].astype(BF16)
        for k, piece in enumerate(pieces):

            @pl.when(at == k)
            def _():
                piece[:, 0:128] = pair
                piece[:, 128:cols] = last

        for copy in span_copies(at):
            copy.start()
        return 0

    lax.fori_loop(0, len(pieces), query_step, 0)
    for copy in whole_copies:
        copy.wait()
    for at in range(len(pieces)):
        for copy in span_copies(at):
            copy.wait()


def attention_forward(scalars, code, token_shards, weights):
    rows, width = token_shards[0].shape
    length = code.shape[0] * BLK
    cols = (weights[0].shape[0] - PAD_ROWS) // 3
    heads = cols // 64
    S = jax.ShapeDtypeStruct
    flops = 2 * length * width * 3 * 256 + 3 * length * length * 128
    return pl.pallas_call(
        lambda *refs: attention_forward_kernel(heads, *refs),
        out_shape=[S((rows, cols), BF16)] * 4
        + [pltpu.HBM((heads, length, 128), BF16)] * 3
        + [pltpu.HBM((heads, length, 128), F32)],
        in_specs=[SMEM_SPEC] * 2 + [VMEM_SPEC] * 8,
        out_specs=[VMEM_SPEC] * 4 + [HBM_SPEC] * 4,
        scratch_shapes=[
            pltpu.VMEM((3 * 256, width), BF16),
            pltpu.VMEM((heads, rows, 128), F32),
            pltpu.VMEM((heads, rows, 128), F32),
        ]
        + [pltpu.VMEM((heads, length, 128), BF16)] * 3
        + [
            pltpu.VMEM((heads, length, 128), F32),
            pltpu.SemaphoreType.DMA((2,)),
            pltpu.SemaphoreType.DMA((2, 4)),
        ],
        compiler_params=pltpu.CompilerParams(vmem_limit_bytes=32 << 20),
        cost_estimate=pl.CostEstimate(
            flops=3 * flops, bytes_accessed=16 << 20, transcendentals=heads * length * 1024
        ),
        name="attention_forward",
    )(scalars, code, code, *token_shards, *weights)


def attention_backward_kernel(heads, scalars, code, *refs):
    code_rows = refs[0]
    span_rows = refs[1].shape[0]
    term_hbm, grad_hbm = refs[16:20], refs[20:22]
    grad_pad, query_sum, key_sum, value_sum, low_scr, grad_scr, bias_sum = refs[22:29]
    query_pad, key_pad, value_pad, out_pad = refs[29:33]
    shards_in = refs[33:37]
    weights = refs[37]
    grads = refs[38:42]
    terms, own_grad, other_grad, out_sems, in_sems = refs[42:]
    side = weights.shape[1] // 2
    last_half = span_rows // 2
    pairs = list(zip(refs[1:9], grads + refs[29:33]))
    pairs += list(zip(refs[9:12], shards_in[:3]))
    pairs += [
        (refs[12], shards_in[3].at[:last_half, :]),
        (refs[13], shards_in[3].at[last_half:, :]),
    ]
    pairs += [(refs[14], weights.at[:, :side]), (refs[15], weights.at[:, side:])]
    copies = [
        pltpu.make_async_copy(source, target, in_sems.at[i])
        for i, (source, target) in enumerate(pairs)
    ]
    for i in (7, 0, 1, 2, 3, 4, 5, 6, 8, 9, 10, 11, 12, 13, 14):
        copies[i].start()
    key_sum[...] = jnp.zeros_like(key_sum)
    value_sum[...] = jnp.zeros_like(value_sum)
    query_sum[...] = jnp.zeros_like(query_sum)
    for i in (7, 0, 1, 2, 3):
        copies[i].wait()
    flip = scalars[1]
    per = span_rows // BLK
    blocks = query_pad.shape[1] // BLK
    lane = lane_index(span_rows)
    gap = jnp.zeros((span_rows, 64), BF16)
    for shard, grad in enumerate(grads):
        rows = slice(shard * span_rows, (shard + 1) * span_rows)
        pair = grad[:, 0:128].astype(F32)
        last = jnp.concatenate([grad[:, 128:192], gap], 1).astype(F32)
        for h, block in enumerate((pair, pltpu.roll(pair, 64, 1), last)):
            block = jnp.where(lane < 64, block, 0.0)
            delta = jnp.sum(block * out_pad[h, rows, :], axis=1, keepdims=True)
            high, middle, rest = split3(-delta)
            block = jnp.where(
                lane == 64,
                high,
                jnp.where(lane == 65, middle, jnp.where(lane == 66, rest, block)),
            )
            grad_pad[h, rows, :] = block.astype(BF16)
    for i in (4, 5, 6):
        copies[i].wait()
    no_valid_lane = jnp.where(lane == 80, 0.0, 1.0).astype(BF16)

    def query_step(span, _):
        at = span ^ flip
        rows = pl.ds(pl.multiple_of(at * span_rows, span_rows), span_rows)
        low, below, count = key_range(code, span, span_rows, blocks)

        def visit(block, allowed):
            place = (block // per ^ flip) * per + block % per
            keys = pl.ds(pl.multiple_of(place * BLK, BLK), BLK)
            for h in range(heads):
                query, grad = query_pad[h, rows, :], grad_pad[h, rows, :]
                key, value = key_pad[h, keys, :], value_pad[h, keys, :]
                if allowed is None:
                    scores = dot(key, query, NT)
                else:
                    scores = jnp.where(allowed, dot(key, query * no_valid_lane, NT), MASKED)
                probs = jnp.exp(scores)
                d_scores = (probs * dot(value, grad, NT)).astype(BF16)
                value_sum[h, keys, :] += dot(probs.astype(BF16), grad)
                key_sum[h, keys, :] += dot(d_scores, query)
                query_sum[h, rows, :] += dot(d_scores, key, TN)

        for part in range(per):
            block = span * per + part
            key_at = lax.broadcasted_iota(jnp.int32, (BLK, span_rows), 0)
            query_at = lax.broadcasted_iota(jnp.int32, (BLK, span_rows), 1)
            marks = jnp.broadcast_to(
                code_rows[pl.ds(block, 1), :].astype(F32), (128, BLK)
            ).T.astype(jnp.int32)
            valid = jnp.concatenate([marks] * (span_rows // 128), 1) % 2 == 1
            visit(block, valid | (query_at == key_at + part * BLK))

        def step_fn(step, _):
            visit(key_block(step, low, below, (span + 1) * per), None)
            return 0

        lax.fori_loop(0, count, step_fn, 0)
        return 0

    lax.fori_loop(0, len(grads), query_step, 0)
    for i in range(8, 15):
        copies[i].wait()
    bias_sum[...] = jnp.zeros_like(bias_sum)
    stores = []
    for shard in range(len(grads)):
        rows = slice(shard * span_rows, (shard + 1) * span_rows)
        parts = [query_sum[h, rows, :] * 0.125 for h in range(heads)]
        parts += [sums[h, rows, :] for sums in (key_sum, value_sum) for h in range(heads)]
        for at in range(0, len(parts), 2):
            if at + 1 < len(parts):
                value = jnp.where(lane < 64, parts[at], pltpu.roll(parts[at + 1], 64, 1))
            else:
                value = parts[at][:, :64]
            low = value.astype(BF16)
            cols = slice(at * 64, at * 64 + low.shape[1])
            low_scr[:, cols] = low
            bias_sum[0:1, cols] += column_sum(low.astype(F32))
        low = low_scr[...]
        depth = low.shape[1]
        term = dot(low, weights[:depth, :]).astype(BF16)
        terms[shard] = term
        copy = pltpu.make_async_copy(
            terms.at[shard], term_hbm[shard], out_sems.at[shard]
        )
        copy.start()
        stores.append(copy)
        part = dot(low, shards_in[shard][...], TN)
        if shard == 0:
            grad_scr[...] = part
        elif shard < 3:
            grad_scr[...] += part
        else:
            total = (grad_scr[...] + part).astype(BF16)
            half = total.shape[1] // 2
            own_grad[:depth, :] = total[:, :half]
            other_grad[:depth, :] = total[:, half:]
    cols = heads * 64
    bias = jnp.concatenate([bias_sum[:, 0:cols], bias_sum[:, 2 * cols :]], 1).astype(BF16)
    bias = jnp.concatenate([bias] * ((own_grad.shape[0] - depth) // bias.shape[0]), 0)
    own_grad[depth:, :] = bias
    other_grad[depth:, :] = bias
    for i, source in enumerate((own_grad, other_grad)):
        copy = pltpu.make_async_copy(source, grad_hbm[i], out_sems.at[4 + i])
        copy.start()
        stores.append(copy)
    for copy in stores:
        copy.wait()


def attention_backward(scalars, code, grads, saved, token_shards, weights):
    length = code.shape[0] * BLK
    heads = saved[0].shape[0]
    rows, width = token_shards[0].shape
    cols = 3 * heads * 64
    S = jax.ShapeDtypeStruct
    return pl.pallas_call(
        lambda *refs: attention_backward_kernel(heads, *refs),
        out_shape=[
            *[pltpu.HBM((rows, width), BF16)] * 4,
            *[pltpu.HBM((cols + GRAD_PAD, width // 2), BF16)] * 2,
        ],
        in_specs=[SMEM_SPEC] * 2 + [VMEM_SPEC] + [HBM_SPEC] * 15,
        out_specs=[HBM_SPEC] * 6,
        scratch_shapes=[
            pltpu.VMEM((heads, length, 128), BF16),
            pltpu.VMEM((heads, length, 128), F32),
            pltpu.VMEM((heads, length, 128), F32),
            pltpu.VMEM((heads, length, 128), F32),
            pltpu.VMEM((rows, cols), BF16),
            pltpu.VMEM((cols, width), F32),
            pltpu.VMEM((16, cols), F32),
        ]
        + [pltpu.VMEM(a.shape, a.dtype) for a in saved]
        + [pltpu.VMEM((rows, width), BF16)] * 4
        + [pltpu.VMEM((weights[0].shape[0], width), BF16)]
        + [pltpu.VMEM(a.shape, a.dtype) for a in grads]
        + [
            pltpu.VMEM((4, rows, width), BF16),
            pltpu.VMEM((cols + GRAD_PAD, width // 2), BF16),
            pltpu.VMEM((cols + GRAD_PAD, width // 2), BF16),
            pltpu.SemaphoreType.DMA((6,)),
            pltpu.SemaphoreType.DMA((15,)),
        ],
        compiler_params=pltpu.CompilerParams(vmem_limit_bytes=46 << 20),
        cost_estimate=pl.CostEstimate(
            flops=heads * length * length * 1500, bytes_accessed=8 << 20, transcendentals=0
        ),
        name="attention_backward",
    )(
        scalars,
        code,
        code,
        *(in_hbm(a) for a in (*grads, *saved, *token_shards, *weights)),
    )


CHIP = [[(c, c ^ k) for c in range(4)] for k in range(4)]
PLANE = [[(p, p ^ k) for p in range(4)] for k in range(4)]
CORE = [(0, 1), (1, 0)]


def to_chip(value, k):
    return lax.ppermute(value, "gz", CHIP[k])


def to_core(value):
    return lax.ppermute(value, "gy", CORE)


def to_plane(value, k):
    return lax.ppermute(value, "gx", PLANE[k])


def after(value, *others):
    return lax.optimization_barrier((value,) + others)[0]


def swap_halves(flip, value):
    half = value.shape[-1] // 2
    swapped = jnp.concatenate([value[..., half:], value[..., :half]], -1)
    return jnp.where(flip, swapped, value)


def add_low(left, right):
    return (left.astype(F32) + right.astype(F32)).astype(BF16)


def sum_planes(dense, qkv, waits):
    if lax.axis_size("gx") != 4:
        dense, other = jnp.stack(dense), jnp.stack(qkv(dense[0]))
        total = lax.psum((dense, other), "gx")
        return [(t[0], t[1]) for t in total], waits
    near = dense[0].astype(F32) + to_plane(dense[1], 1).astype(F32)
    step = near[1].astype(BF16)
    keep, send = qkv(step)
    total = (near[0] + to_plane(step, 2).astype(F32)).astype(BF16)
    near = keep.astype(F32) + to_plane(send, 1).astype(F32)
    step = after(near[1].astype(BF16), total)
    pair = jnp.stack([total, to_plane(total, 2)])
    other = (near[0] + to_plane(step, 2).astype(F32)).astype(BF16)
    other = after(other, pair)
    back = to_plane(pair, 1)
    last = to_plane(other, 2)
    waits = lax.optimization_barrier((*waits, last))[:-1]
    other_pair = after(jnp.stack([other, last]), *waits)
    return [(pair, back), (other_pair, to_plane(other_pair, 1))], waits


def shards(
    tokens,
    segment_ids,
    valid_mask,
    cotangent,
    teacher,
    w_query,
    b_query,
    w_key,
    w_value,
    b_value,
    w_out,
    b_out,
    norm1_gain,
    norm1_bias,
    w_up,
    b_up,
    w_down,
    b_down,
    norm2_gain,
    norm2_bias,
):
    row_count, width = tokens.shape
    half = width // 2
    core = lax.axis_index("gy")
    chip = lax.axis_index("gz")
    flip = core == 1
    block_col = w_query.shape[1]
    hidden_col = w_up.shape[1]
    plane = lax.axis_index("gx") if lax.axis_size("gx") == 4 else jnp.int32(0)
    scalars = jnp.stack([core, chip, plane, chip]).astype(jnp.int32)

    own_tokens = swap_halves(flip, tokens)
    along_x, along_y = to_chip(own_tokens, 1), to_chip(own_tokens, 2)
    code = (segment_ids * 2 + valid_mask).reshape(-1, BLK)
    bias_row = jnp.concatenate([b_query, b_value])[None, :]
    qkv_own = jnp.concatenate(
        [w_query.T, w_key.T, w_value.T, jnp.broadcast_to(bias_row, (PAD_ROWS, half))], 0
    )
    vectors = jnp.stack([b_out, norm1_gain, norm1_bias, b_down, norm2_gain, norm2_bias] + [b_out] * 2)
    vectors = swap_halves(flip, vectors.astype(F32))
    own_valid = lax.dynamic_slice_in_dim(valid_mask, chip * row_count, row_count, 1).astype(F32)
    count = jnp.concatenate([own_valid, jnp.zeros((1, width - row_count), F32)], 1)
    count = jnp.broadcast_to(count, (8, width))
    own_valid = own_valid.T
    packed = jnp.concatenate(
        [
            jnp.concatenate([w_down[: hidden_col // 2], w_down[hidden_col // 2 :]], 1),
            w_up,
            jnp.concatenate([w_out[: block_col // 2], w_out[block_col // 2 :]], 1),
            jnp.broadcast_to(b_up[None, :], (PAD_ROWS, hidden_col)),
        ],
        0,
    )

    code, qkv_own, scalars, packed, vectors, own_valid, count, *_ = lax.optimization_barrier(
        (code, qkv_own, scalars, packed, vectors, own_valid, count, own_tokens)
    )
    qkv = (qkv_own, to_core(qkv_own))
    along_x, along_y, *qkv = lax.optimization_barrier((along_x, along_y, *qkv))
    middle = row_count // 2
    far = (to_chip(along_x[:middle], 2), to_chip(along_y[middle:], 1))
    token_shards = (own_tokens, along_x, along_y, *far)
    packed = after(packed, *far)
    pack_x, pack_y = to_chip(packed, 1), to_chip(packed, 2)

    scalars = after(scalars, packed)
    results = attention_forward(scalars, code, token_shards, qkv)
    saved = results[4:]
    attended = [results[0]] + [to_chip(results[k], k) for k in (1, 2, 3)]

    deep = hidden_col // 2
    pack_x, pack_y = lax.optimization_barrier((pack_x, pack_y, results[0]))[:2]
    far = (to_chip(pack_x[:, :half], 2), to_chip(pack_y[:, half:], 1))
    packs = (packed, pack_x, pack_y, *far)
    packs += (to_core(packed), *(to_core(after(v, *attended[1:])) for v in packs[1:]))

    inv_std, output, d_resid2, d_branch, sums_mid, act, normed, hidden_low, slope = ffn_forward(
        scalars, attended, own_tokens, own_valid, vectors, cotangent, teacher, packs, deep
    )
    pieces = (4, hidden_col, half)
    d_down_other = jnp.einsum("lf,lm->fm", act, d_branch[:, half:], preferred_element_type=F32)
    d_down_came = to_core(d_down_other.astype(BF16).reshape(pieces))
    d_down = jnp.einsum("lf,lm->fm", act, d_branch[:, :half], preferred_element_type=F32)
    down_x, down_y, down_upper, down_lower = split_cores(
        d_down.astype(BF16).reshape(pieces), d_down_came
    )
    d_branch = after(d_branch, down_upper)
    down_x, down_y = to_chip(down_x, 1), to_chip(down_y, 2)
    d_resid1, *back, own_grads, other_grads = ffn_back(
        scalars,
        d_branch,
        inv_std,
        vectors,
        d_resid2,
        sums_mid,
        count,
        attended,
        normed,
        slope,
        hidden_low,
        packs,
        deep,
    )
    d_pieces = [back[0]] + [to_chip(back[k], k) for k in (1, 2, 3)]

    down_y, down_x, down_kept = second_step(down_upper, down_x, down_lower, down_y)
    d_dense = fold_cores(own_grads, to_core(after(other_grads, down_y)))
    down_total = add_halves(down_kept, to_chip(down_y, 2), to_chip(down_x, 1))
    grad_down = lax.psum(down_total, "gx")
    d_pieces[0] = after(d_pieces[0], d_dense[0], down_total)
    d_dense = [d_dense[0]] + [to_chip(d_dense[k], k) for k in (1, 2, 3)]

    *terms, d_own, d_other = attention_backward(
        scalars, code, d_pieces, saved, token_shards, qkv
    )
    d_dense[0] = after(d_dense[0], grad_down, terms[0])
    quarters = fold_quarters(d_dense, scalars)
    d_own, d_other, *terms, _, _ = lax.optimization_barrier((d_own, d_other, *terms, *quarters))
    d_w = (d_own, to_core(d_other))
    terms = [terms[0]] + [to_chip(terms[k], k) for k in (1, 2, 3)]
    (dense_grad, qkv_grad), came = sum_planes(
        quarters, lambda first: fold_quarters((after(d_w[0], first), d_w[1]), scalars), terms[1:]
    )
    d_tokens = d_resid1 + sum(t.astype(F32) for t in (terms[0], *came))
    grad_up, grad_out, table, grad_query, grad_key, grad_value, d_bias = finish(
        dense_grad, qkv_grad, half, block_col, scalars
    )

    mean_loss = jnp.sum(table[3]) / (jnp.sum(table[7]) * width)
    return (
        output,
        mean_loss,
        swap_halves(flip, d_tokens.astype(BF16)),
        grad_query.T,
        d_bias[0, :block_col],
        grad_key.T,
        grad_value.T,
        d_bias[0, block_col:],
        grad_out,
        table[6],
        table[4],
        table[5],
        grad_up,
        table[8],
        grad_down.astype(F32),
        table[2],
        table[0],
        table[1],
    )


def solution(mesh):
    placed = (
        P(("gx", "gy", "gz"), None),
        P(("gx", "gy"), None),
        P(("gx", "gy"), None),
        P(("gx", "gy", "gz"), None),
        P(("gx", "gy", "gz"), None),
        P("gy", "gz"),
        P("gz"),
        P("gy", "gz"),
        P("gy", "gz"),
        P("gz"),
        P("gz", "gy"),
        P(),
        P(),
        P(),
        P("gy", "gz"),
        P("gz"),
        P("gz", "gy"),
        P(),
        P(),
        P(),
    )
    return jax.shard_map(
        shards,
        mesh=mesh,
        in_specs=placed,
        out_specs=(
            P(("gx", "gy", "gz"), None),
            P(),
            P(("gx", "gy", "gz"), None),
            P("gy", "gz"),
            P("gz"),
            P("gy", "gz"),
            P("gy", "gz"),
            P("gz"),
            P("gz", "gy"),
            P(),
            P(),
            P(),
            P("gy", "gz"),
            P("gz"),
            P("gz", "gy"),
            P(),
            P(),
            P(),
        ),
        check_vma=False,
    )
```

```python
import math

import jax
import jax.numpy as jnp
from jax import lax
from jax.experimental import pallas as pl
from jax.experimental.pallas import tpu as pltpu
from jax.sharding import PartitionSpec as P

EPSILON = 1e-05
MASKED = -1e30
PAD_ROWS = 16
GRAD_PAD = 64
BLK = 256
F32 = jnp.float32
BF16 = jnp.bfloat16
NT = (((1,), (1,)), ((), ()))
NN = (((1,), (0,)), ((), ()))
TN = (((0,), (0,)), ((), ()))


VMEM_SPEC = pl.BlockSpec(memory_space=pltpu.VMEM)
SMEM_SPEC = pl.BlockSpec(memory_space=pltpu.SMEM)
HBM_SPEC = pl.BlockSpec(memory_space=pltpu.HBM)
VMEM_LIMIT = 24 << 20
SMALL_LIMIT = 20 << 20
FFN_LIMIT = 40 << 20
SMALL_COST = pl.CostEstimate(flops=1 << 16, bytes_accessed=1 << 12, transcendentals=0)


def in_hbm(array):
    return pltpu.with_memory_space_constraint(array, pltpu.HBM)


class Loads:
    def __init__(self, packs, sems):
        self.packs, self.sems, self.used, self.groups = packs, sems, 0, {}

    def add(self, group, source, target):
        copy = pltpu.make_async_copy(source, target, self.sems.at[self.used])
        self.used += 1
        self.groups.setdefault(group, []).append(copy)

    def start(self, *groups):
        for group in groups:
            for copy in self.groups.get(group, ()):
                copy.start()

    def wait(self, *groups):
        for group in groups:
            for copy in self.groups.get(group, ()):
                copy.wait()

    def blocks(self, core):
        packs = self.packs[5 * core : 5 * core + 5]
        half = packs[4].shape[1]
        blocks = [(k, i, packs[k], i * half) for k in range(3) for i in range(2)]
        return half, blocks + [(3, 0, packs[3], 0), (3, 1, packs[4], 0)]

    def lay_out(self, deep, block_col, up_full, down_full, out_full, bias_full):
        for core in range(2):
            half, blocks = self.blocks(core)
            top = deep + half
            out_deep = block_col // 2
            side = slice(core * half, (core + 1) * half)
            for k, i, pack, col in blocks:
                cols = slice(col, col + half)
                hidden = slice((2 * k + i) * half, (2 * k + i + 1) * half)
                self.add(("up", k), pack.at[deep:top, cols], up_full.at[side, hidden])
                self.add(("down", k), pack.at[0:deep, cols], down_full.at[hidden, side])
                first = k * block_col + i * out_deep
                self.add(
                    "out",
                    pack.at[top : top + out_deep, cols],
                    out_full.at[first : first + out_deep, side],
                )
                if core == 0 and bias_full is not None:
                    low = top + out_deep
                    self.add("out", pack.at[low : low + PAD_ROWS, cols], bias_full.at[:, hidden])


def half_start(scalars, second, half):
    flip = scalars[0]
    return pl.multiple_of(jnp.where(second, 1 - flip, flip) * half, 128)


def read_swapped(ref, scalars):
    half = ref.shape[-1] // 2
    return jnp.concatenate(
        [
            ref[:, pl.ds(half_start(scalars, False, half), half)].astype(F32),
            ref[:, pl.ds(half_start(scalars, True, half), half)].astype(F32),
        ],
        1,
    )


def write_swapped(ref, rows, value, scalars):
    half = ref.shape[-1] // 2
    ref[rows, pl.ds(half_start(scalars, False, half), half)] = value[:, :half].astype(ref.dtype)
    ref[rows, pl.ds(half_start(scalars, True, half), half)] = value[:, half:].astype(ref.dtype)


def column_sum(value):
    return jnp.sum(value, 0, keepdims=True)


def layer_norm(resid):
    average = jnp.mean(resid, -1, keepdims=True)
    centered = resid - average
    inv_std = lax.rsqrt(jnp.mean(centered * centered, -1, keepdims=True) + EPSILON)
    return centered * inv_std, inv_std


def layer_norm_back(upstream, gain, normed, inv_std):
    scaled = upstream * gain
    return inv_std * (
        scaled
        - jnp.mean(scaled, -1, keepdims=True)
        - normed * jnp.mean(scaled * normed, -1, keepdims=True)
    )


def ffn_forward_kernel(deep, scalars, *refs):
    att = refs[:4]
    own_tokens, valid, vectors = refs[4:7]
    cot_source, teach_source = refs[7:9]
    packs = refs[9:19]
    std_out, output, resid_out, branch_out, sums, act_out = refs[19:25]
    normed_hbm, low_hbm, slope_hbm = refs[25:28]
    up_full, down_full, out_full, bias_full = refs[28:32]
    cotangent, teacher, normed_out, low_out, slope_out = refs[32:37]
    sems, row_sems, chunk_sems = refs[37:]
    block_col = att[0].shape[1]
    width = own_tokens.shape[1]
    loads = Loads(packs, sems)
    loads.lay_out(deep, block_col, up_full, down_full, out_full, bias_full)
    row_loads = [
        pltpu.make_async_copy(cot_source, cotangent, row_sems.at[0]),
        pltpu.make_async_copy(teach_source, teacher, row_sems.at[1]),
    ]
    loads.start("out", ("up", 0))
    loads.wait("out")
    loads.start(("down", 0), ("up", 1))
    mixed = jnp.zeros(own_tokens.shape, F32)
    for k in range(4):
        mixed += dot(att[k][...], out_full[k * block_col : (k + 1) * block_col, :])
    resid = own_tokens[...].astype(F32) + (mixed + vectors[0:1, :])
    normed, inv_std = layer_norm(resid)
    hidden = normed * vectors[1:2, :] + vectors[2:3, :]
    normed_out[...] = normed
    std_out[...] = inv_std
    low_out[...] = hidden.astype(BF16)
    stores = [
        pltpu.make_async_copy(normed_out, normed_hbm, row_sems.at[2]),
        pltpu.make_async_copy(low_out, low_hbm, row_sems.at[3]),
    ]
    for copy in stores:
        copy.start()
    branch = jnp.zeros(own_tokens.shape, F32)
    for k in range(4):
        loads.wait(("up", k))
        loads.start(("down", k + 1), ("up", k + 2))
        if k == 2:
            for copy in row_loads:
                copy.start()
        place = slice(k * width, (k + 1) * width)
        preact = dot(low_out[...], up_full[:, place]) + bias_full[0:1, place].astype(F32)
        normal_cdf = 0.5 * (1.0 + lax.erf(preact * (1.0 / math.sqrt(2.0))))
        slope = normal_cdf + preact * jnp.exp(-0.5 * preact * preact) * (
            1.0 / math.sqrt(2.0 * math.pi)
        )
        act = (preact * normal_cdf).astype(BF16)
        act_out[:, place] = act
        slope_out[:, place] = slope.astype(BF16)
        copy = pltpu.make_async_copy(
            slope_out.at[:, place], slope_hbm.at[:, place], chunk_sems.at[k]
        )
        copy.start()
        stores.append(copy)
        loads.wait(("down", k))
        branch += dot(act, down_full[place, :])
    for copy in row_loads:
        copy.wait()
    gain = vectors[4:5, :]
    hidden = normed_out[...] * vectors[1:2, :] + vectors[2:3, :]
    resid = hidden + (branch + vectors[3:4, :])
    normed, inv_std = layer_norm(resid)
    full = normed * gain + vectors[5:6, :]
    write_swapped(output, slice(None), full, scalars)
    mismatch = full - read_swapped(teacher, scalars)
    masked = valid[...] * mismatch
    d_output = read_swapped(cotangent, scalars) + masked
    d_resid = layer_norm_back(d_output, gain, normed, inv_std)
    resid_out[...] = d_resid
    low = d_resid.astype(BF16)
    branch_out[...] = low
    sums[...] = jnp.zeros_like(sums)
    rows = (
        column_sum(d_output * normed),
        column_sum(d_output),
        column_sum(low.astype(F32)),
        column_sum(masked * mismatch),
    )
    for at, row in enumerate(rows):
        write_swapped(sums, slice(at, at + 1), row, scalars)
    for copy in stores:
        copy.wait()


def full_scratch(width, inner, block_col):
    return [
        pltpu.VMEM((width, inner), BF16),
        pltpu.VMEM((inner, width), BF16),
        pltpu.VMEM((4 * block_col, width), BF16),
    ]


def ffn_forward(scalars, attended, own_tokens, valid, vectors, cotangent, teacher, packs, deep):
    rows, width = own_tokens.shape
    inner = 4 * width
    full = (rows, width)
    S = jax.ShapeDtypeStruct
    return pl.pallas_call(
        lambda *refs: ffn_forward_kernel(deep, *refs),
        out_shape=[S((rows, 1), F32), S(full, BF16), S(full, F32), S(full, BF16)]
        + [S((8, width), F32), S((rows, inner), BF16)]
        + [pltpu.HBM(full, F32), pltpu.HBM(full, BF16), pltpu.HBM((rows, inner), BF16)],
        in_specs=[SMEM_SPEC] + [VMEM_SPEC] * 7 + [HBM_SPEC] * 12,
        out_specs=[VMEM_SPEC] * 6 + [HBM_SPEC] * 3,
        scratch_shapes=full_scratch(width, inner, attended[0].shape[1])
        + [pltpu.VMEM((PAD_ROWS, inner), BF16)]
        + [pltpu.VMEM(full, BF16)] * 2
        + [pltpu.VMEM(full, F32), pltpu.VMEM(full, BF16), pltpu.VMEM((rows, inner), BF16)]
        + [
            pltpu.SemaphoreType.DMA((56,)),
            pltpu.SemaphoreType.DMA((4,)),
            pltpu.SemaphoreType.DMA((4,)),
        ],
        compiler_params=pltpu.CompilerParams(vmem_limit_bytes=FFN_LIMIT),
        cost_estimate=pl.CostEstimate(
            flops=10 * rows * width * inner, bytes_accessed=24 << 20, transcendentals=0
        ),
        name="ffn_forward",
    )(
        scalars,
        *attended,
        own_tokens,
        valid,
        vectors,
        *(in_hbm(a) for a in (cotangent, teacher, *packs)),
    )


def ffn_back_kernel(deep, scalars, *refs):
    d_branch, std_ref, vectors, d_resid2, sums_mid, count = refs[:6]
    att = refs[6:10]
    normed_source, slope_source, hidden_source = refs[10:13]
    packs = refs[13:23]
    resid_hbm = refs[23]
    piece_hbm = refs[24:28]
    own_hbm, other_hbm = refs[28:30]
    up_full, down_full, out_full = refs[30:33]
    normed_ref, slope, hidden, flipped, own, other, sums, resid_out = refs[33:41]
    pieces = refs[41:45]
    sems, row_sem, chunk_sems, grad_sems, out_sems = refs[45:]
    width = d_branch.shape[1]
    half = width // 2
    block_col = pieces[0].shape[1]
    out_deep = block_col // 2
    loads = Loads(packs, sems)
    loads.lay_out(deep, block_col, up_full, down_full, out_full, None)
    normed_load = pltpu.make_async_copy(normed_source, normed_ref, row_sem.at[0])
    hidden_load = pltpu.make_async_copy(hidden_source, hidden, row_sem.at[1])
    slopes = []
    for k in range(4):
        place = slice(k * width, (k + 1) * width)
        slopes.append(
            pltpu.make_async_copy(slope_source.at[:, place], slope.at[:, place], chunk_sems.at[k])
        )
    stores = []

    def store(i, source, target, k, rows):
        copy = pltpu.make_async_copy(
            source.at[k, rows, :], target.at[k, rows, :], grad_sems.at[i, len(stores) // 2]
        )
        copy.start()
        stores.append(copy)

    loads.start(("down", 0))
    hidden_load.start()
    slopes[0].start()
    loads.start(("up", 0), ("down", 1))
    sums[...] = jnp.zeros_like(sums)
    hidden_load.wait()
    flipped[...] = hidden[...].astype(F32).T.astype(BF16)
    d_hidden = d_resid2[...]
    for k in range(4):
        loads.wait(("down", k))
        loads.start(("up", k + 1), ("down", k + 2))
        if k < 3:
            slopes[k + 1].start()
        else:
            normed_load.start()
            loads.start("out")
        place = slice(k * width, (k + 1) * width)
        d_act = dot(d_branch[...], down_full[place, :], NT)
        slopes[k].wait()
        d_pre = (d_act * slope[:, place].astype(F32)).astype(BF16)
        sums[4 + k : 5 + k, :] = column_sum(d_pre.astype(F32))
        loads.wait(("up", k))
        d_hidden += dot(d_pre, up_full[:, place], NT)
        grad = dot(flipped[...], d_pre).astype(BF16)
        own[k, 0:half, :] = grad[:half, :]
        other[k, 0:half, :] = grad[half:, :]
        store(0, other, other_hbm, k, slice(0, half))
        store(1, own, own_hbm, k, slice(0, half))
    normed_load.wait()
    normed = normed_ref[...]
    d_resid = layer_norm_back(d_hidden, vectors[1:2, :], normed, std_ref[...])
    resid_out[...] = d_resid
    out_copies = [pltpu.make_async_copy(resid_out, resid_hbm, out_sems.at[4])]
    out_copies[0].start()
    mixed = d_resid.astype(BF16)
    loads.wait("out")
    for k in range(4):
        rows = slice(k * block_col, (k + 1) * block_col)
        pieces[k][...] = dot(mixed, out_full[rows, :], NT).astype(BF16)
        copy = pltpu.make_async_copy(pieces[k], piece_hbm[k], out_sems.at[k])
        copy.start()
        out_copies.append(copy)
    for at, row in enumerate(
        (column_sum(d_hidden * normed), column_sum(d_hidden), column_sum(mixed.astype(F32)))
    ):
        write_swapped(sums, slice(at, at + 1), row, scalars)
    for k in range(4):
        out_grad = dot(att[k][...], mixed, TN)
        low = half + out_deep
        table = jnp.concatenate(
            [
                sums_mid[0:4, :],
                sums[0:3, :],
                count[0:1, :],
                sums[4 + k : 5 + k, :],
                jnp.zeros((own.shape[1] - low - 9, own.shape[2]), F32),
            ],
            0,
        ).astype(BF16)
        for i, target in enumerate((own, other)):
            part = out_grad[:, i * half : (i + 1) * half].astype(BF16)
            target[k, half:low, 0:half] = part[:out_deep, :]
            target[k, half:low, half:] = part[out_deep:, :]
            target[k, low:, :] = table
        store(0, other, other_hbm, k, slice(half, own.shape[1]))
        store(1, own, own_hbm, k, slice(half, own.shape[1]))
    for copy in stores + out_copies:
        copy.wait()


def ffn_back(
    scalars, d_branch, inv_std, vectors, d_resid2, sums_mid, count, attended, normed, slope, hidden, packs, deep
):
    rows, width = d_branch.shape
    inner = 4 * width
    full = (rows, width)
    block_col = attended[0].shape[1]
    grads = ((4, width // 2 + 128, width), BF16)
    S = jax.ShapeDtypeStruct
    return pl.pallas_call(
        lambda *refs: ffn_back_kernel(deep, *refs),
        out_shape=[pltpu.HBM(full, F32)]
        + [pltpu.HBM((rows, block_col), BF16)] * 4
        + [pltpu.HBM(*grads)] * 2,
        in_specs=[SMEM_SPEC] + [VMEM_SPEC] * 10 + [HBM_SPEC] * 13,
        out_specs=[HBM_SPEC] * 7,
        scratch_shapes=full_scratch(width, inner, block_col)
        + [pltpu.VMEM(full, F32), pltpu.VMEM((rows, inner), BF16), pltpu.VMEM(full, BF16)]
        + [pltpu.VMEM((width, rows), BF16)]
        + [pltpu.VMEM(*grads)] * 2
        + [pltpu.VMEM((8, width), F32), pltpu.VMEM(full, F32)]
        + [pltpu.VMEM((rows, block_col), BF16)] * 4
        + [
            pltpu.SemaphoreType.DMA((48,)),
            pltpu.SemaphoreType.DMA((2,)),
            pltpu.SemaphoreType.DMA((4,)),
            pltpu.SemaphoreType.DMA((2, 8)),
            pltpu.SemaphoreType.DMA((5,)),
        ],
        compiler_params=pltpu.CompilerParams(vmem_limit_bytes=FFN_LIMIT),
        cost_estimate=pl.CostEstimate(
            flops=10 * rows * width * inner, bytes_accessed=24 << 20, transcendentals=0
        ),
        name="ffn_back",
    )(
        scalars,
        d_branch,
        inv_std,
        vectors,
        d_resid2,
        sums_mid,
        count,
        *attended,
        *(in_hbm(a) for a in (normed, slope, hidden, *packs)),
    )


def whole_call(kernel, name, args, outs, scalars=None, cost=SMALL_COST):
    return pl.pallas_call(
        kernel,
        out_shape=[o if hasattr(o, "memory_space") else jax.ShapeDtypeStruct(*o) for o in outs],
        in_specs=([] if scalars is None else [SMEM_SPEC]) + [VMEM_SPEC] * len(args),
        out_specs=[VMEM_SPEC] * len(outs),
        compiler_params=pltpu.CompilerParams(vmem_limit_bytes=SMALL_LIMIT),
        cost_estimate=cost,
        name=name,
    )(*(() if scalars is None else (scalars,)), *args)


def fold_cores(own, came):
    _, rows, cols = own.shape

    def kernel(own_ref, came_ref, *outs):
        for k, out in enumerate(outs):
            out[...] = (own_ref[k].astype(F32) + came_ref[k].astype(F32)).astype(BF16)

    outs = [pltpu.HBM((rows, cols), BF16)] * 4
    return whole_call(kernel, "fold_cores", (own, came), outs)


def split_cores(own, came):
    _, rows, cols = own.shape
    half = rows // 2

    def kernel(own_ref, came_ref, send_x, send_y, keep_upper, keep_lower):
        def total(upper, k):
            at = slice(0, half) if upper else slice(half, rows)
            return (own_ref[k, at, :].astype(F32) + came_ref[k, at, :].astype(F32)).astype(BF16)

        for i, k in enumerate((1, 3)):
            send_x[i] = total(True, k)
        for i, k in enumerate((2, 3)):
            send_y[i] = total(False, k)
        for i, k in enumerate((0, 2)):
            keep_upper[i] = total(True, k)
        for i, k in enumerate((0, 1)):
            keep_lower[i] = total(False, k)

    return whole_call(kernel, "split_cores", (own, came), [((2, half, cols), BF16)] * 4)


def second_step(keep_upper, came_x, keep_lower, came_y):
    def kernel(upper, upper_came, lower, lower_came, send_y, send_x, kept):
        half = upper.shape[1]
        send_y[...] = (upper[1].astype(F32) + upper_came[1].astype(F32)).astype(BF16)
        send_x[...] = (lower[1].astype(F32) + lower_came[1].astype(F32)).astype(BF16)
        kept[:half, :] = upper[0].astype(F32) + upper_came[0].astype(F32)
        kept[half:, :] = lower[0].astype(F32) + lower_came[0].astype(F32)

    half, cols = keep_upper.shape[1:]
    return whole_call(
        kernel,
        "second_step",
        (keep_upper, came_x, keep_lower, came_y),
        [((half, cols), BF16)] * 2 + [((2 * half, cols), F32)],
    )


def add_halves(kept, upper, lower):
    def kernel(kept, upper, lower, out):
        half = upper.shape[0]
        out[:half, :] = (kept[:half, :] + upper[...].astype(F32)).astype(BF16)
        out[half:, :] = (kept[half:, :] + lower[...].astype(F32)).astype(BF16)

    outs = [pltpu.HBM(kept.shape, BF16)]
    return whole_call(kernel, "add_halves", (kept, upper, lower), outs)[0]


def fold_quarters(terms, scalars):
    rows, cols = terms[0].shape
    part = rows // 4
    count = len(terms)

    def kernel(scalars, *refs):
        for k in range(4):
            at = pl.ds(pl.multiple_of((scalars[2] ^ k) * part, 8), part)
            total = sum(term[at, :].astype(F32) for term in refs[:count])
            refs[count + k % 2][k // 2] = total.astype(BF16)

    return whole_call(kernel, "fold_quarters", terms, [((2, part, cols), BF16)] * 2, scalars)


def finish(dense, qkv, half, block_col, scalars):
    _, part, cols = dense[0].shape
    qkv_part = qkv[0].shape[1]
    deep = block_col // 2

    def kernel(scalars, *refs):
        up, out, query, key, value, loss = refs[4:10]
        vectors, query_bias, value_bias = refs[10:17], refs[17], refs[18]
        dense_all, qkv_all = refs[19:]
        for parts, target in ((refs[:2], dense_all), (refs[2:4], qkv_all)):
            for k in range(4):
                piece = parts[k % 2].at[k // 2]
                rows = piece.shape[0]
                at = pl.ds(pl.multiple_of((scalars[2] ^ k) * rows, 8), rows)
                target[at, :] = piece[...].astype(F32)
        up[...] = dense_all[:half, :]
        out[:deep, :] = dense_all[half : half + deep, :half]
        out[deep:, :] = dense_all[half : half + deep, half:]
        table = dense_all[half + deep : half + deep + 16, :]
        for row, target in zip((6, 4, 5, 8, 2, 0, 1), vectors):
            target[...] = table[row, :]
        error = jnp.sum(table[3:4, :], axis=1, keepdims=True)
        tokens = jnp.sum(table[7:8, :], axis=1, keepdims=True)
        loss[...] = error / (tokens * cols)
        for i, target in enumerate((query, key, value)):
            target[...] = qkv_all[i * block_col : (i + 1) * block_col, :]
        bias = qkv_all[3 * block_col : 3 * block_col + 8, :]
        query_bias[...] = bias[0, :block_col]
        value_bias[...] = bias[0, block_col:]

    S = jax.ShapeDtypeStruct
    return pl.pallas_call(
        kernel,
        out_shape=[S((half, cols), F32), S((block_col, half), F32)]
        + [S((block_col, half), F32)] * 3
        + [S((1, 1), F32)]
        + [S((cols,), F32)] * 7
        + [S((block_col,), F32)] * 2,
        in_specs=[SMEM_SPEC] + [VMEM_SPEC] * 4,
        out_specs=[VMEM_SPEC] * 15,
        scratch_shapes=[
            pltpu.VMEM((4 * part, cols), F32),
            pltpu.VMEM((4 * qkv_part, half), F32),
        ],
        compiler_params=pltpu.CompilerParams(vmem_limit_bytes=SMALL_LIMIT),
        cost_estimate=SMALL_COST,
        name="finish",
    )(scalars, *dense, *qkv)


def dot(left, right, dims=NN):
    return lax.dot_general(left, right, dims, preferred_element_type=F32)


def split3(value):
    high = value.astype(BF16)
    rest = value - high.astype(F32)
    middle = rest.astype(BF16)
    low = (rest - middle.astype(F32)).astype(BF16)
    return high.astype(F32), middle.astype(F32), low.astype(F32)


def key_range(code, span, span_rows, blocks):
    per = span_rows // BLK
    first_seg = code[span * per, 0] // 2
    last_seg = code[span * per + per - 1, BLK - 1] // 2
    low = jnp.int32(0)
    high = jnp.int32(0)
    for other in range(blocks):
        start = code[other, 0]
        low += (code[other, BLK - 1] // 2 < first_seg).astype(jnp.int32)
        high += ((start // 2 <= last_seg) & (start % 2 == 1)).astype(jnp.int32)
    below = jnp.maximum(jnp.minimum(high, span * per) - low, 0)
    above = jnp.maximum(high - (span + 1) * per, 0)
    return low, below, below + above


def key_block(step, low, below, after):
    return jnp.where(step < below, low + step, after + step - below)


def lane_index(rows):
    return lax.broadcasted_iota(jnp.int32, (rows, 128), 1)


def allowed_block(code_rows, block, offset, span_rows):
    row = lax.broadcasted_iota(jnp.int32, (span_rows, BLK), 0)
    col = lax.broadcasted_iota(jnp.int32, (span_rows, BLK), 1)
    return (code_rows[pl.ds(block, 1), :] % 2 == 1) | (row == col + offset)


def attention_forward_kernel(heads, scalars, code, *refs):
    code_rows = refs[0]
    token_parts = refs[1:6]
    weights = refs[6:8]
    pieces = refs[8:12]
    saved = refs[12:16]
    padded, max_scr, acc_scr, query_pad, key_pad, value_pad, out_pad, whole_sem, span_sem = refs[16:]
    span_rows, width = token_parts[0].shape
    cols = 64 * heads
    flip = scalars[1]
    per = span_rows // BLK
    blocks = query_pad.shape[1] // BLK
    lane = lane_index(span_rows)
    for i in range(3):
        src = slice(i * cols, (i + 1) * cols)
        padded[i * 256 : i * 256 + cols, : width // 2] = weights[0][src, :]
        padded[i * 256 : i * 256 + cols, width // 2 :] = weights[1][src, :]
        padded[i * 256 + cols : (i + 1) * 256, :] = jnp.zeros((256 - cols, width), BF16)
    marks_bias = weights[0][3 * cols : 3 * cols + 1, :].astype(F32)
    no_bias = jnp.zeros((1, 256 - cols), F32)
    biases = (
        jnp.concatenate([marks_bias[:, :cols], no_bias], 1),
        None,
        jnp.concatenate([marks_bias[:, cols : 2 * cols], no_bias], 1),
    )
    first = 0
    for tokens in token_parts:
        rows = slice(first, first + tokens.shape[0])
        marks = []
        for block in range(rows.start // BLK, rows.stop // BLK):
            place = (block // per ^ flip) * per + block % per
            marks.append(
                jnp.broadcast_to(code_rows[pl.ds(place, 1), :].astype(F32), (128, BLK)).T
            )
        first = rows.stop
        lane = lane_index(tokens.shape[0])
        value_ones = jnp.where((lane >= 64) & (lane < 67), 1.0, 0.0)
        marks = jnp.concatenate(marks, 0).astype(jnp.int32)
        same = lane - 64 == marks // 2
        ids = (lane >= 64) & (lane < 80)
        query_marks = jnp.where((ids & same) | (lane == 80), 1.0, 0.0)
        key_marks = jnp.where(
            (ids & ~same) | ((lane == 80) & (marks % 2 == 0)),
            MASKED,
            jnp.where((lane >= 81) & (lane < 84), -1.0, 0.0),
        )
        for i, (out, extra) in enumerate(
            ((query_pad, query_marks), (key_pad, key_marks), (value_pad, value_ones))
        ):
            projected = dot(tokens[...], padded[i * 256 : (i + 1) * 256, :], NT)
            if biases[i] is not None:
                projected += biases[i]
            if i == 0:
                projected = projected.astype(BF16).astype(F32) * 0.125
            out[0, rows, :] = jnp.where(lane < 64, projected[:, :128], extra).astype(BF16)
            out[1, rows, :] = jnp.where(
                lane < 64, pltpu.roll(projected[:, :128], 64, 1), extra
            ).astype(BF16)
            out[2, rows, :] = jnp.where(lane < 64, projected[:, 128:], extra).astype(BF16)
    lane = lane_index(span_rows)
    no_valid_lane = jnp.where(lane == 80, 0.0, 1.0).astype(BF16)
    whole_copies = [
        pltpu.make_async_copy(key_pad, saved[1], whole_sem.at[0]),
        pltpu.make_async_copy(value_pad, saved[2], whole_sem.at[1]),
    ]
    for copy in whole_copies:
        copy.start()

    def span_copies(at):
        rows = pl.ds(pl.multiple_of(at * span_rows, span_rows), span_rows)
        return [
            pltpu.make_async_copy(
                source.at[:, rows, :], saved[i].at[:, rows, :], span_sem.at[i // 3, at]
            )
            for source, i in ((query_pad, 0), (out_pad, 3))
        ]

    def query_step(span, _):
        at = span ^ flip
        rows = pl.ds(pl.multiple_of(at * span_rows, span_rows), span_rows)
        low, below, count = key_range(code, span, span_rows, blocks)

        def keys_of(block):
            place = (block // per ^ flip) * per + block % per
            return pl.ds(pl.multiple_of(place * BLK, BLK), BLK)

        def scores_of(h, keys, allowed=None):
            if allowed is None:
                return dot(query_pad[h, rows, :], key_pad[h, keys, :], NT)
            scores = dot(query_pad[h, rows, :] * no_valid_lane, key_pad[h, keys, :], NT)
            return jnp.where(allowed, scores, MASKED)

        def each_block(visit):
            for part in range(per):
                block = span * per + part
                visit(keys_of(block), allowed_block(code_rows, block, part * BLK, span_rows))

            def step_fn(step, _):
                visit(keys_of(key_block(step, low, below, (span + 1) * per)), None)
                return 0

            lax.fori_loop(0, count, step_fn, 0)

        acc_scr[...] = jnp.zeros_like(acc_scr)
        max_scr[...] = jnp.zeros_like(max_scr)

        def plain(keys, allowed):
            for h in range(heads):
                probs = jnp.exp(scores_of(h, keys, allowed)).astype(BF16)
                acc_scr[h] += dot(probs, value_pad[h, keys, :])

        each_block(plain)
        least, most = jnp.float32(1.0), jnp.float32(1.0)
        for h in range(heads):
            total = jnp.where(lane == 64, acc_scr[h], 1.0)
            good = (total > 1e-25) & (total < 1e30)
            least = jnp.minimum(least, jnp.min(jnp.where(good, 1.0, 0.0)))

        @pl.when(least < 0.5)
        def _():
            max_scr[...] = jnp.full_like(max_scr, MASKED)

            def find_max(keys, allowed):
                for h in range(heads):
                    scores = scores_of(h, keys, allowed)
                    max_scr[h] = jnp.maximum(
                        max_scr[h], jnp.maximum(scores[:, :128], scores[:, 128:])
                    )

            each_block(find_max)
            for h in range(heads):
                max_scr[h] = jnp.broadcast_to(
                    jnp.max(max_scr[h], axis=1, keepdims=True), (span_rows, 128)
                )
            acc_scr[...] = jnp.zeros_like(acc_scr)

            def shifted(keys, allowed):
                for h in range(heads):
                    row_max = max_scr[h]
                    scores = scores_of(h, keys, allowed)
                    probs = jnp.exp(scores - jnp.concatenate([row_max, row_max], 1))
                    acc_scr[h] += dot(probs.astype(BF16), value_pad[h, keys, :])

            each_block(shifted)

        outs = []
        for h in range(heads):
            acc = acc_scr[h]
            total = jnp.broadcast_to(acc[:, 64:65], acc.shape)
            out = acc / total
            out_pad[h, rows, :] = out
            outs.append(out)
            high, middle, rest = split3(max_scr[h] + jnp.log(total))
            extra = jnp.where(
                lane == 81,
                high,
                jnp.where(lane == 82, middle, jnp.where(lane == 83, rest, 0.0)),
            )
            query_pad[h, rows, :] = query_pad[h, rows, :] + extra.astype(BF16)
        pair = jnp.where(lane < 64, outs[0], pltpu.roll(outs[1], 64, 1)).astype(BF16)
        last = outs[2][:, :64].astype(BF16)
        for k, piece in enumerate(pieces):

            @pl.when(at == k)
            def _():
                piece[:, 0:128] = pair
                piece[:, 128:cols] = last

        for copy in span_copies(at):
            copy.start()
        return 0

    lax.fori_loop(0, len(pieces), query_step, 0)
    for copy in whole_copies:
        copy.wait()
    for at in range(len(pieces)):
        for copy in span_copies(at):
            copy.wait()


def attention_forward(scalars, code, token_shards, weights):
    rows, width = token_shards[0].shape
    length = code.shape[0] * BLK
    cols = (weights[0].shape[0] - PAD_ROWS) // 3
    heads = cols // 64
    S = jax.ShapeDtypeStruct
    flops = 2 * length * width * 3 * 256 + 3 * length * length * 128
    return pl.pallas_call(
        lambda *refs: attention_forward_kernel(heads, *refs),
        out_shape=[S((rows, cols), BF16)] * 4
        + [pltpu.HBM((heads, length, 128), BF16)] * 3
        + [pltpu.HBM((heads, length, 128), F32)],
        in_specs=[SMEM_SPEC] * 2 + [VMEM_SPEC] * 8,
        out_specs=[VMEM_SPEC] * 4 + [HBM_SPEC] * 4,
        scratch_shapes=[
            pltpu.VMEM((3 * 256, width), BF16),
            pltpu.VMEM((heads, rows, 128), F32),
            pltpu.VMEM((heads, rows, 128), F32),
        ]
        + [pltpu.VMEM((heads, length, 128), BF16)] * 3
        + [
            pltpu.VMEM((heads, length, 128), F32),
            pltpu.SemaphoreType.DMA((2,)),
            pltpu.SemaphoreType.DMA((2, 4)),
        ],
        compiler_params=pltpu.CompilerParams(vmem_limit_bytes=32 << 20),
        cost_estimate=pl.CostEstimate(
            flops=3 * flops, bytes_accessed=16 << 20, transcendentals=heads * length * 1024
        ),
        name="attention_forward",
    )(scalars, code, code, *token_shards, *weights)


def attention_backward_kernel(heads, scalars, code, *refs):
    code_rows = refs[0]
    span_rows = refs[1].shape[0]
    term_hbm, grad_hbm = refs[16:20], refs[20:22]
    grad_pad, query_sum, key_sum, value_sum, low_scr, grad_scr, bias_sum = refs[22:29]
    query_pad, key_pad, value_pad, out_pad = refs[29:33]
    shards_in = refs[33:37]
    weights = refs[37]
    grads = refs[38:42]
    terms, own_grad, other_grad, out_sems, in_sems = refs[42:]
    side = weights.shape[1] // 2
    last_half = span_rows // 2
    pairs = list(zip(refs[1:9], grads + refs[29:33]))
    pairs += list(zip(refs[9:12], shards_in[:3]))
    pairs += [
        (refs[12], shards_in[3].at[:last_half, :]),
        (refs[13], shards_in[3].at[last_half:, :]),
    ]
    pairs += [(refs[14], weights.at[:, :side]), (refs[15], weights.at[:, side:])]
    copies = [
        pltpu.make_async_copy(source, target, in_sems.at[i])
        for i, (source, target) in enumerate(pairs)
    ]
    for i in (7, 0, 1, 2, 3, 4, 5, 6):
        copies[i].start()
    key_sum[...] = jnp.zeros_like(key_sum)
    value_sum[...] = jnp.zeros_like(value_sum)
    query_sum[...] = jnp.zeros_like(query_sum)
    for i in (7, 0, 1, 2, 3):
        copies[i].wait()
    flip = scalars[1]
    per = span_rows // BLK
    blocks = query_pad.shape[1] // BLK
    lane = lane_index(span_rows)
    gap = jnp.zeros((span_rows, 64), BF16)
    for shard, grad in enumerate(grads):
        rows = slice(shard * span_rows, (shard + 1) * span_rows)
        pair = grad[:, 0:128].astype(F32)
        last = jnp.concatenate([grad[:, 128:192], gap], 1).astype(F32)
        for h, block in enumerate((pair, pltpu.roll(pair, 64, 1), last)):
            block = jnp.where(lane < 64, block, 0.0)
            delta = jnp.sum(block * out_pad[h, rows, :], axis=1, keepdims=True)
            high, middle, rest = split3(-delta)
            block = jnp.where(
                lane == 64,
                high,
                jnp.where(lane == 65, middle, jnp.where(lane == 66, rest, block)),
            )
            grad_pad[h, rows, :] = block.astype(BF16)
    for i in (4, 5, 6):
        copies[i].wait()
    for i in range(8, 15):
        copies[i].start()
    no_valid_lane = jnp.where(lane == 80, 0.0, 1.0).astype(BF16)

    def query_step(span, _):
        at = span ^ flip
        rows = pl.ds(pl.multiple_of(at * span_rows, span_rows), span_rows)
        low, below, count = key_range(code, span, span_rows, blocks)

        def visit(block, allowed):
            place = (block // per ^ flip) * per + block % per
            keys = pl.ds(pl.multiple_of(place * BLK, BLK), BLK)
            for h in range(heads):
                query, grad = query_pad[h, rows, :], grad_pad[h, rows, :]
                key, value = key_pad[h, keys, :], value_pad[h, keys, :]
                if allowed is None:
                    scores = dot(key, query, NT)
                else:
                    scores = jnp.where(allowed, dot(key, query * no_valid_lane, NT), MASKED)
                probs = jnp.exp(scores)
                d_scores = (probs * dot(value, grad, NT)).astype(BF16)
                value_sum[h, keys, :] += dot(probs.astype(BF16), grad)
                key_sum[h, keys, :] += dot(d_scores, query)
                query_sum[h, rows, :] += dot(d_scores, key, TN)

        for part in range(per):
            block = span * per + part
            key_at = lax.broadcasted_iota(jnp.int32, (BLK, span_rows), 0)
            query_at = lax.broadcasted_iota(jnp.int32, (BLK, span_rows), 1)
            marks = jnp.broadcast_to(
                code_rows[pl.ds(block, 1), :].astype(F32), (128, BLK)
            ).T.astype(jnp.int32)
            valid = jnp.concatenate([marks] * (span_rows // 128), 1) % 2 == 1
            visit(block, valid | (query_at == key_at + part * BLK))

        def step_fn(step, _):
            visit(key_block(step, low, below, (span + 1) * per), None)
            return 0

        lax.fori_loop(0, count, step_fn, 0)
        return 0

    lax.fori_loop(0, len(grads), query_step, 0)
    for i in range(8, 15):
        copies[i].wait()
    bias_sum[...] = jnp.zeros_like(bias_sum)
    stores = []
    for shard in range(len(grads)):
        rows = slice(shard * span_rows, (shard + 1) * span_rows)
        parts = [query_sum[h, rows, :] * 0.125 for h in range(heads)]
        parts += [sums[h, rows, :] for sums in (key_sum, value_sum) for h in range(heads)]
        for at in range(0, len(parts), 2):
            if at + 1 < len(parts):
                value = jnp.where(lane < 64, parts[at], pltpu.roll(parts[at + 1], 64, 1))
            else:
                value = parts[at][:, :64]
            low = value.astype(BF16)
            cols = slice(at * 64, at * 64 + low.shape[1])
            low_scr[:, cols] = low
            bias_sum[0:1, cols] += column_sum(low.astype(F32))
        low = low_scr[...]
        depth = low.shape[1]
        term = dot(low, weights[:depth, :]).astype(BF16)
        terms[shard] = term
        copy = pltpu.make_async_copy(
            terms.at[shard], term_hbm[shard], out_sems.at[shard]
        )
        copy.start()
        stores.append(copy)
        part = dot(low, shards_in[shard][...], TN)
        if shard == 0:
            grad_scr[...] = part
        elif shard < 3:
            grad_scr[...] += part
        else:
            total = (grad_scr[...] + part).astype(BF16)
            half = total.shape[1] // 2
            own_grad[:depth, :] = total[:, :half]
            other_grad[:depth, :] = total[:, half:]
    cols = heads * 64
    bias = jnp.concatenate([bias_sum[:, 0:cols], bias_sum[:, 2 * cols :]], 1).astype(BF16)
    bias = jnp.concatenate([bias] * ((own_grad.shape[0] - depth) // bias.shape[0]), 0)
    own_grad[depth:, :] = bias
    other_grad[depth:, :] = bias
    for i, source in enumerate((own_grad, other_grad)):
        copy = pltpu.make_async_copy(source, grad_hbm[i], out_sems.at[4 + i])
        copy.start()
        stores.append(copy)
    for copy in stores:
        copy.wait()


def attention_backward(scalars, code, grads, saved, token_shards, weights):
    length = code.shape[0] * BLK
    heads = saved[0].shape[0]
    rows, width = token_shards[0].shape
    cols = 3 * heads * 64
    S = jax.ShapeDtypeStruct
    return pl.pallas_call(
        lambda *refs: attention_backward_kernel(heads, *refs),
        out_shape=[
            *[pltpu.HBM((rows, width), BF16)] * 4,
            *[pltpu.HBM((cols + GRAD_PAD, width // 2), BF16)] * 2,
        ],
        in_specs=[SMEM_SPEC] * 2 + [VMEM_SPEC] + [HBM_SPEC] * 15,
        out_specs=[HBM_SPEC] * 6,
        scratch_shapes=[
            pltpu.VMEM((heads, length, 128), BF16),
            pltpu.VMEM((heads, length, 128), F32),
            pltpu.VMEM((heads, length, 128), F32),
            pltpu.VMEM((heads, length, 128), F32),
            pltpu.VMEM((rows, cols), BF16),
            pltpu.VMEM((cols, width), F32),
            pltpu.VMEM((16, cols), F32),
        ]
        + [pltpu.VMEM(a.shape, a.dtype) for a in saved]
        + [pltpu.VMEM((rows, width), BF16)] * 4
        + [pltpu.VMEM((weights[0].shape[0], width), BF16)]
        + [pltpu.VMEM(a.shape, a.dtype) for a in grads]
        + [
            pltpu.VMEM((4, rows, width), BF16),
            pltpu.VMEM((cols + GRAD_PAD, width // 2), BF16),
            pltpu.VMEM((cols + GRAD_PAD, width // 2), BF16),
            pltpu.SemaphoreType.DMA((6,)),
            pltpu.SemaphoreType.DMA((15,)),
        ],
        compiler_params=pltpu.CompilerParams(vmem_limit_bytes=46 << 20),
        cost_estimate=pl.CostEstimate(
            flops=heads * length * length * 1500, bytes_accessed=8 << 20, transcendentals=0
        ),
        name="attention_backward",
    )(
        scalars,
        code,
        code,
        *(in_hbm(a) for a in (*grads, *saved, *token_shards, *weights)),
    )


CHIP = [[(c, c ^ k) for c in range(4)] for k in range(4)]
PLANE = [[(p, p ^ k) for p in range(4)] for k in range(4)]
CORE = [(0, 1), (1, 0)]


def to_chip(value, k):
    return lax.ppermute(value, "gz", CHIP[k])


def to_core(value):
    return lax.ppermute(value, "gy", CORE)


def to_plane(value, k):
    return lax.ppermute(value, "gx", PLANE[k])


def after(value, *others):
    return lax.optimization_barrier((value,) + others)[0]


def swap_halves(flip, value):
    half = value.shape[-1] // 2
    swapped = jnp.concatenate([value[..., half:], value[..., :half]], -1)
    return jnp.where(flip, swapped, value)


def add_low(left, right):
    return (left.astype(F32) + right.astype(F32)).astype(BF16)


def sum_planes(dense, qkv, waits):
    if lax.axis_size("gx") != 4:
        dense, other = jnp.stack(dense), jnp.stack(qkv(dense[0]))
        total = lax.psum((dense, other), "gx")
        return [(t[0], t[1]) for t in total], waits
    near = dense[0].astype(F32) + to_plane(dense[1], 1).astype(F32)
    step = near[1].astype(BF16)
    keep, send = qkv(step)
    total = (near[0] + to_plane(step, 2).astype(F32)).astype(BF16)
    near = keep.astype(F32) + to_plane(send, 1).astype(F32)
    step = after(near[1].astype(BF16), total)
    pair = jnp.stack([total, to_plane(total, 2)])
    other = (near[0] + to_plane(step, 2).astype(F32)).astype(BF16)
    other = after(other, pair)
    back = to_plane(pair, 1)
    other_pair = jnp.stack([other, to_plane(other, 2)])
    other_back = to_plane(other_pair, 1)
    *waits, back = lax.optimization_barrier((*waits, back))
    return [(pair, back), (other_pair, other_back)], waits


def shards(
    tokens,
    segment_ids,
    valid_mask,
    cotangent,
    teacher,
    w_query,
    b_query,
    w_key,
    w_value,
    b_value,
    w_out,
    b_out,
    norm1_gain,
    norm1_bias,
    w_up,
    b_up,
    w_down,
    b_down,
    norm2_gain,
    norm2_bias,
):
    row_count, width = tokens.shape
    half = width // 2
    core = lax.axis_index("gy")
    chip = lax.axis_index("gz")
    flip = core == 1
    block_col = w_query.shape[1]
    hidden_col = w_up.shape[1]
    plane = lax.axis_index("gx") if lax.axis_size("gx") == 4 else jnp.int32(0)
    scalars = jnp.stack([core, chip, plane, chip]).astype(jnp.int32)

    own_tokens = swap_halves(flip, tokens)
    along_x, along_y = to_chip(own_tokens, 1), to_chip(own_tokens, 2)
    code = (segment_ids * 2 + valid_mask).reshape(-1, BLK)
    bias_row = jnp.concatenate([b_query, b_value])[None, :]
    qkv_own = jnp.concatenate(
        [w_query.T, w_key.T, w_value.T, jnp.broadcast_to(bias_row, (PAD_ROWS, half))], 0
    )
    vectors = jnp.stack([b_out, norm1_gain, norm1_bias, b_down, norm2_gain, norm2_bias] + [b_out] * 2)
    vectors = swap_halves(flip, vectors.astype(F32))
    own_valid = lax.dynamic_slice_in_dim(valid_mask, chip * row_count, row_count, 1).astype(F32)
    count = jnp.concatenate([own_valid, jnp.zeros((1, width - row_count), F32)], 1)
    count = jnp.broadcast_to(count, (8, width))
    own_valid = own_valid.T
    packed = jnp.concatenate(
        [
            jnp.concatenate([w_down[: hidden_col // 2], w_down[hidden_col // 2 :]], 1),
            w_up,
            jnp.concatenate([w_out[: block_col // 2], w_out[block_col // 2 :]], 1),
            jnp.broadcast_to(b_up[None, :], (PAD_ROWS, hidden_col)),
        ],
        0,
    )

    code, qkv_own, scalars, packed, vectors, own_valid, count, *_ = lax.optimization_barrier(
        (code, qkv_own, scalars, packed, vectors, own_valid, count, own_tokens)
    )
    qkv = (qkv_own, to_core(qkv_own))
    along_x, along_y, *qkv = lax.optimization_barrier((along_x, along_y, *qkv))
    middle = row_count // 2
    far = (to_chip(along_x[:middle], 2), to_chip(along_y[middle:], 1))
    token_shards = (own_tokens, along_x, along_y, *far)
    packed = after(packed, *far)
    pack_x, pack_y = to_chip(packed, 1), to_chip(packed, 2)

    scalars = after(scalars, packed)
    results = attention_forward(scalars, code, token_shards, qkv)
    saved = results[4:]
    attended = [results[0]] + [to_chip(results[k], k) for k in (1, 2, 3)]

    deep = hidden_col // 2
    pack_x, pack_y = lax.optimization_barrier((pack_x, pack_y, results[0]))[:2]
    far = (to_chip(pack_x[:, :half], 2), to_chip(pack_y[:, half:], 1))
    packs = (packed, pack_x, pack_y, *far)
    packs += (to_core(packed), *(to_core(after(v, *attended[1:])) for v in packs[1:]))

    inv_std, output, d_resid2, d_branch, sums_mid, act, normed, hidden_low, slope = ffn_forward(
        scalars, attended, own_tokens, own_valid, vectors, cotangent, teacher, packs, deep
    )
    pieces = (4, hidden_col, half)
    d_down_other = jnp.einsum("lf,lm->fm", act, d_branch[:, half:], preferred_element_type=F32)
    d_down_came = to_core(d_down_other.astype(BF16).reshape(pieces))
    d_down = jnp.einsum("lf,lm->fm", act, d_branch[:, :half], preferred_element_type=F32)
    down_x, down_y, down_upper, down_lower = split_cores(
        d_down.astype(BF16).reshape(pieces), d_down_came
    )
    d_branch = after(d_branch, down_upper)
    down_x, down_y = to_chip(down_x, 1), to_chip(down_y, 2)
    d_resid1, *back, own_grads, other_grads = ffn_back(
        scalars,
        d_branch,
        inv_std,
        vectors,
        d_resid2,
        sums_mid,
        count,
        attended,
        normed,
        slope,
        hidden_low,
        packs,
        deep,
    )
    d_pieces = [back[0]] + [to_chip(back[k], k) for k in (1, 2, 3)]

    down_y, down_x, down_kept = second_step(down_upper, down_x, down_lower, down_y)
    d_dense = fold_cores(own_grads, to_core(after(other_grads, down_y)))
    down_total = add_halves(down_kept, to_chip(down_y, 2), to_chip(down_x, 1))
    grad_down = lax.psum(down_total, "gx")
    d_pieces[0] = after(d_pieces[0], d_dense[0], down_total)
    d_dense = [d_dense[0]] + [to_chip(d_dense[k], k) for k in (1, 2, 3)]

    *terms, d_own, d_other = attention_backward(
        scalars, code, d_pieces, saved, token_shards, qkv
    )
    d_dense[0] = after(d_dense[0], grad_down, terms[0])
    quarters = fold_quarters(d_dense, scalars)
    d_own, d_other, *terms, _, _ = lax.optimization_barrier((d_own, d_other, *terms, *quarters))
    d_w = (d_own, to_core(d_other))
    terms = [terms[0]] + [to_chip(terms[k], k) for k in (1, 2, 3)]
    (dense_grad, qkv_grad), came = sum_planes(
        quarters, lambda first: fold_quarters(d_w, scalars), terms[1:]
    )
    d_tokens = d_resid1 + sum(t.astype(F32) for t in (terms[0], *came))
    grad_up, grad_out, grad_query, grad_key, grad_value, loss, *vectors = finish(
        dense_grad, qkv_grad, half, block_col, scalars
    )
    b_out_grad, gain1_grad, shift1_grad, b_up_grad, b_down_grad, gain2_grad, shift2_grad = vectors[:7]

    return (
        output,
        loss[0, 0],
        swap_halves(flip, d_tokens.astype(BF16)),
        grad_query.T,
        vectors[7],
        grad_key.T,
        grad_value.T,
        vectors[8],
        grad_out,
        b_out_grad,
        gain1_grad,
        shift1_grad,
        grad_up,
        b_up_grad,
        grad_down.astype(F32),
        b_down_grad,
        gain2_grad,
        shift2_grad,
    )


def solution(mesh):
    placed = (
        P(("gx", "gy", "gz"), None),
        P(("gx", "gy"), None),
        P(("gx", "gy"), None),
        P(("gx", "gy", "gz"), None),
        P(("gx", "gy", "gz"), None),
        P("gy", "gz"),
        P("gz"),
        P("gy", "gz"),
        P("gy", "gz"),
        P("gz"),
        P("gz", "gy"),
        P(),
        P(),
        P(),
        P("gy", "gz"),
        P("gz"),
        P("gz", "gy"),
        P(),
        P(),
        P(),
    )
    return jax.shard_map(
        shards,
        mesh=mesh,
        in_specs=placed,
        out_specs=(
            P(("gx", "gy", "gz"), None),
            P(),
            P(("gx", "gy", "gz"), None),
            P("gy", "gz"),
            P("gz"),
            P("gy", "gz"),
            P("gy", "gz"),
            P("gz"),
            P("gz", "gy"),
            P(),
            P(),
            P(),
            P("gy", "gz"),
            P("gz"),
            P("gz", "gy"),
            P(),
            P(),
            P(),
        ),
        check_vma=False,
    )
```

```python
import math

import jax
import jax.numpy as jnp
from jax import lax
from jax.experimental import pallas as pl
from jax.experimental.pallas import tpu as pltpu
from jax.sharding import PartitionSpec as P

EPSILON = 1e-05
MASKED = -1e30
PAD_ROWS = 16
GRAD_PAD = 64
BLK = 256
F32 = jnp.float32
BF16 = jnp.bfloat16
NT = (((1,), (1,)), ((), ()))
NN = (((1,), (0,)), ((), ()))
TN = (((0,), (0,)), ((), ()))


VMEM_SPEC = pl.BlockSpec(memory_space=pltpu.VMEM)
SMEM_SPEC = pl.BlockSpec(memory_space=pltpu.SMEM)
HBM_SPEC = pl.BlockSpec(memory_space=pltpu.HBM)
VMEM_LIMIT = 24 << 20
SMALL_LIMIT = 20 << 20
FFN_LIMIT = 40 << 20
SMALL_COST = pl.CostEstimate(flops=1 << 16, bytes_accessed=1 << 12, transcendentals=0)


def in_hbm(array):
    return pltpu.with_memory_space_constraint(array, pltpu.HBM)


class Loads:
    def __init__(self, packs, sems):
        self.packs, self.sems, self.used, self.groups = packs, sems, 0, {}

    def add(self, group, source, target):
        copy = pltpu.make_async_copy(source, target, self.sems.at[self.used])
        self.used += 1
        self.groups.setdefault(group, []).append(copy)

    def start(self, *groups):
        for group in groups:
            for copy in self.groups.get(group, ()):
                copy.start()

    def wait(self, *groups):
        for group in groups:
            for copy in self.groups.get(group, ()):
                copy.wait()

    def blocks(self, core):
        packs = self.packs[5 * core : 5 * core + 5]
        half = packs[4].shape[1]
        blocks = [(k, i, packs[k], i * half) for k in range(3) for i in range(2)]
        return half, blocks + [(3, 0, packs[3], 0), (3, 1, packs[4], 0)]

    def lay_out(self, deep, block_col, up_full, down_full, out_full, bias_full):
        for core in range(2):
            half, blocks = self.blocks(core)
            top = deep + half
            out_deep = block_col // 2
            side = slice(core * half, (core + 1) * half)
            for k, i, pack, col in blocks:
                cols = slice(col, col + half)
                hidden = slice((2 * k + i) * half, (2 * k + i + 1) * half)
                self.add(("up", k), pack.at[deep:top, cols], up_full.at[side, hidden])
                self.add(("down", k), pack.at[0:deep, cols], down_full.at[hidden, side])
                first = k * block_col + i * out_deep
                self.add(
                    "out",
                    pack.at[top : top + out_deep, cols],
                    out_full.at[first : first + out_deep, side],
                )
                if core == 0 and bias_full is not None:
                    low = top + out_deep
                    self.add("out", pack.at[low : low + PAD_ROWS, cols], bias_full.at[:, hidden])


def half_start(scalars, second, half):
    flip = scalars[0]
    return pl.multiple_of(jnp.where(second, 1 - flip, flip) * half, 128)


def read_swapped(ref, scalars):
    half = ref.shape[-1] // 2
    return jnp.concatenate(
        [
            ref[:, pl.ds(half_start(scalars, False, half), half)].astype(F32),
            ref[:, pl.ds(half_start(scalars, True, half), half)].astype(F32),
        ],
        1,
    )


def write_swapped(ref, rows, value, scalars):
    half = ref.shape[-1] // 2
    ref[rows, pl.ds(half_start(scalars, False, half), half)] = value[:, :half].astype(ref.dtype)
    ref[rows, pl.ds(half_start(scalars, True, half), half)] = value[:, half:].astype(ref.dtype)


def column_sum(value):
    return jnp.sum(value, 0, keepdims=True)


def layer_norm(resid):
    average = jnp.mean(resid, -1, keepdims=True)
    centered = resid - average
    inv_std = lax.rsqrt(jnp.mean(centered * centered, -1, keepdims=True) + EPSILON)
    return centered * inv_std, inv_std


def layer_norm_back(upstream, gain, normed, inv_std):
    scaled = upstream * gain
    return inv_std * (
        scaled
        - jnp.mean(scaled, -1, keepdims=True)
        - normed * jnp.mean(scaled * normed, -1, keepdims=True)
    )


def unpack_heads(packed, target):
    rows = target.shape[0]
    middle = rows // 2
    last = packed[rows:, :].astype(F32)
    target[:, 0:128] = packed[:rows, :]
    target[:middle, 128:] = last[:, :64].astype(BF16)
    target[middle:, 128:] = pltpu.roll(last, 64, 1)[:, :64].astype(BF16)


def ffn_forward_kernel(deep, scalars, *refs):
    att = refs[:4]
    own_tokens, valid, vectors = refs[4:7]
    cot_source, teach_source = refs[7:9]
    packs = refs[9:19]
    std_out, output, resid_out, branch_out, sums, act_out = refs[19:25]
    normed_hbm, low_hbm, slope_hbm = refs[25:28]
    up_full, down_full, out_full, bias_full = refs[28:32]
    cotangent, teacher, normed_out, low_out, slope_out, heads = refs[32:38]
    sems, row_sems, chunk_sems = refs[38:]
    width = own_tokens.shape[1]
    block_col = width // 4
    loads = Loads(packs, sems)
    loads.lay_out(deep, block_col, up_full, down_full, out_full, bias_full)
    row_loads = [
        pltpu.make_async_copy(cot_source, cotangent, row_sems.at[0]),
        pltpu.make_async_copy(teach_source, teacher, row_sems.at[1]),
    ]
    loads.start("out", ("up", 0))
    for k in range(4):
        unpack_heads(att[k], heads.at[k])
    loads.wait("out")
    loads.start(("down", 0), ("up", 1))
    mixed = jnp.zeros(own_tokens.shape, F32)
    for k in range(4):
        mixed += dot(heads[k], out_full[k * block_col : (k + 1) * block_col, :])
    resid = own_tokens[...].astype(F32) + (mixed + vectors[0:1, :])
    normed, inv_std = layer_norm(resid)
    hidden = normed * vectors[1:2, :] + vectors[2:3, :]
    normed_out[...] = normed
    std_out[...] = inv_std
    low_out[...] = hidden.astype(BF16)
    stores = [
        pltpu.make_async_copy(normed_out, normed_hbm, row_sems.at[2]),
        pltpu.make_async_copy(low_out, low_hbm, row_sems.at[3]),
    ]
    for copy in stores:
        copy.start()
    branch = jnp.zeros(own_tokens.shape, F32)
    for k in range(4):
        loads.wait(("up", k))
        loads.start(("down", k + 1), ("up", k + 2))
        if k == 2:
            for copy in row_loads:
                copy.start()
        place = slice(k * width, (k + 1) * width)
        preact = dot(low_out[...], up_full[:, place]) + bias_full[0:1, place].astype(F32)
        normal_cdf = 0.5 * (1.0 + lax.erf(preact * (1.0 / math.sqrt(2.0))))
        slope = normal_cdf + preact * jnp.exp(-0.5 * preact * preact) * (
            1.0 / math.sqrt(2.0 * math.pi)
        )
        act = (preact * normal_cdf).astype(BF16)
        act_out[:, place] = act
        slope_out[:, place] = slope.astype(BF16)
        copy = pltpu.make_async_copy(
            slope_out.at[:, place], slope_hbm.at[:, place], chunk_sems.at[k]
        )
        copy.start()
        stores.append(copy)
        loads.wait(("down", k))
        branch += dot(act, down_full[place, :])
    for copy in row_loads:
        copy.wait()
    gain = vectors[4:5, :]
    hidden = normed_out[...] * vectors[1:2, :] + vectors[2:3, :]
    resid = hidden + (branch + vectors[3:4, :])
    normed, inv_std = layer_norm(resid)
    full = normed * gain + vectors[5:6, :]
    write_swapped(output, slice(None), full, scalars)
    mismatch = full - read_swapped(teacher, scalars)
    masked = valid[...] * mismatch
    d_output = read_swapped(cotangent, scalars) + masked
    d_resid = layer_norm_back(d_output, gain, normed, inv_std)
    resid_out[...] = d_resid
    low = d_resid.astype(BF16)
    branch_out[...] = low
    sums[...] = jnp.zeros_like(sums)
    rows = (
        column_sum(d_output * normed),
        column_sum(d_output),
        column_sum(low.astype(F32)),
        column_sum(masked * mismatch),
    )
    for at, row in enumerate(rows):
        write_swapped(sums, slice(at, at + 1), row, scalars)
    for copy in stores:
        copy.wait()


def full_scratch(width, inner, block_col):
    return [
        pltpu.VMEM((width, inner), BF16),
        pltpu.VMEM((inner, width), BF16),
        pltpu.VMEM((4 * block_col, width), BF16),
    ]


def ffn_forward(scalars, attended, own_tokens, valid, vectors, cotangent, teacher, packs, deep):
    rows, width = own_tokens.shape
    inner = 4 * width
    full = (rows, width)
    S = jax.ShapeDtypeStruct
    return pl.pallas_call(
        lambda *refs: ffn_forward_kernel(deep, *refs),
        out_shape=[S((rows, 1), F32), S(full, BF16), S(full, F32), S(full, BF16)]
        + [S((8, width), F32), S((rows, inner), BF16)]
        + [pltpu.HBM(full, F32), pltpu.HBM(full, BF16), pltpu.HBM((rows, inner), BF16)],
        in_specs=[SMEM_SPEC] + [VMEM_SPEC] * 7 + [HBM_SPEC] * 12,
        out_specs=[VMEM_SPEC] * 6 + [HBM_SPEC] * 3,
        scratch_shapes=full_scratch(width, inner, width // 4)
        + [pltpu.VMEM((PAD_ROWS, inner), BF16)]
        + [pltpu.VMEM(full, BF16)] * 2
        + [pltpu.VMEM(full, F32), pltpu.VMEM(full, BF16), pltpu.VMEM((rows, inner), BF16)]
        + [pltpu.VMEM((4, rows, width // 4), BF16)]
        + [
            pltpu.SemaphoreType.DMA((56,)),
            pltpu.SemaphoreType.DMA((4,)),
            pltpu.SemaphoreType.DMA((4,)),
        ],
        compiler_params=pltpu.CompilerParams(vmem_limit_bytes=FFN_LIMIT),
        cost_estimate=pl.CostEstimate(
            flops=10 * rows * width * inner, bytes_accessed=24 << 20, transcendentals=0
        ),
        name="ffn_forward",
    )(
        scalars,
        *attended,
        own_tokens,
        valid,
        vectors,
        *(in_hbm(a) for a in (cotangent, teacher, *packs)),
    )


def ffn_back_kernel(deep, scalars, *refs):
    d_branch, std_ref, vectors, d_resid2, sums_mid, count = refs[:6]
    att = refs[6:10]
    normed_source, slope_source, hidden_source = refs[10:13]
    packs = refs[13:23]
    resid_hbm = refs[23]
    piece_hbm = refs[24:28]
    own_hbm, other_hbm = refs[28:30]
    up_full, down_full, out_full = refs[30:33]
    normed_ref, slope, hidden, flipped, own, other, sums, resid_out = refs[33:41]
    pieces = refs[41:45]
    heads = refs[45]
    sems, row_sem, chunk_sems, grad_sems, out_sems = refs[46:]
    rows_here, width = d_branch.shape
    half = width // 2
    block_col = width // 4
    out_deep = block_col // 2
    loads = Loads(packs, sems)
    loads.lay_out(deep, block_col, up_full, down_full, out_full, None)
    normed_load = pltpu.make_async_copy(normed_source, normed_ref, row_sem.at[0])
    hidden_load = pltpu.make_async_copy(hidden_source, hidden, row_sem.at[1])
    slopes = []
    for k in range(4):
        place = slice(k * width, (k + 1) * width)
        slopes.append(
            pltpu.make_async_copy(slope_source.at[:, place], slope.at[:, place], chunk_sems.at[k])
        )
    stores = []

    def store(i, source, target, k, rows):
        copy = pltpu.make_async_copy(
            source.at[k, rows, :], target.at[k, rows, :], grad_sems.at[i, len(stores) // 2]
        )
        copy.start()
        stores.append(copy)

    loads.start(("down", 0))
    hidden_load.start()
    slopes[0].start()
    loads.start(("up", 0), ("down", 1))
    sums[...] = jnp.zeros_like(sums)
    for k in range(4):
        unpack_heads(att[k], heads.at[k])
    hidden_load.wait()
    flipped[...] = hidden[...].astype(F32).T.astype(BF16)
    d_hidden = d_resid2[...]
    for k in range(4):
        loads.wait(("down", k))
        loads.start(("up", k + 1), ("down", k + 2))
        if k < 3:
            slopes[k + 1].start()
        else:
            normed_load.start()
            loads.start("out")
        place = slice(k * width, (k + 1) * width)
        d_act = dot(d_branch[...], down_full[place, :], NT)
        slopes[k].wait()
        d_pre = (d_act * slope[:, place].astype(F32)).astype(BF16)
        sums[4 + k : 5 + k, :] = column_sum(d_pre.astype(F32))
        loads.wait(("up", k))
        d_hidden += dot(d_pre, up_full[:, place], NT)
        grad = dot(flipped[...], d_pre).astype(BF16)
        own[k, 0:half, :] = grad[:half, :]
        other[k, 0:half, :] = grad[half:, :]
        store(0, other, other_hbm, k, slice(0, half))
        store(1, own, own_hbm, k, slice(0, half))
    normed_load.wait()
    normed = normed_ref[...]
    d_resid = layer_norm_back(d_hidden, vectors[1:2, :], normed, std_ref[...])
    resid_out[...] = d_resid
    out_copies = [pltpu.make_async_copy(resid_out, resid_hbm, out_sems.at[4])]
    out_copies[0].start()
    mixed = d_resid.astype(BF16)
    loads.wait("out")
    for k in range(4):
        rows = slice(k * block_col, (k + 1) * block_col)
        piece = dot(mixed, out_full[rows, :], NT).astype(BF16)
        middle = rows_here // 2
        pieces[k][:rows_here, :] = piece[:, :128]
        pieces[k][rows_here:, :] = jnp.concatenate(
            [piece[:middle, 128:], piece[middle:, 128:]], 1
        )
        copy = pltpu.make_async_copy(pieces[k], piece_hbm[k], out_sems.at[k])
        copy.start()
        out_copies.append(copy)
    for at, row in enumerate(
        (column_sum(d_hidden * normed), column_sum(d_hidden), column_sum(mixed.astype(F32)))
    ):
        write_swapped(sums, slice(at, at + 1), row, scalars)
    for k in range(4):
        out_grad = dot(heads[k], mixed, TN)
        low = half + out_deep
        table = jnp.concatenate(
            [
                sums_mid[0:4, :],
                sums[0:3, :],
                count[0:1, :],
                sums[4 + k : 5 + k, :],
                jnp.zeros((own.shape[1] - low - 9, own.shape[2]), F32),
            ],
            0,
        ).astype(BF16)
        for i, target in enumerate((own, other)):
            part = out_grad[:, i * half : (i + 1) * half].astype(BF16)
            target[k, half:low, 0:half] = part[:out_deep, :]
            target[k, half:low, half:] = part[out_deep:, :]
            target[k, low:, :] = table
        store(0, other, other_hbm, k, slice(half, own.shape[1]))
        store(1, own, own_hbm, k, slice(half, own.shape[1]))
    for copy in stores + out_copies:
        copy.wait()


def ffn_back(
    scalars, d_branch, inv_std, vectors, d_resid2, sums_mid, count, attended, normed, slope, hidden, packs, deep
):
    rows, width = d_branch.shape
    inner = 4 * width
    full = (rows, width)
    block_col = width // 4
    grads = ((4, width // 2 + 128, width), BF16)
    S = jax.ShapeDtypeStruct
    return pl.pallas_call(
        lambda *refs: ffn_back_kernel(deep, *refs),
        out_shape=[pltpu.HBM(full, F32)]
        + [pltpu.HBM(attended[0].shape, BF16)] * 4
        + [pltpu.HBM(*grads)] * 2,
        in_specs=[SMEM_SPEC] + [VMEM_SPEC] * 10 + [HBM_SPEC] * 13,
        out_specs=[HBM_SPEC] * 7,
        scratch_shapes=full_scratch(width, inner, block_col)
        + [pltpu.VMEM(full, F32), pltpu.VMEM((rows, inner), BF16), pltpu.VMEM(full, BF16)]
        + [pltpu.VMEM((width, rows), BF16)]
        + [pltpu.VMEM(*grads)] * 2
        + [pltpu.VMEM((8, width), F32), pltpu.VMEM(full, F32)]
        + [pltpu.VMEM(attended[0].shape, BF16)] * 4
        + [pltpu.VMEM((4, rows, block_col), BF16)]
        + [
            pltpu.SemaphoreType.DMA((48,)),
            pltpu.SemaphoreType.DMA((2,)),
            pltpu.SemaphoreType.DMA((4,)),
            pltpu.SemaphoreType.DMA((2, 8)),
            pltpu.SemaphoreType.DMA((5,)),
        ],
        compiler_params=pltpu.CompilerParams(vmem_limit_bytes=FFN_LIMIT),
        cost_estimate=pl.CostEstimate(
            flops=10 * rows * width * inner, bytes_accessed=24 << 20, transcendentals=0
        ),
        name="ffn_back",
    )(
        scalars,
        d_branch,
        inv_std,
        vectors,
        d_resid2,
        sums_mid,
        count,
        *attended,
        *(in_hbm(a) for a in (normed, slope, hidden, *packs)),
    )


def whole_call(kernel, name, args, outs, scalars=None, cost=SMALL_COST):
    return pl.pallas_call(
        kernel,
        out_shape=[o if hasattr(o, "memory_space") else jax.ShapeDtypeStruct(*o) for o in outs],
        in_specs=([] if scalars is None else [SMEM_SPEC]) + [VMEM_SPEC] * len(args),
        out_specs=[VMEM_SPEC] * len(outs),
        compiler_params=pltpu.CompilerParams(vmem_limit_bytes=SMALL_LIMIT),
        cost_estimate=cost,
        name=name,
    )(*(() if scalars is None else (scalars,)), *args)


def fold_cores(own, came):
    _, rows, cols = own.shape

    def kernel(own_ref, came_ref, *outs):
        for k, out in enumerate(outs):
            out[...] = (own_ref[k].astype(F32) + came_ref[k].astype(F32)).astype(BF16)

    outs = [pltpu.HBM((rows, cols), BF16)] * 4
    return whole_call(kernel, "fold_cores", (own, came), outs)


def split_cores(own, came):
    _, rows, cols = own.shape
    half = rows // 2

    def kernel(own_ref, came_ref, send_x, send_y, keep_upper, keep_lower):
        def total(upper, k):
            at = slice(0, half) if upper else slice(half, rows)
            return (own_ref[k, at, :].astype(F32) + came_ref[k, at, :].astype(F32)).astype(BF16)

        for i, k in enumerate((1, 3)):
            send_x[i] = total(True, k)
        for i, k in enumerate((2, 3)):
            send_y[i] = total(False, k)
        for i, k in enumerate((0, 2)):
            keep_upper[i] = total(True, k)
        for i, k in enumerate((0, 1)):
            keep_lower[i] = total(False, k)

    return whole_call(kernel, "split_cores", (own, came), [((2, half, cols), BF16)] * 4)


def second_step(keep_upper, came_x, keep_lower, came_y):
    def kernel(upper, upper_came, lower, lower_came, send_y, send_x, kept):
        half = upper.shape[1]
        send_y[...] = (upper[1].astype(F32) + upper_came[1].astype(F32)).astype(BF16)
        send_x[...] = (lower[1].astype(F32) + lower_came[1].astype(F32)).astype(BF16)
        kept[:half, :] = upper[0].astype(F32) + upper_came[0].astype(F32)
        kept[half:, :] = lower[0].astype(F32) + lower_came[0].astype(F32)

    half, cols = keep_upper.shape[1:]
    return whole_call(
        kernel,
        "second_step",
        (keep_upper, came_x, keep_lower, came_y),
        [((half, cols), BF16)] * 2 + [((2 * half, cols), F32)],
    )


def add_halves(kept, upper, lower):
    def kernel(kept, upper, lower, out):
        half = upper.shape[0]
        out[:half, :] = (kept[:half, :] + upper[...].astype(F32)).astype(BF16)
        out[half:, :] = (kept[half:, :] + lower[...].astype(F32)).astype(BF16)

    outs = [pltpu.HBM(kept.shape, BF16)]
    return whole_call(kernel, "add_halves", (kept, upper, lower), outs)[0]


def fold_quarters(terms, scalars):
    rows, cols = terms[0].shape
    part = rows // 4
    count = len(terms)

    def kernel(scalars, *refs):
        for k in range(4):
            at = pl.ds(pl.multiple_of((scalars[2] ^ k) * part, 8), part)
            total = sum(term[at, :].astype(F32) for term in refs[:count])
            refs[count + k % 2][k // 2] = total.astype(BF16)

    return whole_call(kernel, "fold_quarters", terms, [((2, part, cols), BF16)] * 2, scalars)


def finish(dense, qkv, half, block_col, scalars):
    _, part, cols = dense[0].shape
    qkv_part = qkv[0].shape[1]
    deep = block_col // 2

    def kernel(scalars, *refs):
        up, out, query, key, value, loss = refs[4:10]
        vectors, query_bias, value_bias = refs[10:17], refs[17], refs[18]
        dense_all, qkv_all = refs[19:]
        for parts, target in ((refs[:2], dense_all), (refs[2:4], qkv_all)):
            for k in range(4):
                piece = parts[k % 2].at[k // 2]
                rows = piece.shape[0]
                at = pl.ds(pl.multiple_of((scalars[2] ^ k) * rows, 8), rows)
                target[at, :] = piece[...].astype(F32)
        up[...] = dense_all[:half, :]
        out[:deep, :] = dense_all[half : half + deep, :half]
        out[deep:, :] = dense_all[half : half + deep, half:]
        table = dense_all[half + deep : half + deep + 16, :]
        for row, target in zip((6, 4, 5, 8, 2, 0, 1), vectors):
            target[...] = table[row, :]
        error = jnp.sum(table[3:4, :], axis=1, keepdims=True)
        tokens = jnp.sum(table[7:8, :], axis=1, keepdims=True)
        loss[...] = error / (tokens * cols)
        for i, target in enumerate((query, key, value)):
            target[...] = qkv_all[i * block_col : (i + 1) * block_col, :]
        bias = qkv_all[3 * block_col : 3 * block_col + 8, :]
        query_bias[...] = bias[0, :block_col]
        value_bias[...] = bias[0, block_col:]

    S = jax.ShapeDtypeStruct
    return pl.pallas_call(
        kernel,
        out_shape=[S((half, cols), F32), S((block_col, half), F32)]
        + [S((block_col, half), F32)] * 3
        + [S((1, 1), F32)]
        + [S((cols,), F32)] * 7
        + [S((block_col,), F32)] * 2,
        in_specs=[SMEM_SPEC] + [VMEM_SPEC] * 4,
        out_specs=[VMEM_SPEC] * 15,
        scratch_shapes=[
            pltpu.VMEM((4 * part, cols), F32),
            pltpu.VMEM((4 * qkv_part, half), F32),
        ],
        compiler_params=pltpu.CompilerParams(vmem_limit_bytes=SMALL_LIMIT),
        cost_estimate=SMALL_COST,
        name="finish",
    )(scalars, *dense, *qkv)


def dot(left, right, dims=NN):
    return lax.dot_general(left, right, dims, preferred_element_type=F32)


def split3(value):
    high = value.astype(BF16)
    rest = value - high.astype(F32)
    middle = rest.astype(BF16)
    low = (rest - middle.astype(F32)).astype(BF16)
    return high.astype(F32), middle.astype(F32), low.astype(F32)


def key_range(code, span, span_rows, blocks):
    per = span_rows // BLK
    first_seg = code[span * per, 0] // 2
    last_seg = code[span * per + per - 1, BLK - 1] // 2
    low = jnp.int32(0)
    high = jnp.int32(0)
    for other in range(blocks):
        start = code[other, 0]
        low += (code[other, BLK - 1] // 2 < first_seg).astype(jnp.int32)
        high += ((start // 2 <= last_seg) & (start % 2 == 1)).astype(jnp.int32)
    below = jnp.maximum(jnp.minimum(high, span * per) - low, 0)
    above = jnp.maximum(high - (span + 1) * per, 0)
    return low, below, below + above


def key_block(step, low, below, after):
    return jnp.where(step < below, low + step, after + step - below)


def lane_index(rows):
    return lax.broadcasted_iota(jnp.int32, (rows, 128), 1)


def allowed_block(code_rows, block, offset, span_rows):
    row = lax.broadcasted_iota(jnp.int32, (span_rows, BLK), 0)
    col = lax.broadcasted_iota(jnp.int32, (span_rows, BLK), 1)
    return (code_rows[pl.ds(block, 1), :] % 2 == 1) | (row == col + offset)


def attention_forward_kernel(heads, scalars, code, *refs):
    code_rows = refs[0]
    token_parts = refs[1:6]
    weights = refs[6:8]
    pieces = refs[8:12]
    saved = refs[12:16]
    padded, max_scr, acc_scr, query_pad, key_pad, value_pad, out_pad, whole_sem, span_sem = refs[16:]
    span_rows, width = token_parts[0].shape
    cols = 64 * heads
    flip = scalars[1]
    per = span_rows // BLK
    blocks = query_pad.shape[1] // BLK
    lane = lane_index(span_rows)
    for i in range(3):
        src = slice(i * cols, (i + 1) * cols)
        padded[i * 256 : i * 256 + cols, : width // 2] = weights[0][src, :]
        padded[i * 256 : i * 256 + cols, width // 2 :] = weights[1][src, :]
        padded[i * 256 + cols : (i + 1) * 256, :] = jnp.zeros((256 - cols, width), BF16)
    marks_bias = weights[0][3 * cols : 3 * cols + 1, :].astype(F32)
    no_bias = jnp.zeros((1, 256 - cols), F32)
    biases = (
        jnp.concatenate([marks_bias[:, :cols], no_bias], 1),
        None,
        jnp.concatenate([marks_bias[:, cols : 2 * cols], no_bias], 1),
    )
    first = 0
    for tokens in token_parts:
        rows = slice(first, first + tokens.shape[0])
        marks = []
        for block in range(rows.start // BLK, rows.stop // BLK):
            place = (block // per ^ flip) * per + block % per
            marks.append(
                jnp.broadcast_to(code_rows[pl.ds(place, 1), :].astype(F32), (128, BLK)).T
            )
        first = rows.stop
        lane = lane_index(tokens.shape[0])
        value_ones = jnp.where((lane >= 64) & (lane < 67), 1.0, 0.0)
        marks = jnp.concatenate(marks, 0).astype(jnp.int32)
        same = lane - 64 == marks // 2
        ids = (lane >= 64) & (lane < 80)
        query_marks = jnp.where((ids & same) | (lane == 80), 1.0, 0.0)
        key_marks = jnp.where(
            (ids & ~same) | ((lane == 80) & (marks % 2 == 0)),
            MASKED,
            jnp.where((lane >= 81) & (lane < 84), -1.0, 0.0),
        )
        for i, (out, extra) in enumerate(
            ((query_pad, query_marks), (key_pad, key_marks), (value_pad, value_ones))
        ):
            projected = dot(tokens[...], padded[i * 256 : (i + 1) * 256, :], NT)
            if biases[i] is not None:
                projected += biases[i]
            if i == 0:
                projected = projected.astype(BF16).astype(F32) * 0.125
            out[0, rows, :] = jnp.where(lane < 64, projected[:, :128], extra).astype(BF16)
            out[1, rows, :] = jnp.where(
                lane < 64, pltpu.roll(projected[:, :128], 64, 1), extra
            ).astype(BF16)
            out[2, rows, :] = jnp.where(lane < 64, projected[:, 128:], extra).astype(BF16)
    lane = lane_index(span_rows)
    no_valid_lane = jnp.where(lane == 80, 0.0, 1.0).astype(BF16)
    whole_copies = [
        pltpu.make_async_copy(key_pad, saved[1], whole_sem.at[0]),
        pltpu.make_async_copy(value_pad, saved[2], whole_sem.at[1]),
    ]
    for copy in whole_copies:
        copy.start()

    def span_copies(at):
        rows = pl.ds(pl.multiple_of(at * span_rows, span_rows), span_rows)
        return [
            pltpu.make_async_copy(
                source.at[:, rows, :], saved[i].at[:, rows, :], span_sem.at[i // 3, at]
            )
            for source, i in ((query_pad, 0), (out_pad, 3))
        ]

    def query_step(span, _):
        at = span ^ flip
        rows = pl.ds(pl.multiple_of(at * span_rows, span_rows), span_rows)
        low, below, count = key_range(code, span, span_rows, blocks)

        def keys_of(block):
            place = (block // per ^ flip) * per + block % per
            return pl.ds(pl.multiple_of(place * BLK, BLK), BLK)

        def scores_of(h, keys, allowed=None):
            if allowed is None:
                return dot(query_pad[h, rows, :], key_pad[h, keys, :], NT)
            scores = dot(query_pad[h, rows, :] * no_valid_lane, key_pad[h, keys, :], NT)
            return jnp.where(allowed, scores, MASKED)

        def each_block(visit):
            for part in range(per):
                block = span * per + part
                visit(keys_of(block), allowed_block(code_rows, block, part * BLK, span_rows))

            def step_fn(step, _):
                visit(keys_of(key_block(step, low, below, (span + 1) * per)), None)
                return 0

            lax.fori_loop(0, count, step_fn, 0)

        acc_scr[...] = jnp.zeros_like(acc_scr)
        max_scr[...] = jnp.zeros_like(max_scr)

        def plain(keys, allowed):
            for h in range(heads):
                probs = jnp.exp(scores_of(h, keys, allowed)).astype(BF16)
                acc_scr[h] += dot(probs, value_pad[h, keys, :])

        each_block(plain)
        least, most = jnp.float32(1.0), jnp.float32(1.0)
        for h in range(heads):
            total = jnp.where(lane == 64, acc_scr[h], 1.0)
            good = (total > 1e-25) & (total < 1e30)
            least = jnp.minimum(least, jnp.min(jnp.where(good, 1.0, 0.0)))

        @pl.when(least < 0.5)
        def _():
            max_scr[...] = jnp.full_like(max_scr, MASKED)

            def find_max(keys, allowed):
                for h in range(heads):
                    scores = scores_of(h, keys, allowed)
                    max_scr[h] = jnp.maximum(
                        max_scr[h], jnp.maximum(scores[:, :128], scores[:, 128:])
                    )

            each_block(find_max)
            for h in range(heads):
                max_scr[h] = jnp.broadcast_to(
                    jnp.max(max_scr[h], axis=1, keepdims=True), (span_rows, 128)
                )
            acc_scr[...] = jnp.zeros_like(acc_scr)

            def shifted(keys, allowed):
                for h in range(heads):
                    row_max = max_scr[h]
                    scores = scores_of(h, keys, allowed)
                    probs = jnp.exp(scores - jnp.concatenate([row_max, row_max], 1))
                    acc_scr[h] += dot(probs.astype(BF16), value_pad[h, keys, :])

            each_block(shifted)

        outs = []
        for h in range(heads):
            acc = acc_scr[h]
            total = jnp.broadcast_to(acc[:, 64:65], acc.shape)
            out = acc / total
            out_pad[h, rows, :] = out
            outs.append(out)
            high, middle, rest = split3(max_scr[h] + jnp.log(total))
            extra = jnp.where(
                lane == 81,
                high,
                jnp.where(lane == 82, middle, jnp.where(lane == 83, rest, 0.0)),
            )
            query_pad[h, rows, :] = query_pad[h, rows, :] + extra.astype(BF16)
        pair = jnp.where(lane < 64, outs[0], pltpu.roll(outs[1], 64, 1)).astype(BF16)
        middle = span_rows // 2
        last = jnp.where(
            lane_index(middle) < 64, outs[2][:middle], pltpu.roll(outs[2][middle:], 64, 1)
        ).astype(BF16)
        for k, piece in enumerate(pieces):

            @pl.when(at == k)
            def _():
                piece[:span_rows, :] = pair
                piece[span_rows:, :] = last

        for copy in span_copies(at):
            copy.start()
        return 0

    lax.fori_loop(0, len(pieces), query_step, 0)
    for copy in whole_copies:
        copy.wait()
    for at in range(len(pieces)):
        for copy in span_copies(at):
            copy.wait()


def attention_forward(scalars, code, token_shards, weights):
    rows, width = token_shards[0].shape
    length = code.shape[0] * BLK
    cols = (weights[0].shape[0] - PAD_ROWS) // 3
    heads = cols // 64
    S = jax.ShapeDtypeStruct
    flops = 2 * length * width * 3 * 256 + 3 * length * length * 128
    return pl.pallas_call(
        lambda *refs: attention_forward_kernel(heads, *refs),
        out_shape=[S((rows * cols // 128, 128), BF16)] * 4
        + [pltpu.HBM((heads, length, 128), BF16)] * 3
        + [pltpu.HBM((heads, length, 128), F32)],
        in_specs=[SMEM_SPEC] * 2 + [VMEM_SPEC] * 8,
        out_specs=[VMEM_SPEC] * 4 + [HBM_SPEC] * 4,
        scratch_shapes=[
            pltpu.VMEM((3 * 256, width), BF16),
            pltpu.VMEM((heads, rows, 128), F32),
            pltpu.VMEM((heads, rows, 128), F32),
        ]
        + [pltpu.VMEM((heads, length, 128), BF16)] * 3
        + [
            pltpu.VMEM((heads, length, 128), F32),
            pltpu.SemaphoreType.DMA((2,)),
            pltpu.SemaphoreType.DMA((2, 4)),
        ],
        compiler_params=pltpu.CompilerParams(vmem_limit_bytes=32 << 20),
        cost_estimate=pl.CostEstimate(
            flops=3 * flops, bytes_accessed=16 << 20, transcendentals=heads * length * 1024
        ),
        name="attention_forward",
    )(scalars, code, code, *token_shards, *weights)


def attention_backward_kernel(heads, scalars, code, *refs):
    code_rows = refs[0]
    span_rows = refs[1].shape[0] * 128 // (64 * heads)
    term_hbm, grad_hbm = refs[16:20], refs[20:22]
    grad_pad, query_sum, key_sum, value_sum, low_scr, grad_scr, bias_sum = refs[22:29]
    query_pad, key_pad, value_pad, out_pad = refs[29:33]
    shards_in = refs[33:37]
    weights = refs[37]
    grads = refs[38:42]
    terms, own_grad, other_grad, out_sems, in_sems = refs[42:]
    side = weights.shape[1] // 2
    last_half = span_rows // 2
    pairs = list(zip(refs[1:9], grads + refs[29:33]))
    pairs += list(zip(refs[9:12], shards_in[:3]))
    pairs += [
        (refs[12], shards_in[3].at[:last_half, :]),
        (refs[13], shards_in[3].at[last_half:, :]),
    ]
    pairs += [(refs[14], weights.at[:, :side]), (refs[15], weights.at[:, side:])]
    copies = [
        pltpu.make_async_copy(source, target, in_sems.at[i])
        for i, (source, target) in enumerate(pairs)
    ]
    for i in (7, 0, 1, 2, 3, 4, 5, 6):
        copies[i].start()
    key_sum[...] = jnp.zeros_like(key_sum)
    value_sum[...] = jnp.zeros_like(value_sum)
    query_sum[...] = jnp.zeros_like(query_sum)
    for i in (7, 0, 1, 2, 3):
        copies[i].wait()
    flip = scalars[1]
    per = span_rows // BLK
    blocks = query_pad.shape[1] // BLK
    lane = lane_index(span_rows)
    for shard, grad in enumerate(grads):
        rows = slice(shard * span_rows, (shard + 1) * span_rows)
        pair = grad[:span_rows, :].astype(F32)
        last = grad[span_rows:, :].astype(F32)
        last = jnp.concatenate([last, pltpu.roll(last, 64, 1)], 0)
        for h, block in enumerate((pair, pltpu.roll(pair, 64, 1), last)):
            block = jnp.where(lane < 64, block, 0.0)
            delta = jnp.sum(block * out_pad[h, rows, :], axis=1, keepdims=True)
            high, middle, rest = split3(-delta)
            block = jnp.where(
                lane == 64,
                high,
                jnp.where(lane == 65, middle, jnp.where(lane == 66, rest, block)),
            )
            grad_pad[h, rows, :] = block.astype(BF16)
    for i in (4, 5, 6):
        copies[i].wait()
    for i in range(8, 15):
        copies[i].start()
    no_valid_lane = jnp.where(lane == 80, 0.0, 1.0).astype(BF16)

    def query_step(span, _):
        at = span ^ flip
        rows = pl.ds(pl.multiple_of(at * span_rows, span_rows), span_rows)
        low, below, count = key_range(code, span, span_rows, blocks)

        def visit(block, allowed):
            place = (block // per ^ flip) * per + block % per
            keys = pl.ds(pl.multiple_of(place * BLK, BLK), BLK)
            for h in range(heads):
                query, grad = query_pad[h, rows, :], grad_pad[h, rows, :]
                key, value = key_pad[h, keys, :], value_pad[h, keys, :]
                if allowed is None:
                    scores = dot(key, query, NT)
                else:
                    scores = jnp.where(allowed, dot(key, query * no_valid_lane, NT), MASKED)
                probs = jnp.exp(scores)
                d_scores = (probs * dot(value, grad, NT)).astype(BF16)
                value_sum[h, keys, :] += dot(probs.astype(BF16), grad)
                key_sum[h, keys, :] += dot(d_scores, query)
                query_sum[h, rows, :] += dot(d_scores, key, TN)

        for part in range(per):
            block = span * per + part
            key_at = lax.broadcasted_iota(jnp.int32, (BLK, span_rows), 0)
            query_at = lax.broadcasted_iota(jnp.int32, (BLK, span_rows), 1)
            marks = jnp.broadcast_to(
                code_rows[pl.ds(block, 1), :].astype(F32), (128, BLK)
            ).T.astype(jnp.int32)
            valid = jnp.concatenate([marks] * (span_rows // 128), 1) % 2 == 1
            visit(block, valid | (query_at == key_at + part * BLK))

        def step_fn(step, _):
            visit(key_block(step, low, below, (span + 1) * per), None)
            return 0

        lax.fori_loop(0, count, step_fn, 0)
        return 0

    lax.fori_loop(0, len(grads), query_step, 0)
    for i in range(8, 15):
        copies[i].wait()
    bias_sum[...] = jnp.zeros_like(bias_sum)
    stores = []
    for shard in range(len(grads)):
        rows = slice(shard * span_rows, (shard + 1) * span_rows)
        parts = [query_sum[h, rows, :] * 0.125 for h in range(heads)]
        parts += [sums[h, rows, :] for sums in (key_sum, value_sum) for h in range(heads)]
        for at in range(0, len(parts), 2):
            if at + 1 < len(parts):
                value = jnp.where(lane < 64, parts[at], pltpu.roll(parts[at + 1], 64, 1))
            else:
                value = parts[at][:, :64]
            low = value.astype(BF16)
            cols = slice(at * 64, at * 64 + low.shape[1])
            low_scr[:, cols] = low
            bias_sum[0:1, cols] += column_sum(low.astype(F32))
        low = low_scr[...]
        depth = low.shape[1]
        term = dot(low, weights[:depth, :]).astype(BF16)
        terms[shard] = term
        copy = pltpu.make_async_copy(
            terms.at[shard], term_hbm[shard], out_sems.at[shard]
        )
        copy.start()
        stores.append(copy)
        part = dot(low, shards_in[shard][...], TN)
        if shard == 0:
            grad_scr[...] = part
        elif shard < 3:
            grad_scr[...] += part
        else:
            total = (grad_scr[...] + part).astype(BF16)
            half = total.shape[1] // 2
            own_grad[:depth, :] = total[:, :half]
            other_grad[:depth, :] = total[:, half:]
    cols = heads * 64
    bias = jnp.concatenate([bias_sum[:, 0:cols], bias_sum[:, 2 * cols :]], 1).astype(BF16)
    bias = jnp.concatenate([bias] * ((own_grad.shape[0] - depth) // bias.shape[0]), 0)
    own_grad[depth:, :] = bias
    other_grad[depth:, :] = bias
    for i, source in enumerate((own_grad, other_grad)):
        copy = pltpu.make_async_copy(source, grad_hbm[i], out_sems.at[4 + i])
        copy.start()
        stores.append(copy)
    for copy in stores:
        copy.wait()


def attention_backward(scalars, code, grads, saved, token_shards, weights):
    length = code.shape[0] * BLK
    heads = saved[0].shape[0]
    rows, width = token_shards[0].shape
    cols = 3 * heads * 64
    S = jax.ShapeDtypeStruct
    return pl.pallas_call(
        lambda *refs: attention_backward_kernel(heads, *refs),
        out_shape=[
            *[pltpu.HBM((rows, width), BF16)] * 4,
            *[pltpu.HBM((cols + GRAD_PAD, width // 2), BF16)] * 2,
        ],
        in_specs=[SMEM_SPEC] * 2 + [VMEM_SPEC] + [HBM_SPEC] * 15,
        out_specs=[HBM_SPEC] * 6,
        scratch_shapes=[
            pltpu.VMEM((heads, length, 128), BF16),
            pltpu.VMEM((heads, length, 128), F32),
            pltpu.VMEM((heads, length, 128), F32),
            pltpu.VMEM((heads, length, 128), F32),
            pltpu.VMEM((rows, cols), BF16),
            pltpu.VMEM((cols, width), F32),
            pltpu.VMEM((16, cols), F32),
        ]
        + [pltpu.VMEM(a.shape, a.dtype) for a in saved]
        + [pltpu.VMEM((rows, width), BF16)] * 4
        + [pltpu.VMEM((weights[0].shape[0], width), BF16)]
        + [pltpu.VMEM(a.shape, a.dtype) for a in grads]
        + [
            pltpu.VMEM((4, rows, width), BF16),
            pltpu.VMEM((cols + GRAD_PAD, width // 2), BF16),
            pltpu.VMEM((cols + GRAD_PAD, width // 2), BF16),
            pltpu.SemaphoreType.DMA((6,)),
            pltpu.SemaphoreType.DMA((15,)),
        ],
        compiler_params=pltpu.CompilerParams(vmem_limit_bytes=46 << 20),
        cost_estimate=pl.CostEstimate(
            flops=heads * length * length * 1500, bytes_accessed=8 << 20, transcendentals=0
        ),
        name="attention_backward",
    )(
        scalars,
        code,
        code,
        *(in_hbm(a) for a in (*grads, *saved, *token_shards, *weights)),
    )


CHIP = [[(c, c ^ k) for c in range(4)] for k in range(4)]
PLANE = [[(p, p ^ k) for p in range(4)] for k in range(4)]
CORE = [(0, 1), (1, 0)]


def to_chip(value, k):
    return lax.ppermute(value, "gz", CHIP[k])


def to_core(value):
    return lax.ppermute(value, "gy", CORE)


def to_plane(value, k):
    return lax.ppermute(value, "gx", PLANE[k])


def after(value, *others):
    return lax.optimization_barrier((value,) + others)[0]


def swap_halves(flip, value):
    half = value.shape[-1] // 2
    swapped = jnp.concatenate([value[..., half:], value[..., :half]], -1)
    return jnp.where(flip, swapped, value)


def add_low(left, right):
    return (left.astype(F32) + right.astype(F32)).astype(BF16)


def sum_planes(dense, qkv, waits):
    if lax.axis_size("gx") != 4:
        dense, other = jnp.stack(dense), jnp.stack(qkv(dense[0]))
        total = lax.psum((dense, other), "gx")
        return [(t[0], t[1]) for t in total], waits
    near = dense[0].astype(F32) + to_plane(dense[1], 1).astype(F32)
    step = near[1].astype(BF16)
    keep, send = qkv(step)
    total = (near[0] + to_plane(step, 2).astype(F32)).astype(BF16)
    near = keep.astype(F32) + to_plane(send, 1).astype(F32)
    step = after(near[1].astype(BF16), total)
    pair = jnp.stack([total, to_plane(total, 2)])
    other = (near[0] + to_plane(step, 2).astype(F32)).astype(BF16)
    other = after(other, pair)
    back = to_plane(pair, 1)
    other_pair = jnp.stack([other, to_plane(other, 2)])
    other_back = to_plane(other_pair, 1)
    *waits, back = lax.optimization_barrier((*waits, back))
    return [(pair, back), (other_pair, other_back)], waits


def shards(
    tokens,
    segment_ids,
    valid_mask,
    cotangent,
    teacher,
    w_query,
    b_query,
    w_key,
    w_value,
    b_value,
    w_out,
    b_out,
    norm1_gain,
    norm1_bias,
    w_up,
    b_up,
    w_down,
    b_down,
    norm2_gain,
    norm2_bias,
):
    row_count, width = tokens.shape
    half = width // 2
    core = lax.axis_index("gy")
    chip = lax.axis_index("gz")
    flip = core == 1
    block_col = w_query.shape[1]
    hidden_col = w_up.shape[1]
    plane = lax.axis_index("gx") if lax.axis_size("gx") == 4 else jnp.int32(0)
    scalars = jnp.stack([core, chip, plane, chip]).astype(jnp.int32)

    own_tokens = swap_halves(flip, tokens)
    along_x, along_y = to_chip(own_tokens, 1), to_chip(own_tokens, 2)
    code = (segment_ids * 2 + valid_mask).reshape(-1, BLK)
    bias_row = jnp.concatenate([b_query, b_value])[None, :]
    qkv_own = jnp.concatenate(
        [w_query.T, w_key.T, w_value.T, jnp.broadcast_to(bias_row, (PAD_ROWS, half))], 0
    )
    vectors = jnp.stack([b_out, norm1_gain, norm1_bias, b_down, norm2_gain, norm2_bias] + [b_out] * 2)
    vectors = swap_halves(flip, vectors.astype(F32))
    own_valid = lax.dynamic_slice_in_dim(valid_mask, chip * row_count, row_count, 1).astype(F32)
    count = jnp.concatenate([own_valid, jnp.zeros((1, width - row_count), F32)], 1)
    count = jnp.broadcast_to(count, (8, width))
    own_valid = own_valid.T
    packed = jnp.concatenate(
        [
            jnp.concatenate([w_down[: hidden_col // 2], w_down[hidden_col // 2 :]], 1),
            w_up,
            jnp.concatenate([w_out[: block_col // 2], w_out[block_col // 2 :]], 1),
            jnp.broadcast_to(b_up[None, :], (PAD_ROWS, hidden_col)),
        ],
        0,
    )

    code, qkv_own, scalars, packed, vectors, own_valid, count, *_ = lax.optimization_barrier(
        (code, qkv_own, scalars, packed, vectors, own_valid, count, own_tokens)
    )
    qkv = (qkv_own, to_core(qkv_own))
    along_x, along_y, *qkv = lax.optimization_barrier((along_x, along_y, *qkv))
    middle = row_count // 2
    far = (to_chip(along_x[:middle], 2), to_chip(along_y[middle:], 1))
    token_shards = (own_tokens, along_x, along_y, *far)
    packed = after(packed, *far)
    pack_x, pack_y = to_chip(packed, 1), to_chip(packed, 2)

    scalars = after(scalars, packed)
    results = attention_forward(scalars, code, token_shards, qkv)
    saved = results[4:]
    attended = [results[0]] + [to_chip(results[k], k) for k in (1, 2, 3)]

    deep = hidden_col // 2
    pack_x, pack_y = lax.optimization_barrier((pack_x, pack_y, results[0]))[:2]
    far = (to_chip(pack_x[:, :half], 2), to_chip(pack_y[:, half:], 1))
    packs = (packed, pack_x, pack_y, *far)
    packs += (to_core(packed), *(to_core(after(v, *attended[1:])) for v in packs[1:]))

    inv_std, output, d_resid2, d_branch, sums_mid, act, normed, hidden_low, slope = ffn_forward(
        scalars, attended, own_tokens, own_valid, vectors, cotangent, teacher, packs, deep
    )
    pieces = (4, hidden_col, half)
    d_down_other = jnp.einsum("lf,lm->fm", act, d_branch[:, half:], preferred_element_type=F32)
    d_down_came = to_core(d_down_other.astype(BF16).reshape(pieces))
    d_down = jnp.einsum("lf,lm->fm", act, d_branch[:, :half], preferred_element_type=F32)
    down_x, down_y, down_upper, down_lower = split_cores(
        d_down.astype(BF16).reshape(pieces), d_down_came
    )
    d_branch = after(d_branch, down_upper)
    down_x, down_y = to_chip(down_x, 1), to_chip(down_y, 2)
    d_resid1, *back, own_grads, other_grads = ffn_back(
        scalars,
        d_branch,
        inv_std,
        vectors,
        d_resid2,
        sums_mid,
        count,
        attended,
        normed,
        slope,
        hidden_low,
        packs,
        deep,
    )
    d_pieces = [back[0]] + [to_chip(back[k], k) for k in (1, 2, 3)]

    down_y, down_x, down_kept = second_step(down_upper, down_x, down_lower, down_y)
    d_dense = fold_cores(own_grads, to_core(after(other_grads, down_y)))
    down_total = add_halves(down_kept, to_chip(down_y, 2), to_chip(down_x, 1))
    grad_down = lax.psum(down_total, "gx")
    d_pieces[0] = after(d_pieces[0], d_dense[0], down_total)
    d_dense = [d_dense[0]] + [to_chip(d_dense[k], k) for k in (1, 2, 3)]

    *terms, d_own, d_other = attention_backward(
        scalars, code, d_pieces, saved, token_shards, qkv
    )
    d_dense[0] = after(d_dense[0], grad_down, terms[0])
    quarters = fold_quarters(d_dense, scalars)
    d_own, d_other, *terms, _, _ = lax.optimization_barrier((d_own, d_other, *terms, *quarters))
    d_w = (d_own, to_core(d_other))
    terms = [terms[0]] + [to_chip(terms[k], k) for k in (1, 2, 3)]
    (dense_grad, qkv_grad), came = sum_planes(
        quarters, lambda first: fold_quarters(d_w, scalars), terms[1:]
    )
    d_tokens = d_resid1 + sum(t.astype(F32) for t in (terms[0], *came))
    grad_up, grad_out, grad_query, grad_key, grad_value, loss, *vectors = finish(
        dense_grad, qkv_grad, half, block_col, scalars
    )
    b_out_grad, gain1_grad, shift1_grad, b_up_grad, b_down_grad, gain2_grad, shift2_grad = vectors[:7]

    return (
        output,
        loss[0, 0],
        swap_halves(flip, d_tokens.astype(BF16)),
        grad_query.T,
        vectors[7],
        grad_key.T,
        grad_value.T,
        vectors[8],
        grad_out,
        b_out_grad,
        gain1_grad,
        shift1_grad,
        grad_up,
        b_up_grad,
        grad_down.astype(F32),
        b_down_grad,
        gain2_grad,
        shift2_grad,
    )


def solution(mesh):
    placed = (
        P(("gx", "gy", "gz"), None),
        P(("gx", "gy"), None),
        P(("gx", "gy"), None),
        P(("gx", "gy", "gz"), None),
        P(("gx", "gy", "gz"), None),
        P("gy", "gz"),
        P("gz"),
        P("gy", "gz"),
        P("gy", "gz"),
        P("gz"),
        P("gz", "gy"),
        P(),
        P(),
        P(),
        P("gy", "gz"),
        P("gz"),
        P("gz", "gy"),
        P(),
        P(),
        P(),
    )
    return jax.shard_map(
        shards,
        mesh=mesh,
        in_specs=placed,
        out_specs=(
            P(("gx", "gy", "gz"), None),
            P(),
            P(("gx", "gy", "gz"), None),
            P("gy", "gz"),
            P("gz"),
            P("gy", "gz"),
            P("gy", "gz"),
            P("gz"),
            P("gz", "gy"),
            P(),
            P(),
            P(),
            P("gy", "gz"),
            P("gz"),
            P("gz", "gy"),
            P(),
            P(),
            P(),
        ),
        check_vma=False,
    )
```

```python
import math

import jax
import jax.numpy as jnp
from jax import lax
from jax.experimental import pallas as pl
from jax.experimental.pallas import tpu as pltpu
from jax.sharding import PartitionSpec as P

EPSILON = 1e-05
MASKED = -1e30
PAD_ROWS = 16
GRAD_PAD = 64
BLK = 256
F32 = jnp.float32
BF16 = jnp.bfloat16
NT = (((1,), (1,)), ((), ()))
NN = (((1,), (0,)), ((), ()))
TN = (((0,), (0,)), ((), ()))


VMEM_SPEC = pl.BlockSpec(memory_space=pltpu.VMEM)
SMEM_SPEC = pl.BlockSpec(memory_space=pltpu.SMEM)
HBM_SPEC = pl.BlockSpec(memory_space=pltpu.HBM)
VMEM_LIMIT = 24 << 20
SMALL_LIMIT = 20 << 20
FFN_LIMIT = 40 << 20
SMALL_COST = pl.CostEstimate(flops=1 << 16, bytes_accessed=1 << 12, transcendentals=0)


def in_hbm(array):
    return pltpu.with_memory_space_constraint(array, pltpu.HBM)


class Loads:
    def __init__(self, packs, sems):
        self.packs, self.sems, self.used, self.groups = packs, sems, 0, {}

    def add(self, group, source, target):
        copy = pltpu.make_async_copy(source, target, self.sems.at[self.used])
        self.used += 1
        self.groups.setdefault(group, []).append(copy)

    def start(self, *groups):
        for group in groups:
            for copy in self.groups.get(group, ()):
                copy.start()

    def wait(self, *groups):
        for group in groups:
            for copy in self.groups.get(group, ()):
                copy.wait()

    def blocks(self, core):
        packs = self.packs[5 * core : 5 * core + 5]
        half = packs[4].shape[1]
        blocks = [(k, i, packs[k], i * half) for k in range(3) for i in range(2)]
        return half, blocks + [(3, 0, packs[3], 0), (3, 1, packs[4], 0)]

    def lay_out(self, deep, block_col, up_full, down_full, out_full, bias_full):
        for core in range(2):
            half, blocks = self.blocks(core)
            top = deep + half
            out_deep = block_col // 2
            side = slice(core * half, (core + 1) * half)
            for k, i, pack, col in blocks:
                cols = slice(col, col + half)
                hidden = slice((2 * k + i) * half, (2 * k + i + 1) * half)
                self.add(("up", k), pack.at[deep:top, cols], up_full.at[side, hidden])
                self.add(("down", k), pack.at[0:deep, cols], down_full.at[hidden, side])
                first = k * block_col + i * out_deep
                self.add(
                    "out",
                    pack.at[top : top + out_deep, cols],
                    out_full.at[first : first + out_deep, side],
                )
                if core == 0 and bias_full is not None:
                    low = top + out_deep
                    self.add("out", pack.at[low : low + PAD_ROWS, cols], bias_full.at[:, hidden])


def half_start(scalars, second, half):
    flip = scalars[0]
    return pl.multiple_of(jnp.where(second, 1 - flip, flip) * half, 128)


def read_swapped(ref, scalars):
    half = ref.shape[-1] // 2
    return jnp.concatenate(
        [
            ref[:, pl.ds(half_start(scalars, False, half), half)].astype(F32),
            ref[:, pl.ds(half_start(scalars, True, half), half)].astype(F32),
        ],
        1,
    )


def write_swapped(ref, rows, value, scalars):
    half = ref.shape[-1] // 2
    ref[rows, pl.ds(half_start(scalars, False, half), half)] = value[:, :half].astype(ref.dtype)
    ref[rows, pl.ds(half_start(scalars, True, half), half)] = value[:, half:].astype(ref.dtype)


def column_sum(value):
    return jnp.sum(value, 0, keepdims=True)


def layer_norm(resid):
    average = jnp.mean(resid, -1, keepdims=True)
    centered = resid - average
    inv_std = lax.rsqrt(jnp.mean(centered * centered, -1, keepdims=True) + EPSILON)
    return centered * inv_std, inv_std


def layer_norm_back(upstream, gain, normed, inv_std):
    scaled = upstream * gain
    return inv_std * (
        scaled
        - jnp.mean(scaled, -1, keepdims=True)
        - normed * jnp.mean(scaled * normed, -1, keepdims=True)
    )


def unpack_heads(packed, target):
    rows = target.shape[0]
    middle = rows // 2
    last = packed[rows:, :].astype(F32)
    target[:, 0:128] = packed[:rows, :]
    target[:middle, 128:] = last[:, :64].astype(BF16)
    target[middle:, 128:] = pltpu.roll(last, 64, 1)[:, :64].astype(BF16)


def ffn_forward_kernel(deep, scalars, *refs):
    att = refs[:4]
    own_tokens, valid, vectors = refs[4:7]
    cot_source, teach_source = refs[7:9]
    packs = refs[9:19]
    std_out, output, resid_out, branch_out, sums, act_out = refs[19:25]
    normed_hbm, low_hbm, slope_hbm = refs[25:28]
    up_full, down_full, out_full, bias_full = refs[28:32]
    cotangent, teacher, normed_out, low_out, slope_out, heads = refs[32:38]
    sems, row_sems, chunk_sems = refs[38:]
    width = own_tokens.shape[1]
    block_col = width // 4
    loads = Loads(packs, sems)
    loads.lay_out(deep, block_col, up_full, down_full, out_full, bias_full)
    row_loads = [
        pltpu.make_async_copy(cot_source, cotangent, row_sems.at[0]),
        pltpu.make_async_copy(teach_source, teacher, row_sems.at[1]),
    ]
    loads.start("out", ("up", 0))
    for k in range(4):
        unpack_heads(att[k], heads.at[k])
    loads.wait("out")
    loads.start(("down", 0), ("up", 1))
    mixed = jnp.zeros(own_tokens.shape, F32)
    for k in range(4):
        mixed += dot(heads[k], out_full[k * block_col : (k + 1) * block_col, :])
    resid = read_swapped(own_tokens, scalars) + (mixed + vectors[0:1, :])
    normed, inv_std = layer_norm(resid)
    hidden = normed * vectors[1:2, :] + vectors[2:3, :]
    normed_out[...] = normed
    std_out[...] = inv_std
    low_out[...] = hidden.astype(BF16)
    stores = [
        pltpu.make_async_copy(normed_out, normed_hbm, row_sems.at[2]),
        pltpu.make_async_copy(low_out, low_hbm, row_sems.at[3]),
    ]
    for copy in stores:
        copy.start()
    branch = jnp.zeros(own_tokens.shape, F32)
    for k in range(4):
        loads.wait(("up", k))
        loads.start(("down", k + 1), ("up", k + 2))
        if k == 2:
            for copy in row_loads:
                copy.start()
        place = slice(k * width, (k + 1) * width)
        preact = dot(low_out[...], up_full[:, place]) + bias_full[0:1, place].astype(F32)
        normal_cdf = 0.5 * (1.0 + lax.erf(preact * (1.0 / math.sqrt(2.0))))
        slope = normal_cdf + preact * jnp.exp(-0.5 * preact * preact) * (
            1.0 / math.sqrt(2.0 * math.pi)
        )
        act = (preact * normal_cdf).astype(BF16)
        act_out[:, place] = act
        slope_out[:, place] = slope.astype(BF16)
        copy = pltpu.make_async_copy(
            slope_out.at[:, place], slope_hbm.at[:, place], chunk_sems.at[k]
        )
        copy.start()
        stores.append(copy)
        loads.wait(("down", k))
        branch += dot(act, down_full[place, :])
    for copy in row_loads:
        copy.wait()
    gain = vectors[4:5, :]
    hidden = normed_out[...] * vectors[1:2, :] + vectors[2:3, :]
    resid = hidden + (branch + vectors[3:4, :])
    normed, inv_std = layer_norm(resid)
    full = normed * gain + vectors[5:6, :]
    write_swapped(output, slice(None), full, scalars)
    mismatch = full - read_swapped(teacher, scalars)
    masked = valid[...] * mismatch
    d_output = read_swapped(cotangent, scalars) + masked
    d_resid = layer_norm_back(d_output, gain, normed, inv_std)
    resid_out[...] = d_resid
    low = d_resid.astype(BF16)
    branch_out[...] = low
    sums[...] = jnp.zeros_like(sums)
    rows = (
        column_sum(d_output * normed),
        column_sum(d_output),
        column_sum(low.astype(F32)),
        column_sum(masked * mismatch),
    )
    for at, row in enumerate(rows):
        write_swapped(sums, slice(at, at + 1), row, scalars)
    for copy in stores:
        copy.wait()


def full_scratch(width, inner, block_col):
    return [
        pltpu.VMEM((width, inner), BF16),
        pltpu.VMEM((inner, width), BF16),
        pltpu.VMEM((4 * block_col, width), BF16),
    ]


def ffn_forward(scalars, attended, own_tokens, valid, vectors, cotangent, teacher, packs, deep):
    rows, width = own_tokens.shape
    inner = 4 * width
    full = (rows, width)
    S = jax.ShapeDtypeStruct
    return pl.pallas_call(
        lambda *refs: ffn_forward_kernel(deep, *refs),
        out_shape=[S((rows, 1), F32), S(full, BF16), S(full, F32), S(full, BF16)]
        + [S((8, width), F32), S((rows, inner), BF16)]
        + [pltpu.HBM(full, F32), pltpu.HBM(full, BF16), pltpu.HBM((rows, inner), BF16)],
        in_specs=[SMEM_SPEC] + [VMEM_SPEC] * 7 + [HBM_SPEC] * 12,
        out_specs=[VMEM_SPEC] * 6 + [HBM_SPEC] * 3,
        scratch_shapes=full_scratch(width, inner, width // 4)
        + [pltpu.VMEM((PAD_ROWS, inner), BF16)]
        + [pltpu.VMEM(full, BF16)] * 2
        + [pltpu.VMEM(full, F32), pltpu.VMEM(full, BF16), pltpu.VMEM((rows, inner), BF16)]
        + [pltpu.VMEM((4, rows, width // 4), BF16)]
        + [
            pltpu.SemaphoreType.DMA((56,)),
            pltpu.SemaphoreType.DMA((4,)),
            pltpu.SemaphoreType.DMA((4,)),
        ],
        compiler_params=pltpu.CompilerParams(vmem_limit_bytes=FFN_LIMIT),
        cost_estimate=pl.CostEstimate(
            flops=10 * rows * width * inner, bytes_accessed=24 << 20, transcendentals=0
        ),
        name="ffn_forward",
    )(
        scalars,
        *attended,
        own_tokens,
        valid,
        vectors,
        *(in_hbm(a) for a in (cotangent, teacher, *packs)),
    )


def ffn_back_kernel(deep, scalars, *refs):
    d_branch, std_ref, vectors, d_resid2, sums_mid, count = refs[:6]
    att = refs[6:10]
    normed_source, slope_source, hidden_source = refs[10:13]
    packs = refs[13:23]
    resid_hbm = refs[23]
    piece_hbm = refs[24:28]
    own_hbm, other_hbm = refs[28:30]
    up_full, down_full, out_full = refs[30:33]
    normed_ref, slope, hidden, flipped, own, other, sums, resid_out = refs[33:41]
    pieces = refs[41:45]
    heads = refs[45]
    sems, row_sem, chunk_sems, grad_sems, out_sems = refs[46:]
    rows_here, width = d_branch.shape
    half = width // 2
    block_col = width // 4
    out_deep = block_col // 2
    loads = Loads(packs, sems)
    loads.lay_out(deep, block_col, up_full, down_full, out_full, None)
    normed_load = pltpu.make_async_copy(normed_source, normed_ref, row_sem.at[0])
    hidden_load = pltpu.make_async_copy(hidden_source, hidden, row_sem.at[1])
    slopes = []
    for k in range(4):
        place = slice(k * width, (k + 1) * width)
        slopes.append(
            pltpu.make_async_copy(slope_source.at[:, place], slope.at[:, place], chunk_sems.at[k])
        )
    stores = []

    def store(i, source, target, k, rows):
        copy = pltpu.make_async_copy(
            source.at[k, rows, :], target.at[k, rows, :], grad_sems.at[i, len(stores) // 2]
        )
        copy.start()
        stores.append(copy)

    loads.start(("down", 0))
    hidden_load.start()
    slopes[0].start()
    loads.start(("up", 0), ("down", 1))
    sums[...] = jnp.zeros_like(sums)
    for k in range(4):
        unpack_heads(att[k], heads.at[k])
    hidden_load.wait()
    flipped[...] = hidden[...].astype(F32).T.astype(BF16)
    d_hidden = d_resid2[...]
    for k in range(4):
        loads.wait(("down", k))
        loads.start(("up", k + 1), ("down", k + 2))
        if k < 3:
            slopes[k + 1].start()
        else:
            normed_load.start()
            loads.start("out")
        place = slice(k * width, (k + 1) * width)
        d_act = dot(d_branch[...], down_full[place, :], NT)
        slopes[k].wait()
        d_pre = (d_act * slope[:, place].astype(F32)).astype(BF16)
        sums[4 + k : 5 + k, :] = column_sum(d_pre.astype(F32))
        loads.wait(("up", k))
        d_hidden += dot(d_pre, up_full[:, place], NT)
        grad = dot(flipped[...], d_pre).astype(BF16)
        own[k, 0:half, :] = grad[:half, :]
        other[k, 0:half, :] = grad[half:, :]
        store(0, other, other_hbm, k, slice(0, half))
        store(1, own, own_hbm, k, slice(0, half))
    normed_load.wait()
    normed = normed_ref[...]
    d_resid = layer_norm_back(d_hidden, vectors[1:2, :], normed, std_ref[...])
    write_swapped(resid_out, slice(None), d_resid, scalars)
    out_copies = [pltpu.make_async_copy(resid_out, resid_hbm, out_sems.at[4])]
    out_copies[0].start()
    mixed = d_resid.astype(BF16)
    loads.wait("out")
    for k in range(4):
        rows = slice(k * block_col, (k + 1) * block_col)
        piece = dot(mixed, out_full[rows, :], NT).astype(BF16)
        middle = rows_here // 2
        pieces[k][:rows_here, :] = piece[:, :128]
        pieces[k][rows_here:, :] = jnp.concatenate(
            [piece[:middle, 128:], piece[middle:, 128:]], 1
        )
        copy = pltpu.make_async_copy(pieces[k], piece_hbm[k], out_sems.at[k])
        copy.start()
        out_copies.append(copy)
    for at, row in enumerate(
        (column_sum(d_hidden * normed), column_sum(d_hidden), column_sum(mixed.astype(F32)))
    ):
        write_swapped(sums, slice(at, at + 1), row, scalars)
    for k in range(4):
        out_grad = dot(heads[k], mixed, TN)
        low = half + out_deep
        table = jnp.concatenate(
            [
                sums_mid[0:4, :],
                sums[0:3, :],
                count[0:1, :],
                sums[4 + k : 5 + k, :],
                jnp.zeros((own.shape[1] - low - 9, own.shape[2]), F32),
            ],
            0,
        ).astype(BF16)
        for i, target in enumerate((own, other)):
            part = out_grad[:, i * half : (i + 1) * half].astype(BF16)
            target[k, half:low, 0:half] = part[:out_deep, :]
            target[k, half:low, half:] = part[out_deep:, :]
            target[k, low:, :] = table
        store(0, other, other_hbm, k, slice(half, own.shape[1]))
        store(1, own, own_hbm, k, slice(half, own.shape[1]))
    for copy in stores + out_copies:
        copy.wait()


def ffn_back(
    scalars, d_branch, inv_std, vectors, d_resid2, sums_mid, count, attended, normed, slope, hidden, packs, deep
):
    rows, width = d_branch.shape
    inner = 4 * width
    full = (rows, width)
    block_col = width // 4
    grads = ((4, width // 2 + 128, width), BF16)
    S = jax.ShapeDtypeStruct
    return pl.pallas_call(
        lambda *refs: ffn_back_kernel(deep, *refs),
        out_shape=[pltpu.HBM(full, F32)]
        + [pltpu.HBM(attended[0].shape, BF16)] * 4
        + [pltpu.HBM(*grads)] * 2,
        in_specs=[SMEM_SPEC] + [VMEM_SPEC] * 10 + [HBM_SPEC] * 13,
        out_specs=[HBM_SPEC] * 7,
        scratch_shapes=full_scratch(width, inner, block_col)
        + [pltpu.VMEM(full, F32), pltpu.VMEM((rows, inner), BF16), pltpu.VMEM(full, BF16)]
        + [pltpu.VMEM((width, rows), BF16)]
        + [pltpu.VMEM(*grads)] * 2
        + [pltpu.VMEM((8, width), F32), pltpu.VMEM(full, F32)]
        + [pltpu.VMEM(attended[0].shape, BF16)] * 4
        + [pltpu.VMEM((4, rows, block_col), BF16)]
        + [
            pltpu.SemaphoreType.DMA((48,)),
            pltpu.SemaphoreType.DMA((2,)),
            pltpu.SemaphoreType.DMA((4,)),
            pltpu.SemaphoreType.DMA((2, 8)),
            pltpu.SemaphoreType.DMA((5,)),
        ],
        compiler_params=pltpu.CompilerParams(vmem_limit_bytes=FFN_LIMIT),
        cost_estimate=pl.CostEstimate(
            flops=10 * rows * width * inner, bytes_accessed=24 << 20, transcendentals=0
        ),
        name="ffn_back",
    )(
        scalars,
        d_branch,
        inv_std,
        vectors,
        d_resid2,
        sums_mid,
        count,
        *attended,
        *(in_hbm(a) for a in (normed, slope, hidden, *packs)),
    )


def whole_call(kernel, name, args, outs, scalars=None, cost=SMALL_COST):
    return pl.pallas_call(
        kernel,
        out_shape=[o if hasattr(o, "memory_space") else jax.ShapeDtypeStruct(*o) for o in outs],
        in_specs=([] if scalars is None else [SMEM_SPEC]) + [VMEM_SPEC] * len(args),
        out_specs=[VMEM_SPEC] * len(outs),
        compiler_params=pltpu.CompilerParams(vmem_limit_bytes=SMALL_LIMIT),
        cost_estimate=cost,
        name=name,
    )(*(() if scalars is None else (scalars,)), *args)


def fold_cores(own, came):
    _, rows, cols = own.shape

    def kernel(own_ref, came_ref, *outs):
        for k, out in enumerate(outs):
            out[...] = (own_ref[k].astype(F32) + came_ref[k].astype(F32)).astype(BF16)

    outs = [pltpu.HBM((rows, cols), BF16)] * 4
    return whole_call(kernel, "fold_cores", (own, came), outs)


def split_cores(own, came):
    _, rows, cols = own.shape
    half = rows // 2

    def kernel(own_ref, came_ref, send_x, send_y, keep_upper, keep_lower):
        def total(upper, k):
            at = slice(0, half) if upper else slice(half, rows)
            return (own_ref[k, at, :].astype(F32) + came_ref[k, at, :].astype(F32)).astype(BF16)

        for i, k in enumerate((1, 3)):
            send_x[i] = total(True, k)
        for i, k in enumerate((2, 3)):
            send_y[i] = total(False, k)
        for i, k in enumerate((0, 2)):
            keep_upper[i] = total(True, k)
        for i, k in enumerate((0, 1)):
            keep_lower[i] = total(False, k)

    return whole_call(kernel, "split_cores", (own, came), [((2, half, cols), BF16)] * 4)


def second_step(keep_upper, came_x, keep_lower, came_y):
    def kernel(upper, upper_came, lower, lower_came, send_y, send_x, kept):
        half = upper.shape[1]
        send_y[...] = (upper[1].astype(F32) + upper_came[1].astype(F32)).astype(BF16)
        send_x[...] = (lower[1].astype(F32) + lower_came[1].astype(F32)).astype(BF16)
        kept[:half, :] = upper[0].astype(F32) + upper_came[0].astype(F32)
        kept[half:, :] = lower[0].astype(F32) + lower_came[0].astype(F32)

    half, cols = keep_upper.shape[1:]
    return whole_call(
        kernel,
        "second_step",
        (keep_upper, came_x, keep_lower, came_y),
        [((half, cols), BF16)] * 2 + [((2 * half, cols), F32)],
    )


def add_halves(kept, upper, lower):
    def kernel(kept, upper, lower, out):
        half = upper.shape[0]
        out[:half, :] = (kept[:half, :] + upper[...].astype(F32)).astype(BF16)
        out[half:, :] = (kept[half:, :] + lower[...].astype(F32)).astype(BF16)

    outs = [pltpu.HBM(kept.shape, BF16)]
    return whole_call(kernel, "add_halves", (kept, upper, lower), outs)[0]


def fold_quarters(terms, scalars):
    rows, cols = terms[0].shape
    part = rows // 4
    count = len(terms)

    def kernel(scalars, *refs):
        for k in range(4):
            at = pl.ds(pl.multiple_of((scalars[2] ^ k) * part, 8), part)
            total = sum(term[at, :].astype(F32) for term in refs[:count])
            refs[count + k % 2][k // 2] = total.astype(BF16)

    return whole_call(kernel, "fold_quarters", terms, [((2, part, cols), BF16)] * 2, scalars)


def finish(dense, qkv, half, block_col, scalars):
    _, part, cols = dense[0].shape
    qkv_part = qkv[0].shape[1]
    deep = block_col // 2

    def kernel(scalars, *refs):
        up, out, query, key, value, loss = refs[4:10]
        vectors, query_bias, value_bias = refs[10:17], refs[17], refs[18]
        dense_all, qkv_all = refs[19:]
        for parts, target in ((refs[:2], dense_all), (refs[2:4], qkv_all)):
            for k in range(4):
                piece = parts[k % 2].at[k // 2]
                rows = piece.shape[0]
                at = pl.ds(pl.multiple_of((scalars[2] ^ k) * rows, 8), rows)
                target[at, :] = piece[...].astype(F32)
        up[...] = dense_all[:half, :]
        out[:deep, :] = dense_all[half : half + deep, :half]
        out[deep:, :] = dense_all[half : half + deep, half:]
        table = dense_all[half + deep : half + deep + 16, :]
        for row, target in zip((6, 4, 5, 8, 2, 0, 1), vectors):
            target[...] = table[row, :]
        error = jnp.sum(table[3:4, :], axis=1, keepdims=True)
        tokens = jnp.sum(table[7:8, :], axis=1, keepdims=True)
        loss[...] = error / (tokens * cols)
        for i, target in enumerate((query, key, value)):
            target[...] = qkv_all[i * block_col : (i + 1) * block_col, :]
        bias = qkv_all[3 * block_col : 3 * block_col + 8, :]
        query_bias[...] = bias[0, :block_col]
        value_bias[...] = bias[0, block_col:]

    S = jax.ShapeDtypeStruct
    return pl.pallas_call(
        kernel,
        out_shape=[S((half, cols), F32), S((block_col, half), F32)]
        + [S((block_col, half), F32)] * 3
        + [S((1, 1), F32)]
        + [S((cols,), F32)] * 7
        + [S((block_col,), F32)] * 2,
        in_specs=[SMEM_SPEC] + [VMEM_SPEC] * 4,
        out_specs=[VMEM_SPEC] * 15,
        scratch_shapes=[
            pltpu.VMEM((4 * part, cols), F32),
            pltpu.VMEM((4 * qkv_part, half), F32),
        ],
        compiler_params=pltpu.CompilerParams(vmem_limit_bytes=SMALL_LIMIT),
        cost_estimate=SMALL_COST,
        name="finish",
    )(scalars, *dense, *qkv)


def dot(left, right, dims=NN):
    return lax.dot_general(left, right, dims, preferred_element_type=F32)


def split3(value):
    high = value.astype(BF16)
    rest = value - high.astype(F32)
    middle = rest.astype(BF16)
    low = (rest - middle.astype(F32)).astype(BF16)
    return high.astype(F32), middle.astype(F32), low.astype(F32)


def key_range(code, span, span_rows, blocks):
    per = span_rows // BLK
    first_seg = code[span * per, 0] // 2
    last_seg = code[span * per + per - 1, BLK - 1] // 2
    low = jnp.int32(0)
    high = jnp.int32(0)
    for other in range(blocks):
        start = code[other, 0]
        low += (code[other, BLK - 1] // 2 < first_seg).astype(jnp.int32)
        high += ((start // 2 <= last_seg) & (start % 2 == 1)).astype(jnp.int32)
    below = jnp.maximum(jnp.minimum(high, span * per) - low, 0)
    above = jnp.maximum(high - (span + 1) * per, 0)
    return low, below, below + above


def key_block(step, low, below, after):
    return jnp.where(step < below, low + step, after + step - below)


def lane_index(rows):
    return lax.broadcasted_iota(jnp.int32, (rows, 128), 1)


def allowed_block(code_rows, block, offset, span_rows):
    row = lax.broadcasted_iota(jnp.int32, (span_rows, BLK), 0)
    col = lax.broadcasted_iota(jnp.int32, (span_rows, BLK), 1)
    return (code_rows[pl.ds(block, 1), :] % 2 == 1) | (row == col + offset)


def attention_forward_kernel(heads, scalars, code, *refs):
    code_rows = refs[0]
    token_parts = refs[1:6]
    weights = refs[6:8]
    pieces = refs[8:12]
    saved = refs[12:16]
    padded, max_scr, acc_scr, query_pad, key_pad, value_pad, out_pad, whole_sem, span_sem = refs[16:]
    span_rows, width = token_parts[0].shape
    cols = 64 * heads
    flip = scalars[1]
    per = span_rows // BLK
    blocks = query_pad.shape[1] // BLK
    lane = lane_index(span_rows)
    for i in range(3):
        src = slice(i * cols, (i + 1) * cols)
        dst = slice(i * 256, i * 256 + cols)
        for second, half_weights in enumerate(weights):
            side = pl.ds(half_start(scalars, bool(second), width // 2), width // 2)
            padded[dst, side] = half_weights[src, :]
        padded[i * 256 + cols : (i + 1) * 256, :] = jnp.zeros((256 - cols, width), BF16)
    marks_bias = weights[0][3 * cols : 3 * cols + 1, :].astype(F32)
    no_bias = jnp.zeros((1, 256 - cols), F32)
    biases = (
        jnp.concatenate([marks_bias[:, :cols], no_bias], 1),
        None,
        jnp.concatenate([marks_bias[:, cols : 2 * cols], no_bias], 1),
    )
    first = 0
    for tokens in token_parts:
        rows = slice(first, first + tokens.shape[0])
        marks = []
        for block in range(rows.start // BLK, rows.stop // BLK):
            place = (block // per ^ flip) * per + block % per
            marks.append(
                jnp.broadcast_to(code_rows[pl.ds(place, 1), :].astype(F32), (128, BLK)).T
            )
        first = rows.stop
        lane = lane_index(tokens.shape[0])
        value_ones = jnp.where((lane >= 64) & (lane < 67), 1.0, 0.0)
        marks = jnp.concatenate(marks, 0).astype(jnp.int32)
        same = lane - 64 == marks // 2
        ids = (lane >= 64) & (lane < 80)
        query_marks = jnp.where((ids & same) | (lane == 80), 1.0, 0.0)
        key_marks = jnp.where(
            (ids & ~same) | ((lane == 80) & (marks % 2 == 0)),
            MASKED,
            jnp.where((lane >= 81) & (lane < 84), -1.0, 0.0),
        )
        for i, (out, extra) in enumerate(
            ((query_pad, query_marks), (key_pad, key_marks), (value_pad, value_ones))
        ):
            projected = dot(tokens[...], padded[i * 256 : (i + 1) * 256, :], NT)
            if biases[i] is not None:
                projected += biases[i]
            if i == 0:
                projected = projected.astype(BF16).astype(F32) * 0.125
            out[0, rows, :] = jnp.where(lane < 64, projected[:, :128], extra).astype(BF16)
            out[1, rows, :] = jnp.where(
                lane < 64, pltpu.roll(projected[:, :128], 64, 1), extra
            ).astype(BF16)
            out[2, rows, :] = jnp.where(lane < 64, projected[:, 128:], extra).astype(BF16)
    lane = lane_index(span_rows)
    no_valid_lane = jnp.where(lane == 80, 0.0, 1.0).astype(BF16)
    whole_copies = [
        pltpu.make_async_copy(key_pad, saved[1], whole_sem.at[0]),
        pltpu.make_async_copy(value_pad, saved[2], whole_sem.at[1]),
    ]
    for copy in whole_copies:
        copy.start()

    def span_copies(at):
        rows = pl.ds(pl.multiple_of(at * span_rows, span_rows), span_rows)
        return [
            pltpu.make_async_copy(
                source.at[:, rows, :], saved[i].at[:, rows, :], span_sem.at[i // 3, at]
            )
            for source, i in ((query_pad, 0), (out_pad, 3))
        ]

    def query_step(span, _):
        at = span ^ flip
        rows = pl.ds(pl.multiple_of(at * span_rows, span_rows), span_rows)
        low, below, count = key_range(code, span, span_rows, blocks)

        def keys_of(block):
            place = (block // per ^ flip) * per + block % per
            return pl.ds(pl.multiple_of(place * BLK, BLK), BLK)

        def scores_of(h, keys, allowed=None):
            if allowed is None:
                return dot(query_pad[h, rows, :], key_pad[h, keys, :], NT)
            scores = dot(query_pad[h, rows, :] * no_valid_lane, key_pad[h, keys, :], NT)
            return jnp.where(allowed, scores, MASKED)

        def each_block(visit):
            for part in range(per):
                block = span * per + part
                visit(keys_of(block), allowed_block(code_rows, block, part * BLK, span_rows))

            def step_fn(step, _):
                visit(keys_of(key_block(step, low, below, (span + 1) * per)), None)
                return 0

            lax.fori_loop(0, count, step_fn, 0)

        acc_scr[...] = jnp.zeros_like(acc_scr)
        max_scr[...] = jnp.zeros_like(max_scr)

        def plain(keys, allowed):
            for h in range(heads):
                probs = jnp.exp(scores_of(h, keys, allowed)).astype(BF16)
                acc_scr[h] += dot(probs, value_pad[h, keys, :])

        each_block(plain)
        least, most = jnp.float32(1.0), jnp.float32(1.0)
        for h in range(heads):
            total = jnp.where(lane == 64, acc_scr[h], 1.0)
            good = (total > 1e-25) & (total < 1e30)
            least = jnp.minimum(least, jnp.min(jnp.where(good, 1.0, 0.0)))

        @pl.when(least < 0.5)
        def _():
            max_scr[...] = jnp.full_like(max_scr, MASKED)

            def find_max(keys, allowed):
                for h in range(heads):
                    scores = scores_of(h, keys, allowed)
                    max_scr[h] = jnp.maximum(
                        max_scr[h], jnp.maximum(scores[:, :128], scores[:, 128:])
                    )

            each_block(find_max)
            for h in range(heads):
                max_scr[h] = jnp.broadcast_to(
                    jnp.max(max_scr[h], axis=1, keepdims=True), (span_rows, 128)
                )
            acc_scr[...] = jnp.zeros_like(acc_scr)

            def shifted(keys, allowed):
                for h in range(heads):
                    row_max = max_scr[h]
                    scores = scores_of(h, keys, allowed)
                    probs = jnp.exp(scores - jnp.concatenate([row_max, row_max], 1))
                    acc_scr[h] += dot(probs.astype(BF16), value_pad[h, keys, :])

            each_block(shifted)

        outs = []
        for h in range(heads):
            acc = acc_scr[h]
            total = jnp.broadcast_to(acc[:, 64:65], acc.shape)
            out = acc / total
            out_pad[h, rows, :] = out
            outs.append(out)
            high, middle, rest = split3(max_scr[h] + jnp.log(total))
            extra = jnp.where(
                lane == 81,
                high,
                jnp.where(lane == 82, middle, jnp.where(lane == 83, rest, 0.0)),
            )
            query_pad[h, rows, :] = query_pad[h, rows, :] + extra.astype(BF16)
        pair = jnp.where(lane < 64, outs[0], pltpu.roll(outs[1], 64, 1)).astype(BF16)
        middle = span_rows // 2
        last = jnp.where(
            lane_index(middle) < 64, outs[2][:middle], pltpu.roll(outs[2][middle:], 64, 1)
        ).astype(BF16)
        for k, piece in enumerate(pieces):

            @pl.when(at == k)
            def _():
                piece[:span_rows, :] = pair
                piece[span_rows:, :] = last

        for copy in span_copies(at):
            copy.start()
        return 0

    lax.fori_loop(0, len(pieces), query_step, 0)
    for copy in whole_copies:
        copy.wait()
    for at in range(len(pieces)):
        for copy in span_copies(at):
            copy.wait()


def attention_forward(scalars, code, token_shards, weights):
    rows, width = token_shards[0].shape
    length = code.shape[0] * BLK
    cols = (weights[0].shape[0] - PAD_ROWS) // 3
    heads = cols // 64
    S = jax.ShapeDtypeStruct
    flops = 2 * length * width * 3 * 256 + 3 * length * length * 128
    return pl.pallas_call(
        lambda *refs: attention_forward_kernel(heads, *refs),
        out_shape=[S((rows * cols // 128, 128), BF16)] * 4
        + [pltpu.HBM((heads, length, 128), BF16)] * 3
        + [pltpu.HBM((heads, length, 128), F32)],
        in_specs=[SMEM_SPEC] * 2 + [VMEM_SPEC] * 8,
        out_specs=[VMEM_SPEC] * 4 + [HBM_SPEC] * 4,
        scratch_shapes=[
            pltpu.VMEM((3 * 256, width), BF16),
            pltpu.VMEM((heads, rows, 128), F32),
            pltpu.VMEM((heads, rows, 128), F32),
        ]
        + [pltpu.VMEM((heads, length, 128), BF16)] * 3
        + [
            pltpu.VMEM((heads, length, 128), F32),
            pltpu.SemaphoreType.DMA((2,)),
            pltpu.SemaphoreType.DMA((2, 4)),
        ],
        compiler_params=pltpu.CompilerParams(vmem_limit_bytes=32 << 20),
        cost_estimate=pl.CostEstimate(
            flops=3 * flops, bytes_accessed=16 << 20, transcendentals=heads * length * 1024
        ),
        name="attention_forward",
    )(scalars, code, code, *token_shards, *weights)


def attention_backward_kernel(heads, scalars, code, *refs):
    code_rows = refs[0]
    span_rows = refs[1].shape[0] * 128 // (64 * heads)
    term_hbm, grad_hbm = refs[16:20], refs[20:22]
    grad_pad, query_sum, key_sum, value_sum, low_scr, grad_scr, bias_sum = refs[22:29]
    query_pad, key_pad, value_pad, out_pad = refs[29:33]
    shards_in = refs[33:37]
    weights = refs[37]
    grads = refs[38:42]
    terms, own_grad, other_grad, out_sems, in_sems = refs[42:]
    side = weights.shape[1] // 2
    last_half = span_rows // 2
    pairs = list(zip(refs[1:9], grads + refs[29:33]))
    pairs += list(zip(refs[9:12], shards_in[:3]))
    pairs += [
        (refs[12], shards_in[3].at[:last_half, :]),
        (refs[13], shards_in[3].at[last_half:, :]),
    ]
    sides = [pl.ds(half_start(scalars, second, side), side) for second in (False, True)]
    pairs += [(refs[14 + i], weights.at[:, sides[i]]) for i in range(2)]
    copies = [
        pltpu.make_async_copy(source, target, in_sems.at[i])
        for i, (source, target) in enumerate(pairs)
    ]
    for i in (7, 0, 1, 2, 3, 4, 5, 6):
        copies[i].start()
    key_sum[...] = jnp.zeros_like(key_sum)
    value_sum[...] = jnp.zeros_like(value_sum)
    query_sum[...] = jnp.zeros_like(query_sum)
    for i in (7, 0, 1, 2, 3):
        copies[i].wait()
    flip = scalars[1]
    per = span_rows // BLK
    blocks = query_pad.shape[1] // BLK
    lane = lane_index(span_rows)
    for shard, grad in enumerate(grads):
        rows = slice(shard * span_rows, (shard + 1) * span_rows)
        pair = grad[:span_rows, :].astype(F32)
        last = grad[span_rows:, :].astype(F32)
        last = jnp.concatenate([last, pltpu.roll(last, 64, 1)], 0)
        for h, block in enumerate((pair, pltpu.roll(pair, 64, 1), last)):
            block = jnp.where(lane < 64, block, 0.0)
            delta = jnp.sum(block * out_pad[h, rows, :], axis=1, keepdims=True)
            high, middle, rest = split3(-delta)
            block = jnp.where(
                lane == 64,
                high,
                jnp.where(lane == 65, middle, jnp.where(lane == 66, rest, block)),
            )
            grad_pad[h, rows, :] = block.astype(BF16)
    for i in (4, 5, 6):
        copies[i].wait()
    for i in range(8, 15):
        copies[i].start()
    no_valid_lane = jnp.where(lane == 80, 0.0, 1.0).astype(BF16)

    def query_step(span, _):
        at = span ^ flip
        rows = pl.ds(pl.multiple_of(at * span_rows, span_rows), span_rows)
        low, below, count = key_range(code, span, span_rows, blocks)

        def visit(block, allowed):
            place = (block // per ^ flip) * per + block % per
            keys = pl.ds(pl.multiple_of(place * BLK, BLK), BLK)
            for h in range(heads):
                query, grad = query_pad[h, rows, :], grad_pad[h, rows, :]
                key, value = key_pad[h, keys, :], value_pad[h, keys, :]
                if allowed is None:
                    scores = dot(key, query, NT)
                else:
                    scores = jnp.where(allowed, dot(key, query * no_valid_lane, NT), MASKED)
                probs = jnp.exp(scores)
                d_scores = (probs * dot(value, grad, NT)).astype(BF16)
                value_sum[h, keys, :] += dot(probs.astype(BF16), grad)
                key_sum[h, keys, :] += dot(d_scores, query)
                query_sum[h, rows, :] += dot(d_scores, key, TN)

        for part in range(per):
            block = span * per + part
            key_at = lax.broadcasted_iota(jnp.int32, (BLK, span_rows), 0)
            query_at = lax.broadcasted_iota(jnp.int32, (BLK, span_rows), 1)
            marks = jnp.broadcast_to(
                code_rows[pl.ds(block, 1), :].astype(F32), (128, BLK)
            ).T.astype(jnp.int32)
            valid = jnp.concatenate([marks] * (span_rows // 128), 1) % 2 == 1
            visit(block, valid | (query_at == key_at + part * BLK))

        def step_fn(step, _):
            visit(key_block(step, low, below, (span + 1) * per), None)
            return 0

        lax.fori_loop(0, count, step_fn, 0)
        return 0

    lax.fori_loop(0, len(grads), query_step, 0)
    for i in range(8, 15):
        copies[i].wait()
    bias_sum[...] = jnp.zeros_like(bias_sum)
    stores = []
    for shard in range(len(grads)):
        rows = slice(shard * span_rows, (shard + 1) * span_rows)
        parts = [query_sum[h, rows, :] * 0.125 for h in range(heads)]
        parts += [sums[h, rows, :] for sums in (key_sum, value_sum) for h in range(heads)]
        for at in range(0, len(parts), 2):
            if at + 1 < len(parts):
                value = jnp.where(lane < 64, parts[at], pltpu.roll(parts[at + 1], 64, 1))
            else:
                value = parts[at][:, :64]
            low = value.astype(BF16)
            cols = slice(at * 64, at * 64 + low.shape[1])
            low_scr[:, cols] = low
            bias_sum[0:1, cols] += column_sum(low.astype(F32))
        low = low_scr[...]
        depth = low.shape[1]
        term = dot(low, weights[:depth, :]).astype(BF16)
        terms[shard] = term
        copy = pltpu.make_async_copy(
            terms.at[shard], term_hbm[shard], out_sems.at[shard]
        )
        copy.start()
        stores.append(copy)
        part = dot(low, shards_in[shard][...], TN)
        if shard == 0:
            grad_scr[...] = part
        elif shard < 3:
            grad_scr[...] += part
        else:
            grad_scr[...] += part
            own_grad[:depth, :] = grad_scr[:, sides[0]].astype(BF16)
            other_grad[:depth, :] = grad_scr[:, sides[1]].astype(BF16)
    cols = heads * 64
    bias = jnp.concatenate([bias_sum[:, 0:cols], bias_sum[:, 2 * cols :]], 1).astype(BF16)
    bias = jnp.concatenate([bias] * ((own_grad.shape[0] - depth) // bias.shape[0]), 0)
    own_grad[depth:, :] = bias
    other_grad[depth:, :] = bias
    for i, source in enumerate((own_grad, other_grad)):
        copy = pltpu.make_async_copy(source, grad_hbm[i], out_sems.at[4 + i])
        copy.start()
        stores.append(copy)
    for copy in stores:
        copy.wait()


def attention_backward(scalars, code, grads, saved, token_shards, weights):
    length = code.shape[0] * BLK
    heads = saved[0].shape[0]
    rows, width = token_shards[0].shape
    cols = 3 * heads * 64
    S = jax.ShapeDtypeStruct
    return pl.pallas_call(
        lambda *refs: attention_backward_kernel(heads, *refs),
        out_shape=[
            *[pltpu.HBM((rows, width), BF16)] * 4,
            *[pltpu.HBM((cols + GRAD_PAD, width // 2), BF16)] * 2,
        ],
        in_specs=[SMEM_SPEC] * 2 + [VMEM_SPEC] + [HBM_SPEC] * 15,
        out_specs=[HBM_SPEC] * 6,
        scratch_shapes=[
            pltpu.VMEM((heads, length, 128), BF16),
            pltpu.VMEM((heads, length, 128), F32),
            pltpu.VMEM((heads, length, 128), F32),
            pltpu.VMEM((heads, length, 128), F32),
            pltpu.VMEM((rows, cols), BF16),
            pltpu.VMEM((cols, width), F32),
            pltpu.VMEM((16, cols), F32),
        ]
        + [pltpu.VMEM(a.shape, a.dtype) for a in saved]
        + [pltpu.VMEM((rows, width), BF16)] * 4
        + [pltpu.VMEM((weights[0].shape[0], width), BF16)]
        + [pltpu.VMEM(a.shape, a.dtype) for a in grads]
        + [
            pltpu.VMEM((4, rows, width), BF16),
            pltpu.VMEM((cols + GRAD_PAD, width // 2), BF16),
            pltpu.VMEM((cols + GRAD_PAD, width // 2), BF16),
            pltpu.SemaphoreType.DMA((6,)),
            pltpu.SemaphoreType.DMA((15,)),
        ],
        compiler_params=pltpu.CompilerParams(vmem_limit_bytes=46 << 20),
        cost_estimate=pl.CostEstimate(
            flops=heads * length * length * 1500, bytes_accessed=8 << 20, transcendentals=0
        ),
        name="attention_backward",
    )(
        scalars,
        code,
        code,
        *(in_hbm(a) for a in (*grads, *saved, *token_shards, *weights)),
    )


CHIP = [[(c, c ^ k) for c in range(4)] for k in range(4)]
PLANE = [[(p, p ^ k) for p in range(4)] for k in range(4)]
CORE = [(0, 1), (1, 0)]


def to_chip(value, k):
    return lax.ppermute(value, "gz", CHIP[k])


def to_core(value):
    return lax.ppermute(value, "gy", CORE)


def to_plane(value, k):
    return lax.ppermute(value, "gx", PLANE[k])


def after(value, *others):
    return lax.optimization_barrier((value,) + others)[0]


def swap_halves(flip, value):
    half = value.shape[-1] // 2
    swapped = jnp.concatenate([value[..., half:], value[..., :half]], -1)
    return jnp.where(flip, swapped, value)


def add_low(left, right):
    return (left.astype(F32) + right.astype(F32)).astype(BF16)


def sum_planes(dense, qkv, waits):
    if lax.axis_size("gx") != 4:
        dense, other = jnp.stack(dense), jnp.stack(qkv(dense[0]))
        total = lax.psum((dense, other), "gx")
        return [(t[0], t[1]) for t in total], waits
    near = dense[0].astype(F32) + to_plane(dense[1], 1).astype(F32)
    step = near[1].astype(BF16)
    keep, send = qkv(step)
    total = (near[0] + to_plane(step, 2).astype(F32)).astype(BF16)
    near = keep.astype(F32) + to_plane(send, 1).astype(F32)
    step = after(near[1].astype(BF16), total)
    pair = jnp.stack([total, to_plane(total, 2)])
    other = (near[0] + to_plane(step, 2).astype(F32)).astype(BF16)
    other = after(other, pair)
    back = to_plane(pair, 1)
    other_pair = jnp.stack([other, to_plane(other, 2)])
    other_back = to_plane(other_pair, 1)
    *waits, back = lax.optimization_barrier((*waits, back))
    return [(pair, back), (other_pair, other_back)], waits


def shards(
    tokens,
    segment_ids,
    valid_mask,
    cotangent,
    teacher,
    w_query,
    b_query,
    w_key,
    w_value,
    b_value,
    w_out,
    b_out,
    norm1_gain,
    norm1_bias,
    w_up,
    b_up,
    w_down,
    b_down,
    norm2_gain,
    norm2_bias,
):
    row_count, width = tokens.shape
    half = width // 2
    core = lax.axis_index("gy")
    chip = lax.axis_index("gz")
    flip = core == 1
    block_col = w_query.shape[1]
    hidden_col = w_up.shape[1]
    plane = lax.axis_index("gx") if lax.axis_size("gx") == 4 else jnp.int32(0)
    scalars = jnp.stack([core, chip, plane, chip]).astype(jnp.int32)

    own_tokens = tokens
    along_x, along_y = to_chip(own_tokens, 1), to_chip(own_tokens, 2)
    code = (segment_ids * 2 + valid_mask).reshape(-1, BLK)
    bias_row = jnp.concatenate([b_query, b_value])[None, :]
    qkv_own = jnp.concatenate(
        [w_query.T, w_key.T, w_value.T, jnp.broadcast_to(bias_row, (PAD_ROWS, half))], 0
    )
    vectors = jnp.stack([b_out, norm1_gain, norm1_bias, b_down, norm2_gain, norm2_bias] + [b_out] * 2)
    vectors = swap_halves(flip, vectors.astype(F32))
    own_valid = lax.dynamic_slice_in_dim(valid_mask, chip * row_count, row_count, 1).astype(F32)
    count = jnp.concatenate([own_valid, jnp.zeros((1, width - row_count), F32)], 1)
    count = jnp.broadcast_to(count, (8, width))
    own_valid = own_valid.T
    packed = jnp.concatenate(
        [
            jnp.concatenate([w_down[: hidden_col // 2], w_down[hidden_col // 2 :]], 1),
            w_up,
            jnp.concatenate([w_out[: block_col // 2], w_out[block_col // 2 :]], 1),
            jnp.broadcast_to(b_up[None, :], (PAD_ROWS, hidden_col)),
        ],
        0,
    )

    code, qkv_own, scalars, packed, vectors, own_valid, count, *_ = lax.optimization_barrier(
        (code, qkv_own, scalars, packed, vectors, own_valid, count, own_tokens)
    )
    qkv = (qkv_own, to_core(qkv_own))
    along_x, along_y, *qkv = lax.optimization_barrier((along_x, along_y, *qkv))
    middle = row_count // 2
    far = (to_chip(along_x[:middle], 2), to_chip(along_y[middle:], 1))
    token_shards = (own_tokens, along_x, along_y, *far)
    packed = after(packed, *far)
    pack_x, pack_y = to_chip(packed, 1), to_chip(packed, 2)

    scalars = after(scalars, packed)
    results = attention_forward(scalars, code, token_shards, qkv)
    saved = results[4:]
    attended = [results[0]] + [to_chip(results[k], k) for k in (1, 2, 3)]

    deep = hidden_col // 2
    pack_x, pack_y = lax.optimization_barrier((pack_x, pack_y, results[0]))[:2]
    far = (pack_x[:, :half], pack_y[:, half:])
    packed_late = after(packed, *far)
    far = (to_chip(far[0], 2), to_chip(far[1], 1))
    packs = (packed, pack_x, pack_y, *far)
    packs += (to_core(packed_late), *(to_core(after(v, *attended[1:])) for v in packs[1:]))

    inv_std, output, d_resid2, d_branch, sums_mid, act, normed, hidden_low, slope = ffn_forward(
        scalars, attended, own_tokens, own_valid, vectors, cotangent, teacher, packs, deep
    )
    pieces = (4, hidden_col, half)
    d_down_other = jnp.einsum("lf,lm->fm", act, d_branch[:, half:], preferred_element_type=F32)
    d_down_came = to_core(d_down_other.astype(BF16).reshape(pieces))
    d_down = jnp.einsum("lf,lm->fm", act, d_branch[:, :half], preferred_element_type=F32)
    down_x, down_y, down_upper, down_lower = split_cores(
        d_down.astype(BF16).reshape(pieces), d_down_came
    )
    d_branch = after(d_branch, down_upper)
    down_x, down_y = to_chip(down_x, 1), to_chip(down_y, 2)
    d_resid1, *back, own_grads, other_grads = ffn_back(
        scalars,
        d_branch,
        inv_std,
        vectors,
        d_resid2,
        sums_mid,
        count,
        attended,
        normed,
        slope,
        hidden_low,
        packs,
        deep,
    )
    d_pieces = [back[0]] + [to_chip(back[k], k) for k in (1, 2, 3)]

    down_y, down_x, down_kept = second_step(down_upper, down_x, down_lower, down_y)
    d_dense = fold_cores(own_grads, to_core(after(other_grads, down_y)))
    down_total = add_halves(down_kept, to_chip(down_y, 2), to_chip(down_x, 1))
    grad_down = lax.psum(down_total, "gx")
    d_pieces[0] = after(d_pieces[0], d_dense[0], down_total)
    d_dense = [d_dense[0]] + [to_chip(d_dense[k], k) for k in (1, 2, 3)]

    *terms, d_own, d_other = attention_backward(
        scalars, code, d_pieces, saved, token_shards, qkv
    )
    d_dense[0] = after(d_dense[0], grad_down, terms[0])
    quarters = fold_quarters(d_dense, scalars)
    d_own, d_other, *terms, _, _ = lax.optimization_barrier((d_own, d_other, *terms, *quarters))
    d_w = (d_own, to_core(d_other))
    terms = [terms[0]] + [to_chip(terms[k], k) for k in (1, 2, 3)]
    (dense_grad, qkv_grad), came = sum_planes(
        quarters, lambda first: fold_quarters(d_w, scalars), terms[1:]
    )
    d_tokens = d_resid1 + sum(t.astype(F32) for t in (terms[0], *came))
    grad_up, grad_out, grad_query, grad_key, grad_value, loss, *vectors = finish(
        dense_grad, qkv_grad, half, block_col, scalars
    )
    b_out_grad, gain1_grad, shift1_grad, b_up_grad, b_down_grad, gain2_grad, shift2_grad = vectors[:7]

    return (
        output,
        loss[0, 0],
        d_tokens.astype(BF16),
        grad_query.T,
        vectors[7],
        grad_key.T,
        grad_value.T,
        vectors[8],
        grad_out,
        b_out_grad,
        gain1_grad,
        shift1_grad,
        grad_up,
        b_up_grad,
        grad_down.astype(F32),
        b_down_grad,
        gain2_grad,
        shift2_grad,
    )


def solution(mesh):
    placed = (
        P(("gx", "gy", "gz"), None),
        P(("gx", "gy"), None),
        P(("gx", "gy"), None),
        P(("gx", "gy", "gz"), None),
        P(("gx", "gy", "gz"), None),
        P("gy", "gz"),
        P("gz"),
        P("gy", "gz"),
        P("gy", "gz"),
        P("gz"),
        P("gz", "gy"),
        P(),
        P(),
        P(),
        P("gy", "gz"),
        P("gz"),
        P("gz", "gy"),
        P(),
        P(),
        P(),
    )
    return jax.shard_map(
        shards,
        mesh=mesh,
        in_specs=placed,
        out_specs=(
            P(("gx", "gy", "gz"), None),
            P(),
            P(("gx", "gy", "gz"), None),
            P("gy", "gz"),
            P("gz"),
            P("gy", "gz"),
            P("gy", "gz"),
            P("gz"),
            P("gz", "gy"),
            P(),
            P(),
            P(),
            P("gy", "gz"),
            P("gz"),
            P("gz", "gy"),
            P(),
            P(),
            P(),
        ),
        check_vma=False,
    )
```

```python
import math

import jax
import jax.numpy as jnp
from jax import lax
from jax.experimental import pallas as pl
from jax.experimental.pallas import tpu as pltpu
from jax.sharding import PartitionSpec as P

EPSILON = 1e-05
MASKED = -1e30
PAD_ROWS = 16
GRAD_PAD = 32
BLK = 256
F32 = jnp.float32
BF16 = jnp.bfloat16
NT = (((1,), (1,)), ((), ()))
NN = (((1,), (0,)), ((), ()))
TN = (((0,), (0,)), ((), ()))


VMEM_SPEC = pl.BlockSpec(memory_space=pltpu.VMEM)
SMEM_SPEC = pl.BlockSpec(memory_space=pltpu.SMEM)
HBM_SPEC = pl.BlockSpec(memory_space=pltpu.HBM)
VMEM_LIMIT = 24 << 20
SMALL_LIMIT = 20 << 20
FFN_LIMIT = 40 << 20
SMALL_COST = pl.CostEstimate(flops=1 << 16, bytes_accessed=1 << 12, transcendentals=0)


def in_hbm(array):
    return pltpu.with_memory_space_constraint(array, pltpu.HBM)


class Loads:
    def __init__(self, packs, sems):
        self.packs, self.sems, self.used, self.groups = packs, sems, 0, {}

    def add(self, group, source, target):
        copy = pltpu.make_async_copy(source, target, self.sems.at[self.used])
        self.used += 1
        self.groups.setdefault(group, []).append(copy)

    def start(self, *groups):
        for group in groups:
            for copy in self.groups.get(group, ()):
                copy.start()

    def wait(self, *groups):
        for group in groups:
            for copy in self.groups.get(group, ()):
                copy.wait()

    def blocks(self, core):
        packs = self.packs[5 * core : 5 * core + 5]
        half = packs[4].shape[1]
        blocks = [(k, i, packs[k], i * half) for k in range(3) for i in range(2)]
        return half, blocks + [(3, 0, packs[3], 0), (3, 1, packs[4], 0)]

    def lay_out(self, deep, block_col, up_full, down_full, out_full, bias_full):
        for core in range(2):
            half, blocks = self.blocks(core)
            top = deep + half
            out_deep = block_col // 2
            side = slice(core * half, (core + 1) * half)
            for k, i, pack, col in blocks:
                cols = slice(col, col + half)
                hidden = slice((2 * k + i) * half, (2 * k + i + 1) * half)
                self.add(("up", k), pack.at[deep:top, cols], up_full.at[side, hidden])
                self.add(("down", k), pack.at[0:deep, cols], down_full.at[hidden, side])
                first = k * block_col + i * out_deep
                self.add(
                    "out",
                    pack.at[top : top + out_deep, cols],
                    out_full.at[first : first + out_deep, side],
                )
                if core == 0 and bias_full is not None:
                    low = top + out_deep
                    self.add("out", pack.at[low : low + PAD_ROWS, cols], bias_full.at[:, hidden])


def half_start(scalars, second, half):
    flip = scalars[0]
    return pl.multiple_of(jnp.where(second, 1 - flip, flip) * half, 128)


def read_swapped(ref, scalars):
    half = ref.shape[-1] // 2
    return jnp.concatenate(
        [
            ref[:, pl.ds(half_start(scalars, False, half), half)].astype(F32),
            ref[:, pl.ds(half_start(scalars, True, half), half)].astype(F32),
        ],
        1,
    )


def write_swapped(ref, rows, value, scalars):
    half = ref.shape[-1] // 2
    ref[rows, pl.ds(half_start(scalars, False, half), half)] = value[:, :half].astype(ref.dtype)
    ref[rows, pl.ds(half_start(scalars, True, half), half)] = value[:, half:].astype(ref.dtype)


def column_sum(value):
    return jnp.sum(value, 0, keepdims=True)


def layer_norm(resid):
    average = jnp.mean(resid, -1, keepdims=True)
    centered = resid - average
    inv_std = lax.rsqrt(jnp.mean(centered * centered, -1, keepdims=True) + EPSILON)
    return centered * inv_std, inv_std


def layer_norm_back(upstream, gain, normed, inv_std):
    scaled = upstream * gain
    return inv_std * (
        scaled
        - jnp.mean(scaled, -1, keepdims=True)
        - normed * jnp.mean(scaled * normed, -1, keepdims=True)
    )


def unpack_heads(packed, target):
    rows = target.shape[0]
    middle = rows // 2
    last = packed[rows:, :].astype(F32)
    target[:, 0:128] = packed[:rows, :]
    target[:middle, 128:] = last[:, :64].astype(BF16)
    target[middle:, 128:] = pltpu.roll(last, 64, 1)[:, :64].astype(BF16)


def ffn_forward_kernel(deep, scalars, *refs):
    att = refs[:4]
    own_tokens, valid, vectors = refs[4:7]
    cot_source, teach_source = refs[7:9]
    packs = refs[9:19]
    std_out, output, resid_out, branch_out, sums, act_out = refs[19:25]
    normed_hbm, low_hbm, slope_hbm = refs[25:28]
    up_full, down_full, out_full, bias_full = refs[28:32]
    cotangent, teacher, normed_out, low_out, slope_out, heads = refs[32:38]
    sems, row_sems, chunk_sems = refs[38:]
    width = own_tokens.shape[1]
    block_col = width // 4
    loads = Loads(packs, sems)
    loads.lay_out(deep, block_col, up_full, down_full, out_full, bias_full)
    row_loads = [
        pltpu.make_async_copy(cot_source, cotangent, row_sems.at[0]),
        pltpu.make_async_copy(teach_source, teacher, row_sems.at[1]),
    ]
    loads.start("out", ("up", 0))
    for k in range(4):
        unpack_heads(att[k], heads.at[k])
    loads.wait("out")
    loads.start(("down", 0), ("up", 1))
    mixed = jnp.zeros(own_tokens.shape, F32)
    for k in range(4):
        mixed += dot(heads[k], out_full[k * block_col : (k + 1) * block_col, :])
    resid = read_swapped(own_tokens, scalars) + (mixed + vectors[0:1, :])
    normed, inv_std = layer_norm(resid)
    hidden = normed * vectors[1:2, :] + vectors[2:3, :]
    normed_out[...] = normed
    std_out[...] = inv_std
    low_out[...] = hidden.astype(BF16)
    stores = [
        pltpu.make_async_copy(normed_out, normed_hbm, row_sems.at[2]),
        pltpu.make_async_copy(low_out, low_hbm, row_sems.at[3]),
    ]
    for copy in stores:
        copy.start()
    branch = jnp.zeros(own_tokens.shape, F32)
    for k in range(4):
        loads.wait(("up", k))
        loads.start(("down", k + 1), ("up", k + 2))
        if k == 2:
            for copy in row_loads:
                copy.start()
        place = slice(k * width, (k + 1) * width)
        preact = dot(low_out[...], up_full[:, place]) + bias_full[0:1, place].astype(F32)
        normal_cdf = 0.5 * (1.0 + lax.erf(preact * (1.0 / math.sqrt(2.0))))
        slope = normal_cdf + preact * jnp.exp(-0.5 * preact * preact) * (
            1.0 / math.sqrt(2.0 * math.pi)
        )
        act = (preact * normal_cdf).astype(BF16)
        act_out[:, place] = act
        slope_out[:, place] = slope.astype(BF16)
        copy = pltpu.make_async_copy(
            slope_out.at[:, place], slope_hbm.at[:, place], chunk_sems.at[k]
        )
        copy.start()
        stores.append(copy)
        loads.wait(("down", k))
        branch += dot(act, down_full[place, :])
    for copy in row_loads:
        copy.wait()
    gain = vectors[4:5, :]
    hidden = normed_out[...] * vectors[1:2, :] + vectors[2:3, :]
    resid = hidden + (branch + vectors[3:4, :])
    normed, inv_std = layer_norm(resid)
    full = normed * gain + vectors[5:6, :]
    write_swapped(output, slice(None), full, scalars)
    mismatch = full - read_swapped(teacher, scalars)
    masked = valid[...] * mismatch
    d_output = read_swapped(cotangent, scalars) + masked
    d_resid = layer_norm_back(d_output, gain, normed, inv_std)
    resid_out[...] = d_resid
    low = d_resid.astype(BF16)
    branch_out[...] = low
    sums[...] = jnp.zeros_like(sums)
    rows = (
        column_sum(d_output * normed),
        column_sum(d_output),
        column_sum(low.astype(F32)),
        column_sum(masked * mismatch),
    )
    for at, row in enumerate(rows):
        write_swapped(sums, slice(at, at + 1), row, scalars)
    for copy in stores:
        copy.wait()


def full_scratch(width, inner, block_col):
    return [
        pltpu.VMEM((width, inner), BF16),
        pltpu.VMEM((inner, width), BF16),
        pltpu.VMEM((4 * block_col, width), BF16),
    ]


def ffn_forward(scalars, attended, own_tokens, valid, vectors, cotangent, teacher, packs, deep):
    rows, width = own_tokens.shape
    inner = 4 * width
    full = (rows, width)
    S = jax.ShapeDtypeStruct
    return pl.pallas_call(
        lambda *refs: ffn_forward_kernel(deep, *refs),
        out_shape=[S((rows, 1), F32), S(full, BF16), S(full, F32), S(full, BF16)]
        + [S((8, width), F32), S((rows, inner), BF16)]
        + [pltpu.HBM(full, F32), pltpu.HBM(full, BF16), pltpu.HBM((rows, inner), BF16)],
        in_specs=[SMEM_SPEC] + [VMEM_SPEC] * 7 + [HBM_SPEC] * 12,
        out_specs=[VMEM_SPEC] * 6 + [HBM_SPEC] * 3,
        scratch_shapes=full_scratch(width, inner, width // 4)
        + [pltpu.VMEM((PAD_ROWS, inner), BF16)]
        + [pltpu.VMEM(full, BF16)] * 2
        + [pltpu.VMEM(full, F32), pltpu.VMEM(full, BF16), pltpu.VMEM((rows, inner), BF16)]
        + [pltpu.VMEM((4, rows, width // 4), BF16)]
        + [
            pltpu.SemaphoreType.DMA((56,)),
            pltpu.SemaphoreType.DMA((4,)),
            pltpu.SemaphoreType.DMA((4,)),
        ],
        compiler_params=pltpu.CompilerParams(vmem_limit_bytes=FFN_LIMIT),
        cost_estimate=pl.CostEstimate(
            flops=10 * rows * width * inner, bytes_accessed=24 << 20, transcendentals=0
        ),
        name="ffn_forward",
    )(
        scalars,
        *attended,
        own_tokens,
        valid,
        vectors,
        *(in_hbm(a) for a in (cotangent, teacher, *packs)),
    )


def ffn_back_kernel(deep, scalars, *refs):
    d_branch, std_ref, vectors, d_resid2, sums_mid, count = refs[:6]
    att = refs[6:10]
    normed_source, slope_source, hidden_source = refs[10:13]
    packs = refs[13:23]
    resid_hbm = refs[23]
    piece_hbm = refs[24:28]
    own_hbm, other_hbm = refs[28:30]
    up_full, down_full, out_full = refs[30:33]
    normed_ref, slope, hidden, flipped, own, other, sums, resid_out = refs[33:41]
    pieces = refs[41:45]
    heads = refs[45]
    sems, row_sem, chunk_sems, grad_sems, out_sems = refs[46:]
    rows_here, width = d_branch.shape
    half = width // 2
    block_col = width // 4
    out_deep = block_col // 2
    loads = Loads(packs, sems)
    loads.lay_out(deep, block_col, up_full, down_full, out_full, None)
    normed_load = pltpu.make_async_copy(normed_source, normed_ref, row_sem.at[0])
    hidden_load = pltpu.make_async_copy(hidden_source, hidden, row_sem.at[1])
    slopes = []
    for k in range(4):
        place = slice(k * width, (k + 1) * width)
        slopes.append(
            pltpu.make_async_copy(slope_source.at[:, place], slope.at[:, place], chunk_sems.at[k])
        )
    stores = []

    def store(i, source, target, k, rows):
        copy = pltpu.make_async_copy(
            source.at[k, rows, :], target.at[k, rows, :], grad_sems.at[i, len(stores) // 2]
        )
        copy.start()
        stores.append(copy)

    loads.start(("down", 0))
    hidden_load.start()
    slopes[0].start()
    loads.start(("up", 0), ("down", 1))
    sums[...] = jnp.zeros_like(sums)
    for k in range(4):
        unpack_heads(att[k], heads.at[k])
    hidden_load.wait()
    flipped[...] = hidden[...].astype(F32).T.astype(BF16)
    d_hidden = d_resid2[...]
    for k in range(4):
        loads.wait(("down", k))
        loads.start(("up", k + 1), ("down", k + 2))
        if k < 3:
            slopes[k + 1].start()
        else:
            normed_load.start()
            loads.start("out")
        place = slice(k * width, (k + 1) * width)
        d_act = dot(d_branch[...], down_full[place, :], NT)
        slopes[k].wait()
        d_pre = (d_act * slope[:, place].astype(F32)).astype(BF16)
        sums[4 + k : 5 + k, :] = column_sum(d_pre.astype(F32))
        loads.wait(("up", k))
        d_hidden += dot(d_pre, up_full[:, place], NT)
        grad = dot(flipped[...], d_pre).astype(BF16)
        own[k, 0:half, :] = grad[:half, :]
        other[k, 0:half, :] = grad[half:, :]
        store(0, other, other_hbm, k, slice(0, half))
        store(1, own, own_hbm, k, slice(0, half))
    normed_load.wait()
    normed = normed_ref[...]
    d_resid = layer_norm_back(d_hidden, vectors[1:2, :], normed, std_ref[...])
    write_swapped(resid_out, slice(None), d_resid, scalars)
    out_copies = [pltpu.make_async_copy(resid_out, resid_hbm, out_sems.at[4])]
    out_copies[0].start()
    mixed = d_resid.astype(BF16)
    loads.wait("out")
    for k in range(4):
        rows = slice(k * block_col, (k + 1) * block_col)
        piece = dot(mixed, out_full[rows, :], NT).astype(BF16)
        middle = rows_here // 2
        pieces[k][:rows_here, :] = piece[:, :128]
        pieces[k][rows_here:, :] = jnp.concatenate(
            [piece[:middle, 128:], piece[middle:, 128:]], 1
        )
        copy = pltpu.make_async_copy(pieces[k], piece_hbm[k], out_sems.at[k])
        copy.start()
        out_copies.append(copy)
    for at, row in enumerate(
        (column_sum(d_hidden * normed), column_sum(d_hidden), column_sum(mixed.astype(F32)))
    ):
        write_swapped(sums, slice(at, at + 1), row, scalars)
    for k in range(4):
        out_grad = dot(heads[k], mixed, TN)
        low = half + out_deep
        table = jnp.concatenate(
            [
                sums_mid[0:4, :],
                sums[0:3, :],
                count[0:1, :],
                sums[4 + k : 5 + k, :],
                jnp.zeros((own.shape[1] - low - 9, own.shape[2]), F32),
            ],
            0,
        ).astype(BF16)
        for i, target in enumerate((own, other)):
            part = out_grad[:, i * half : (i + 1) * half].astype(BF16)
            target[k, half:low, 0:half] = part[:out_deep, :]
            target[k, half:low, half:] = part[out_deep:, :]
            target[k, low:, :] = table
        store(0, other, other_hbm, k, slice(half, own.shape[1]))
        store(1, own, own_hbm, k, slice(half, own.shape[1]))
    for copy in stores + out_copies:
        copy.wait()


def ffn_back(
    scalars, d_branch, inv_std, vectors, d_resid2, sums_mid, count, attended, normed, slope, hidden, packs, deep
):
    rows, width = d_branch.shape
    inner = 4 * width
    full = (rows, width)
    block_col = width // 4
    grads = ((4, width // 2 + 128, width), BF16)
    S = jax.ShapeDtypeStruct
    return pl.pallas_call(
        lambda *refs: ffn_back_kernel(deep, *refs),
        out_shape=[pltpu.HBM(full, F32)]
        + [pltpu.HBM(attended[0].shape, BF16)] * 4
        + [pltpu.HBM(*grads)] * 2,
        in_specs=[SMEM_SPEC] + [VMEM_SPEC] * 10 + [HBM_SPEC] * 13,
        out_specs=[HBM_SPEC] * 7,
        scratch_shapes=full_scratch(width, inner, block_col)
        + [pltpu.VMEM(full, F32), pltpu.VMEM((rows, inner), BF16), pltpu.VMEM(full, BF16)]
        + [pltpu.VMEM((width, rows), BF16)]
        + [pltpu.VMEM(*grads)] * 2
        + [pltpu.VMEM((8, width), F32), pltpu.VMEM(full, F32)]
        + [pltpu.VMEM(attended[0].shape, BF16)] * 4
        + [pltpu.VMEM((4, rows, block_col), BF16)]
        + [
            pltpu.SemaphoreType.DMA((48,)),
            pltpu.SemaphoreType.DMA((2,)),
            pltpu.SemaphoreType.DMA((4,)),
            pltpu.SemaphoreType.DMA((2, 8)),
            pltpu.SemaphoreType.DMA((5,)),
        ],
        compiler_params=pltpu.CompilerParams(vmem_limit_bytes=FFN_LIMIT),
        cost_estimate=pl.CostEstimate(
            flops=10 * rows * width * inner, bytes_accessed=24 << 20, transcendentals=0
        ),
        name="ffn_back",
    )(
        scalars,
        d_branch,
        inv_std,
        vectors,
        d_resid2,
        sums_mid,
        count,
        *attended,
        *(in_hbm(a) for a in (normed, slope, hidden, *packs)),
    )


def whole_call(kernel, name, args, outs, scalars=None, cost=SMALL_COST):
    return pl.pallas_call(
        kernel,
        out_shape=[o if hasattr(o, "memory_space") else jax.ShapeDtypeStruct(*o) for o in outs],
        in_specs=([] if scalars is None else [SMEM_SPEC]) + [VMEM_SPEC] * len(args),
        out_specs=[VMEM_SPEC] * len(outs),
        compiler_params=pltpu.CompilerParams(vmem_limit_bytes=SMALL_LIMIT),
        cost_estimate=cost,
        name=name,
    )(*(() if scalars is None else (scalars,)), *args)


def fold_cores(own, came):
    _, rows, cols = own.shape

    def kernel(own_ref, came_ref, *outs):
        for k, out in enumerate(outs):
            out[...] = (own_ref[k].astype(F32) + came_ref[k].astype(F32)).astype(BF16)

    outs = [pltpu.HBM((rows, cols), BF16)] * 4
    return whole_call(kernel, "fold_cores", (own, came), outs)


def split_cores(own, came):
    _, rows, cols = own.shape
    half = rows // 2

    def kernel(own_ref, came_ref, send_x, send_y, keep_upper, keep_lower):
        def total(upper, k):
            at = slice(0, half) if upper else slice(half, rows)
            return (own_ref[k, at, :].astype(F32) + came_ref[k, at, :].astype(F32)).astype(BF16)

        for i, k in enumerate((1, 3)):
            send_x[i] = total(True, k)
        for i, k in enumerate((2, 3)):
            send_y[i] = total(False, k)
        for i, k in enumerate((0, 2)):
            keep_upper[i] = total(True, k)
        for i, k in enumerate((0, 1)):
            keep_lower[i] = total(False, k)

    return whole_call(kernel, "split_cores", (own, came), [((2, half, cols), BF16)] * 4)


def second_step(keep_upper, came_x, keep_lower, came_y):
    def kernel(upper, upper_came, lower, lower_came, send_y, send_x, kept):
        half = upper.shape[1]
        send_y[...] = (upper[1].astype(F32) + upper_came[1].astype(F32)).astype(BF16)
        send_x[...] = (lower[1].astype(F32) + lower_came[1].astype(F32)).astype(BF16)
        kept[:half, :] = upper[0].astype(F32) + upper_came[0].astype(F32)
        kept[half:, :] = lower[0].astype(F32) + lower_came[0].astype(F32)

    half, cols = keep_upper.shape[1:]
    return whole_call(
        kernel,
        "second_step",
        (keep_upper, came_x, keep_lower, came_y),
        [((half, cols), BF16)] * 2 + [((2 * half, cols), F32)],
    )


def add_halves(kept, upper, lower):
    def kernel(kept, upper, lower, out):
        half = upper.shape[0]
        out[:half, :] = (kept[:half, :] + upper[...].astype(F32)).astype(BF16)
        out[half:, :] = (kept[half:, :] + lower[...].astype(F32)).astype(BF16)

    outs = [pltpu.HBM(kept.shape, BF16)]
    return whole_call(kernel, "add_halves", (kept, upper, lower), outs)[0]


def fold_quarters(terms, scalars):
    rows, cols = terms[0].shape
    part = rows // 4
    count = len(terms)

    def kernel(scalars, *refs):
        for k in range(4):
            at = pl.ds(pl.multiple_of((scalars[2] ^ k) * part, 8), part)
            total = sum(term[at, :].astype(F32) for term in refs[:count])
            refs[count + k % 2][k // 2] = total.astype(BF16)

    return whole_call(kernel, "fold_quarters", terms, [((2, part, cols), BF16)] * 2, scalars)


def finish(dense, qkv, half, block_col, scalars):
    _, part, cols = dense[0].shape
    qkv_part = qkv[0].shape[1]
    deep = block_col // 2

    def kernel(scalars, *refs):
        up, out, query, key, value, loss = refs[4:10]
        vectors, query_bias, value_bias = refs[10:17], refs[17], refs[18]
        dense_all, qkv_all = refs[19:]
        for parts, target in ((refs[:2], dense_all), (refs[2:4], qkv_all)):
            for k in range(4):
                piece = parts[k % 2].at[k // 2]
                rows = piece.shape[0]
                at = pl.ds(pl.multiple_of((scalars[2] ^ k) * rows, 8), rows)
                target[at, :] = piece[...].astype(F32)
        up[...] = dense_all[:half, :]
        out[:deep, :] = dense_all[half : half + deep, :half]
        out[deep:, :] = dense_all[half : half + deep, half:]
        table = dense_all[half + deep : half + deep + 16, :]
        for row, target in zip((6, 4, 5, 8, 2, 0, 1), vectors):
            target[...] = table[row, :]
        error = jnp.sum(table[3:4, :], axis=1, keepdims=True)
        tokens = jnp.sum(table[7:8, :], axis=1, keepdims=True)
        loss[...] = error / (tokens * cols)
        for i, target in enumerate((query, key, value)):
            target[...] = qkv_all[i * block_col : (i + 1) * block_col, :]
        bias = qkv_all[3 * block_col : 3 * block_col + 8, :]
        query_bias[...] = bias[0, :block_col]
        value_bias[...] = bias[0, block_col:]

    S = jax.ShapeDtypeStruct
    return pl.pallas_call(
        kernel,
        out_shape=[S((half, cols), F32), S((block_col, half), F32)]
        + [S((block_col, half), F32)] * 3
        + [S((1, 1), F32)]
        + [S((cols,), F32)] * 7
        + [S((block_col,), F32)] * 2,
        in_specs=[SMEM_SPEC] + [VMEM_SPEC] * 4,
        out_specs=[VMEM_SPEC] * 15,
        scratch_shapes=[
            pltpu.VMEM((4 * part, cols), F32),
            pltpu.VMEM((4 * qkv_part, half), F32),
        ],
        compiler_params=pltpu.CompilerParams(vmem_limit_bytes=SMALL_LIMIT),
        cost_estimate=SMALL_COST,
        name="finish",
    )(scalars, *dense, *qkv)


def dot(left, right, dims=NN):
    return lax.dot_general(left, right, dims, preferred_element_type=F32)


def split3(value):
    high = value.astype(BF16)
    rest = value - high.astype(F32)
    middle = rest.astype(BF16)
    low = (rest - middle.astype(F32)).astype(BF16)
    return high.astype(F32), middle.astype(F32), low.astype(F32)


def key_range(code, span, span_rows, blocks):
    per = span_rows // BLK
    first_seg = code[span * per, 0] // 2
    last_seg = code[span * per + per - 1, BLK - 1] // 2
    low = jnp.int32(0)
    high = jnp.int32(0)
    for other in range(blocks):
        start = code[other, 0]
        low += (code[other, BLK - 1] // 2 < first_seg).astype(jnp.int32)
        high += ((start // 2 <= last_seg) & (start % 2 == 1)).astype(jnp.int32)
    below = jnp.maximum(jnp.minimum(high, span * per) - low, 0)
    above = jnp.maximum(high - (span + 1) * per, 0)
    return low, below, below + above


def key_block(step, low, below, after):
    return jnp.where(step < below, low + step, after + step - below)


def lane_index(rows):
    return lax.broadcasted_iota(jnp.int32, (rows, 128), 1)


def allowed_block(code_rows, block, offset, span_rows):
    row = lax.broadcasted_iota(jnp.int32, (span_rows, BLK), 0)
    col = lax.broadcasted_iota(jnp.int32, (span_rows, BLK), 1)
    return (code_rows[pl.ds(block, 1), :] % 2 == 1) | (row == col + offset)


def attention_forward_kernel(heads, scalars, code, *refs):
    code_rows = refs[0]
    token_parts = refs[1:6]
    weights = refs[6:8]
    pieces = refs[8:12]
    saved = refs[12:16]
    padded, max_scr, acc_scr, query_pad, key_pad, value_pad, out_pad, whole_sem, span_sem = refs[16:]
    span_rows, width = token_parts[0].shape
    cols = 64 * heads
    flip = scalars[1]
    per = span_rows // BLK
    blocks = query_pad.shape[1] // BLK
    lane = lane_index(span_rows)
    for i in range(3):
        src = slice(i * cols, (i + 1) * cols)
        dst = slice(i * 256, i * 256 + cols)
        for second, half_weights in enumerate(weights):
            side = pl.ds(half_start(scalars, bool(second), width // 2), width // 2)
            padded[dst, side] = half_weights[src, :]
        padded[i * 256 + cols : (i + 1) * 256, :] = jnp.zeros((256 - cols, width), BF16)
    marks_bias = weights[0][3 * cols : 3 * cols + 1, :].astype(F32)
    no_bias = jnp.zeros((1, 256 - cols), F32)
    biases = (
        jnp.concatenate([marks_bias[:, :cols], no_bias], 1),
        None,
        jnp.concatenate([marks_bias[:, cols : 2 * cols], no_bias], 1),
    )
    first = 0
    for tokens in token_parts:
        rows = slice(first, first + tokens.shape[0])
        marks = []
        for block in range(rows.start // BLK, rows.stop // BLK):
            place = (block // per ^ flip) * per + block % per
            marks.append(
                jnp.broadcast_to(code_rows[pl.ds(place, 1), :].astype(F32), (128, BLK)).T
            )
        first = rows.stop
        lane = lane_index(tokens.shape[0])
        value_ones = jnp.where((lane >= 64) & (lane < 67), 1.0, 0.0)
        marks = jnp.concatenate(marks, 0).astype(jnp.int32)
        same = lane - 64 == marks // 2
        ids = (lane >= 64) & (lane < 80)
        query_marks = jnp.where((ids & same) | (lane == 80), 1.0, 0.0)
        key_marks = jnp.where(
            (ids & ~same) | ((lane == 80) & (marks % 2 == 0)),
            MASKED,
            jnp.where((lane >= 81) & (lane < 84), -1.0, 0.0),
        )
        for i, (out, extra) in enumerate(
            ((query_pad, query_marks), (key_pad, key_marks), (value_pad, value_ones))
        ):
            projected = dot(tokens[...], padded[i * 256 : (i + 1) * 256, :], NT)
            if biases[i] is not None:
                projected += biases[i]
            if i == 0:
                projected = projected.astype(BF16).astype(F32) * 0.125
            out[0, rows, :] = jnp.where(lane < 64, projected[:, :128], extra).astype(BF16)
            out[1, rows, :] = jnp.where(
                lane < 64, pltpu.roll(projected[:, :128], 64, 1), extra
            ).astype(BF16)
            out[2, rows, :] = jnp.where(lane < 64, projected[:, 128:], extra).astype(BF16)
    lane = lane_index(span_rows)
    no_valid_lane = jnp.where(lane == 80, 0.0, 1.0).astype(BF16)
    whole_copies = [
        pltpu.make_async_copy(key_pad, saved[1], whole_sem.at[0]),
        pltpu.make_async_copy(value_pad, saved[2], whole_sem.at[1]),
    ]
    for copy in whole_copies:
        copy.start()

    def span_copies(at):
        rows = pl.ds(pl.multiple_of(at * span_rows, span_rows), span_rows)
        return [
            pltpu.make_async_copy(
                source.at[:, rows, :], saved[i].at[:, rows, :], span_sem.at[i // 3, at]
            )
            for source, i in ((query_pad, 0), (out_pad, 3))
        ]

    def query_step(span, _):
        at = span ^ flip
        rows = pl.ds(pl.multiple_of(at * span_rows, span_rows), span_rows)
        low, below, count = key_range(code, span, span_rows, blocks)

        def keys_of(block):
            place = (block // per ^ flip) * per + block % per
            return pl.ds(pl.multiple_of(place * BLK, BLK), BLK)

        def scores_of(h, keys, allowed=None):
            if allowed is None:
                return dot(query_pad[h, rows, :], key_pad[h, keys, :], NT)
            scores = dot(query_pad[h, rows, :] * no_valid_lane, key_pad[h, keys, :], NT)
            return jnp.where(allowed, scores, MASKED)

        def each_block(visit):
            for part in range(per):
                block = span * per + part
                visit(keys_of(block), allowed_block(code_rows, block, part * BLK, span_rows))

            def step_fn(step, _):
                visit(keys_of(key_block(step, low, below, (span + 1) * per)), None)
                return 0

            lax.fori_loop(0, count, step_fn, 0)

        acc_scr[...] = jnp.zeros_like(acc_scr)
        max_scr[...] = jnp.zeros_like(max_scr)

        def plain(keys, allowed):
            for h in range(heads):
                probs = jnp.exp(scores_of(h, keys, allowed)).astype(BF16)
                acc_scr[h] += dot(probs, value_pad[h, keys, :])

        each_block(plain)
        least, most = jnp.float32(1.0), jnp.float32(1.0)
        for h in range(heads):
            total = jnp.where(lane == 64, acc_scr[h], 1.0)
            good = (total > 1e-25) & (total < 1e30)
            least = jnp.minimum(least, jnp.min(jnp.where(good, 1.0, 0.0)))

        @pl.when(least < 0.5)
        def _():
            max_scr[...] = jnp.full_like(max_scr, MASKED)

            def find_max(keys, allowed):
                for h in range(heads):
                    scores = scores_of(h, keys, allowed)
                    max_scr[h] = jnp.maximum(
                        max_scr[h], jnp.maximum(scores[:, :128], scores[:, 128:])
                    )

            each_block(find_max)
            for h in range(heads):
                max_scr[h] = jnp.broadcast_to(
                    jnp.max(max_scr[h], axis=1, keepdims=True), (span_rows, 128)
                )
            acc_scr[...] = jnp.zeros_like(acc_scr)

            def shifted(keys, allowed):
                for h in range(heads):
                    row_max = max_scr[h]
                    scores = scores_of(h, keys, allowed)
                    probs = jnp.exp(scores - jnp.concatenate([row_max, row_max], 1))
                    acc_scr[h] += dot(probs.astype(BF16), value_pad[h, keys, :])

            each_block(shifted)

        outs = []
        for h in range(heads):
            acc = acc_scr[h]
            total = jnp.broadcast_to(acc[:, 64:65], acc.shape)
            out = acc / total
            out_pad[h, rows, :] = out
            outs.append(out)
            high, middle, rest = split3(max_scr[h] + jnp.log(total))
            extra = jnp.where(
                lane == 81,
                high,
                jnp.where(lane == 82, middle, jnp.where(lane == 83, rest, 0.0)),
            )
            query_pad[h, rows, :] = query_pad[h, rows, :] + extra.astype(BF16)
        pair = jnp.where(lane < 64, outs[0], pltpu.roll(outs[1], 64, 1)).astype(BF16)
        middle = span_rows // 2
        last = jnp.where(
            lane_index(middle) < 64, outs[2][:middle], pltpu.roll(outs[2][middle:], 64, 1)
        ).astype(BF16)
        for k, piece in enumerate(pieces):

            @pl.when(at == k)
            def _():
                piece[:span_rows, :] = pair
                piece[span_rows:, :] = last

        for copy in span_copies(at):
            copy.start()
        return 0

    lax.fori_loop(0, len(pieces), query_step, 0)
    for copy in whole_copies:
        copy.wait()
    for at in range(len(pieces)):
        for copy in span_copies(at):
            copy.wait()


def attention_forward(scalars, code, token_shards, weights):
    rows, width = token_shards[0].shape
    length = code.shape[0] * BLK
    cols = (weights[0].shape[0] - PAD_ROWS) // 3
    heads = cols // 64
    S = jax.ShapeDtypeStruct
    flops = 2 * length * width * 3 * 256 + 3 * length * length * 128
    return pl.pallas_call(
        lambda *refs: attention_forward_kernel(heads, *refs),
        out_shape=[S((rows * cols // 128, 128), BF16)] * 4
        + [pltpu.HBM((heads, length, 128), BF16)] * 3
        + [pltpu.HBM((heads, length, 128), F32)],
        in_specs=[SMEM_SPEC] * 2 + [VMEM_SPEC] * 8,
        out_specs=[VMEM_SPEC] * 4 + [HBM_SPEC] * 4,
        scratch_shapes=[
            pltpu.VMEM((3 * 256, width), BF16),
            pltpu.VMEM((heads, rows, 128), F32),
            pltpu.VMEM((heads, rows, 128), F32),
        ]
        + [pltpu.VMEM((heads, length, 128), BF16)] * 3
        + [
            pltpu.VMEM((heads, length, 128), F32),
            pltpu.SemaphoreType.DMA((2,)),
            pltpu.SemaphoreType.DMA((2, 4)),
        ],
        compiler_params=pltpu.CompilerParams(vmem_limit_bytes=32 << 20),
        cost_estimate=pl.CostEstimate(
            flops=3 * flops, bytes_accessed=16 << 20, transcendentals=heads * length * 1024
        ),
        name="attention_forward",
    )(scalars, code, code, *token_shards, *weights)


def attention_backward_kernel(heads, scalars, code, *refs):
    code_rows = refs[0]
    span_rows = refs[1].shape[0] * 128 // (64 * heads)
    term_hbm, grad_hbm = refs[16:20], refs[20:22]
    grad_pad, query_sum, key_sum, value_sum, low_scr, grad_scr, bias_sum = refs[22:29]
    query_pad, key_pad, value_pad, out_pad = refs[29:33]
    shards_in = refs[33:37]
    weights = refs[37]
    grads = refs[38:42]
    terms, own_grad, other_grad, out_sems, in_sems = refs[42:]
    side = weights.shape[1] // 2
    last_half = span_rows // 2
    pairs = list(zip(refs[1:9], grads + refs[29:33]))
    pairs += list(zip(refs[9:12], shards_in[:3]))
    pairs += [
        (refs[12], shards_in[3].at[:last_half, :]),
        (refs[13], shards_in[3].at[last_half:, :]),
    ]
    sides = [pl.ds(half_start(scalars, second, side), side) for second in (False, True)]
    pairs += [(refs[14 + i], weights.at[:, sides[i]]) for i in range(2)]
    copies = [
        pltpu.make_async_copy(source, target, in_sems.at[i])
        for i, (source, target) in enumerate(pairs)
    ]
    for i in (7, 0, 1, 2, 3, 4, 5, 6):
        copies[i].start()
    key_sum[...] = jnp.zeros_like(key_sum)
    value_sum[...] = jnp.zeros_like(value_sum)
    query_sum[...] = jnp.zeros_like(query_sum)
    for i in (7, 0, 1, 2, 3):
        copies[i].wait()
    flip = scalars[1]
    per = span_rows // BLK
    blocks = query_pad.shape[1] // BLK
    lane = lane_index(span_rows)
    for shard, grad in enumerate(grads):
        rows = slice(shard * span_rows, (shard + 1) * span_rows)
        pair = grad[:span_rows, :].astype(F32)
        last = grad[span_rows:, :].astype(F32)
        last = jnp.concatenate([last, pltpu.roll(last, 64, 1)], 0)
        for h, block in enumerate((pair, pltpu.roll(pair, 64, 1), last)):
            block = jnp.where(lane < 64, block, 0.0)
            delta = jnp.sum(block * out_pad[h, rows, :], axis=1, keepdims=True)
            high, middle, rest = split3(-delta)
            block = jnp.where(
                lane == 64,
                high,
                jnp.where(lane == 65, middle, jnp.where(lane == 66, rest, block)),
            )
            grad_pad[h, rows, :] = block.astype(BF16)
    for i in (4, 5, 6):
        copies[i].wait()
    for i in range(8, 15):
        copies[i].start()
    no_valid_lane = jnp.where(lane == 80, 0.0, 1.0).astype(BF16)

    def query_step(span, _):
        at = span ^ flip
        rows = pl.ds(pl.multiple_of(at * span_rows, span_rows), span_rows)
        low, below, count = key_range(code, span, span_rows, blocks)

        def visit(block, allowed):
            place = (block // per ^ flip) * per + block % per
            keys = pl.ds(pl.multiple_of(place * BLK, BLK), BLK)
            for h in range(heads):
                query, grad = query_pad[h, rows, :], grad_pad[h, rows, :]
                key, value = key_pad[h, keys, :], value_pad[h, keys, :]
                if allowed is None:
                    scores = dot(key, query, NT)
                else:
                    scores = jnp.where(allowed, dot(key, query * no_valid_lane, NT), MASKED)
                probs = jnp.exp(scores)
                d_scores = (probs * dot(value, grad, NT)).astype(BF16)
                value_sum[h, keys, :] += dot(probs.astype(BF16), grad)
                key_sum[h, keys, :] += dot(d_scores, query)
                query_sum[h, rows, :] += dot(d_scores, key, TN)

        for part in range(per):
            block = span * per + part
            key_at = lax.broadcasted_iota(jnp.int32, (BLK, span_rows), 0)
            query_at = lax.broadcasted_iota(jnp.int32, (BLK, span_rows), 1)
            marks = jnp.broadcast_to(
                code_rows[pl.ds(block, 1), :].astype(F32), (128, BLK)
            ).T.astype(jnp.int32)
            valid = jnp.concatenate([marks] * (span_rows // 128), 1) % 2 == 1
            visit(block, valid | (query_at == key_at + part * BLK))

        def step_fn(step, _):
            visit(key_block(step, low, below, (span + 1) * per), None)
            return 0

        lax.fori_loop(0, count, step_fn, 0)
        return 0

    lax.fori_loop(0, len(grads), query_step, 0)
    for i in range(8, 15):
        copies[i].wait()
    bias_sum[...] = jnp.zeros_like(bias_sum)
    stores = []
    for shard in range(len(grads)):
        rows = slice(shard * span_rows, (shard + 1) * span_rows)
        parts = [query_sum[h, rows, :] * 0.125 for h in range(heads)]
        parts += [sums[h, rows, :] for sums in (key_sum, value_sum) for h in range(heads)]
        for at in range(0, len(parts), 2):
            if at + 1 < len(parts):
                value = jnp.where(lane < 64, parts[at], pltpu.roll(parts[at + 1], 64, 1))
            else:
                value = parts[at][:, :64]
            low = value.astype(BF16)
            cols = slice(at * 64, at * 64 + low.shape[1])
            low_scr[:, cols] = low
            bias_sum[0:1, cols] += column_sum(low.astype(F32))
        low = low_scr[...]
        depth = low.shape[1]
        term = dot(low, weights[:depth, :]).astype(BF16)
        terms[shard] = term
        copy = pltpu.make_async_copy(
            terms.at[shard], term_hbm[shard], out_sems.at[shard]
        )
        copy.start()
        stores.append(copy)
        part = dot(low, shards_in[shard][...], TN)
        if shard == 0:
            grad_scr[...] = part
        elif shard < 3:
            grad_scr[...] += part
        else:
            grad_scr[...] += part
            own_grad[:depth, :] = grad_scr[:, sides[0]].astype(BF16)
            other_grad[:depth, :] = grad_scr[:, sides[1]].astype(BF16)
    cols = heads * 64
    bias = jnp.concatenate([bias_sum[:, 0:cols], bias_sum[:, 2 * cols :]], 1).astype(BF16)
    bias = jnp.concatenate([bias] * ((own_grad.shape[0] - depth) // bias.shape[0]), 0)
    own_grad[depth:, :] = bias
    other_grad[depth:, :] = bias
    for i, source in enumerate((own_grad, other_grad)):
        copy = pltpu.make_async_copy(source, grad_hbm[i], out_sems.at[4 + i])
        copy.start()
        stores.append(copy)
    for copy in stores:
        copy.wait()


def attention_backward(scalars, code, grads, saved, token_shards, weights):
    length = code.shape[0] * BLK
    heads = saved[0].shape[0]
    rows, width = token_shards[0].shape
    cols = 3 * heads * 64
    S = jax.ShapeDtypeStruct
    return pl.pallas_call(
        lambda *refs: attention_backward_kernel(heads, *refs),
        out_shape=[
            *[pltpu.HBM((rows, width), BF16)] * 4,
            *[pltpu.HBM((cols + GRAD_PAD, width // 2), BF16)] * 2,
        ],
        in_specs=[SMEM_SPEC] * 2 + [VMEM_SPEC] + [HBM_SPEC] * 15,
        out_specs=[HBM_SPEC] * 6,
        scratch_shapes=[
            pltpu.VMEM((heads, length, 128), BF16),
            pltpu.VMEM((heads, length, 128), F32),
            pltpu.VMEM((heads, length, 128), F32),
            pltpu.VMEM((heads, length, 128), F32),
            pltpu.VMEM((rows, cols), BF16),
            pltpu.VMEM((cols, width), F32),
            pltpu.VMEM((16, cols), F32),
        ]
        + [pltpu.VMEM(a.shape, a.dtype) for a in saved]
        + [pltpu.VMEM((rows, width), BF16)] * 4
        + [pltpu.VMEM((weights[0].shape[0], width), BF16)]
        + [pltpu.VMEM(a.shape, a.dtype) for a in grads]
        + [
            pltpu.VMEM((4, rows, width), BF16),
            pltpu.VMEM((cols + GRAD_PAD, width // 2), BF16),
            pltpu.VMEM((cols + GRAD_PAD, width // 2), BF16),
            pltpu.SemaphoreType.DMA((6,)),
            pltpu.SemaphoreType.DMA((15,)),
        ],
        compiler_params=pltpu.CompilerParams(vmem_limit_bytes=46 << 20),
        cost_estimate=pl.CostEstimate(
            flops=heads * length * length * 1500, bytes_accessed=8 << 20, transcendentals=0
        ),
        name="attention_backward",
    )(
        scalars,
        code,
        code,
        *(in_hbm(a) for a in (*grads, *saved, *token_shards, *weights)),
    )


CHIP = [[(c, c ^ k) for c in range(4)] for k in range(4)]
PLANE = [[(p, p ^ k) for p in range(4)] for k in range(4)]
CORE = [(0, 1), (1, 0)]


def to_chip(value, k):
    return lax.ppermute(value, "gz", CHIP[k])


def to_core(value):
    return lax.ppermute(value, "gy", CORE)


def to_plane(value, k):
    return lax.ppermute(value, "gx", PLANE[k])


def after(value, *others):
    return lax.optimization_barrier((value,) + others)[0]


def swap_halves(flip, value):
    half = value.shape[-1] // 2
    swapped = jnp.concatenate([value[..., half:], value[..., :half]], -1)
    return jnp.where(flip, swapped, value)


def add_low(left, right):
    return (left.astype(F32) + right.astype(F32)).astype(BF16)


def sum_planes(dense, qkv, waits):
    if lax.axis_size("gx") != 4:
        dense, other = jnp.stack(dense), jnp.stack(qkv(dense[0]))
        total = lax.psum((dense, other), "gx")
        return [(t[0], t[1]) for t in total], waits
    near = dense[0].astype(F32) + to_plane(dense[1], 1).astype(F32)
    step = near[1].astype(BF16)
    keep, send = qkv(step)
    total = (near[0] + to_plane(step, 2).astype(F32)).astype(BF16)
    near = keep.astype(F32) + to_plane(send, 1).astype(F32)
    step = after(near[1].astype(BF16), total)
    pair = jnp.stack([total, to_plane(total, 2)])
    other = (near[0] + to_plane(step, 2).astype(F32)).astype(BF16)
    other = after(other, pair)
    back = to_plane(pair, 1)
    other_pair = jnp.stack([other, to_plane(other, 2)])
    other_back = to_plane(other_pair, 1)
    *waits, back = lax.optimization_barrier((*waits, back))
    return [(pair, back), (other_pair, other_back)], waits


def shards(
    tokens,
    segment_ids,
    valid_mask,
    cotangent,
    teacher,
    w_query,
    b_query,
    w_key,
    w_value,
    b_value,
    w_out,
    b_out,
    norm1_gain,
    norm1_bias,
    w_up,
    b_up,
    w_down,
    b_down,
    norm2_gain,
    norm2_bias,
):
    row_count, width = tokens.shape
    half = width // 2
    core = lax.axis_index("gy")
    chip = lax.axis_index("gz")
    flip = core == 1
    block_col = w_query.shape[1]
    hidden_col = w_up.shape[1]
    plane = lax.axis_index("gx") if lax.axis_size("gx") == 4 else jnp.int32(0)
    scalars = jnp.stack([core, chip, plane, chip]).astype(jnp.int32)

    own_tokens = tokens
    along_x, along_y = to_chip(own_tokens, 1), to_chip(own_tokens, 2)
    code = (segment_ids * 2 + valid_mask).reshape(-1, BLK)
    bias_row = jnp.concatenate([b_query, b_value])[None, :]
    qkv_own = jnp.concatenate(
        [w_query.T, w_key.T, w_value.T, jnp.broadcast_to(bias_row, (PAD_ROWS, half))], 0
    )
    vectors = jnp.stack([b_out, norm1_gain, norm1_bias, b_down, norm2_gain, norm2_bias] + [b_out] * 2)
    vectors = swap_halves(flip, vectors.astype(F32))
    own_valid = lax.dynamic_slice_in_dim(valid_mask, chip * row_count, row_count, 1).astype(F32)
    count = jnp.concatenate([own_valid, jnp.zeros((1, width - row_count), F32)], 1)
    count = jnp.broadcast_to(count, (8, width))
    own_valid = own_valid.T
    packed = jnp.concatenate(
        [
            jnp.concatenate([w_down[: hidden_col // 2], w_down[hidden_col // 2 :]], 1),
            w_up,
            jnp.concatenate([w_out[: block_col // 2], w_out[block_col // 2 :]], 1),
            jnp.broadcast_to(b_up[None, :], (PAD_ROWS, hidden_col)),
        ],
        0,
    )

    code, qkv_own, scalars, packed, vectors, own_valid, count, *_ = lax.optimization_barrier(
        (code, qkv_own, scalars, packed, vectors, own_valid, count, own_tokens)
    )
    qkv = (qkv_own, to_core(qkv_own))
    along_x, along_y, *qkv = lax.optimization_barrier((along_x, along_y, *qkv))
    middle = row_count // 2
    far = (to_chip(along_x[:middle], 2), to_chip(along_y[middle:], 1))
    token_shards = (own_tokens, along_x, along_y, *far)
    packed = after(packed, *far)
    pack_x, pack_y = to_chip(packed, 1), to_chip(packed, 2)

    scalars = after(scalars, packed)
    results = attention_forward(scalars, code, token_shards, qkv)
    saved = results[4:]
    attended = [results[0]] + [to_chip(results[k], k) for k in (1, 2, 3)]

    deep = hidden_col // 2
    pack_x, pack_y = lax.optimization_barrier((pack_x, pack_y, results[0]))[:2]
    far = (pack_x[:, :half], pack_y[:, half:])
    packed_late = after(packed, *far)
    far = (to_chip(far[0], 2), to_chip(far[1], 1))
    packs = (packed, pack_x, pack_y, *far)
    packs += (to_core(packed_late), *(to_core(after(v, *attended[1:])) for v in packs[1:]))

    inv_std, output, d_resid2, d_branch, sums_mid, act, normed, hidden_low, slope = ffn_forward(
        scalars, attended, own_tokens, own_valid, vectors, cotangent, teacher, packs, deep
    )
    pieces = (4, hidden_col, half)
    d_down_other = jnp.einsum("lf,lm->fm", act, d_branch[:, half:], preferred_element_type=F32)
    d_down_came = to_core(d_down_other.astype(BF16).reshape(pieces))
    d_down = jnp.einsum("lf,lm->fm", act, d_branch[:, :half], preferred_element_type=F32)
    down_x, down_y, down_upper, down_lower = split_cores(
        d_down.astype(BF16).reshape(pieces), d_down_came
    )
    d_branch = after(d_branch, down_upper)
    down_x, down_y = to_chip(down_x, 1), to_chip(down_y, 2)
    d_resid1, *back, own_grads, other_grads = ffn_back(
        scalars,
        d_branch,
        inv_std,
        vectors,
        d_resid2,
        sums_mid,
        count,
        attended,
        normed,
        slope,
        hidden_low,
        packs,
        deep,
    )
    d_pieces = [back[0]] + [to_chip(back[k], k) for k in (1, 2, 3)]

    down_y, down_x, down_kept = second_step(down_upper, down_x, down_lower, down_y)
    d_dense = fold_cores(own_grads, to_core(after(other_grads, down_y)))
    down_total = add_halves(down_kept, to_chip(down_y, 2), to_chip(down_x, 1))
    grad_down = lax.psum(down_total, "gx")
    d_pieces[0] = after(d_pieces[0], d_dense[0], down_total)
    d_dense = [d_dense[0]] + [to_chip(d_dense[k], k) for k in (1, 2, 3)]

    *terms, d_own, d_other = attention_backward(
        scalars, code, d_pieces, saved, token_shards, qkv
    )
    d_dense[0] = after(d_dense[0], grad_down, terms[0])
    quarters = fold_quarters(d_dense, scalars)
    d_own, d_other, *terms, _, _ = lax.optimization_barrier((d_own, d_other, *terms, *quarters))
    d_w = (d_own, to_core(d_other))
    terms = [terms[0]] + [to_chip(terms[k], k) for k in (1, 2, 3)]
    (dense_grad, qkv_grad), came = sum_planes(
        quarters, lambda first: fold_quarters(d_w, scalars), terms[1:]
    )
    d_tokens = d_resid1 + sum(t.astype(F32) for t in (terms[0], *came))
    grad_up, grad_out, grad_query, grad_key, grad_value, loss, *vectors = finish(
        dense_grad, qkv_grad, half, block_col, scalars
    )
    b_out_grad, gain1_grad, shift1_grad, b_up_grad, b_down_grad, gain2_grad, shift2_grad = vectors[:7]

    return (
        output,
        loss[0, 0],
        d_tokens.astype(BF16),
        grad_query.T,
        vectors[7],
        grad_key.T,
        grad_value.T,
        vectors[8],
        grad_out,
        b_out_grad,
        gain1_grad,
        shift1_grad,
        grad_up,
        b_up_grad,
        grad_down.astype(F32),
        b_down_grad,
        gain2_grad,
        shift2_grad,
    )


def solution(mesh):
    placed = (
        P(("gx", "gy", "gz"), None),
        P(("gx", "gy"), None),
        P(("gx", "gy"), None),
        P(("gx", "gy", "gz"), None),
        P(("gx", "gy", "gz"), None),
        P("gy", "gz"),
        P("gz"),
        P("gy", "gz"),
        P("gy", "gz"),
        P("gz"),
        P("gz", "gy"),
        P(),
        P(),
        P(),
        P("gy", "gz"),
        P("gz"),
        P("gz", "gy"),
        P(),
        P(),
        P(),
    )
    return jax.shard_map(
        shards,
        mesh=mesh,
        in_specs=placed,
        out_specs=(
            P(("gx", "gy", "gz"), None),
            P(),
            P(("gx", "gy", "gz"), None),
            P("gy", "gz"),
            P("gz"),
            P("gy", "gz"),
            P("gy", "gz"),
            P("gz"),
            P("gz", "gy"),
            P(),
            P(),
            P(),
            P("gy", "gz"),
            P("gz"),
            P("gz", "gy"),
            P(),
            P(),
            P(),
        ),
        check_vma=False,
    )
```
